32 devices in a mesh: dp: 8 (over z, y), fsdp: 4 (over x, core).
Axes of the slice: x: 2, y: 2, z: 4, core: 2. Of those that a mesh axis runs over, the one named last changes fastest.
Arguments:
- tokens: bfloat16 [64, 1024, 768], P('fsdp', 'dp'), may hold values from -6 to 6
- passes: int32 [64, 1024], P('fsdp'), may hold values from 0 to 4
- lengths: int32 [4, 16], P('fsdp'), may hold values from 1 to 1024, 12288 in all within a row
- dealing: int32 [8, 4, 16], P('dp', 'fsdp'), may hold values from 0 to 15, each once within a row
- pass_table: bfloat16 [5, 768], replicated, may hold values from -3 to 3
- gain_first: bfloat16 [768], replicated, may hold values from 0.5 to 1.5
- to_heads: bfloat16 [768, 2304], P(('dp', 'fsdp')), may hold values from -0.21875 to 0.21875
- from_heads: bfloat16 [768, 768], P(('dp', 'fsdp')), may hold values from -0.875 to 0.875
- gain_second: bfloat16 [768], replicated, may hold values from 0.5 to 1.5
- expand: bfloat16 [768, 3072], P(('dp', 'fsdp')), may hold values from -0.21875 to 0.21875
- shrink: bfloat16 [3072, 768], P(('dp', 'fsdp')), may hold values from -0.109375 to 0.109375
- cotangent: bfloat16 [64, 1024, 768], P('fsdp', 'dp'), may hold values from -6 to 6
Outputs:
- layer_output: float32 [64, 1024, 768], P('fsdp', 'dp')
- grad_tokens: float32 [64, 1024, 768], P('fsdp', 'dp')
- grad_table: float32 [5, 768], replicated
- grad_gain_first: float32 [768], replicated
- grad_to_heads: float32 [768, 2304], P(('dp', 'fsdp'))
- grad_from_heads: float32 [768, 768], P(('dp', 'fsdp'))
- grad_gain_second: float32 [768], replicated
- grad_expand: float32 [768, 3072], P(('dp', 'fsdp'))
- grad_shrink: float32 [3072, 768], P(('dp', 'fsdp'))
- root_squares: float32 [3], replicated
The draws below stay inside these ranges and needn't reach their ends.
Inputs may be any that keep to these rules, and one draw needn't show every extreme that they name: Each row dealing[e, f, :] lists every number of 0 to 15 once. Each row of lengths adds up to 12288, and one of its entries is 1024.
All inputs are finite; a program needn't handle non-finite values.
Results may differ from the reference program's by a relative error of at most 0.01.
Values may be sent and summed in bfloat16 or wider, within the bound.
No kernel may reach another device: no remote copies, remote signals or barrier semaphores. Data moves between devices by JAX's collectives and lax.ppermute only.
A program may use at most 384 MiB of HBM per device.

```python
import math
import jax
import jax.numpy as jnp
import numpy as np
from jax import lax

D = 768
HEADS = 12
HEAD = 64
FF = 3072
PASSES = 5
LEN = 1024
SEQ_F = 16
SEQS = 64
N_DP = 8
N_FSDP = 4


def with_ends(values, stream_key, least, high):
    index_at = [jax.random.randint(jax.random.fold_in(stream_key, axis), (), 0, length) for axis, length in enumerate(values.shape)]
    main_axis = values.shape.index(max(values.shape))
    neighbour = index_at[:main_axis] + [(index_at[main_axis] + 1) % values.shape[main_axis]] + index_at[main_axis + 1:]
    return values.at[tuple(index_at)].set(least).at[tuple(neighbour)].set(high)


def steps_of(key, dims, pieces, low, high):
    loudness, own = 1.0, jax.random.fold_in(key, 6)
    for axis_at, blocks in pieces:
        steps = jnp.exp(jax.random.uniform(jax.random.fold_in(own, axis_at), (blocks,), jnp.float32, low / len(pieces), high / len(pieces)))
        loudness = loudness * jnp.repeat(steps, dims[axis_at] // blocks).reshape([-1 if axis == axis_at else 1 for axis in range(len(dims))])
    return loudness


def profile(amount, total, most, lean):
    loads = [(1 << 20) // math.isqrt(grade ** lean) + 1 for grade in range(2, amount + 1)]
    rest, holding = total - most - (amount - 1), [1] * (amount - 1)
    while rest > 0:
        free = [i for i in range(amount - 1) if holding[i] < most]
        pool, remaining = sum([loads[i] for i in free]), rest
        for i in free:
            more = min(most - holding[i], max(1, remaining * loads[i] // pool), rest)
            holding[i] = holding[i] + more
            rest = rest - more
    return np.array([most] + holding)


def ragged(own_key, amount, total, limit, slope):
    if amount == 2:
        one = jax.random.randint(own_key, (), max(1, total - limit), min(limit, total - 1) + 1)
        return jnp.stack([one, total - one])
    sizes = jnp.asarray(profile(amount, total, limit, slope), jnp.int32)
    twos = (amount - 1) // 2
    source_of, receiver = sizes[1:1 + 2 * twos:2], sizes[2:2 + 2 * twos:2]
    slack = jnp.minimum(source_of - 1, limit - receiver)
    passed = jax.random.randint(jax.random.fold_in(own_key, 1), (twos,), 0, 1 << 20) % (slack + 1)
    sizes = sizes.at[1:1 + 2 * twos:2].set(source_of - passed).at[2:2 + 2 * twos:2].set(receiver + passed)
    return sizes[jax.random.permutation(jax.random.fold_in(own_key, 2), amount)]


def gaussian(rng, dims, scale, bound, cuts=(), kind=jnp.bfloat16):
    values = jax.random.normal(rng, dims, jnp.float32) * scale
    if len(cuts) > 0:
        values = steps_of(rng, dims, cuts, -0.22, 0.18) * values
    return jnp.clip(values, min=-bound, max=bound).astype(kind)


def setup_inputs(seed: int = 0) -> dict:
    keys = jax.random.split(jax.random.key(seed), 13)
    tokens = gaussian(keys[0], (SEQS, LEN, D), 1.0, 6.0, ((0, 4), (1, 8)))
    passes = with_ends(jax.random.randint(keys[1], (SEQS, LEN), 0, PASSES), jax.random.fold_in(keys[1], 1), 0, PASSES - 1).astype(jnp.int32)
    lengths = jax.vmap(lambda own: ragged(own, SEQ_F, SEQ_F * LEN * 3 // 4, LEN, 2))(jax.random.split(keys[2], N_FSDP)).reshape((N_FSDP, SEQ_F)).astype(jnp.int32)
    dealing = jax.vmap(lambda own: jax.random.permutation(own, SEQ_F))(jax.random.split(keys[3], N_DP * N_FSDP)).reshape((N_DP, N_FSDP, SEQ_F)).astype(jnp.int32)
    pass_table = gaussian(keys[4], (PASSES, D), 0.5, 3.0)
    gain_first = jnp.clip(1.0 + 0.1 * jax.random.normal(keys[5], (D,), jnp.float32), 0.5, 1.5).astype(jnp.bfloat16)
    to_heads = gaussian(keys[6], (D, 3 * D), D ** -0.5, 0.21875, ((0, 32),))
    from_heads = gaussian(keys[7], (D, D), (D // 16) ** -0.5, 0.875, ((0, 32),))
    gain_second = jnp.clip(1.0 + 0.1 * jax.random.normal(keys[8], (D,), jnp.float32), 0.5, 1.5).astype(jnp.bfloat16)
    expand = gaussian(keys[9], (D, FF), D ** -0.5, 0.21875, ((0, 32),))
    shrink = gaussian(keys[10], (FF, D), FF ** -0.5, 0.109375, ((0, 32),))
    cotangent = gaussian(keys[11], (SEQS, LEN, D), 1.0, 6.0, ((0, 4), (1, 8)))
    return {"tokens": tokens, "passes": passes, "lengths": lengths, "dealing": dealing, "pass_table": pass_table, "gain_first": gain_first, "to_heads": to_heads, "from_heads": from_heads, "gain_second": gain_second, "expand": expand, "shrink": shrink, "cotangent": cotangent}


@jax.custom_vjp
def low(v):
    return lax.optimization_barrier(v.astype(jnp.bfloat16)).astype(jnp.float32)

@jax.custom_vjp
def low_back(v):
    return v

def low_keep(v):
    return (low(v), None)

def low_pass(kept, grad):
    return (grad,)

def back_keep(v):
    return (v, None)

def back_low(kept, grad):
    return (low(grad),)
low.defvjp(low_keep, low_pass)
low_back.defvjp(back_keep, back_low)
epsilon = 1e-05
highest = lax.Precision.HIGHEST

def layer_norm(values, gain_row):
    centred = values - lax.optimization_barrier(jnp.mean(values, axis=-1, keepdims=True))
    spread = lax.optimization_barrier(jnp.mean(centred * centred, axis=-1, keepdims=True))
    return centred * lax.rsqrt(spread + epsilon) * gain_row

def one_sequence(weights, inputs):
    pass_table, gain_first, to_heads, from_heads, gain_second, expand, shrink = weights
    tokens_seq, pass_seq, length = inputs
    seq_len = tokens_seq.shape[0]
    onehot = (pass_seq[:, None] == jnp.arange(PASSES, dtype=jnp.int32)[None, :]).astype(tokens_seq.dtype)
    entry = tokens_seq + jnp.dot(onehot, pass_table, precision=highest)
    positions = jnp.arange(seq_len, dtype=jnp.int32)
    live_rows = (positions < length).astype(entry.dtype)[:, None]
    normed_first = low(layer_norm(entry, gain_first))
    projected = low(low_back(jnp.dot(normed_first, to_heads, precision=highest)))
    queries = projected[:, :D].reshape(seq_len, HEADS, HEAD)
    key_rows = projected[:, D:2 * D].reshape(seq_len, HEADS, HEAD)
    value_rows = projected[:, 2 * D:].reshape(seq_len, HEADS, HEAD)
    scaling = 1.0 / math.sqrt(HEAD)
    scores = low_back(jnp.einsum('qhd,khd->hqk', queries, key_rows, precision=highest) * scaling)
    allowed = (positions[None, :] <= positions[:, None]) & (positions[None, :] < length)
    scores = jnp.where(allowed[None], scores, -1e+30)
    largest = lax.optimization_barrier(jnp.max(scores, axis=-1, keepdims=True))
    exponent = jnp.exp(scores - largest)
    probability = exponent / lax.optimization_barrier(jnp.sum(exponent, axis=-1, keepdims=True))
    mixed = jnp.einsum('hqk,khd->qhd', low(probability), value_rows, precision=highest)
    heads_out = low(low_back(mixed)).reshape(seq_len, D)
    attention = low_back(jnp.dot(heads_out, from_heads, precision=highest))
    hidden = entry + attention
    normed_second = low(layer_norm(hidden, gain_second))
    widened = low_back(jnp.dot(normed_second, expand, precision=highest))
    activated = low(jax.nn.gelu(widened, approximate=True))
    feed = low_back(jnp.dot(activated, shrink, precision=highest))
    result = (hidden + feed) * live_rows
    squares = jnp.stack([jnp.sum(entry * entry * live_rows), jnp.sum(attention * attention * live_rows), jnp.sum(feed * feed * live_rows)])
    return (result, squares)

def forward(tokens_seq, pass_table, gain_first, to_heads, from_heads, gain_second, expand, shrink, passes, length_all):
    weights = (pass_table, gain_first, to_heads, from_heads, gain_second, expand, shrink)
    per_sequence = jax.checkpoint(lambda inputs: one_sequence(weights, inputs))
    result, squares = lax.map(per_sequence, (tokens_seq, passes, length_all))
    return (result, lax.optimization_barrier(jnp.sum(squares, axis=0)))

def to_sequences(array, dealing):
    blocks = array.reshape(N_FSDP, SEQ_F, N_DP, LEN // N_DP, D).transpose(0, 2, 1, 3, 4)
    inverse = jnp.argsort(dealing, axis=-1).astype(jnp.int32).transpose(1, 0, 2)
    chosen = jnp.take_along_axis(blocks, inverse[:, :, :, None, None], axis=2)
    return chosen.transpose(0, 2, 1, 3, 4).reshape(SEQ_F * N_FSDP, LEN, D)

def from_sequences(array, dealing):
    blocks = array.reshape(N_FSDP, SEQ_F, N_DP, LEN // N_DP, D).transpose(0, 2, 1, 3, 4)
    chosen = jnp.take_along_axis(blocks, dealing.transpose(1, 0, 2)[:, :, :, None, None], axis=2)
    return chosen.transpose(0, 2, 1, 3, 4).reshape(SEQ_F * N_FSDP, LEN, D)

def reference(tokens, passes, lengths, dealing, pass_table, gain_first, to_heads, from_heads, gain_second, expand, shrink, cotangent):
    seq_tokens = to_sequences(tokens.astype(jnp.float32), dealing)
    seq_grads = to_sequences(cotangent.astype(jnp.float32), dealing)
    length_all = lengths.reshape(-1)
    weights = (pass_table.astype(jnp.float32), gain_first.astype(jnp.float32), to_heads.astype(jnp.float32), from_heads.astype(jnp.float32), gain_second.astype(jnp.float32), expand.astype(jnp.float32), shrink.astype(jnp.float32))

    def wrapped(tokens_seq, table_w, gain_one, heads_in, heads_back, gain_two, expand_w, shrink_w):
        return forward(tokens_seq, table_w, gain_one, heads_in, heads_back, gain_two, expand_w, shrink_w, passes, length_all)
    result, pullback, squares = jax.vjp(wrapped, seq_tokens, *weights, has_aux=True)
    gradient = pullback(seq_grads)
    counted = jnp.sum(length_all).astype(jnp.float32) * D
    root_squares = jnp.sqrt(squares / counted)
    return (from_sequences(result, dealing), from_sequences(gradient[0], dealing), gradient[1], gradient[2], gradient[3], gradient[4], gradient[5], gradient[6], gradient[7], root_squares)
```

```python
import math
import functools

import jax
import jax.numpy as jnp
from jax import lax
from jax.experimental import pallas as pl
from jax.experimental.pallas import tpu as pltpu
from jax.sharding import PartitionSpec as P

D = 768
HEADS = 12
HEAD = 64
FF = 3072
PASSES = 5
EPS = 1e-05
ROWS = 256
CHUNKS = FF // D
VMEM_MOST = 64000 * 1024

f32 = jnp.float32
bf16 = jnp.bfloat16


def dot_nn(a, b):
    return lax.dot_general(a, b, (((1,), (0,)), ((), ())), preferred_element_type=f32)


def dot_nt(a, b):
    return lax.dot_general(a, b, (((1,), (1,)), ((), ())), preferred_element_type=f32)


def dot_tn(a, b):
    return lax.dot_general(a, b, (((0,), (0,)), ((), ())), preferred_element_type=f32)


def params(**more):
    return pltpu.CompilerParams(vmem_limit_bytes=VMEM_MOST, **more)


def normalized(values):
    centred = values - jnp.mean(values, axis=-1, keepdims=True)
    spread = jnp.mean(centred * centred, axis=-1, keepdims=True)
    scale = lax.rsqrt(spread + EPS)
    return centred * scale, scale


def norm_back(grad_unit, unit, scale):
    first = jnp.mean(grad_unit, axis=-1, keepdims=True)
    second = jnp.mean(grad_unit * unit, axis=-1, keepdims=True)
    return scale * (grad_unit - first - unit * second)


def onehot_rows(pass_row):
    ids = lax.broadcasted_iota(jnp.int32, (8, pass_row.shape[-1]), 0)
    return (ids == pass_row).astype(f32).astype(bf16)


def fold_rows(values):
    rows, width = values.shape
    return jnp.sum(values.reshape(rows // 8, 8, width), axis=0)


def last_block(length):
    return lax.div(length + (ROWS - 1), ROWS) - 1


def project_kernel(len_ref, tok_ref, pass_ref, table_ref, gain_ref, w_ref, out_ref):
    @pl.when(pl.program_id(0) <= last_block(len_ref[0]))
    def work():
        hot = onehot_rows(pass_ref[0])
        entry = tok_ref[...].astype(f32) + dot_tn(hot, table_ref[...])
        unit, unused = normalized(entry)
        normed = (unit * gain_ref[...]).astype(bf16)
        for part in range(3):
            out_ref[part] = dot_nn(normed, w_ref[:, part * D : (part + 1) * D]).astype(bf16)


def project(length, tokens, pass_rows, table, gain, weight):
    rows = tokens.shape[0]
    at = lambda b, n: jnp.minimum(b, last_block(n[0]))
    return pl.pallas_call(
        project_kernel,
        grid_spec=pltpu.PrefetchScalarGridSpec(
            num_scalar_prefetch=1,
            grid=(rows // ROWS,),
            in_specs=[
                pl.BlockSpec((ROWS, D), lambda b, n: (at(b, n), 0)),
                pl.BlockSpec((1, 1, ROWS), lambda b, n: (at(b, n), 0, 0)),
                pl.BlockSpec((8, D), lambda b, n: (0, 0)),
                pl.BlockSpec((1, D), lambda b, n: (0, 0)),
                pl.BlockSpec((D, 3 * D), lambda b, n: (0, 0), pipeline_mode=pl.Buffered(1)),
            ],
            out_specs=pl.BlockSpec((3, ROWS, D), lambda b, n: (0, at(b, n), 0)),
        ),
        out_shape=jax.ShapeDtypeStruct((3, rows, D), bf16),
        compiler_params=params(),
        cost_estimate=pl.CostEstimate(
            flops=2 * rows * D * 3 * D, bytes_accessed=rows * D * 8 + D * D * 6, transcendentals=0
        ),
        name="project",
    )(length, tokens, pass_rows, table, gain, weight)


def attend_kernel(len_ref, p_ref, out_ref, lse_ref):
    blocks = p_ref.shape[1] // ROWS
    lane = lax.broadcasted_iota(jnp.int32, (ROWS, 128), 1)
    first_head = lane < HEAD
    here = lax.broadcasted_iota(jnp.int32, (ROWS, ROWS), 0)
    there = lax.broadcasted_iota(jnp.int32, (ROWS, ROWS), 1)
    allowed = there <= here
    for i in range(blocks):
        rows = slice(i * ROWS, (i + 1) * ROWS)

        @pl.when(i * ROWS < len_ref[0])
        def work():
            query = p_ref[0, rows, :] * jnp.asarray(1.0 / math.sqrt(HEAD), bf16)
            found = []
            for head in range(2):
                mine = first_head if head == 0 else jnp.logical_not(first_head)
                q = jnp.where(mine, query, jnp.zeros_like(query))
                diag = dot_nt(q, p_ref[1, rows, :])
                diag = jnp.where(allowed, diag, -1e30)
                largest = jnp.max(diag, axis=-1, keepdims=True)
                if i > 0:
                    before = dot_nt(q, p_ref[1, : i * ROWS, :])
                    largest = jnp.maximum(largest, jnp.max(before, axis=-1, keepdims=True))
                diag = jnp.exp(diag - largest)
                total = jnp.sum(diag, axis=-1, keepdims=True)
                if i > 0:
                    before = jnp.exp(before - largest)
                    total = total + jnp.sum(before, axis=-1, keepdims=True)
                inverse = 1.0 / total
                out = dot_nn((diag * inverse).astype(bf16), p_ref[2, rows, :])
                if i > 0:
                    out = out + dot_nn((before * inverse).astype(bf16), p_ref[2, : i * ROWS, :])
                found.append(out)
                lse = jnp.broadcast_to(largest + jnp.log(total), (ROWS, 128))
                lse_ref[0, head : head + 1, rows] = lse.T[0:1]
            out_ref[rows, :] = jnp.where(first_head, found[0], found[1]).astype(bf16)


def attend(length, projected):
    rows = projected.shape[1]
    pairs = HEADS // 2
    return pl.pallas_call(
        attend_kernel,
        grid_spec=pltpu.PrefetchScalarGridSpec(
            num_scalar_prefetch=1,
            grid=(pairs,),
            in_specs=[pl.BlockSpec((3, rows, 128), lambda h, n: (0, 0, h))],
            out_specs=[
                pl.BlockSpec((rows, 128), lambda h, n: (0, h)),
                pl.BlockSpec((1, 8, rows), lambda h, n: (h, 0, 0)),
            ],
        ),
        out_shape=[
            jax.ShapeDtypeStruct((rows, D), bf16),
            jax.ShapeDtypeStruct((pairs, 8, rows), f32),
        ],
        compiler_params=params(),
        cost_estimate=pl.CostEstimate(
            flops=2 * rows * rows * D, bytes_accessed=rows * D * 8, transcendentals=HEADS * rows * rows // 2
        ),
        name="attend",
    )(length, projected)


def attend_back_kernel(len_ref, p_ref, o_ref, g_ref, lse_ref, out_ref, dk_ref, dv_ref):
    blocks = p_ref.shape[1] // ROWS
    scaling = 1.0 / math.sqrt(HEAD)
    lane = lax.broadcasted_iota(jnp.int32, (ROWS, 128), 1)
    first_head = lane < HEAD
    row8 = lax.broadcasted_iota(jnp.int32, (8, 128), 0)
    lane8 = lax.broadcasted_iota(jnp.int32, (8, 128), 1)
    chooser = (lax.div(lane8, HEAD) == row8).astype(f32)
    key_at = lax.broadcasted_iota(jnp.int32, (ROWS, ROWS), 0)
    row_at = lax.broadcasted_iota(jnp.int32, (ROWS, ROWS), 1)
    allowed = key_at <= row_at
    for i in range(blocks):
        rows = slice(i * ROWS, (i + 1) * ROWS)

        @pl.when(i * ROWS < len_ref[0])
        def work():
            dk_ref[:, rows, :] = jnp.zeros((2, ROWS, 128), f32)
            dv_ref[:, rows, :] = jnp.zeros((2, ROWS, 128), f32)
            query = p_ref[0, rows, :] * jnp.asarray(scaling, bf16)
            grad = g_ref[rows, :]
            product = grad.astype(f32) * o_ref[rows, :].astype(f32)
            delta = lax.dot_general(
                chooser,
                product,
                (((1,), (1,)), ((), ())),
                precision=lax.Precision.HIGHEST,
                preferred_element_type=f32,
            )
            grad_query = jnp.zeros((ROWS, 128), f32)
            for j in range(i + 1):
                cols = slice(j * ROWS, (j + 1) * ROWS)
                key = p_ref[1, cols, :]
                value = p_ref[2, cols, :]
                for head in range(2):
                    mine = first_head if head == 0 else jnp.logical_not(first_head)
                    k = jnp.where(mine, key, jnp.zeros_like(key))
                    v = jnp.where(mine, value, jnp.zeros_like(value))
                    scores = dot_nt(k, query)
                    prob = jnp.exp(scores - lse_ref[0, head : head + 1, rows])
                    if i == j:
                        prob = jnp.where(allowed, prob, 0.0)
                    grad_prob = dot_nt(v, grad)
                    grad_scores = (prob * (grad_prob - delta[head : head + 1])).astype(bf16)
                    dv_ref[head, cols, :] += dot_nn(prob.astype(bf16), grad)
                    dk_ref[head, cols, :] += dot_nn(grad_scores, query)
                    grad_query = grad_query + dot_tn(grad_scores, k)
            out_ref[0, rows, :] = (grad_query * scaling).astype(bf16)

    for i in range(blocks):
        rows = slice(i * ROWS, (i + 1) * ROWS)

        @pl.when(i * ROWS < len_ref[0])
        def finish():
            out_ref[1, rows, :] = jnp.where(first_head, dk_ref[0, rows, :], dk_ref[1, rows, :]).astype(bf16)
            out_ref[2, rows, :] = jnp.where(first_head, dv_ref[0, rows, :], dv_ref[1, rows, :]).astype(bf16)


def attend_back(length, projected, heads_out, grad_heads, lse):
    rows = projected.shape[1]
    pairs = HEADS // 2
    return pl.pallas_call(
        attend_back_kernel,
        grid_spec=pltpu.PrefetchScalarGridSpec(
            num_scalar_prefetch=1,
            grid=(pairs,),
            in_specs=[
                pl.BlockSpec((3, rows, 128), lambda h, n: (0, 0, h)),
                pl.BlockSpec((rows, 128), lambda h, n: (0, h)),
                pl.BlockSpec((rows, 128), lambda h, n: (0, h)),
                pl.BlockSpec((1, 8, rows), lambda h, n: (h, 0, 0)),
            ],
            out_specs=pl.BlockSpec((3, rows, 128), lambda h, n: (0, 0, h)),
            scratch_shapes=[pltpu.VMEM((2, rows, 128), f32), pltpu.VMEM((2, rows, 128), f32)],
        ),
        out_shape=jax.ShapeDtypeStruct((3, rows, D), bf16),
        compiler_params=params(),
        cost_estimate=pl.CostEstimate(
            flops=5 * rows * rows * D, bytes_accessed=rows * D * 16, transcendentals=HEADS * rows * rows // 2
        ),
        name="attend_back",
    )(length, projected, heads_out, grad_heads, lse)


def feed_kernel(
    len_ref, tok0, tok1, pass0, pass1, ho0, ho1, cot0, cot1, table_ref, gain_ref, w_ref,
    res0, res1, gh0, gh1, hid0, hid1, grads_ref, small_ref,
    acc_ref, stage_ref, sem_ref,
):
    b = pl.program_id(0)
    many0 = last_block(len_ref[0]) + 1
    many1 = last_block(len_ref[1]) + 1
    early = b < many0

    @pl.when(b == 0)
    def clear():
        acc_ref[...] = jnp.zeros_like(acc_ref)
        small_ref[...] = jnp.zeros_like(small_ref)

    def block(tok, pas, ho, cot, res, gh, hid, start, length):
        hot = onehot_rows(pas[0])
        entry = tok[...].astype(f32) + dot_tn(hot, table_ref[...])
        at = start + lax.broadcasted_iota(jnp.int32, (ROWS, 1), 0)
        live = at < length
        heads = ho[...]
        attention = dot_nn(heads, w_ref[:, 0:D])
        hidden = entry + attention
        unit, scale = normalized(hidden)
        gain = gain_ref[...]
        normed = (unit * gain).astype(bf16)
        grad_feed = jnp.where(live, cot[...].astype(f32), 0.0).astype(bf16)
        feed = jnp.zeros((ROWS, D), f32)
        grad_normed = jnp.zeros((ROWS, D), f32)
        for k in range(CHUNKS):
            up = slice(D + k * D, D + (k + 1) * D)
            down = slice(D + FF + k * D, D + FF + (k + 1) * D)
            x = dot_nn(normed, w_ref[:, up])
            grad_act = dot_nt(grad_feed, w_ref[:, down])
            c0 = math.sqrt(2.0 / math.pi)
            square = x * x
            bent = jnp.tanh(x * (c0 + (c0 * 0.044715) * square))
            half = 0.5 + 0.5 * bent
            slope = half + (0.5 * x) * (1.0 - bent * bent) * (c0 + (3.0 * c0 * 0.044715) * square)
            act = (x * half).astype(bf16)
            grad_x = (slope * grad_act).astype(bf16)
            feed = feed + dot_nn(act, w_ref[:, down])
            grad_normed = grad_normed + dot_nt(grad_x, w_ref[:, up])
            acc_ref[:, up] += dot_tn(normed, grad_x)
            acc_ref[:, down] += dot_tn(act, grad_feed)
        res[...] = jnp.where(live, hidden + feed, 0.0).astype(bf16)
        small_ref[0:8] += fold_rows(grad_normed * unit)
        small_ref[8:16] += fold_rows(jnp.where(live, entry * entry, 0.0))
        small_ref[16:24] += fold_rows(jnp.where(live, attention * attention, 0.0))
        small_ref[24:32] += fold_rows(jnp.where(live, feed * feed, 0.0))
        grad_hidden = grad_feed.astype(f32) + norm_back(grad_normed * gain, unit, scale)
        hid[...] = grad_hidden
        grad_attention = grad_hidden.astype(bf16)
        acc_ref[:, 0:D] += dot_tn(heads, grad_attention)
        gh[...] = dot_nt(grad_attention, w_ref[:, 0:D]).astype(bf16)

    @pl.when(early)
    def first():
        block(tok0, pass0, ho0, cot0, res0, gh0, hid0, b * ROWS, len_ref[0])

    @pl.when(jnp.logical_and(jnp.logical_not(early), b < many0 + many1))
    def second():
        block(tok1, pass1, ho1, cot1, res1, gh1, hid1, (b - many0) * ROWS, len_ref[1])

    @pl.when(b == pl.num_programs(0) - 1)
    def finish():
        pieces = acc_ref.shape[1] // D
        for n in range(pieces):
            slot = n % 2
            cols = slice(n * D, (n + 1) * D)
            copy = pltpu.make_async_copy(stage_ref.at[slot], grads_ref.at[:, cols], sem_ref.at[slot])
            if n >= 2:
                before = slice((n - 2) * D, (n - 1) * D)
                pltpu.make_async_copy(stage_ref.at[slot], grads_ref.at[:, before], sem_ref.at[slot]).wait()
            stage_ref[slot] = acc_ref[:, cols].astype(bf16)
            copy.start()
        for n in (pieces - 2, pieces - 1):
            slot = n % 2
            cols = slice(n * D, (n + 1) * D)
            pltpu.make_async_copy(stage_ref.at[slot], grads_ref.at[:, cols], sem_ref.at[slot]).wait()


def feed(lengths, tokens, pass_rows, heads_out, cotangent, table, gain, weight):
    rows = tokens[0].shape[0]
    width = weight.shape[1]
    at0 = lambda b, n: jnp.minimum(b, last_block(n[0]))
    at1 = lambda b, n: jnp.clip(b - last_block(n[0]) - 1, 0, last_block(n[1]))
    row0 = pl.BlockSpec((ROWS, D), lambda b, n: (at0(b, n), 0))
    row1 = pl.BlockSpec((ROWS, D), lambda b, n: (at1(b, n), 0))
    pas0 = pl.BlockSpec((1, 1, ROWS), lambda b, n: (at0(b, n), 0, 0))
    pas1 = pl.BlockSpec((1, 1, ROWS), lambda b, n: (at1(b, n), 0, 0))
    narrow = jax.ShapeDtypeStruct((rows, D), bf16)
    wide = jax.ShapeDtypeStruct((rows, D), f32)
    return pl.pallas_call(
        feed_kernel,
        grid_spec=pltpu.PrefetchScalarGridSpec(
            num_scalar_prefetch=1,
            grid=(2 * rows // ROWS,),
            in_specs=[
                row0, row1, pas0, pas1, row0, row1, row0, row1,
                pl.BlockSpec((8, D), lambda b, n: (0, 0)),
                pl.BlockSpec((1, D), lambda b, n: (0, 0)),
                pl.BlockSpec((D, width), lambda b, n: (0, 0), pipeline_mode=pl.Buffered(1)),
            ],
            out_specs=[
                row0, row1, row0, row1, row0, row1,
                pl.BlockSpec(memory_space=pl.ANY),
                pl.BlockSpec((32, D), lambda b, n: (0, 0)),
            ],
            scratch_shapes=[
                pltpu.VMEM((D, width), f32),
                pltpu.VMEM((2, D, D), bf16),
                pltpu.SemaphoreType.DMA((2,)),
            ],
        ),
        out_shape=[narrow, narrow, narrow, narrow, wide, wide,
                   jax.ShapeDtypeStruct((D, width), bf16), jax.ShapeDtypeStruct((32, D), f32)],
        compiler_params=params(),
        cost_estimate=pl.CostEstimate(
            flops=2 * 6 * rows * D * width, bytes_accessed=2 * rows * D * 14 + D * width * 4, transcendentals=2 * rows * FF
        ),
        name="feed",
    )(lengths, tokens[0], tokens[1], pass_rows[0], pass_rows[1], heads_out[0], heads_out[1],
      cotangent[0], cotangent[1], table, gain, weight)


def project_back_kernel(final, len_ref, tok_ref, pass_ref, g_ref, hid_ref, table_ref, gain_ref, w_ref, *rest):
    if final:
        before_ref, out_ref, grads_ref, small_ref, acc_ref = rest
    else:
        out_ref, acc_ref, small_ref = rest
    b = pl.program_id(0)

    @pl.when(b == 0)
    def clear():
        acc_ref[...] = before_ref[...] if final else jnp.zeros_like(acc_ref)
        small_ref[...] = jnp.zeros_like(small_ref)

    @pl.when(b <= last_block(len_ref[0]))
    def work():
        hot = onehot_rows(pass_ref[0])
        entry = tok_ref[...].astype(f32) + dot_tn(hot, table_ref[...])
        unit, scale = normalized(entry)
        gain = gain_ref[...]
        normed = (unit * gain).astype(bf16)
        grad_normed = jnp.zeros((ROWS, D), f32)
        for part in range(3):
            cols = slice(part * D, (part + 1) * D)
            grad = g_ref[part]
            acc_ref[:, cols] += dot_tn(normed, grad)
            grad_normed = grad_normed + dot_nt(grad, w_ref[:, cols])
        small_ref[0:8] += fold_rows(grad_normed * unit)
        grad_entry = hid_ref[...] + norm_back(grad_normed * gain, unit, scale)
        out_ref[...] = grad_entry.astype(bf16)
        high = grad_entry.astype(bf16)
        rest_one = grad_entry - high.astype(f32)
        low = rest_one.astype(bf16)
        lower = (rest_one - low.astype(f32)).astype(bf16)
        small_ref[8:16] += dot_nn(hot, high) + dot_nn(hot, low) + dot_nn(hot, lower)

    if final:
        @pl.when(b == pl.num_programs(0) - 1)
        def finish():
            grads_ref[...] = acc_ref[...].astype(bf16)


def project_back(length, tokens, pass_rows, grads, grad_hidden, table, gain, weight, before=None):
    rows = tokens.shape[0]
    final = before is not None
    at = lambda b, n: jnp.minimum(b, last_block(n[0]))
    whole = pl.BlockSpec((D, 3 * D), lambda b, n: (0, 0), pipeline_mode=pl.Buffered(1))
    in_specs = [
        pl.BlockSpec((ROWS, D), lambda b, n: (at(b, n), 0)),
        pl.BlockSpec((1, 1, ROWS), lambda b, n: (at(b, n), 0, 0)),
        pl.BlockSpec((3, ROWS, D), lambda b, n: (0, at(b, n), 0)),
        pl.BlockSpec((ROWS, D), lambda b, n: (at(b, n), 0)),
        pl.BlockSpec((8, D), lambda b, n: (0, 0)),
        pl.BlockSpec((1, D), lambda b, n: (0, 0)),
        whole,
    ]
    operands = [length, tokens, pass_rows, grads, grad_hidden, table, gain, weight]
    if final:
        in_specs.append(whole)
        operands.append(before)
    return pl.pallas_call(
        functools.partial(project_back_kernel, final),
        grid_spec=pltpu.PrefetchScalarGridSpec(
            num_scalar_prefetch=1,
            grid=(rows // ROWS,),
            in_specs=in_specs,
            out_specs=[
                pl.BlockSpec((ROWS, D), lambda b, n: (at(b, n), 0)),
                pl.BlockSpec((D, 3 * D), lambda b, n: (0, 0)),
                pl.BlockSpec((16, D), lambda b, n: (0, 0)),
            ],
            scratch_shapes=[pltpu.VMEM((D, 3 * D), f32)] if final else [],
        ),
        out_shape=[
            jax.ShapeDtypeStruct((rows, D), bf16),
            jax.ShapeDtypeStruct((D, 3 * D), bf16 if final else f32),
            jax.ShapeDtypeStruct((16, D), f32),
        ],
        compiler_params=params(),
        cost_estimate=pl.CostEstimate(
            flops=4 * rows * D * 3 * D, bytes_accessed=rows * D * 14 + D * D * 18, transcendentals=0
        ),
        name="project_back",
    )(*operands)


def pick_kernel(index_ref, in_ref, out_ref):
    out_ref[...] = in_ref[...]


def pick(index, blocks):
    many = index.shape[0]
    shape = (1,) + blocks.shape[1:]
    return pl.pallas_call(
        pick_kernel,
        grid_spec=pltpu.PrefetchScalarGridSpec(
            num_scalar_prefetch=1,
            grid=(many,),
            in_specs=[pl.BlockSpec(shape, lambda b, n: (n[b], 0, 0))],
            out_specs=pl.BlockSpec(shape, lambda b, n: (b, 0, 0)),
        ),
        out_shape=jax.ShapeDtypeStruct((many,) + blocks.shape[1:], blocks.dtype),
        compiler_params=params(),
        cost_estimate=pl.CostEstimate(flops=0, bytes_accessed=4 * many * blocks[0].size, transcendentals=0),
        name="pick",
    )(index, blocks)


def settle_kernel(index_ref, early_ref, late_ref, out_ref):
    b = pl.program_id(0)
    rows = out_ref.shape[1]
    live = lax.broadcasted_iota(jnp.int32, (rows, 1), 0) < index_ref[2, b]

    @pl.when(index_ref[0, b] == 0)
    def early():
        out_ref[0] = jnp.where(live, early_ref[0].astype(f32), 0.0)

    @pl.when(index_ref[0, b] != 0)
    def late():
        out_ref[0] = jnp.where(live, late_ref[0].astype(f32), 0.0)


def settle(index, early, late):
    many = index.shape[1]
    shape = (1,) + early.shape[1:]
    return pl.pallas_call(
        settle_kernel,
        grid_spec=pltpu.PrefetchScalarGridSpec(
            num_scalar_prefetch=1,
            grid=(many,),
            in_specs=[
                pl.BlockSpec(shape, lambda b, n: (n[1, b], 0, 0)),
                pl.BlockSpec(shape, lambda b, n: (n[1, b], 0, 0)),
            ],
            out_specs=pl.BlockSpec(shape, lambda b, n: (b, 0, 0)),
        ),
        out_shape=jax.ShapeDtypeStruct((many,) + early.shape[1:], f32),
        compiler_params=params(),
        cost_estimate=pl.CostEstimate(flops=0, bytes_accessed=8 * many * early[0].size, transcendentals=0),
        name="settle",
    )(index, early, late)


def swap(blocks):
    return lax.all_to_all(blocks, "dp", split_axis=0, concat_axis=0, tiled=True)


def total_over(values, axes, devices):
    flat = values.reshape(devices, -1)
    parts = lax.all_to_all(flat, axes, split_axis=0, concat_axis=0, tiled=True)
    mine = jnp.sum(parts, axis=0, keepdims=True)
    spread = jnp.broadcast_to(mine, flat.shape)
    return lax.all_to_all(spread, axes, split_axis=0, concat_axis=0, tiled=True).reshape(values.shape)


def per_device(
    groups,
    width_all,
    tokens,
    passes,
    lengths,
    dealing,
    pass_table,
    gain_first,
    to_heads,
    from_heads,
    gain_second,
    expand,
    shrink,
    cotangent,
):
    axes = ("dp", "fsdp")
    slots, part, unused_width = tokens.shape
    seq_len = part * groups
    order = jnp.arange(slots, dtype=jnp.int32)
    here = lax.axis_index("dp")
    ordering = dealing[0, 0]
    sizes = lengths[0]

    ahead = (sizes[None, :] > sizes[:, None]) | (
        (sizes[None, :] == sizes[:, None]) & (order[None, :] < order[:, None])
    )
    rank = jnp.sum(ahead.astype(jnp.int32), axis=1)
    ranked = jnp.sum(jnp.where(rank[None, :] == order[:, None], order[None, :], 0), axis=1)
    place = jnp.sum(jnp.where(ordering[None, :] == order[:, None], order[None, :], 0), axis=1)
    early_seqs = ranked[:groups]
    late_seqs = ranked[groups:][::-1]
    from_early = jnp.sum(jnp.where(early_seqs[:, None] == order[None, :], place[None, :], 0), axis=1)
    from_late = jnp.sum(jnp.where(late_seqs[:, None] == order[None, :], place[None, :], 0), axis=1)
    slot_rank = jnp.sum(jnp.where(ordering[:, None] == order[None, :], rank[None, :], 0), axis=1)
    slot_size = jnp.sum(jnp.where(ordering[:, None] == order[None, :], sizes[None, :], 0), axis=1)
    is_late = (slot_rank >= groups).astype(jnp.int32)
    source = jnp.where(is_late == 1, slots - 1 - slot_rank, slot_rank)
    back_index = jnp.stack([is_late, source, slot_size - here * part])
    my_seqs = jnp.stack([early_seqs[here], late_seqs[here]])
    my_sizes = jnp.sum(jnp.where(my_seqs[:, None] == order[None, :], sizes[None, :], 0), axis=1)

    row_count = to_heads.shape[0]
    narrow = jnp.concatenate(
        [
            from_heads,
            expand.reshape(row_count, D, CHUNKS).transpose(0, 2, 1).reshape(row_count, FF),
            shrink.reshape(row_count, CHUNKS * D),
        ],
        axis=1,
    )
    head_weight = lax.all_gather(to_heads, axes, axis=0, tiled=True)
    wide_weight = lax.all_gather(narrow, axes, axis=0, tiled=True)

    my_tokens = [swap(pick(index, tokens)).reshape(seq_len, D) for index in (from_early, from_late)]
    my_grads = [swap(pick(index, cotangent)).reshape(seq_len, D) for index in (from_early, from_late)]
    my_passes = [passes[my_seqs[m]].reshape(seq_len // ROWS, 1, ROWS) for m in range(2)]
    one_size = [my_sizes[m : m + 1] for m in range(2)]
    table = jnp.zeros((8, D), bf16).at[:PASSES].set(pass_table)
    gain_one = gain_first.astype(f32).reshape(1, D)
    gain_two = gain_second.astype(f32).reshape(1, D)

    projected, heads_out, lse = [], [], []
    for m in range(2):
        projected.append(project(one_size[m], my_tokens[m], my_passes[m], table, gain_one, head_weight))
        mixed, logs = attend(one_size[m], projected[m])
        heads_out.append(mixed)
        lse.append(logs)
    res0, res1, gh0, gh1, hid0, hid1, wide_grads, feed_small = feed(
        my_sizes, my_tokens, my_passes, heads_out, my_grads, table, gain_two, wide_weight
    )
    results = [swap(r.reshape(groups, part, D)) for r in (res0, res1)]
    wide_owned = lax.psum_scatter(wide_grads, axes, scatter_dimension=0, tiled=True)
    grad_parts = [
        attend_back(one_size[m], projected[m], heads_out[m], (gh0, gh1)[m], lse[m]) for m in range(2)
    ]
    entry0, head_sum, small0 = project_back(
        one_size[0], my_tokens[0], my_passes[0], grad_parts[0], hid0, table, gain_one, head_weight
    )
    entry1, head_grads, small1 = project_back(
        one_size[1], my_tokens[1], my_passes[1], grad_parts[1], hid1, table, gain_one, head_weight, head_sum
    )
    head_owned = lax.psum_scatter(head_grads, axes, scatter_dimension=0, tiled=True)
    entries = [swap(r.reshape(groups, part, D)) for r in (entry0, entry1)]

    squares = jnp.sum(feed_small[8:].reshape(3, 8 * D), axis=1)
    counted = jnp.sum(my_sizes).astype(f32)
    last_row = jnp.zeros((1, D), f32).at[0, :3].set(squares).at[0, 3].set(counted)
    small = small0 + small1
    gathered = jnp.concatenate(
        [
            small[8 : 8 + PASSES],
            jnp.sum(small[:8], axis=0, keepdims=True),
            jnp.sum(feed_small[:8], axis=0, keepdims=True),
            last_row,
        ],
        axis=0,
    )
    totals = total_over(gathered, axes, width_all)
    root_squares = jnp.sqrt(totals[7, :3] / (totals[7, 3] * D))

    grad_expand = wide_owned[:, D : D + FF].reshape(row_count, CHUNKS, D).transpose(0, 2, 1)
    return (
        settle(back_index, results[0], results[1]),
        settle(back_index, entries[0], entries[1]),
        totals[:PASSES],
        totals[PASSES],
        head_owned.astype(f32),
        wide_owned[:, :D].astype(f32),
        totals[PASSES + 1],
        grad_expand.reshape(row_count, FF).astype(f32),
        wide_owned[:, D + FF :].reshape(row_count * CHUNKS, D).astype(f32),
        root_squares,
    )


def solution(mesh):
    groups = mesh.shape["dp"]
    weight_spec = P(("dp", "fsdp"), None)
    block_spec = P("fsdp", "dp", None)
    in_specs = (
        block_spec,
        P("fsdp", None),
        P("fsdp", None),
        P("dp", "fsdp", None),
        P(),
        P(),
        weight_spec,
        weight_spec,
        P(),
        weight_spec,
        weight_spec,
        block_spec,
    )
    out_specs = (
        block_spec,
        block_spec,
        P(),
        P(),
        weight_spec,
        weight_spec,
        P(),
        weight_spec,
        weight_spec,
        P(),
    )
    body = functools.partial(per_device, groups, groups * mesh.shape["fsdp"])
    return jax.shard_map(body, mesh=mesh, in_specs=in_specs, out_specs=out_specs, check_vma=False)
```

```python
import math
import functools

import jax
import jax.numpy as jnp
from jax import lax
from jax.experimental import pallas as pl
from jax.experimental.pallas import tpu as pltpu
from jax.sharding import PartitionSpec as P

D = 768
HEADS = 12
HEAD = 64
FF = 3072
PASSES = 5
EPS = 1e-05
ROWS = 256
CHUNKS = FF // D
VMEM_MOST = 64000 * 1024

f32 = jnp.float32
bf16 = jnp.bfloat16


def dot_nn(a, b):
    return lax.dot_general(a, b, (((1,), (0,)), ((), ())), preferred_element_type=f32)


def dot_nt(a, b):
    return lax.dot_general(a, b, (((1,), (1,)), ((), ())), preferred_element_type=f32)


def dot_tn(a, b):
    return lax.dot_general(a, b, (((0,), (0,)), ((), ())), preferred_element_type=f32)


def params(**more):
    return pltpu.CompilerParams(vmem_limit_bytes=VMEM_MOST, **more)


def normalized(values):
    centred = values - jnp.mean(values, axis=-1, keepdims=True)
    spread = jnp.mean(centred * centred, axis=-1, keepdims=True)
    scale = lax.rsqrt(spread + EPS)
    return centred * scale, scale


def norm_back(grad_unit, unit, scale):
    first = jnp.mean(grad_unit, axis=-1, keepdims=True)
    second = jnp.mean(grad_unit * unit, axis=-1, keepdims=True)
    return scale * (grad_unit - first - unit * second)


def onehot_rows(pass_row):
    ids = lax.broadcasted_iota(jnp.int32, (8, pass_row.shape[-1]), 0)
    return (ids == pass_row).astype(f32).astype(bf16)


def fold_rows(values):
    rows, width = values.shape
    return jnp.sum(values.reshape(rows // 8, 8, width), axis=0)


def last_block(length):
    return lax.div(length + (ROWS - 1), ROWS) - 1


def bits_of(count):
    return count.bit_length() - 1


class Plan:
    def __init__(self, groups, sharers, rows):
        self.groups, self.sharers, self.rows = groups, sharers, rows
        self.count = groups * sharers
        self.paired = rows % 8 == 0 and self.count & (self.count - 1) == 0 and sharers >= 4 and groups >= 2
        over_dp = [("dp", bit) for bit in range(bits_of(groups))]
        over_x = [("fsdp", bit) for bit in range(1, bits_of(sharers))]
        self.gather_dp = over_dp[::-1]
        self.gather_fsdp = over_x[::-1] + [("fsdp", 0)]
        self.orders = (
            [("fsdp", 0)] + over_x + over_dp,
            [("fsdp", 0)] + over_dp[:1] + over_x + over_dp[1:],
        )

    def size(self, axis):
        return self.groups if axis == "dp" else self.sharers

    def exchange(self, values, axis, bit):
        pairs = [(i, i ^ (1 << bit)) for i in range(self.size(axis))]
        return lax.ppermute(values, axis, pairs)

    def gather_groups(self, shard):
        held = shard[None]
        for axis, bit in self.gather_dp:
            held = jnp.concatenate([held, self.exchange(held, axis, bit)], axis=0)
        return held

    def gather_sharers(self, held):
        pieces = {0: held}
        for axis, bit in self.gather_fsdp:
            for name in list(pieces):
                pieces[name | (1 << bit)] = self.exchange(pieces[name], axis, bit)
        return tuple(pieces[name] for name in range(self.sharers))

    def piece_rows(self, dp, fsdp):
        found = []
        for f in range(self.sharers):
            for n in range(self.groups):
                rel = sum(((n >> k) & 1) << bit for k, (axis, bit) in enumerate(self.gather_dp))
                found.append(((dp ^ rel) * self.sharers + (fsdp ^ f)) * self.rows)
        return jnp.stack(found).astype(jnp.int32)

    def grad_rows(self, dp, fsdp):
        found = []
        for order in self.orders:
            for place in range(self.count):
                rel = {"dp": 0, "fsdp": 0}
                for k, (axis, bit) in enumerate(order):
                    rel[axis] |= ((place >> (len(order) - 1 - k)) & 1) << bit
                found.append(((dp ^ rel["dp"]) * self.sharers + (fsdp ^ rel["fsdp"])) * self.rows)
        return jnp.stack(found).astype(jnp.int32)

    def reduce(self, keep, send, order):
        for step, (axis, bit) in enumerate(order):
            other = self.exchange(send, axis, bit).astype(f32)
            total = keep.astype(f32)
            half = keep.shape[0] // 2
            if step == len(order) - 1:
                return (total + other)[0]
            send = (total[half:] + other[half:]).astype(bf16)
            keep = (total[:half] + other[:half]).astype(bf16)


def load_weight(plan, rows_ref, pieces, weight_ref, sem_ref):
    if not plan.paired:
        copies = [pltpu.make_async_copy(pieces[0], weight_ref, sem_ref)]
    else:
        copies = []
        for f in range(plan.sharers):
            for n in range(plan.groups):
                at = pl.multiple_of(rows_ref[f * plan.groups + n], 8)
                target = weight_ref.at[pl.ds(at, plan.rows), :]
                copies.append(pltpu.make_async_copy(pieces[f].at[n], target, sem_ref))
    for copy in copies:
        copy.start()
    for copy in copies:
        copy.wait()


def grad_shapes(plan, width):
    if not plan.paired:
        return [jax.ShapeDtypeStruct((D, width), bf16)]
    half = plan.count // 2
    cut = first_part(width)
    return [jax.ShapeDtypeStruct((half, plan.rows, w), bf16) for w in (cut, cut, width - cut, width - cut)]


def first_part(width):
    step = grad_step(width)
    return (width // step + 1) // 2 * step


def grad_step(width):
    return D if width % D == 0 and width // D > 3 else D // 2


def stage_shape(plan, width):
    step = grad_step(width)
    return (2, plan.count, plan.rows, step) if plan.paired else (2, D, step)


def store_grads(plan, rows_ref, acc_ref, outs, stage_ref, sem_ref):
    width = acc_ref.shape[1]
    step = grad_step(width)
    cut = first_part(width)
    half = plan.count // 2
    waiting = []
    for n in range(width // step):
        slot = n % 2
        cols = slice(n * step, (n + 1) * step)
        if len(waiting) == 2:
            for copy in waiting.pop(0):
                copy.wait()
        if not plan.paired:
            stage_ref[slot] = acc_ref[:, cols].astype(bf16)
            copies = [pltpu.make_async_copy(stage_ref.at[slot], outs[0].at[:, cols], sem_ref.at[slot])]
        else:
            late = n * step >= cut
            base = plan.count if late else 0
            start = n * step - (cut if late else 0)

            def fill(place, carry):
                at = pl.multiple_of(rows_ref[base + place], 8)
                stage_ref[slot, place] = acc_ref[pl.ds(at, plan.rows), cols].astype(bf16)
                return carry

            lax.fori_loop(0, plan.count, fill, 0)
            keep, send = outs[2:4] if late else outs[0:2]
            there = slice(start, start + step)
            copies = [
                pltpu.make_async_copy(stage_ref.at[slot, 0:half], keep.at[:, :, there], sem_ref.at[slot]),
                pltpu.make_async_copy(stage_ref.at[slot, half:], send.at[:, :, there], sem_ref.at[slot]),
            ]
        for copy in copies:
            copy.start()
        waiting.append(copies)
    for copies in waiting:
        for copy in copies:
            copy.wait()


def project_kernel(plan, len_ref, row_ref, tok_ref, pass_ref, table_ref, gain_ref, *rest):
    pieces, (out_ref, w_ref, sem_ref) = rest[:-3], rest[-3:]

    @pl.when(pl.program_id(0) == 0)
    def load():
        load_weight(plan, row_ref, pieces, w_ref, sem_ref)

    @pl.when(pl.program_id(0) <= last_block(len_ref[0]))
    def work():
        hot = onehot_rows(pass_ref[0])
        entry = tok_ref[...].astype(f32) + dot_tn(hot, table_ref[...])
        unit, unused = normalized(entry)
        normed = (unit * gain_ref[...]).astype(bf16)
        for part in range(3):
            out_ref[part] = dot_nn(normed, w_ref[:, part * D : (part + 1) * D]).astype(bf16)


def project(plan, length, piece_rows, tokens, pass_rows, table, gain, pieces):
    rows = tokens.shape[0]
    at = lambda b, n, r: (jnp.minimum(b, last_block(n[0])), 0)
    return pl.pallas_call(
        functools.partial(project_kernel, plan),
        grid_spec=pltpu.PrefetchScalarGridSpec(
            num_scalar_prefetch=2,
            grid=(rows // ROWS,),
            in_specs=[
                pl.BlockSpec((ROWS, D), at),
                pl.BlockSpec((1, 1, ROWS), lambda b, n, r: at(b, n, r) + (0,)),
                pl.BlockSpec((8, D), lambda b, n, r: (0, 0)),
                pl.BlockSpec((1, D), lambda b, n, r: (0, 0)),
            ]
            + [pl.BlockSpec(memory_space=pl.ANY)] * len(pieces),
            out_specs=pl.BlockSpec((3, ROWS, D), lambda b, n, r: (0,) + at(b, n, r)),
            scratch_shapes=[pltpu.VMEM((D, 3 * D), bf16), pltpu.SemaphoreType.DMA],
        ),
        out_shape=jax.ShapeDtypeStruct((3, rows, D), bf16),
        compiler_params=params(),
        cost_estimate=pl.CostEstimate(
            flops=2 * rows * D * 3 * D, bytes_accessed=rows * D * 8 + D * D * 6, transcendentals=0
        ),
        name="project",
    )(length, piece_rows, tokens, pass_rows, table, gain, *pieces)


def attend_kernel(len_ref, p_ref, out_ref, lse_ref):
    blocks = p_ref.shape[1] // ROWS
    lane = lax.broadcasted_iota(jnp.int32, (ROWS, 128), 1)
    first_head = lane < HEAD
    here = lax.broadcasted_iota(jnp.int32, (ROWS, ROWS), 0)
    there = lax.broadcasted_iota(jnp.int32, (ROWS, ROWS), 1)
    allowed = there <= here
    for i in range(blocks):
        rows = slice(i * ROWS, (i + 1) * ROWS)

        @pl.when(i * ROWS < len_ref[0])
        def work():
            query = p_ref[0, rows, :] * jnp.asarray(1.0 / math.sqrt(HEAD), bf16)
            found = []
            for head in range(2):
                mine = first_head if head == 0 else jnp.logical_not(first_head)
                q = jnp.where(mine, query, jnp.zeros_like(query))
                diag = dot_nt(q, p_ref[1, rows, :])
                diag = jnp.where(allowed, diag, -1e30)
                largest = jnp.max(diag, axis=-1, keepdims=True)
                if i > 0:
                    before = dot_nt(q, p_ref[1, : i * ROWS, :])
                    largest = jnp.maximum(largest, jnp.max(before, axis=-1, keepdims=True))
                diag = jnp.exp(diag - largest)
                total = jnp.sum(diag, axis=-1, keepdims=True)
                if i > 0:
                    before = jnp.exp(before - largest)
                    total = total + jnp.sum(before, axis=-1, keepdims=True)
                inverse = 1.0 / total
                out = dot_nn((diag * inverse).astype(bf16), p_ref[2, rows, :])
                if i > 0:
                    out = out + dot_nn((before * inverse).astype(bf16), p_ref[2, : i * ROWS, :])
                found.append(out)
                lse = jnp.broadcast_to(largest + jnp.log(total), (ROWS, 128))
                lse_ref[0, head : head + 1, rows] = lse.T[0:1]
            out_ref[rows, :] = jnp.where(first_head, found[0], found[1]).astype(bf16)


def attend(length, projected):
    rows = projected.shape[1]
    pairs = HEADS // 2
    return pl.pallas_call(
        attend_kernel,
        grid_spec=pltpu.PrefetchScalarGridSpec(
            num_scalar_prefetch=1,
            grid=(pairs,),
            in_specs=[pl.BlockSpec((3, rows, 128), lambda h, n: (0, 0, h))],
            out_specs=[
                pl.BlockSpec((rows, 128), lambda h, n: (0, h)),
                pl.BlockSpec((1, 8, rows), lambda h, n: (h, 0, 0)),
            ],
        ),
        out_shape=[
            jax.ShapeDtypeStruct((rows, D), bf16),
            jax.ShapeDtypeStruct((pairs, 8, rows), f32),
        ],
        compiler_params=params(),
        cost_estimate=pl.CostEstimate(
            flops=2 * rows * rows * D, bytes_accessed=rows * D * 8, transcendentals=HEADS * rows * rows // 2
        ),
        name="attend",
    )(length, projected)


def attend_back_kernel(len_ref, p_ref, o_ref, g_ref, lse_ref, out_ref, dk_ref, dv_ref):
    blocks = p_ref.shape[1] // ROWS
    scaling = 1.0 / math.sqrt(HEAD)
    lane = lax.broadcasted_iota(jnp.int32, (ROWS, 128), 1)
    first_head = lane < HEAD
    row8 = lax.broadcasted_iota(jnp.int32, (8, 128), 0)
    lane8 = lax.broadcasted_iota(jnp.int32, (8, 128), 1)
    chooser = (lax.div(lane8, HEAD) == row8).astype(f32)
    key_at = lax.broadcasted_iota(jnp.int32, (ROWS, ROWS), 0)
    row_at = lax.broadcasted_iota(jnp.int32, (ROWS, ROWS), 1)
    allowed = key_at <= row_at
    for i in range(blocks):
        rows = slice(i * ROWS, (i + 1) * ROWS)

        @pl.when(i * ROWS < len_ref[0])
        def work():
            dk_ref[:, rows, :] = jnp.zeros((2, ROWS, 128), f32)
            dv_ref[:, rows, :] = jnp.zeros((2, ROWS, 128), f32)
            query = p_ref[0, rows, :] * jnp.asarray(scaling, bf16)
            grad = g_ref[rows, :]
            product = grad.astype(f32) * o_ref[rows, :].astype(f32)
            delta = lax.dot_general(
                chooser,
                product,
                (((1,), (1,)), ((), ())),
                precision=lax.Precision.HIGHEST,
                preferred_element_type=f32,
            )
            grad_query = jnp.zeros((ROWS, 128), f32)
            for j in range(i + 1):
                cols = slice(j * ROWS, (j + 1) * ROWS)
                key = p_ref[1, cols, :]
                value = p_ref[2, cols, :]
                for head in range(2):
                    mine = first_head if head == 0 else jnp.logical_not(first_head)
                    k = jnp.where(mine, key, jnp.zeros_like(key))
                    v = jnp.where(mine, value, jnp.zeros_like(value))
                    scores = dot_nt(k, query)
                    prob = jnp.exp(scores - lse_ref[0, head : head + 1, rows])
                    if i == j:
                        prob = jnp.where(allowed, prob, 0.0)
                    grad_prob = dot_nt(v, grad)
                    grad_scores = (prob * (grad_prob - delta[head : head + 1])).astype(bf16)
                    dv_ref[head, cols, :] += dot_nn(prob.astype(bf16), grad)
                    dk_ref[head, cols, :] += dot_nn(grad_scores, query)
                    grad_query = grad_query + dot_tn(grad_scores, k)
            out_ref[0, rows, :] = (grad_query * scaling).astype(bf16)

    for i in range(blocks):
        rows = slice(i * ROWS, (i + 1) * ROWS)

        @pl.when(i * ROWS < len_ref[0])
        def finish():
            out_ref[1, rows, :] = jnp.where(first_head, dk_ref[0, rows, :], dk_ref[1, rows, :]).astype(bf16)
            out_ref[2, rows, :] = jnp.where(first_head, dv_ref[0, rows, :], dv_ref[1, rows, :]).astype(bf16)


def attend_back(length, projected, heads_out, grad_heads, lse):
    rows = projected.shape[1]
    pairs = HEADS // 2
    return pl.pallas_call(
        attend_back_kernel,
        grid_spec=pltpu.PrefetchScalarGridSpec(
            num_scalar_prefetch=1,
            grid=(pairs,),
            in_specs=[
                pl.BlockSpec((3, rows, 128), lambda h, n: (0, 0, h)),
                pl.BlockSpec((rows, 128), lambda h, n: (0, h)),
                pl.BlockSpec((rows, 128), lambda h, n: (0, h)),
                pl.BlockSpec((1, 8, rows), lambda h, n: (h, 0, 0)),
            ],
            out_specs=pl.BlockSpec((3, rows, 128), lambda h, n: (0, 0, h)),
            scratch_shapes=[pltpu.VMEM((2, rows, 128), f32), pltpu.VMEM((2, rows, 128), f32)],
        ),
        out_shape=jax.ShapeDtypeStruct((3, rows, D), bf16),
        compiler_params=params(),
        cost_estimate=pl.CostEstimate(
            flops=5 * rows * rows * D, bytes_accessed=rows * D * 16, transcendentals=HEADS * rows * rows // 2
        ),
        name="attend_back",
    )(length, projected, heads_out, grad_heads, lse)


def feed_kernel(plan, len_ref, row_ref, grad_ref, *refs):
    tok0, tok1, pass0, pass1, ho0, ho1, cot0, cot1, table_ref, gain_ref = refs[:10]
    many = plan.sharers if plan.paired else 1
    pieces, refs = refs[10 : 10 + many], refs[10 + many :]
    res0, res1, gh0, gh1, hid0, hid1, small_ref = refs[:7]
    outs, (w_ref, acc_ref, stage_ref, sem_ref) = refs[7:-4], refs[-4:]
    b = pl.program_id(0)
    many0 = last_block(len_ref[0]) + 1
    many1 = last_block(len_ref[1]) + 1
    early = b < many0

    @pl.when(b == 0)
    def clear():
        load_weight(plan, row_ref, pieces, w_ref, sem_ref.at[0])
        acc_ref[...] = jnp.zeros_like(acc_ref)
        small_ref[...] = jnp.zeros_like(small_ref)

    def block(tok, pas, ho, cot, res, gh, hid, start, length):
        hot = onehot_rows(pas[0])
        entry = tok[...].astype(f32) + dot_tn(hot, table_ref[...])
        at = start + lax.broadcasted_iota(jnp.int32, (ROWS, 1), 0)
        live = at < length
        heads = ho[...]
        attention = dot_nn(heads, w_ref[:, 0:D])
        hidden = entry + attention
        unit, scale = normalized(hidden)
        gain = gain_ref[...]
        normed = (unit * gain).astype(bf16)
        grad_feed = jnp.where(live, cot[...].astype(f32), 0.0).astype(bf16)
        feed = jnp.zeros((ROWS, D), f32)
        grad_normed = jnp.zeros((ROWS, D), f32)
        for k in range(CHUNKS):
            up = slice(D + k * D, D + (k + 1) * D)
            down = slice(D + FF + k * D, D + FF + (k + 1) * D)
            x = dot_nn(normed, w_ref[:, up])
            grad_act = dot_nt(grad_feed, w_ref[:, down])
            c0 = math.sqrt(2.0 / math.pi)
            square = x * x
            bent = jnp.tanh(x * (c0 + (c0 * 0.044715) * square))
            half = 0.5 + 0.5 * bent
            slope = half + (0.5 * x) * (1.0 - bent * bent) * (c0 + (3.0 * c0 * 0.044715) * square)
            act = (x * half).astype(bf16)
            grad_x = (slope * grad_act).astype(bf16)
            feed = feed + dot_nn(act, w_ref[:, down])
            grad_normed = grad_normed + dot_nt(grad_x, w_ref[:, up])
            acc_ref[:, up] += dot_tn(normed, grad_x)
            acc_ref[:, down] += dot_tn(act, grad_feed)
        res[...] = jnp.where(live, hidden + feed, 0.0).astype(bf16)
        small_ref[0:8] += fold_rows(grad_normed * unit)
        small_ref[8:16] += fold_rows(jnp.where(live, entry * entry, 0.0))
        small_ref[16:24] += fold_rows(jnp.where(live, attention * attention, 0.0))
        small_ref[24:32] += fold_rows(jnp.where(live, feed * feed, 0.0))
        grad_hidden = grad_feed.astype(f32) + norm_back(grad_normed * gain, unit, scale)
        hid[...] = grad_hidden
        grad_attention = grad_hidden.astype(bf16)
        acc_ref[:, 0:D] += dot_tn(heads, grad_attention)
        gh[...] = dot_nt(grad_attention, w_ref[:, 0:D]).astype(bf16)

    @pl.when(early)
    def first():
        block(tok0, pass0, ho0, cot0, res0, gh0, hid0, b * ROWS, len_ref[0])

    @pl.when(jnp.logical_and(jnp.logical_not(early), b < many0 + many1))
    def second():
        block(tok1, pass1, ho1, cot1, res1, gh1, hid1, (b - many0) * ROWS, len_ref[1])

    @pl.when(b == pl.num_programs(0) - 1)
    def finish():
        store_grads(plan, grad_ref, acc_ref, outs, stage_ref, sem_ref)


def feed(plan, lengths, piece_rows, grad_rows, tokens, pass_rows, heads_out, cotangent, table, gain, pieces, width):
    rows = tokens[0].shape[0]
    at0 = lambda b, n, r, g: (jnp.minimum(b, last_block(n[0])), 0)
    at1 = lambda b, n, r, g: (jnp.clip(b - last_block(n[0]) - 1, 0, last_block(n[1])), 0)
    row0 = pl.BlockSpec((ROWS, D), at0)
    row1 = pl.BlockSpec((ROWS, D), at1)
    pas0 = pl.BlockSpec((1, 1, ROWS), lambda *a: at0(*a) + (0,))
    pas1 = pl.BlockSpec((1, 1, ROWS), lambda *a: at1(*a) + (0,))
    narrow = jax.ShapeDtypeStruct((rows, D), bf16)
    wide = jax.ShapeDtypeStruct((rows, D), f32)
    grads = grad_shapes(plan, width)
    anywhere = pl.BlockSpec(memory_space=pl.ANY)
    return pl.pallas_call(
        functools.partial(feed_kernel, plan),
        grid_spec=pltpu.PrefetchScalarGridSpec(
            num_scalar_prefetch=3,
            grid=(2 * rows // ROWS,),
            in_specs=[
                row0, row1, pas0, pas1, row0, row1, row0, row1,
                pl.BlockSpec((8, D), lambda *a: (0, 0)),
                pl.BlockSpec((1, D), lambda *a: (0, 0)),
            ]
            + [anywhere] * len(pieces),
            out_specs=[row0, row1, row0, row1, row0, row1, pl.BlockSpec((32, D), lambda *a: (0, 0))]
            + [anywhere] * len(grads),
            scratch_shapes=[
                pltpu.VMEM((D, width), bf16),
                pltpu.VMEM((D, width), f32),
                pltpu.VMEM(stage_shape(plan, width), bf16),
                pltpu.SemaphoreType.DMA((2,)),
            ],
        ),
        out_shape=[narrow, narrow, narrow, narrow, wide, wide, jax.ShapeDtypeStruct((32, D), f32)] + grads,
        compiler_params=params(),
        cost_estimate=pl.CostEstimate(
            flops=2 * 6 * rows * D * width, bytes_accessed=2 * rows * D * 14 + D * width * 4, transcendentals=2 * rows * FF
        ),
        name="feed",
    )(lengths, piece_rows, grad_rows, tokens[0], tokens[1], pass_rows[0], pass_rows[1], heads_out[0], heads_out[1],
      cotangent[0], cotangent[1], table, gain, *pieces)


def project_back_kernel(plan, final, len_ref, row_ref, grad_ref, tok_ref, pass_ref, g_ref, hid_ref, table_ref, gain_ref, *rest):
    many = plan.sharers if plan.paired else 1
    pieces, rest = rest[:many], rest[many:]
    if final:
        before_ref, out_ref, small_ref, *outs, acc_ref, w_ref, stage_ref, sem_ref = rest
    else:
        out_ref, small_ref, acc_ref, w_ref, sem_ref = rest
    b = pl.program_id(0)

    @pl.when(b == 0)
    def clear():
        load_weight(plan, row_ref, pieces, w_ref, sem_ref.at[0])
        acc_ref[...] = before_ref[...] if final else jnp.zeros_like(acc_ref)
        small_ref[...] = jnp.zeros_like(small_ref)

    @pl.when(b <= last_block(len_ref[0]))
    def work():
        hot = onehot_rows(pass_ref[0])
        entry = tok_ref[...].astype(f32) + dot_tn(hot, table_ref[...])
        unit, scale = normalized(entry)
        gain = gain_ref[...]
        normed = (unit * gain).astype(bf16)
        grad_normed = jnp.zeros((ROWS, D), f32)
        for part in range(3):
            cols = slice(part * D, (part + 1) * D)
            grad = g_ref[part]
            acc_ref[:, cols] += dot_tn(normed, grad)
            grad_normed = grad_normed + dot_nt(grad, w_ref[:, cols])
        small_ref[0:8] += fold_rows(grad_normed * unit)
        grad_entry = hid_ref[...] + norm_back(grad_normed * gain, unit, scale)
        out_ref[...] = grad_entry.astype(bf16)
        high = grad_entry.astype(bf16)
        rest_one = grad_entry - high.astype(f32)
        low = rest_one.astype(bf16)
        lower = (rest_one - low.astype(f32)).astype(bf16)
        small_ref[8:16] += dot_nn(hot, high) + dot_nn(hot, low) + dot_nn(hot, lower)

    if final:
        @pl.when(b == pl.num_programs(0) - 1)
        def finish():
            store_grads(plan, grad_ref, acc_ref, outs, stage_ref, sem_ref)


def project_back(plan, length, piece_rows, grad_rows, tokens, pass_rows, grads, grad_hidden, table, gain, pieces, before=None):
    rows = tokens.shape[0]
    final = before is not None
    at = lambda b, n, r, g: (jnp.minimum(b, last_block(n[0])), 0)
    row = pl.BlockSpec((ROWS, D), at)
    anywhere = pl.BlockSpec(memory_space=pl.ANY)
    whole = pl.BlockSpec((D, 3 * D), lambda *a: (0, 0), pipeline_mode=pl.Buffered(1))
    in_specs = [
        row,
        pl.BlockSpec((1, 1, ROWS), lambda *a: at(*a) + (0,)),
        pl.BlockSpec((3, ROWS, D), lambda *a: (0,) + at(*a)),
        row,
        pl.BlockSpec((8, D), lambda *a: (0, 0)),
        pl.BlockSpec((1, D), lambda *a: (0, 0)),
    ] + [anywhere] * len(pieces)
    operands = [length, piece_rows, grad_rows, tokens, pass_rows, grads, grad_hidden, table, gain, *pieces]
    sums = jax.ShapeDtypeStruct((D, 3 * D), f32)
    out_shape = [jax.ShapeDtypeStruct((rows, D), bf16), jax.ShapeDtypeStruct((16, D), f32)]
    out_specs = [row, pl.BlockSpec((16, D), lambda *a: (0, 0))]
    scratch = [pltpu.VMEM((D, 3 * D), bf16)]
    if final:
        in_specs.append(whole)
        operands.append(before)
        shapes = grad_shapes(plan, 3 * D)
        out_shape += shapes
        out_specs += [anywhere] * len(shapes)
        scratch = [pltpu.VMEM((D, 3 * D), f32)] + scratch + [pltpu.VMEM(stage_shape(plan, 3 * D), bf16)]
    else:
        out_shape.append(sums)
        out_specs.append(pl.BlockSpec((D, 3 * D), lambda *a: (0, 0)))
    return pl.pallas_call(
        functools.partial(project_back_kernel, plan, final),
        grid_spec=pltpu.PrefetchScalarGridSpec(
            num_scalar_prefetch=3,
            grid=(rows // ROWS,),
            in_specs=in_specs,
            out_specs=out_specs,
            scratch_shapes=scratch + [pltpu.SemaphoreType.DMA((2,))],
        ),
        out_shape=out_shape,
        compiler_params=params(),
        cost_estimate=pl.CostEstimate(
            flops=4 * rows * D * 3 * D, bytes_accessed=rows * D * 14 + D * D * 18, transcendentals=0
        ),
        name="project_back",
    )(*operands)


def pick_kernel(index_ref, in_ref, out_ref, sem_ref):
    copies = [
        pltpu.make_async_copy(in_ref.at[index_ref[n]], out_ref.at[n], sem_ref) for n in range(out_ref.shape[0])
    ]
    for copy in copies:
        copy.start()
    for copy in copies:
        copy.wait()


def pick(index, blocks):
    shape = index.shape + blocks.shape[1:]
    return pl.pallas_call(
        pick_kernel,
        grid_spec=pltpu.PrefetchScalarGridSpec(
            num_scalar_prefetch=1,
            grid=(1,),
            in_specs=[pl.BlockSpec(memory_space=pl.ANY)],
            out_specs=pl.BlockSpec(shape, lambda b, n: (0, 0, 0)),
            scratch_shapes=[pltpu.SemaphoreType.DMA],
        ),
        out_shape=jax.ShapeDtypeStruct(shape, blocks.dtype),
        compiler_params=params(),
        cost_estimate=pl.CostEstimate(flops=0, bytes_accessed=4 * math.prod(shape), transcendentals=0),
        name="pick",
    )(index, blocks)


def settle_kernel(index_ref, early_ref, late_ref, out_ref):
    first = pl.program_id(0) * out_ref.shape[0]
    rows = out_ref.shape[1]
    at = lax.broadcasted_iota(jnp.int32, (rows, 1), 0)
    for n in range(out_ref.shape[0]):
        live = at < index_ref[2, first + n]
        source = index_ref[1, first + n]

        @pl.when(index_ref[0, first + n] == 0)
        def early():
            out_ref[n] = jnp.where(live, early_ref[source].astype(f32), 0.0)

        @pl.when(index_ref[0, first + n] != 0)
        def late():
            out_ref[n] = jnp.where(live, late_ref[source].astype(f32), 0.0)


def settle(index, early, late):
    many = index.shape[1]
    step = 4
    whole = pl.BlockSpec(early.shape, lambda b, n: (0, 0, 0), pipeline_mode=pl.Buffered(1))
    return pl.pallas_call(
        settle_kernel,
        grid_spec=pltpu.PrefetchScalarGridSpec(
            num_scalar_prefetch=1,
            grid=(many // step,),
            in_specs=[whole, whole],
            out_specs=pl.BlockSpec((step,) + early.shape[1:], lambda b, n: (b, 0, 0)),
        ),
        out_shape=jax.ShapeDtypeStruct((many,) + early.shape[1:], f32),
        compiler_params=params(),
        cost_estimate=pl.CostEstimate(flops=0, bytes_accessed=6 * many * early[0].size, transcendentals=0),
        name="settle",
    )(index, early, late)


def after(values, *others):
    return lax.optimization_barrier((values,) + others)[0]


def swap(blocks):
    return lax.all_to_all(blocks, "dp", split_axis=0, concat_axis=0, tiled=True)


def total_over(values, axes, devices):
    flat = values.reshape(devices, -1)
    parts = lax.all_to_all(flat, axes, split_axis=0, concat_axis=0, tiled=True)
    mine = jnp.sum(parts, axis=0, keepdims=True)
    spread = jnp.broadcast_to(mine, flat.shape)
    return lax.all_to_all(spread, axes, split_axis=0, concat_axis=0, tiled=True).reshape(values.shape)


def per_device(
    groups,
    width_all,
    tokens,
    passes,
    lengths,
    dealing,
    pass_table,
    gain_first,
    to_heads,
    from_heads,
    gain_second,
    expand,
    shrink,
    cotangent,
):
    axes = ("dp", "fsdp")
    slots, part, unused_width = tokens.shape
    seq_len = part * groups
    order = jnp.arange(slots, dtype=jnp.int32)
    here = lax.axis_index("dp")
    ordering = dealing[0, 0]
    sizes = lengths[0]

    ahead = (sizes[None, :] > sizes[:, None]) | (
        (sizes[None, :] == sizes[:, None]) & (order[None, :] < order[:, None])
    )
    rank = jnp.sum(ahead.astype(jnp.int32), axis=1)
    ranked = jnp.sum(jnp.where(rank[None, :] == order[:, None], order[None, :], 0), axis=1)
    place = jnp.sum(jnp.where(ordering[None, :] == order[:, None], order[None, :], 0), axis=1)
    early_seqs = ranked[:groups]
    late_seqs = ranked[groups:][::-1]
    from_early = jnp.sum(jnp.where(early_seqs[:, None] == order[None, :], place[None, :], 0), axis=1)
    from_late = jnp.sum(jnp.where(late_seqs[:, None] == order[None, :], place[None, :], 0), axis=1)
    slot_rank = jnp.sum(jnp.where(ordering[:, None] == order[None, :], rank[None, :], 0), axis=1)
    slot_size = jnp.sum(jnp.where(ordering[:, None] == order[None, :], sizes[None, :], 0), axis=1)
    is_late = (slot_rank >= groups).astype(jnp.int32)
    source = jnp.where(is_late == 1, slots - 1 - slot_rank, slot_rank)
    back_index = jnp.stack([is_late, source, slot_size - here * part])
    my_seqs = jnp.stack([early_seqs[here], late_seqs[here]])
    my_sizes = jnp.sum(jnp.where(my_seqs[:, None] == order[None, :], sizes[None, :], 0), axis=1)

    row_count = to_heads.shape[0]
    narrow = jnp.concatenate(
        [
            from_heads,
            expand.reshape(row_count, D, CHUNKS).transpose(0, 2, 1).reshape(row_count, FF),
            shrink.reshape(row_count, CHUNKS * D),
        ],
        axis=1,
    )
    plan = Plan(groups, width_all // groups, row_count)
    fsdp_here = lax.axis_index("fsdp")
    if plan.paired:
        head_held = plan.gather_groups(to_heads)
        wide_held = plan.gather_groups(after(narrow, head_held))
        head_pieces = plan.gather_sharers(head_held)
        wide_pieces = plan.gather_sharers(after(wide_held, *head_pieces))
        piece_rows = plan.piece_rows(here, fsdp_here)
        grad_rows = plan.grad_rows(here, fsdp_here)
    else:
        head_pieces = (lax.all_gather(to_heads, axes, axis=0, tiled=True),)
        wide_pieces = (lax.all_gather(narrow, axes, axis=0, tiled=True),)
        piece_rows = grad_rows = jnp.zeros((1,), jnp.int32)

    my_passes = [passes[my_seqs[m]].reshape(seq_len // ROWS, 1, ROWS) for m in range(2)]
    one_size = [my_sizes[m : m + 1] for m in range(2)]
    table = jnp.zeros((8, D), bf16).at[:PASSES].set(pass_table)
    gain_one = gain_first.astype(f32).reshape(1, D)
    gain_two = gain_second.astype(f32).reshape(1, D)

    index = (from_early, from_late)
    projected, heads_out, lse = [None, None], [None, None], [None, None]

    def forward(m, rows):
        projected[m] = project(
            plan, one_size[m], piece_rows, rows, my_passes[m], table, gain_one, head_pieces
        )

    def mix(m):
        heads_out[m], lse[m] = attend(one_size[m], projected[m])

    tokens0 = swap(pick(index[0], tokens))
    tokens1 = swap(after(pick(index[1], tokens), tokens0))
    my_tokens = [tokens0.reshape(seq_len, D), tokens1.reshape(seq_len, D)]
    forward(0, my_tokens[0])
    grads0 = swap(after(pick(index[0], cotangent), tokens1, projected[0]))
    mix(0)
    forward(1, my_tokens[1])
    grads1 = swap(after(pick(index[1], cotangent), grads0, projected[1]))
    mix(1)
    my_grads = [grads0.reshape(seq_len, D), grads1.reshape(seq_len, D)]

    res0, res1, gh0, gh1, hid0, hid1, feed_small, *wide_grads = feed(
        plan, my_sizes, piece_rows, grad_rows, my_tokens, my_passes, heads_out, my_grads, table, gain_two,
        wide_pieces, D + 2 * FF,
    )

    def reduce(grads):
        if not plan.paired:
            return lax.psum_scatter(grads[0], axes, scatter_dimension=0, tiled=True).astype(f32)
        parts = [plan.reduce(grads[2 * n], grads[2 * n + 1], plan.orders[n]) for n in range(2)]
        return jnp.concatenate(parts, axis=1)

    wide_owned = reduce(wide_grads)
    result0 = swap(res0.reshape(groups, part, D))
    result1 = swap(after(res1, result0).reshape(groups, part, D))
    back0 = attend_back(one_size[0], projected[0], heads_out[0], gh0, lse[0])
    entry0, small0, head_sum = project_back(
        plan, one_size[0], piece_rows, grad_rows, my_tokens[0], my_passes[0], back0, hid0, table, gain_one,
        head_pieces,
    )
    back1 = attend_back(one_size[1], projected[1], heads_out[1], gh1, lse[1])
    entry1, small1, *head_grads = project_back(
        plan, one_size[1], piece_rows, grad_rows, my_tokens[1], my_passes[1], back1, hid1, table, gain_one,
        head_pieces, head_sum,
    )
    moved0 = swap(after(entry0, result1).reshape(groups, part, D))
    moved1 = swap(after(entry1, moved0).reshape(groups, part, D))
    head_owned = reduce(head_grads)
    results, entries = (result0, result1), (moved0, moved1)

    squares = jnp.sum(feed_small[8:].reshape(3, 8 * D), axis=1)
    counted = jnp.sum(my_sizes).astype(f32)
    last_row = jnp.zeros((1, D), f32).at[0, :3].set(squares).at[0, 3].set(counted)
    small = small0 + small1
    gathered = jnp.concatenate(
        [
            small[8 : 8 + PASSES],
            jnp.sum(small[:8], axis=0, keepdims=True),
            jnp.sum(feed_small[:8], axis=0, keepdims=True),
            last_row,
        ],
        axis=0,
    )
    totals = total_over(gathered, axes, width_all)
    root_squares = jnp.sqrt(totals[7, :3] / (totals[7, 3] * D))

    grad_expand = wide_owned[:, D : D + FF].reshape(row_count, CHUNKS, D).transpose(0, 2, 1)
    return (
        settle(back_index, results[0], results[1]),
        settle(back_index, entries[0], entries[1]),
        totals[:PASSES],
        totals[PASSES],
        head_owned,
        wide_owned[:, :D],
        totals[PASSES + 1],
        grad_expand.reshape(row_count, FF),
        wide_owned[:, D + FF :].reshape(row_count * CHUNKS, D),
        root_squares,
    )


def solution(mesh):
    groups = mesh.shape["dp"]
    weight_spec = P(("dp", "fsdp"), None)
    block_spec = P("fsdp", "dp", None)
    in_specs = (
        block_spec,
        P("fsdp", None),
        P("fsdp", None),
        P("dp", "fsdp", None),
        P(),
        P(),
        weight_spec,
        weight_spec,
        P(),
        weight_spec,
        weight_spec,
        block_spec,
    )
    out_specs = (
        block_spec,
        block_spec,
        P(),
        P(),
        weight_spec,
        weight_spec,
        P(),
        weight_spec,
        weight_spec,
        P(),
    )
    body = functools.partial(per_device, groups, groups * mesh.shape["fsdp"])
    return jax.shard_map(body, mesh=mesh, in_specs=in_specs, out_specs=out_specs, check_vma=False)
```

```python
import math
import functools

import jax
import jax.numpy as jnp
from jax import lax
from jax.experimental import pallas as pl
from jax.experimental.pallas import tpu as pltpu
from jax.sharding import PartitionSpec as P

D = 768
HEADS = 12
HEAD = 64
FF = 3072
PASSES = 5
EPS = 1e-05
ROWS = 256
CHUNKS = FF // D
VMEM_MOST = 64000 * 1024

f32 = jnp.float32
bf16 = jnp.bfloat16


def dot_nn(a, b):
    return lax.dot_general(a, b, (((1,), (0,)), ((), ())), preferred_element_type=f32)


def dot_nt(a, b):
    return lax.dot_general(a, b, (((1,), (1,)), ((), ())), preferred_element_type=f32)


def dot_tn(a, b):
    return lax.dot_general(a, b, (((0,), (0,)), ((), ())), preferred_element_type=f32)


def params(**more):
    return pltpu.CompilerParams(vmem_limit_bytes=VMEM_MOST, **more)


def normalized(values):
    centred = values - jnp.mean(values, axis=-1, keepdims=True)
    spread = jnp.mean(centred * centred, axis=-1, keepdims=True)
    scale = lax.rsqrt(spread + EPS)
    return centred * scale, scale


def norm_back(grad_unit, unit, scale):
    first = jnp.mean(grad_unit, axis=-1, keepdims=True)
    second = jnp.mean(grad_unit * unit, axis=-1, keepdims=True)
    return scale * (grad_unit - first - unit * second)


def onehot_rows(pass_row):
    ids = lax.broadcasted_iota(jnp.int32, (8, pass_row.shape[-1]), 0)
    return (ids == pass_row).astype(f32).astype(bf16)


def fold_rows(values):
    rows, width = values.shape
    return jnp.sum(values.reshape(rows // 8, 8, width), axis=0)


def last_block(length):
    return lax.div(length + (ROWS - 1), ROWS) - 1


def bits_of(count):
    return count.bit_length() - 1


class Plan:
    def __init__(self, groups, sharers, rows):
        self.groups, self.sharers, self.rows = groups, sharers, rows
        self.count = groups * sharers
        self.paired = rows % 8 == 0 and self.count & (self.count - 1) == 0 and sharers >= 4 and groups >= 2
        over_dp = [("dp", bit) for bit in range(bits_of(groups))]
        over_x = [("fsdp", bit) for bit in range(1, bits_of(sharers))]
        self.gather_dp = over_dp[::-1]
        self.gather_fsdp = over_x[::-1] + [("fsdp", 0)]
        self.orders = (
            [("fsdp", 0)] + over_x + over_dp,
            [("fsdp", 0)] + over_dp[:1] + over_x + over_dp[1:],
        )

    def size(self, axis):
        return self.groups if axis == "dp" else self.sharers

    def exchange(self, values, axis, bit):
        pairs = [(i, i ^ (1 << bit)) for i in range(self.size(axis))]
        return lax.ppermute(values, axis, pairs)

    def gather_groups(self, shard):
        held = shard[None]
        for axis, bit in self.gather_dp:
            held = jnp.concatenate([held, self.exchange(held, axis, bit)], axis=0)
        return held

    def gather_x(self, held):
        pieces = {0: held}
        for axis, bit in self.gather_fsdp[:-1]:
            for name in list(pieces):
                pieces[name | (1 << bit)] = self.exchange(pieces[name], axis, bit)
        return pieces

    def gather_core(self, pieces):
        axis, bit = self.gather_fsdp[-1]
        found = dict(pieces)
        for name in pieces:
            found[name | (1 << bit)] = self.exchange(pieces[name], axis, bit)
        return tuple(found[name] for name in range(self.sharers))

    def piece_rows(self, dp, fsdp):
        found = []
        for f in range(self.sharers):
            for n in range(self.groups):
                rel = sum(((n >> k) & 1) << bit for k, (axis, bit) in enumerate(self.gather_dp))
                found.append(((dp ^ rel) * self.sharers + (fsdp ^ f)) * self.rows)
        return jnp.stack(found).astype(jnp.int32)

    def grad_rows(self, dp, fsdp):
        found = []
        for order in self.orders:
            for place in range(self.count):
                rel = {"dp": 0, "fsdp": 0}
                for k, (axis, bit) in enumerate(order):
                    rel[axis] |= ((place >> (len(order) - 1 - k)) & 1) << bit
                found.append(((dp ^ rel["dp"]) * self.sharers + (fsdp ^ rel["fsdp"])) * self.rows)
        return jnp.stack(found).astype(jnp.int32)

    def reduce_step(self, state, step, *gate):
        found = []
        for (keep, send), order in zip(state, self.orders):
            axis, bit = order[step]
            other = self.exchange(after(send, gate), axis, bit).astype(f32)
            total = keep.astype(f32)
            if step == len(order) - 1:
                found.append((total + other)[0])
            else:
                half = keep.shape[0] // 2
                found.append(
                    ((total[:half] + other[:half]).astype(bf16), (total[half:] + other[half:]).astype(bf16))
                )
        return found


def load_weight(plan, rows_ref, pieces, weight_ref, sem_ref):
    if not plan.paired:
        copies = [pltpu.make_async_copy(pieces[0], weight_ref, sem_ref)]
    else:
        copies = []
        for f in range(plan.sharers):
            for n in range(plan.groups):
                at = pl.multiple_of(rows_ref[f * plan.groups + n], 8)
                target = weight_ref.at[pl.ds(at, plan.rows), :]
                copies.append(pltpu.make_async_copy(pieces[f].at[n], target, sem_ref))
    for copy in copies:
        copy.start()
    for copy in copies:
        copy.wait()


def grad_shapes(plan, width):
    if not plan.paired:
        return [jax.ShapeDtypeStruct((D, width), bf16)]
    half = plan.count // 2
    cut = first_part(width)
    return [jax.ShapeDtypeStruct((half, plan.rows, w), bf16) for w in (cut, cut, width - cut, width - cut)]


def first_part(width):
    step = grad_step(width)
    return (width // step + 1) // 2 * step


def grad_step(width):
    return D if width % D == 0 and width // D > 3 else D // 2


def stage_shape(plan, width):
    step = grad_step(width)
    return (2, plan.count, plan.rows, step) if plan.paired else (2, D, step)


def store_grads(plan, rows_ref, acc_ref, outs, stage_ref, sem_ref):
    width = acc_ref.shape[1]
    step = grad_step(width)
    cut = first_part(width)
    half = plan.count // 2
    waiting = []
    for n in range(width // step):
        slot = n % 2
        cols = slice(n * step, (n + 1) * step)
        if len(waiting) == 2:
            for copy in waiting.pop(0):
                copy.wait()
        if not plan.paired:
            stage_ref[slot] = acc_ref[:, cols].astype(bf16)
            copies = [pltpu.make_async_copy(stage_ref.at[slot], outs[0].at[:, cols], sem_ref.at[slot])]
        else:
            late = n * step >= cut
            base = plan.count if late else 0
            start = n * step - (cut if late else 0)

            def fill(place, carry):
                at = pl.multiple_of(rows_ref[base + place], 8)
                stage_ref[slot, place] = acc_ref[pl.ds(at, plan.rows), cols].astype(bf16)
                return carry

            lax.fori_loop(0, plan.count, fill, 0)
            keep, send = outs[2:4] if late else outs[0:2]
            there = slice(start, start + step)
            copies = [
                pltpu.make_async_copy(stage_ref.at[slot, 0:half], keep.at[:, :, there], sem_ref.at[slot]),
                pltpu.make_async_copy(stage_ref.at[slot, half:], send.at[:, :, there], sem_ref.at[slot]),
            ]
        for copy in copies:
            copy.start()
        waiting.append(copies)
    for copies in waiting:
        for copy in copies:
            copy.wait()


def project_kernel(plan, len_ref, row_ref, tok_ref, pass_ref, table_ref, gain_ref, *rest):
    pieces, (out_ref, w_ref, sem_ref) = rest[:-3], rest[-3:]

    @pl.when(pl.program_id(0) == 0)
    def load():
        load_weight(plan, row_ref, pieces, w_ref, sem_ref)

    @pl.when(pl.program_id(0) <= last_block(len_ref[0]))
    def work():
        hot = onehot_rows(pass_ref[0])
        entry = tok_ref[...].astype(f32) + dot_tn(hot, table_ref[...])
        unit, unused = normalized(entry)
        normed = (unit * gain_ref[...]).astype(bf16)
        for part in range(3):
            out_ref[part] = dot_nn(normed, w_ref[:, part * D : (part + 1) * D]).astype(bf16)


def project(plan, length, piece_rows, tokens, pass_rows, table, gain, pieces):
    rows = tokens.shape[0]
    at = lambda b, n, r: (jnp.minimum(b, last_block(n[0])), 0)
    return pl.pallas_call(
        functools.partial(project_kernel, plan),
        grid_spec=pltpu.PrefetchScalarGridSpec(
            num_scalar_prefetch=2,
            grid=(rows // ROWS,),
            in_specs=[
                pl.BlockSpec((ROWS, D), at),
                pl.BlockSpec((1, 1, ROWS), lambda b, n, r: at(b, n, r) + (0,)),
                pl.BlockSpec((8, D), lambda b, n, r: (0, 0)),
                pl.BlockSpec((1, D), lambda b, n, r: (0, 0)),
            ]
            + [pl.BlockSpec(memory_space=pl.ANY)] * len(pieces),
            out_specs=pl.BlockSpec((3, ROWS, D), lambda b, n, r: (0,) + at(b, n, r)),
            scratch_shapes=[pltpu.VMEM((D, 3 * D), bf16), pltpu.SemaphoreType.DMA],
        ),
        out_shape=jax.ShapeDtypeStruct((3, rows, D), bf16),
        compiler_params=params(),
        cost_estimate=pl.CostEstimate(
            flops=2 * rows * D * 3 * D, bytes_accessed=rows * D * 8 + D * D * 6, transcendentals=0
        ),
        name="project",
    )(length, piece_rows, tokens, pass_rows, table, gain, *pieces)


def attend_kernel(len_ref, p_ref, out_ref, lse_ref):
    blocks = p_ref.shape[1] // ROWS
    lane = lax.broadcasted_iota(jnp.int32, (ROWS, 128), 1)
    first_head = lane < HEAD
    here = lax.broadcasted_iota(jnp.int32, (ROWS, ROWS), 0)
    there = lax.broadcasted_iota(jnp.int32, (ROWS, ROWS), 1)
    allowed = there <= here
    for i in range(blocks):
        rows = slice(i * ROWS, (i + 1) * ROWS)

        @pl.when(i * ROWS < len_ref[0])
        def work():
            query = p_ref[0, rows, :] * jnp.asarray(1.0 / math.sqrt(HEAD), bf16)
            found = []
            for head in range(2):
                mine = first_head if head == 0 else jnp.logical_not(first_head)
                q = jnp.where(mine, query, jnp.zeros_like(query))
                diag = dot_nt(q, p_ref[1, rows, :])
                diag = jnp.where(allowed, diag, -1e30)
                largest = jnp.max(diag, axis=-1, keepdims=True)
                if i > 0:
                    before = dot_nt(q, p_ref[1, : i * ROWS, :])
                    largest = jnp.maximum(largest, jnp.max(before, axis=-1, keepdims=True))
                diag = jnp.exp(diag - largest)
                total = jnp.sum(diag, axis=-1, keepdims=True)
                if i > 0:
                    before = jnp.exp(before - largest)
                    total = total + jnp.sum(before, axis=-1, keepdims=True)
                inverse = 1.0 / total
                out = dot_nn((diag * inverse).astype(bf16), p_ref[2, rows, :])
                if i > 0:
                    out = out + dot_nn((before * inverse).astype(bf16), p_ref[2, : i * ROWS, :])
                found.append(out)
                lse = jnp.broadcast_to(largest + jnp.log(total), (ROWS, 128))
                lse_ref[0, head : head + 1, rows] = lse.T[0:1]
            out_ref[rows, :] = jnp.where(first_head, found[0], found[1]).astype(bf16)


def attend(length, projected):
    rows = projected.shape[1]
    pairs = HEADS // 2
    return pl.pallas_call(
        attend_kernel,
        grid_spec=pltpu.PrefetchScalarGridSpec(
            num_scalar_prefetch=1,
            grid=(pairs,),
            in_specs=[pl.BlockSpec((3, rows, 128), lambda h, n: (0, 0, h))],
            out_specs=[
                pl.BlockSpec((rows, 128), lambda h, n: (0, h)),
                pl.BlockSpec((1, 8, rows), lambda h, n: (h, 0, 0)),
            ],
        ),
        out_shape=[
            jax.ShapeDtypeStruct((rows, D), bf16),
            jax.ShapeDtypeStruct((pairs, 8, rows), f32),
        ],
        compiler_params=params(),
        cost_estimate=pl.CostEstimate(
            flops=2 * rows * rows * D, bytes_accessed=rows * D * 8, transcendentals=HEADS * rows * rows // 2
        ),
        name="attend",
    )(length, projected)


def attend_back_kernel(len_ref, p_ref, o_ref, g_ref, lse_ref, out_ref, dk_ref, dv_ref):
    blocks = p_ref.shape[1] // ROWS
    scaling = 1.0 / math.sqrt(HEAD)
    lane = lax.broadcasted_iota(jnp.int32, (ROWS, 128), 1)
    first_head = lane < HEAD
    row8 = lax.broadcasted_iota(jnp.int32, (8, 128), 0)
    lane8 = lax.broadcasted_iota(jnp.int32, (8, 128), 1)
    chooser = (lax.div(lane8, HEAD) == row8).astype(f32)
    key_at = lax.broadcasted_iota(jnp.int32, (ROWS, ROWS), 0)
    row_at = lax.broadcasted_iota(jnp.int32, (ROWS, ROWS), 1)
    allowed = key_at <= row_at
    for i in range(blocks):
        rows = slice(i * ROWS, (i + 1) * ROWS)

        @pl.when(i * ROWS < len_ref[0])
        def work():
            dk_ref[:, rows, :] = jnp.zeros((2, ROWS, 128), f32)
            dv_ref[:, rows, :] = jnp.zeros((2, ROWS, 128), f32)
            query = p_ref[0, rows, :] * jnp.asarray(scaling, bf16)
            grad = g_ref[rows, :]
            product = grad.astype(f32) * o_ref[rows, :].astype(f32)
            delta = lax.dot_general(
                chooser,
                product,
                (((1,), (1,)), ((), ())),
                precision=lax.Precision.HIGHEST,
                preferred_element_type=f32,
            )
            grad_query = jnp.zeros((ROWS, 128), f32)
            for j in range(i + 1):
                cols = slice(j * ROWS, (j + 1) * ROWS)
                key = p_ref[1, cols, :]
                value = p_ref[2, cols, :]
                for head in range(2):
                    mine = first_head if head == 0 else jnp.logical_not(first_head)
                    k = jnp.where(mine, key, jnp.zeros_like(key))
                    v = jnp.where(mine, value, jnp.zeros_like(value))
                    scores = dot_nt(k, query)
                    prob = jnp.exp(scores - lse_ref[0, head : head + 1, rows])
                    if i == j:
                        prob = jnp.where(allowed, prob, 0.0)
                    grad_prob = dot_nt(v, grad)
                    grad_scores = (prob * (grad_prob - delta[head : head + 1])).astype(bf16)
                    dv_ref[head, cols, :] += dot_nn(prob.astype(bf16), grad)
                    dk_ref[head, cols, :] += dot_nn(grad_scores, query)
                    grad_query = grad_query + dot_tn(grad_scores, k)
            out_ref[0, rows, :] = (grad_query * scaling).astype(bf16)

    for i in range(blocks):
        rows = slice(i * ROWS, (i + 1) * ROWS)

        @pl.when(i * ROWS < len_ref[0])
        def finish():
            out_ref[1, rows, :] = jnp.where(first_head, dk_ref[0, rows, :], dk_ref[1, rows, :]).astype(bf16)
            out_ref[2, rows, :] = jnp.where(first_head, dv_ref[0, rows, :], dv_ref[1, rows, :]).astype(bf16)


def attend_back(length, projected, heads_out, grad_heads, lse):
    rows = projected.shape[1]
    pairs = HEADS // 2
    return pl.pallas_call(
        attend_back_kernel,
        grid_spec=pltpu.PrefetchScalarGridSpec(
            num_scalar_prefetch=1,
            grid=(pairs,),
            in_specs=[
                pl.BlockSpec((3, rows, 128), lambda h, n: (0, 0, h)),
                pl.BlockSpec((rows, 128), lambda h, n: (0, h)),
                pl.BlockSpec((rows, 128), lambda h, n: (0, h)),
                pl.BlockSpec((1, 8, rows), lambda h, n: (h, 0, 0)),
            ],
            out_specs=pl.BlockSpec((3, rows, 128), lambda h, n: (0, 0, h)),
            scratch_shapes=[pltpu.VMEM((2, rows, 128), f32), pltpu.VMEM((2, rows, 128), f32)],
        ),
        out_shape=jax.ShapeDtypeStruct((3, rows, D), bf16),
        compiler_params=params(),
        cost_estimate=pl.CostEstimate(
            flops=5 * rows * rows * D, bytes_accessed=rows * D * 16, transcendentals=HEADS * rows * rows // 2
        ),
        name="attend_back",
    )(length, projected, heads_out, grad_heads, lse)


def feed_kernel(plan, len_ref, row_ref, grad_ref, *refs):
    tok0, tok1, pass0, pass1, ho0, ho1, cot0, cot1, table_ref, gain_ref = refs[:10]
    many = plan.sharers if plan.paired else 1
    pieces, refs = refs[10 : 10 + many], refs[10 + many :]
    res0, res1, gh0, gh1, hid0, hid1, small_ref = refs[:7]
    outs, (w_ref, acc_ref, stage_ref, sem_ref) = refs[7:-4], refs[-4:]
    b = pl.program_id(0)
    many0 = last_block(len_ref[0]) + 1
    many1 = last_block(len_ref[1]) + 1
    early = b < many0

    @pl.when(b == 0)
    def clear():
        load_weight(plan, row_ref, pieces, w_ref, sem_ref.at[0])
        acc_ref[...] = jnp.zeros_like(acc_ref)
        small_ref[...] = jnp.zeros_like(small_ref)

    def block(tok, pas, ho, cot, res, gh, hid, start, length):
        hot = onehot_rows(pas[0])
        entry = tok[...].astype(f32) + dot_tn(hot, table_ref[...])
        at = start + lax.broadcasted_iota(jnp.int32, (ROWS, 1), 0)
        live = at < length
        heads = ho[...]
        attention = dot_nn(heads, w_ref[:, 0:D])
        hidden = entry + attention
        unit, scale = normalized(hidden)
        gain = gain_ref[...]
        normed = (unit * gain).astype(bf16)
        grad_feed = jnp.where(live, cot[...].astype(f32), 0.0).astype(bf16)
        feed = jnp.zeros((ROWS, D), f32)
        grad_normed = jnp.zeros((ROWS, D), f32)
        for k in range(CHUNKS):
            up = slice(D + k * D, D + (k + 1) * D)
            down = slice(D + FF + k * D, D + FF + (k + 1) * D)
            x = dot_nn(normed, w_ref[:, up])
            grad_act = dot_nt(grad_feed, w_ref[:, down])
            c0 = math.sqrt(2.0 / math.pi)
            square = x * x
            bent = jnp.tanh(x * (c0 + (c0 * 0.044715) * square))
            half = 0.5 + 0.5 * bent
            slope = half + (0.5 * x) * (1.0 - bent * bent) * (c0 + (3.0 * c0 * 0.044715) * square)
            act = (x * half).astype(bf16)
            grad_x = (slope * grad_act).astype(bf16)
            feed = feed + dot_nn(act, w_ref[:, down])
            grad_normed = grad_normed + dot_nt(grad_x, w_ref[:, up])
            acc_ref[:, up] += dot_tn(normed, grad_x)
            acc_ref[:, down] += dot_tn(act, grad_feed)
        res[...] = jnp.where(live, hidden + feed, 0.0).astype(bf16)
        small_ref[0:8] += fold_rows(grad_normed * unit)
        small_ref[8:16] += fold_rows(jnp.where(live, entry * entry, 0.0))
        small_ref[16:24] += fold_rows(jnp.where(live, attention * attention, 0.0))
        small_ref[24:32] += fold_rows(jnp.where(live, feed * feed, 0.0))
        grad_hidden = grad_feed.astype(f32) + norm_back(grad_normed * gain, unit, scale)
        hid[...] = grad_hidden
        grad_attention = grad_hidden.astype(bf16)
        acc_ref[:, 0:D] += dot_tn(heads, grad_attention)
        gh[...] = dot_nt(grad_attention, w_ref[:, 0:D]).astype(bf16)

    @pl.when(early)
    def first():
        block(tok0, pass0, ho0, cot0, res0, gh0, hid0, b * ROWS, len_ref[0])

    @pl.when(jnp.logical_and(jnp.logical_not(early), b < many0 + many1))
    def second():
        block(tok1, pass1, ho1, cot1, res1, gh1, hid1, (b - many0) * ROWS, len_ref[1])

    @pl.when(b == pl.num_programs(0) - 1)
    def finish():
        store_grads(plan, grad_ref, acc_ref, outs, stage_ref, sem_ref)


def feed(plan, lengths, piece_rows, grad_rows, tokens, pass_rows, heads_out, cotangent, table, gain, pieces, width):
    rows = tokens[0].shape[0]
    at0 = lambda b, n, r, g: (jnp.minimum(b, last_block(n[0])), 0)
    at1 = lambda b, n, r, g: (jnp.clip(b - last_block(n[0]) - 1, 0, last_block(n[1])), 0)
    row0 = pl.BlockSpec((ROWS, D), at0)
    row1 = pl.BlockSpec((ROWS, D), at1)
    pas0 = pl.BlockSpec((1, 1, ROWS), lambda *a: at0(*a) + (0,))
    pas1 = pl.BlockSpec((1, 1, ROWS), lambda *a: at1(*a) + (0,))
    narrow = jax.ShapeDtypeStruct((rows, D), bf16)
    wide = jax.ShapeDtypeStruct((rows, D), f32)
    grads = grad_shapes(plan, width)
    anywhere = pl.BlockSpec(memory_space=pl.ANY)
    return pl.pallas_call(
        functools.partial(feed_kernel, plan),
        grid_spec=pltpu.PrefetchScalarGridSpec(
            num_scalar_prefetch=3,
            grid=(2 * rows // ROWS,),
            in_specs=[
                row0, row1, pas0, pas1, row0, row1, row0, row1,
                pl.BlockSpec((8, D), lambda *a: (0, 0)),
                pl.BlockSpec((1, D), lambda *a: (0, 0)),
            ]
            + [anywhere] * len(pieces),
            out_specs=[row0, row1, row0, row1, row0, row1, pl.BlockSpec((32, D), lambda *a: (0, 0))]
            + [anywhere] * len(grads),
            scratch_shapes=[
                pltpu.VMEM((D, width), bf16),
                pltpu.VMEM((D, width), f32),
                pltpu.VMEM(stage_shape(plan, width), bf16),
                pltpu.SemaphoreType.DMA((2,)),
            ],
        ),
        out_shape=[narrow, narrow, narrow, narrow, wide, wide, jax.ShapeDtypeStruct((32, D), f32)] + grads,
        compiler_params=params(),
        cost_estimate=pl.CostEstimate(
            flops=2 * 6 * rows * D * width, bytes_accessed=2 * rows * D * 14 + D * width * 4, transcendentals=2 * rows * FF
        ),
        name="feed",
    )(lengths, piece_rows, grad_rows, tokens[0], tokens[1], pass_rows[0], pass_rows[1], heads_out[0], heads_out[1],
      cotangent[0], cotangent[1], table, gain, *pieces)


def project_back_kernel(plan, final, len_ref, row_ref, grad_ref, tok_ref, pass_ref, g_ref, hid_ref, table_ref, gain_ref, *rest):
    many = plan.sharers if plan.paired else 1
    pieces, rest = rest[:many], rest[many:]
    if final:
        before_ref, out_ref, small_ref, *outs, acc_ref, w_ref, stage_ref, sem_ref = rest
    else:
        out_ref, small_ref, acc_ref, w_ref, sem_ref = rest
    b = pl.program_id(0)

    @pl.when(b == 0)
    def clear():
        load_weight(plan, row_ref, pieces, w_ref, sem_ref.at[0])
        acc_ref[...] = before_ref[...] if final else jnp.zeros_like(acc_ref)
        small_ref[...] = jnp.zeros_like(small_ref)

    @pl.when(b <= last_block(len_ref[0]))
    def work():
        hot = onehot_rows(pass_ref[0])
        entry = tok_ref[...].astype(f32) + dot_tn(hot, table_ref[...])
        unit, scale = normalized(entry)
        gain = gain_ref[...]
        normed = (unit * gain).astype(bf16)
        grad_normed = jnp.zeros((ROWS, D), f32)
        for part in range(3):
            cols = slice(part * D, (part + 1) * D)
            grad = g_ref[part]
            acc_ref[:, cols] += dot_tn(normed, grad)
            grad_normed = grad_normed + dot_nt(grad, w_ref[:, cols])
        small_ref[0:8] += fold_rows(grad_normed * unit)
        grad_entry = hid_ref[...] + norm_back(grad_normed * gain, unit, scale)
        out_ref[...] = grad_entry.astype(bf16)
        high = grad_entry.astype(bf16)
        rest_one = grad_entry - high.astype(f32)
        low = rest_one.astype(bf16)
        lower = (rest_one - low.astype(f32)).astype(bf16)
        small_ref[8:16] += dot_nn(hot, high) + dot_nn(hot, low) + dot_nn(hot, lower)

    if final:
        @pl.when(b == pl.num_programs(0) - 1)
        def finish():
            store_grads(plan, grad_ref, acc_ref, outs, stage_ref, sem_ref)


def project_back(plan, length, piece_rows, grad_rows, tokens, pass_rows, grads, grad_hidden, table, gain, pieces, before=None):
    rows = tokens.shape[0]
    final = before is not None
    at = lambda b, n, r, g: (jnp.minimum(b, last_block(n[0])), 0)
    row = pl.BlockSpec((ROWS, D), at)
    anywhere = pl.BlockSpec(memory_space=pl.ANY)
    whole = pl.BlockSpec((D, 3 * D), lambda *a: (0, 0), pipeline_mode=pl.Buffered(1))
    in_specs = [
        row,
        pl.BlockSpec((1, 1, ROWS), lambda *a: at(*a) + (0,)),
        pl.BlockSpec((3, ROWS, D), lambda *a: (0,) + at(*a)),
        row,
        pl.BlockSpec((8, D), lambda *a: (0, 0)),
        pl.BlockSpec((1, D), lambda *a: (0, 0)),
    ] + [anywhere] * len(pieces)
    operands = [length, piece_rows, grad_rows, tokens, pass_rows, grads, grad_hidden, table, gain, *pieces]
    sums = jax.ShapeDtypeStruct((D, 3 * D), f32)
    out_shape = [jax.ShapeDtypeStruct((rows, D), bf16), jax.ShapeDtypeStruct((16, D), f32)]
    out_specs = [row, pl.BlockSpec((16, D), lambda *a: (0, 0))]
    scratch = [pltpu.VMEM((D, 3 * D), bf16)]
    if final:
        in_specs.append(whole)
        operands.append(before)
        shapes = grad_shapes(plan, 3 * D)
        out_shape += shapes
        out_specs += [anywhere] * len(shapes)
        scratch = [pltpu.VMEM((D, 3 * D), f32)] + scratch + [pltpu.VMEM(stage_shape(plan, 3 * D), bf16)]
    else:
        out_shape.append(sums)
        out_specs.append(pl.BlockSpec((D, 3 * D), lambda *a: (0, 0)))
    return pl.pallas_call(
        functools.partial(project_back_kernel, plan, final),
        grid_spec=pltpu.PrefetchScalarGridSpec(
            num_scalar_prefetch=3,
            grid=(rows // ROWS,),
            in_specs=in_specs,
            out_specs=out_specs,
            scratch_shapes=scratch + [pltpu.SemaphoreType.DMA((2,))],
        ),
        out_shape=out_shape,
        compiler_params=params(),
        cost_estimate=pl.CostEstimate(
            flops=4 * rows * D * 3 * D, bytes_accessed=rows * D * 14 + D * D * 18, transcendentals=0
        ),
        name="project_back",
    )(*operands)


def pick_kernel(index_ref, in_ref, out_ref, sem_ref):
    copies = [
        pltpu.make_async_copy(in_ref.at[index_ref[n]], out_ref.at[n], sem_ref) for n in range(out_ref.shape[0])
    ]
    for copy in copies:
        copy.start()
    for copy in copies:
        copy.wait()


def pick(index, blocks):
    shape = index.shape + blocks.shape[1:]
    return pl.pallas_call(
        pick_kernel,
        grid_spec=pltpu.PrefetchScalarGridSpec(
            num_scalar_prefetch=1,
            grid=(1,),
            in_specs=[pl.BlockSpec(memory_space=pl.ANY)],
            out_specs=pl.BlockSpec(shape, lambda b, n: (0, 0, 0)),
            scratch_shapes=[pltpu.SemaphoreType.DMA],
        ),
        out_shape=jax.ShapeDtypeStruct(shape, blocks.dtype),
        compiler_params=params(),
        cost_estimate=pl.CostEstimate(flops=0, bytes_accessed=4 * math.prod(shape), transcendentals=0),
        name="pick",
    )(index, blocks)


def settle_kernel(index_ref, early_ref, late_ref, out_ref):
    first = pl.program_id(0) * out_ref.shape[0]
    rows = out_ref.shape[1]
    at = lax.broadcasted_iota(jnp.int32, (rows, 1), 0)
    for n in range(out_ref.shape[0]):
        live = at < index_ref[2, first + n]
        source = index_ref[1, first + n]

        @pl.when(index_ref[0, first + n] == 0)
        def early():
            out_ref[n] = jnp.where(live, early_ref[source].astype(f32), 0.0)

        @pl.when(index_ref[0, first + n] != 0)
        def late():
            out_ref[n] = jnp.where(live, late_ref[source].astype(f32), 0.0)


def settle(index, early, late):
    many = index.shape[1]
    step = 4
    whole = pl.BlockSpec(early.shape, lambda b, n: (0, 0, 0), pipeline_mode=pl.Buffered(1))
    return pl.pallas_call(
        settle_kernel,
        grid_spec=pltpu.PrefetchScalarGridSpec(
            num_scalar_prefetch=1,
            grid=(many // step,),
            in_specs=[whole, whole],
            out_specs=pl.BlockSpec((step,) + early.shape[1:], lambda b, n: (b, 0, 0)),
        ),
        out_shape=jax.ShapeDtypeStruct((many,) + early.shape[1:], f32),
        compiler_params=params(),
        cost_estimate=pl.CostEstimate(flops=0, bytes_accessed=6 * many * early[0].size, transcendentals=0),
        name="settle",
    )(index, early, late)


def after(values, *others):
    return lax.optimization_barrier((values, others))[0]


def swap(blocks):
    return lax.all_to_all(blocks, "dp", split_axis=0, concat_axis=0, tiled=True)


def per_device(
    groups,
    width_all,
    tokens,
    passes,
    lengths,
    dealing,
    pass_table,
    gain_first,
    to_heads,
    from_heads,
    gain_second,
    expand,
    shrink,
    cotangent,
):
    axes = ("dp", "fsdp")
    slots, part, unused_width = tokens.shape
    seq_len = part * groups
    order = jnp.arange(slots, dtype=jnp.int32)
    here = lax.axis_index("dp")
    ordering = dealing[0, 0]
    sizes = lengths[0]

    ahead = (sizes[None, :] > sizes[:, None]) | (
        (sizes[None, :] == sizes[:, None]) & (order[None, :] < order[:, None])
    )
    rank = jnp.sum(ahead.astype(jnp.int32), axis=1)
    ranked = jnp.sum(jnp.where(rank[None, :] == order[:, None], order[None, :], 0), axis=1)
    place = jnp.sum(jnp.where(ordering[None, :] == order[:, None], order[None, :], 0), axis=1)
    early_seqs = ranked[:groups]
    late_seqs = ranked[groups:][::-1]
    from_early = jnp.sum(jnp.where(early_seqs[:, None] == order[None, :], place[None, :], 0), axis=1)
    from_late = jnp.sum(jnp.where(late_seqs[:, None] == order[None, :], place[None, :], 0), axis=1)
    slot_rank = jnp.sum(jnp.where(ordering[:, None] == order[None, :], rank[None, :], 0), axis=1)
    slot_size = jnp.sum(jnp.where(ordering[:, None] == order[None, :], sizes[None, :], 0), axis=1)
    is_late = (slot_rank >= groups).astype(jnp.int32)
    source = jnp.where(is_late == 1, slots - 1 - slot_rank, slot_rank)
    back_index = jnp.stack([is_late, source, slot_size - here * part])
    my_seqs = jnp.stack([early_seqs[here], late_seqs[here]])
    my_sizes = jnp.sum(jnp.where(my_seqs[:, None] == order[None, :], sizes[None, :], 0), axis=1)

    row_count = to_heads.shape[0]
    narrow = jnp.concatenate(
        [
            from_heads,
            expand.reshape(row_count, D, CHUNKS).transpose(0, 2, 1).reshape(row_count, FF),
            shrink.reshape(row_count, CHUNKS * D),
        ],
        axis=1,
    )
    plan = Plan(groups, width_all // groups, row_count)
    fsdp_here = lax.axis_index("fsdp")
    if plan.paired:
        head_held = plan.gather_groups(to_heads)
        wide_held = plan.gather_groups(after(narrow, head_held))
        head_pieces = plan.gather_core(plan.gather_x(head_held))
        wide_x = plan.gather_x(wide_held)
        wide_pieces = plan.gather_core(wide_x)
        piece_rows = plan.piece_rows(here, fsdp_here)
        grad_rows = plan.grad_rows(here, fsdp_here)
    else:
        head_pieces = (lax.all_gather(to_heads, axes, axis=0, tiled=True),)
        wide_pieces = (lax.all_gather(narrow, axes, axis=0, tiled=True),)
        wide_held = wide_x = wide_pieces
        piece_rows = grad_rows = jnp.zeros((1,), jnp.int32)

    my_passes = [passes[my_seqs[m]].reshape(seq_len // ROWS, 1, ROWS) for m in range(2)]
    one_size = [my_sizes[m : m + 1] for m in range(2)]
    table = jnp.zeros((8, D), bf16).at[:PASSES].set(pass_table)
    gain_one = gain_first.astype(f32).reshape(1, D)
    gain_two = gain_second.astype(f32).reshape(1, D)

    def forward(m, *gate):
        return project(
            plan, after(one_size[m], gate), piece_rows, my_tokens[m], my_passes[m], table, gain_one, head_pieces
        )

    def mix(m, *gate):
        return attend(after(one_size[m], gate), projected[m])

    def mix_back(m, *gate):
        return attend_back(after(one_size[m], gate), projected[m], heads_out[m], grad_heads[m], lse[m])

    def forward_back(m, *gate, before=None):
        return project_back(
            plan, after(one_size[m], gate), piece_rows, grad_rows, my_tokens[m], my_passes[m], grad_parts[m],
            grad_hidden[m], table, gain_one, head_pieces, before,
        )

    def send_back(rows, *gate):
        return swap(after(rows, gate).reshape(groups, part, D))

    picked = [pick(index, blocks) for blocks in (tokens, cotangent) for index in (from_early, from_late)]
    projected, heads_out, lse, grad_parts = [None, None], [None, None], [None, None], [None, None]
    tokens0 = swap(picked[0])
    tokens1 = swap(after(picked[1], tokens0, picked[2], picked[3]))
    my_tokens = [tokens0.reshape(seq_len, D), tokens1.reshape(seq_len, D)]
    projected[0] = forward(0)
    heads_out[0], lse[0] = mix(0, wide_held)
    grads0 = swap(after(picked[2], tokens1, lse[0]))
    projected[1] = forward(1, lse[0])
    heads_out[1], lse[1] = mix(1, wide_x)
    grads1 = swap(after(picked[3], grads0, lse[1]))
    my_grads = [grads0.reshape(seq_len, D), grads1.reshape(seq_len, D)]

    res0, res1, gh0, gh1, hid0, hid1, feed_small, *wide_grads = feed(
        plan, my_sizes, piece_rows, grad_rows, my_tokens, my_passes, heads_out, my_grads, table, gain_two,
        wide_pieces, D + 2 * FF,
    )
    grad_heads, grad_hidden = (gh0, gh1), (hid0, hid1)
    steps = len(plan.orders[0])

    def begin(grads):
        if not plan.paired:
            return lax.psum_scatter(grads[0], axes, scatter_dimension=0, tiled=True).astype(f32)
        return [tuple(grads[0:2]), tuple(grads[2:4])]

    def advance(state, step, *gate):
        return plan.reduce_step(state, step, gate) if plan.paired else state

    wide_state = advance(begin(wide_grads), 0)
    result0 = send_back(res0)
    wide_next = advance(wide_state, 1)
    grad_parts[1] = mix_back(1, wide_state)
    result1 = send_back(res1, result0, grad_parts[1])
    wide_last = advance(wide_next, 2, grad_parts[1])
    grad_parts[0] = mix_back(0, wide_next, result0, grad_parts[1])
    wide_next = advance(wide_last, 3, grad_parts[0])
    entry0, small0, head_sum = forward_back(0, wide_last, result1, grad_parts[0])
    moved0 = send_back(entry0, result1)
    wide_last = wide_next
    for step in range(4, steps):
        wide_last = advance(wide_last, step, entry0)
    entry1, small1, *head_grads = forward_back(1, wide_next, before=head_sum)
    moved1 = send_back(entry1, moved0)
    squares = jnp.sum(feed_small[8:].reshape(3, 8 * D), axis=1)
    counted = jnp.sum(my_sizes).astype(f32)
    last_row = jnp.zeros((1, D), f32).at[0, :3].set(squares).at[0, 3].set(counted)
    small = small0 + small1
    totals = jnp.concatenate(
        [
            small[8 : 8 + PASSES],
            jnp.sum(small[:8], axis=0, keepdims=True),
            jnp.sum(feed_small[:8], axis=0, keepdims=True),
            last_row,
        ],
        axis=0,
    )
    if not plan.paired:
        totals = lax.psum(totals, axes)
    head_state = begin(head_grads)
    for step in range(steps):
        if plan.paired:
            totals = totals + plan.exchange(after(totals, head_state), *plan.orders[0][step])
        head_state = advance(head_state, step, *([moved0] if step == 1 else []))
    wide_state = wide_last
    if plan.paired:
        wide_owned, head_owned = [jnp.concatenate(state, axis=1) for state in (wide_state, head_state)]
    else:
        wide_owned, head_owned = wide_state, head_state
    results, entries = (result0, result1), (moved0, moved1)

    root_squares = jnp.sqrt(totals[7, :3] / (totals[7, 3] * D))

    grad_expand = wide_owned[:, D : D + FF].reshape(row_count, CHUNKS, D).transpose(0, 2, 1)
    return (
        settle(back_index, results[0], results[1]),
        settle(back_index, entries[0], entries[1]),
        totals[:PASSES],
        totals[PASSES],
        head_owned,
        wide_owned[:, :D],
        totals[PASSES + 1],
        grad_expand.reshape(row_count, FF),
        wide_owned[:, D + FF :].reshape(row_count * CHUNKS, D),
        root_squares,
    )


def solution(mesh):
    groups = mesh.shape["dp"]
    weight_spec = P(("dp", "fsdp"), None)
    block_spec = P("fsdp", "dp", None)
    in_specs = (
        block_spec,
        P("fsdp", None),
        P("fsdp", None),
        P("dp", "fsdp", None),
        P(),
        P(),
        weight_spec,
        weight_spec,
        P(),
        weight_spec,
        weight_spec,
        block_spec,
    )
    out_specs = (
        block_spec,
        block_spec,
        P(),
        P(),
        weight_spec,
        weight_spec,
        P(),
        weight_spec,
        weight_spec,
        P(),
    )
    body = functools.partial(per_device, groups, groups * mesh.shape["fsdp"])
    return jax.shard_map(body, mesh=mesh, in_specs=in_specs, out_specs=out_specs, check_vma=False)
```

```python
import math
import functools

import jax
import jax.numpy as jnp
from jax import lax
from jax.experimental import pallas as pl
from jax.experimental.pallas import tpu as pltpu
from jax.sharding import PartitionSpec as P

D = 768
HEADS = 12
HEAD = 64
FF = 3072
PASSES = 5
EPS = 1e-05
ROWS = 256
CHUNKS = FF // D
VMEM_MOST = 64000 * 1024

f32 = jnp.float32
bf16 = jnp.bfloat16


def dot_nn(a, b):
    return lax.dot_general(a, b, (((1,), (0,)), ((), ())), preferred_element_type=f32)


def dot_nt(a, b):
    return lax.dot_general(a, b, (((1,), (1,)), ((), ())), preferred_element_type=f32)


def dot_tn(a, b):
    return lax.dot_general(a, b, (((0,), (0,)), ((), ())), preferred_element_type=f32)


def params(**more):
    return pltpu.CompilerParams(vmem_limit_bytes=VMEM_MOST, **more)


def normalized(values):
    centred = values - jnp.mean(values, axis=-1, keepdims=True)
    spread = jnp.mean(centred * centred, axis=-1, keepdims=True)
    scale = lax.rsqrt(spread + EPS)
    return centred * scale, scale


def norm_back(grad_unit, unit, scale):
    first = jnp.mean(grad_unit, axis=-1, keepdims=True)
    second = jnp.mean(grad_unit * unit, axis=-1, keepdims=True)
    return scale * (grad_unit - first - unit * second)


def onehot_rows(pass_row):
    ids = lax.broadcasted_iota(jnp.int32, (8, pass_row.shape[-1]), 0)
    return (ids == pass_row).astype(f32).astype(bf16)


def fold_rows(values):
    rows, width = values.shape
    return jnp.sum(values.reshape(rows // 8, 8, width), axis=0)


def last_block(length):
    return lax.div(length + (ROWS - 1), ROWS) - 1


def bits_of(count):
    return count.bit_length() - 1


class Plan:
    def __init__(self, groups, sharers, rows, allowed=True):
        self.groups, self.sharers, self.rows = groups, sharers, rows
        self.count = groups * sharers
        self.paired = allowed and rows % 8 == 0 and self.count & (self.count - 1) == 0 and sharers >= 4 and groups >= 2
        over_dp = [("dp", bit) for bit in range(bits_of(groups))]
        over_x = [("fsdp", bit) for bit in range(1, bits_of(sharers))]
        self.gather_dp = over_dp[::-1]
        self.gather_fsdp = over_x[::-1] + [("fsdp", 0)]
        self.orders = (
            [("fsdp", 0)] + over_x + over_dp,
            [("fsdp", 0)] + over_dp[:1] + over_x + over_dp[1:],
        )

    def size(self, axis):
        return self.groups if axis == "dp" else self.sharers

    def exchange(self, values, axis, bit):
        pairs = [(i, i ^ (1 << bit)) for i in range(self.size(axis))]
        return lax.ppermute(values, axis, pairs)

    def gather_groups(self, shard):
        held = shard[None]
        for axis, bit in self.gather_dp:
            held = jnp.concatenate([held, self.exchange(held, axis, bit)], axis=0)
        return held

    def gather_x(self, held):
        pieces = {0: held}
        for axis, bit in self.gather_fsdp[:-1]:
            for name in list(pieces):
                pieces[name | (1 << bit)] = self.exchange(pieces[name], axis, bit)
        return pieces

    def gather_core(self, pieces):
        axis, bit = self.gather_fsdp[-1]
        found = dict(pieces)
        for name in pieces:
            found[name | (1 << bit)] = self.exchange(pieces[name], axis, bit)
        return tuple(found[name] for name in range(self.sharers))

    def piece_rows(self, dp, fsdp):
        found = []
        for f in range(self.sharers):
            for n in range(self.groups):
                rel = sum(((n >> k) & 1) << bit for k, (axis, bit) in enumerate(self.gather_dp))
                found.append(((dp ^ rel) * self.sharers + (fsdp ^ f)) * self.rows)
        return jnp.stack(found).astype(jnp.int32)

    def grad_rows(self, dp, fsdp):
        found = []
        for order in self.orders:
            for place in range(self.count):
                rel = {"dp": 0, "fsdp": 0}
                for k, (axis, bit) in enumerate(order):
                    rel[axis] |= ((place >> (len(order) - 1 - k)) & 1) << bit
                found.append(((dp ^ rel["dp"]) * self.sharers + (fsdp ^ rel["fsdp"])) * self.rows)
        return jnp.stack(found).astype(jnp.int32)

    def reduce_step(self, state, step, *gate):
        found = []
        for (keep, send), order in zip(state, self.orders):
            axis, bit = order[step]
            other = self.exchange(after(send, gate), axis, bit).astype(f32)
            total = keep.astype(f32)
            if step == len(order) - 1:
                found.append((total + other)[0])
            else:
                half = keep.shape[0] // 2
                found.append(
                    ((total[:half] + other[:half]).astype(bf16), (total[half:] + other[half:]).astype(bf16))
                )
        return found


def load_weight(plan, rows_ref, pieces, weight_ref, sem_ref):
    if not plan.paired:
        copies = [pltpu.make_async_copy(pieces[0], weight_ref, sem_ref)]
    else:
        copies = []
        for f in range(plan.sharers):
            for n in range(plan.groups):
                at = pl.multiple_of(rows_ref[f * plan.groups + n], 8)
                target = weight_ref.at[pl.ds(at, plan.rows), :]
                copies.append(pltpu.make_async_copy(pieces[f].at[n], target, sem_ref))
    for copy in copies:
        copy.start()
    for copy in copies:
        copy.wait()


def grad_shapes(plan, width):
    if not plan.paired:
        return [jax.ShapeDtypeStruct((D, width), bf16)]
    half = plan.count // 2
    cut = first_part(width)
    return [jax.ShapeDtypeStruct((half, plan.rows, w), bf16) for w in (cut, cut, width - cut, width - cut)]


def first_part(width):
    step = grad_step(width)
    return (width // step + 1) // 2 * step


def grad_step(width):
    return D if width % D == 0 and width // D > 3 else D // 2


def stage_shape(plan, width):
    step = grad_step(width)
    return (2, plan.count, plan.rows, step) if plan.paired else (2, D, step)


def store_grads(plan, rows_ref, acc_ref, outs, stage_ref, sem_ref):
    width = acc_ref.shape[1]
    step = grad_step(width)
    cut = first_part(width)
    half = plan.count // 2
    waiting = []
    for n in range(width // step):
        slot = n % 2
        cols = slice(n * step, (n + 1) * step)
        if len(waiting) == 2:
            for copy in waiting.pop(0):
                copy.wait()
        if not plan.paired:
            stage_ref[slot] = acc_ref[:, cols].astype(bf16)
            copies = [pltpu.make_async_copy(stage_ref.at[slot], outs[0].at[:, cols], sem_ref.at[slot])]
        else:
            late = n * step >= cut
            base = plan.count if late else 0
            start = n * step - (cut if late else 0)

            def fill(place, carry):
                at = pl.multiple_of(rows_ref[base + place], 8)
                stage_ref[slot, place] = acc_ref[pl.ds(at, plan.rows), cols].astype(bf16)
                return carry

            lax.fori_loop(0, plan.count, fill, 0)
            keep, send = outs[2:4] if late else outs[0:2]
            there = slice(start, start + step)
            copies = [
                pltpu.make_async_copy(stage_ref.at[slot, 0:half], keep.at[:, :, there], sem_ref.at[slot]),
                pltpu.make_async_copy(stage_ref.at[slot, half:], send.at[:, :, there], sem_ref.at[slot]),
            ]
        for copy in copies:
            copy.start()
        waiting.append(copies)
    for copies in waiting:
        for copy in copies:
            copy.wait()


def project_kernel(plan, len_ref, row_ref, tok_ref, pass_ref, table_ref, gain_ref, *rest):
    pieces, (out_ref, w_ref, sem_ref) = rest[:-3], rest[-3:]

    @pl.when(pl.program_id(0) == 0)
    def load():
        load_weight(plan, row_ref, pieces, w_ref, sem_ref)

    @pl.when(pl.program_id(0) <= last_block(len_ref[0]))
    def work():
        hot = onehot_rows(pass_ref[0])
        entry = tok_ref[...].astype(f32) + dot_tn(hot, table_ref[...])
        unit, unused = normalized(entry)
        normed = (unit * gain_ref[...]).astype(bf16)
        for part in range(3):
            out_ref[part] = dot_nn(normed, w_ref[:, part * D : (part + 1) * D]).astype(bf16)


def project(plan, length, piece_rows, tokens, pass_rows, table, gain, pieces):
    rows = tokens.shape[0]
    at = lambda b, n, r: (jnp.minimum(b, last_block(n[0])), 0)
    return pl.pallas_call(
        functools.partial(project_kernel, plan),
        grid_spec=pltpu.PrefetchScalarGridSpec(
            num_scalar_prefetch=2,
            grid=(rows // ROWS,),
            in_specs=[
                pl.BlockSpec((ROWS, D), at),
                pl.BlockSpec((1, 1, ROWS), lambda b, n, r: at(b, n, r) + (0,)),
                pl.BlockSpec((8, D), lambda b, n, r: (0, 0)),
                pl.BlockSpec((1, D), lambda b, n, r: (0, 0)),
            ]
            + [pl.BlockSpec(memory_space=pl.ANY)] * len(pieces),
            out_specs=pl.BlockSpec((3, ROWS, D), lambda b, n, r: (0,) + at(b, n, r)),
            scratch_shapes=[pltpu.VMEM((D, 3 * D), bf16), pltpu.SemaphoreType.DMA],
        ),
        out_shape=jax.ShapeDtypeStruct((3, rows, D), bf16),
        compiler_params=params(),
        cost_estimate=pl.CostEstimate(
            flops=2 * rows * D * 3 * D, bytes_accessed=rows * D * 8 + D * D * 6, transcendentals=0
        ),
        name="project",
    )(length, piece_rows, tokens, pass_rows, table, gain, *pieces)


def attend_kernel(len_ref, p_ref, out_ref, lse_ref):
    blocks = p_ref.shape[1] // ROWS
    lane = lax.broadcasted_iota(jnp.int32, (ROWS, 128), 1)
    first_head = lane < HEAD
    here = lax.broadcasted_iota(jnp.int32, (ROWS, ROWS), 0)
    there = lax.broadcasted_iota(jnp.int32, (ROWS, ROWS), 1)
    allowed = there <= here
    for i in range(blocks):
        rows = slice(i * ROWS, (i + 1) * ROWS)

        @pl.when(i * ROWS < len_ref[0])
        def work():
            query = p_ref[0, rows, :] * jnp.asarray(1.0 / math.sqrt(HEAD), bf16)
            found = []
            for head in range(2):
                mine = first_head if head == 0 else jnp.logical_not(first_head)
                q = jnp.where(mine, query, jnp.zeros_like(query))
                diag = dot_nt(q, p_ref[1, rows, :])
                diag = jnp.where(allowed, diag, -1e30)
                largest = jnp.max(diag, axis=-1, keepdims=True)
                if i > 0:
                    before = dot_nt(q, p_ref[1, : i * ROWS, :])
                    largest = jnp.maximum(largest, jnp.max(before, axis=-1, keepdims=True))
                diag = jnp.exp(diag - largest)
                total = jnp.sum(diag, axis=-1, keepdims=True)
                out = dot_nn(diag.astype(bf16), p_ref[2, rows, :])
                if i > 0:
                    before = jnp.exp(before - largest)
                    total = total + jnp.sum(before, axis=-1, keepdims=True)
                    out = out + dot_nn(before.astype(bf16), p_ref[2, : i * ROWS, :])
                found.append(out * (1.0 / total))
                lse = jnp.broadcast_to(largest + jnp.log(total), (ROWS, 128))
                lse_ref[0, head : head + 1, rows] = lse.T[0:1]
            out_ref[rows, :] = jnp.where(first_head, found[0], found[1]).astype(bf16)


def attend(length, projected):
    rows = projected.shape[1]
    pairs = HEADS // 2
    return pl.pallas_call(
        attend_kernel,
        grid_spec=pltpu.PrefetchScalarGridSpec(
            num_scalar_prefetch=1,
            grid=(pairs,),
            in_specs=[pl.BlockSpec((3, rows, 128), lambda h, n: (0, 0, h))],
            out_specs=[
                pl.BlockSpec((rows, 128), lambda h, n: (0, h)),
                pl.BlockSpec((1, 8, rows), lambda h, n: (h, 0, 0)),
            ],
        ),
        out_shape=[
            jax.ShapeDtypeStruct((rows, D), bf16),
            jax.ShapeDtypeStruct((pairs, 8, rows), f32),
        ],
        compiler_params=params(),
        cost_estimate=pl.CostEstimate(
            flops=2 * rows * rows * D, bytes_accessed=rows * D * 8, transcendentals=HEADS * rows * rows // 2
        ),
        name="attend",
    )(length, projected)


def attend_back_kernel(len_ref, p_ref, o_ref, g_ref, lse_ref, out_ref, dk_ref, dv_ref, kz_ref, vz_ref, kt_ref):
    blocks = p_ref.shape[1] // ROWS
    scaling = 1.0 / math.sqrt(HEAD)
    lane = lax.broadcasted_iota(jnp.int32, (ROWS, 128), 1)
    first_head = lane < HEAD
    row8 = lax.broadcasted_iota(jnp.int32, (8, 128), 0)
    lane8 = lax.broadcasted_iota(jnp.int32, (8, 128), 1)
    chooser = (lax.div(lane8, HEAD) == row8).astype(f32)
    key_at = lax.broadcasted_iota(jnp.int32, (2, ROWS, ROWS), 1)
    row_at = lax.broadcasted_iota(jnp.int32, (2, ROWS, ROWS), 2)
    allowed = (key_at <= row_at).reshape(2 * ROWS, ROWS)
    for i in range(blocks):
        rows = slice(i * ROWS, (i + 1) * ROWS)
        two = slice(2 * i * ROWS, 2 * (i + 1) * ROWS)

        @pl.when(i * ROWS < len_ref[0])
        def work():
            dk_ref[two, :] = jnp.zeros((2 * ROWS, 128), f32)
            dv_ref[two, :] = jnp.zeros((2 * ROWS, 128), f32)
            key, value = p_ref[1, rows, :], p_ref[2, rows, :]
            zero = jnp.zeros_like(key)
            k2 = jnp.concatenate([jnp.where(first_head, key, zero), jnp.where(first_head, zero, key)], axis=0)
            kz_ref[two, :] = k2
            kt_ref[:, two] = k2.T
            vz_ref[two, :] = jnp.concatenate([jnp.where(first_head, value, zero), jnp.where(first_head, zero, value)], axis=0)
            query = p_ref[0, rows, :] * jnp.asarray(scaling, bf16)
            grad = g_ref[rows, :]
            product = grad.astype(f32) * o_ref[rows, :].astype(f32)
            delta = lax.dot_general(chooser, product, (((1,), (1,)), ((), ())), precision=lax.Precision.HIGHEST, preferred_element_type=f32)
            def both(a, b):
                return jnp.concatenate([jnp.broadcast_to(a, (ROWS, ROWS)), jnp.broadcast_to(b, (ROWS, ROWS))], axis=0)
            lse2 = both(lse_ref[0, 0:1, rows], lse_ref[0, 1:2, rows])
            delta2 = both(delta[0:1], delta[1:2])
            dqt = jnp.zeros((128, ROWS), f32)
            for j in range(i + 1):
                cols = slice(2 * j * ROWS, 2 * (j + 1) * ROWS)
                prob = jnp.exp(dot_nt(kz_ref[cols, :], query) - lse2)
                if i == j:
                    prob = jnp.where(allowed, prob, 0.0)
                ds = (prob * (dot_nt(vz_ref[cols, :], grad) - delta2)).astype(bf16)
                dv_ref[cols, :] += dot_nn(prob.astype(bf16), grad)
                dk_ref[cols, :] += dot_nn(ds, query)
                dqt = dqt + dot_nn(kt_ref[:, cols], ds)
            out_ref[0, rows, :] = (dqt * scaling).T.astype(bf16)
    for i in range(blocks):
        rows = slice(i * ROWS, (i + 1) * ROWS)
        a = slice(2 * i * ROWS, (2 * i + 1) * ROWS); b = slice((2 * i + 1) * ROWS, 2 * (i + 1) * ROWS)

        @pl.when(i * ROWS < len_ref[0])
        def finish():
            out_ref[1, rows, :] = jnp.where(first_head, dk_ref[a, :], dk_ref[b, :]).astype(bf16)
            out_ref[2, rows, :] = jnp.where(first_head, dv_ref[a, :], dv_ref[b, :]).astype(bf16)


def attend_back(length, projected, heads_out, grad_heads, lse):
    rows = projected.shape[1]
    pairs = HEADS // 2
    return pl.pallas_call(
        attend_back_kernel,
        grid_spec=pltpu.PrefetchScalarGridSpec(
            num_scalar_prefetch=1,
            grid=(pairs,),
            in_specs=[
                pl.BlockSpec((3, rows, 128), lambda h, n: (0, 0, h)),
                pl.BlockSpec((rows, 128), lambda h, n: (0, h)),
                pl.BlockSpec((rows, 128), lambda h, n: (0, h)),
                pl.BlockSpec((1, 8, rows), lambda h, n: (h, 0, 0)),
            ],
            out_specs=pl.BlockSpec((3, rows, 128), lambda h, n: (0, 0, h)),
            scratch_shapes=[
                pltpu.VMEM((2 * rows, 128), f32),
                pltpu.VMEM((2 * rows, 128), f32),
                pltpu.VMEM((2 * rows, 128), bf16),
                pltpu.VMEM((2 * rows, 128), bf16),
                pltpu.VMEM((128, 2 * rows), bf16),
            ],
        ),
        out_shape=jax.ShapeDtypeStruct((3, rows, D), bf16),
        compiler_params=params(),
        cost_estimate=pl.CostEstimate(
            flops=5 * rows * rows * D, bytes_accessed=rows * D * 16, transcendentals=HEADS * rows * rows // 2
        ),
        name="attend_back",
    )(length, projected, heads_out, grad_heads, lse)


def feed_kernel(plan, len_ref, row_ref, grad_ref, *refs):
    tok0, tok1, pass0, pass1, ho0, ho1, cot0, cot1, table_ref, gain_ref = refs[:10]
    many = plan.sharers if plan.paired else 1
    pieces, refs = refs[10 : 10 + many], refs[10 + many :]
    res0, res1, gh0, gh1, hid0, hid1, small_ref = refs[:7]
    outs, (w_ref, acc_ref, stage_ref, sem_ref) = refs[7:-4], refs[-4:]
    b = pl.program_id(0)
    many0 = last_block(len_ref[0]) + 1
    many1 = last_block(len_ref[1]) + 1
    early = b < many0

    @pl.when(b == 0)
    def clear():
        load_weight(plan, row_ref, pieces, w_ref, sem_ref.at[0])
        acc_ref[...] = jnp.zeros_like(acc_ref)
        small_ref[...] = jnp.zeros_like(small_ref)

    def block(tok, pas, ho, cot, res, gh, hid, start, length):
        hot = onehot_rows(pas[0])
        entry = tok[...].astype(f32) + dot_tn(hot, table_ref[...])
        at = start + lax.broadcasted_iota(jnp.int32, (ROWS, 1), 0)
        live = at < length
        heads = ho[...]
        attention = dot_nn(heads, w_ref[:, 0:D])
        hidden = entry + attention
        unit, scale = normalized(hidden)
        gain = gain_ref[...]
        normed = (unit * gain).astype(bf16)
        grad_feed = jnp.where(live, cot[...].astype(f32), 0.0).astype(bf16)
        feed = jnp.zeros((ROWS, D), f32)
        grad_normed = jnp.zeros((ROWS, D), f32)
        for k in range(CHUNKS):
            up = slice(D + k * D, D + (k + 1) * D)
            down = slice(D + FF + k * D, D + FF + (k + 1) * D)
            x = dot_nn(normed, w_ref[:, up])
            grad_act = dot_nt(grad_feed, w_ref[:, down])
            c0 = math.sqrt(2.0 / math.pi)
            square = x * x
            bent = jnp.tanh(x * (c0 + (c0 * 0.044715) * square))
            half = 0.5 + 0.5 * bent
            slope = half + (0.5 * x) * (1.0 - bent * bent) * (c0 + (3.0 * c0 * 0.044715) * square)
            act = (x * half).astype(bf16)
            grad_x = (slope * grad_act).astype(bf16)
            feed = feed + dot_nn(act, w_ref[:, down])
            grad_normed = grad_normed + dot_nt(grad_x, w_ref[:, up])
            acc_ref[:, up] += dot_tn(normed, grad_x)
            acc_ref[:, down] += dot_tn(act, grad_feed)
        res[...] = jnp.where(live, hidden + feed, 0.0).astype(bf16)
        small_ref[0:8] += fold_rows(grad_normed * unit)
        small_ref[8:16] += fold_rows(jnp.where(live, entry * entry, 0.0))
        small_ref[16:24] += fold_rows(jnp.where(live, attention * attention, 0.0))
        small_ref[24:32] += fold_rows(jnp.where(live, feed * feed, 0.0))
        grad_hidden = grad_feed.astype(f32) + norm_back(grad_normed * gain, unit, scale)
        hid[...] = grad_hidden
        grad_attention = grad_hidden.astype(bf16)
        acc_ref[:, 0:D] += dot_tn(heads, grad_attention)
        gh[...] = dot_nt(grad_attention, w_ref[:, 0:D]).astype(bf16)

    @pl.when(early)
    def first():
        block(tok0, pass0, ho0, cot0, res0, gh0, hid0, b * ROWS, len_ref[0])

    @pl.when(jnp.logical_and(jnp.logical_not(early), b < many0 + many1))
    def second():
        block(tok1, pass1, ho1, cot1, res1, gh1, hid1, (b - many0) * ROWS, len_ref[1])

    @pl.when(b == pl.num_programs(0) - 1)
    def finish():
        store_grads(plan, grad_ref, acc_ref, outs, stage_ref, sem_ref)


def feed(plan, lengths, piece_rows, grad_rows, tokens, pass_rows, heads_out, cotangent, table, gain, pieces, width):
    rows = tokens[0].shape[0]
    at0 = lambda b, n, r, g: (jnp.minimum(b, last_block(n[0])), 0)
    at1 = lambda b, n, r, g: (jnp.clip(b - last_block(n[0]) - 1, 0, last_block(n[1])), 0)
    row0 = pl.BlockSpec((ROWS, D), at0)
    row1 = pl.BlockSpec((ROWS, D), at1)
    pas0 = pl.BlockSpec((1, 1, ROWS), lambda *a: at0(*a) + (0,))
    pas1 = pl.BlockSpec((1, 1, ROWS), lambda *a: at1(*a) + (0,))
    narrow = jax.ShapeDtypeStruct((rows, D), bf16)
    wide = jax.ShapeDtypeStruct((rows, D), f32)
    grads = grad_shapes(plan, width)
    anywhere = pl.BlockSpec(memory_space=pl.ANY)
    return pl.pallas_call(
        functools.partial(feed_kernel, plan),
        grid_spec=pltpu.PrefetchScalarGridSpec(
            num_scalar_prefetch=3,
            grid=(2 * rows // ROWS,),
            in_specs=[
                row0, row1, pas0, pas1, row0, row1, row0, row1,
                pl.BlockSpec((8, D), lambda *a: (0, 0)),
                pl.BlockSpec((1, D), lambda *a: (0, 0)),
            ]
            + [anywhere] * len(pieces),
            out_specs=[row0, row1, row0, row1, row0, row1, pl.BlockSpec((32, D), lambda *a: (0, 0))]
            + [anywhere] * len(grads),
            scratch_shapes=[
                pltpu.VMEM((D, width), bf16),
                pltpu.VMEM((D, width), f32),
                pltpu.VMEM(stage_shape(plan, width), bf16),
                pltpu.SemaphoreType.DMA((2,)),
            ],
        ),
        out_shape=[narrow, narrow, narrow, narrow, wide, wide, jax.ShapeDtypeStruct((32, D), f32)] + grads,
        compiler_params=params(),
        cost_estimate=pl.CostEstimate(
            flops=2 * 6 * rows * D * width, bytes_accessed=2 * rows * D * 14 + D * width * 4, transcendentals=2 * rows * FF
        ),
        name="feed",
    )(lengths, piece_rows, grad_rows, tokens[0], tokens[1], pass_rows[0], pass_rows[1], heads_out[0], heads_out[1],
      cotangent[0], cotangent[1], table, gain, *pieces)


def project_weight_kernel(plan, len_ref, grad_ref, tok0, tok1, pass0, pass1, g0, g1, table_ref, gain_ref, *rest):
    outs, (acc_ref, stage_ref, sem_ref) = rest[:-3], rest[-3:]
    b = pl.program_id(0)
    many0 = last_block(len_ref[0]) + 1
    many1 = last_block(len_ref[1]) + 1
    early = b < many0

    @pl.when(b == 0)
    def clear():
        acc_ref[...] = jnp.zeros_like(acc_ref)

    def block(tok, pas, g):
        entry = tok[...].astype(f32) + dot_tn(onehot_rows(pas[0]), table_ref[...])
        unit, unused = normalized(entry)
        normed = (unit * gain_ref[...]).astype(bf16)
        for part in range(3):
            acc_ref[:, part * D : (part + 1) * D] += dot_tn(normed, g[part])

    @pl.when(early)
    def first():
        block(tok0, pass0, g0)

    @pl.when(jnp.logical_and(jnp.logical_not(early), b < many0 + many1))
    def second():
        block(tok1, pass1, g1)

    @pl.when(b == pl.num_programs(0) - 1)
    def finish():
        store_grads(plan, grad_ref, acc_ref, outs, stage_ref, sem_ref)


def project_weight(plan, lengths, grad_rows, tokens, pass_rows, grads, table, gain):
    rows = tokens[0].shape[0]
    at0 = lambda b, n, g: (jnp.minimum(b, last_block(n[0])), 0)
    at1 = lambda b, n, g: (jnp.clip(b - last_block(n[0]) - 1, 0, last_block(n[1])), 0)
    shapes = grad_shapes(plan, 3 * D)
    in_specs = [pl.BlockSpec((ROWS, D), at) for at in (at0, at1)]
    in_specs += [
        pl.BlockSpec((1, 1, ROWS), lambda *a: at0(*a) + (0,)),
        pl.BlockSpec((1, 1, ROWS), lambda *a: at1(*a) + (0,)),
        pl.BlockSpec((3, ROWS, D), lambda *a: (0,) + at0(*a)),
        pl.BlockSpec((3, ROWS, D), lambda *a: (0,) + at1(*a)),
        pl.BlockSpec((8, D), lambda *a: (0, 0)),
        pl.BlockSpec((1, D), lambda *a: (0, 0)),
    ]
    return pl.pallas_call(
        functools.partial(project_weight_kernel, plan),
        grid_spec=pltpu.PrefetchScalarGridSpec(
            num_scalar_prefetch=2,
            grid=(2 * rows // ROWS,),
            in_specs=in_specs,
            out_specs=[pl.BlockSpec(memory_space=pl.ANY)] * len(shapes),
            scratch_shapes=[
                pltpu.VMEM((D, 3 * D), f32),
                pltpu.VMEM(stage_shape(plan, 3 * D), bf16),
                pltpu.SemaphoreType.DMA((2,)),
            ],
        ),
        out_shape=shapes,
        compiler_params=params(),
        cost_estimate=pl.CostEstimate(
            flops=4 * rows * D * 3 * D, bytes_accessed=rows * D * 16 + D * D * 6, transcendentals=0
        ),
        name="project_weight",
    )(lengths, grad_rows, tokens[0], tokens[1], pass_rows[0], pass_rows[1], grads[0], grads[1], table, gain)


def project_back_kernel(plan, len_ref, row_ref, tok_ref, pass_ref, g_ref, hid_ref, table_ref, gain_ref, *rest):
    pieces, (out_ref, small_ref, w_ref, sem_ref) = rest[:-4], rest[-4:]
    b = pl.program_id(0)

    @pl.when(b == 0)
    def clear():
        load_weight(plan, row_ref, pieces, w_ref, sem_ref)
        small_ref[...] = jnp.zeros_like(small_ref)

    @pl.when(b <= last_block(len_ref[0]))
    def work():
        hot = onehot_rows(pass_ref[0])
        entry = tok_ref[...].astype(f32) + dot_tn(hot, table_ref[...])
        unit, scale = normalized(entry)
        gain = gain_ref[...]
        grad_normed = jnp.zeros((ROWS, D), f32)
        for part in range(3):
            cols = slice(part * D, (part + 1) * D)
            grad_normed = grad_normed + dot_nt(g_ref[part], w_ref[:, cols])
        small_ref[0:8] += fold_rows(grad_normed * unit)
        grad_entry = hid_ref[...] + norm_back(grad_normed * gain, unit, scale)
        high = grad_entry.astype(bf16)
        out_ref[...] = high
        rest_one = grad_entry - high.astype(f32)
        low = rest_one.astype(bf16)
        lower = (rest_one - low.astype(f32)).astype(bf16)
        small_ref[8:16] += dot_nn(hot, high) + dot_nn(hot, low) + dot_nn(hot, lower)


def project_back(plan, length, piece_rows, tokens, pass_rows, grads, grad_hidden, table, gain, pieces):
    rows = tokens.shape[0]
    at = lambda b, n, r: (jnp.minimum(b, last_block(n[0])), 0)
    row = pl.BlockSpec((ROWS, D), at)
    return pl.pallas_call(
        functools.partial(project_back_kernel, plan),
        grid_spec=pltpu.PrefetchScalarGridSpec(
            num_scalar_prefetch=2,
            grid=(rows // ROWS,),
            in_specs=[
                row,
                pl.BlockSpec((1, 1, ROWS), lambda *a: at(*a) + (0,)),
                pl.BlockSpec((3, ROWS, D), lambda *a: (0,) + at(*a)),
                row,
                pl.BlockSpec((8, D), lambda *a: (0, 0)),
                pl.BlockSpec((1, D), lambda *a: (0, 0)),
            ]
            + [pl.BlockSpec(memory_space=pl.ANY)] * len(pieces),
            out_specs=[row, pl.BlockSpec((16, D), lambda *a: (0, 0))],
            scratch_shapes=[pltpu.VMEM((D, 3 * D), bf16), pltpu.SemaphoreType.DMA],
        ),
        out_shape=[jax.ShapeDtypeStruct((rows, D), bf16), jax.ShapeDtypeStruct((16, D), f32)],
        compiler_params=params(),
        cost_estimate=pl.CostEstimate(
            flops=2 * rows * D * 3 * D, bytes_accessed=rows * D * 14 + D * D * 6, transcendentals=0
        ),
        name="project_back",
    )(length, piece_rows, tokens, pass_rows, grads, grad_hidden, table, gain, *pieces)


def pick_kernel(index_ref, in_ref, out_ref, sem_ref):
    copies = [
        pltpu.make_async_copy(in_ref.at[index_ref[n]], out_ref.at[n], sem_ref) for n in range(out_ref.shape[0])
    ]
    for copy in copies:
        copy.start()
    for copy in copies:
        copy.wait()


def pick(index, blocks):
    shape = index.shape + blocks.shape[1:]
    return pl.pallas_call(
        pick_kernel,
        grid_spec=pltpu.PrefetchScalarGridSpec(
            num_scalar_prefetch=1,
            grid=(1,),
            in_specs=[pl.BlockSpec(memory_space=pl.ANY)],
            out_specs=pl.BlockSpec(shape, lambda b, n: (0, 0, 0)),
            scratch_shapes=[pltpu.SemaphoreType.DMA],
        ),
        out_shape=jax.ShapeDtypeStruct(shape, blocks.dtype),
        compiler_params=params(),
        cost_estimate=pl.CostEstimate(flops=0, bytes_accessed=4 * math.prod(shape), transcendentals=0),
        name="pick",
    )(index, blocks)


def settle_kernel(index_ref, early_ref, late_ref, out_ref):
    first = pl.program_id(0) * out_ref.shape[0]
    rows = out_ref.shape[1]
    at = lax.broadcasted_iota(jnp.int32, (rows, 1), 0)
    for n in range(out_ref.shape[0]):
        live = at < index_ref[2, first + n]
        source = index_ref[1, first + n]

        @pl.when(index_ref[0, first + n] == 0)
        def early():
            out_ref[n] = jnp.where(live, early_ref[source].astype(f32), 0.0)

        @pl.when(index_ref[0, first + n] != 0)
        def late():
            out_ref[n] = jnp.where(live, late_ref[source].astype(f32), 0.0)


def settle(index, early, late):
    many = index.shape[1]
    step = 4
    whole = pl.BlockSpec(early.shape, lambda b, n: (0, 0, 0), pipeline_mode=pl.Buffered(1))
    return pl.pallas_call(
        settle_kernel,
        grid_spec=pltpu.PrefetchScalarGridSpec(
            num_scalar_prefetch=1,
            grid=(many // step,),
            in_specs=[whole, whole],
            out_specs=pl.BlockSpec((step,) + early.shape[1:], lambda b, n: (b, 0, 0)),
        ),
        out_shape=jax.ShapeDtypeStruct((many,) + early.shape[1:], f32),
        compiler_params=params(),
        cost_estimate=pl.CostEstimate(flops=0, bytes_accessed=6 * many * early[0].size, transcendentals=0),
        name="settle",
    )(index, early, late)


def after(values, *others):
    return lax.optimization_barrier((values, others))[0]


def swap(blocks):
    return lax.all_to_all(blocks, "dp", split_axis=0, concat_axis=0, tiled=True)


def per_device(
    groups,
    width_all,
    tokens,
    passes,
    lengths,
    dealing,
    pass_table,
    gain_first,
    to_heads,
    from_heads,
    gain_second,
    expand,
    shrink,
    cotangent,
):
    axes = ("dp", "fsdp")
    slots, part, unused_width = tokens.shape
    seq_len = part * groups
    order = jnp.arange(slots, dtype=jnp.int32)
    here = lax.axis_index("dp")
    ordering = dealing[0, 0]
    sizes = lengths[0]

    ahead = (sizes[None, :] > sizes[:, None]) | (
        (sizes[None, :] == sizes[:, None]) & (order[None, :] < order[:, None])
    )
    rank = jnp.sum(ahead.astype(jnp.int32), axis=1)
    ranked = jnp.sum(jnp.where(rank[None, :] == order[:, None], order[None, :], 0), axis=1)
    place = jnp.sum(jnp.where(ordering[None, :] == order[:, None], order[None, :], 0), axis=1)
    early_seqs = ranked[:groups]
    late_seqs = ranked[groups:][::-1]
    from_early = jnp.sum(jnp.where(early_seqs[:, None] == order[None, :], place[None, :], 0), axis=1)
    from_late = jnp.sum(jnp.where(late_seqs[:, None] == order[None, :], place[None, :], 0), axis=1)
    slot_rank = jnp.sum(jnp.where(ordering[:, None] == order[None, :], rank[None, :], 0), axis=1)
    slot_size = jnp.sum(jnp.where(ordering[:, None] == order[None, :], sizes[None, :], 0), axis=1)
    is_late = (slot_rank >= groups).astype(jnp.int32)
    source = jnp.where(is_late == 1, slots - 1 - slot_rank, slot_rank)
    back_index = jnp.stack([is_late, source, slot_size - here * part])
    my_seqs = jnp.stack([early_seqs[here], late_seqs[here]])
    my_sizes = jnp.sum(jnp.where(my_seqs[:, None] == order[None, :], sizes[None, :], 0), axis=1)

    row_count = to_heads.shape[0]
    narrow = jnp.concatenate(
        [
            from_heads,
            expand.reshape(row_count, D, CHUNKS).transpose(0, 2, 1).reshape(row_count, FF),
            shrink.reshape(row_count, CHUNKS * D),
        ],
        axis=1,
    )
    plan = Plan(groups, width_all // groups, row_count)
    fsdp_here = lax.axis_index("fsdp")
    plain = Plan(groups, width_all // groups, row_count, False)
    if plan.paired:
        head_pieces = plan.gather_core(plan.gather_x(plan.gather_groups(to_heads)))
        piece_rows = plan.piece_rows(here, fsdp_here)
        grad_rows = plan.grad_rows(here, fsdp_here)
    else:
        head_pieces = (lax.all_gather(to_heads, axes, axis=0, tiled=True),)
        piece_rows = grad_rows = jnp.zeros((1,), jnp.int32)
    wide_pieces = (lax.all_gather(narrow, axes, axis=0, tiled=True),)

    my_passes = [passes[my_seqs[m]].reshape(seq_len // ROWS, 1, ROWS) for m in range(2)]
    one_size = [my_sizes[m : m + 1] for m in range(2)]
    table = jnp.zeros((8, D), bf16).at[:PASSES].set(pass_table)
    gain_one = gain_first.astype(f32).reshape(1, D)
    gain_two = gain_second.astype(f32).reshape(1, D)

    def forward(m, *gate):
        return project(
            plan, after(one_size[m], gate), piece_rows, my_tokens[m], my_passes[m], table, gain_one, head_pieces
        )

    def mix(m, *gate):
        return attend(after(one_size[m], gate), projected[m])

    def mix_back(m, *gate):
        return attend_back(after(one_size[m], gate), projected[m], heads_out[m], grad_heads[m], lse[m])

    def forward_back(m, *gate):
        return project_back(
            plan, after(one_size[m], gate), piece_rows, my_tokens[m], my_passes[m], grad_parts[m], grad_hidden[m],
            table, gain_one, head_pieces,
        )

    def send_back(rows, *gate):
        return swap(after(rows, gate).reshape(groups, part, D))

    picked = [pick(index, blocks) for blocks in (tokens, cotangent) for index in (from_early, from_late)]
    projected, heads_out, lse, grad_parts = [None, None], [None, None], [None, None], [None, None]
    tokens0 = swap(picked[0])
    tokens1 = swap(after(picked[1], tokens0, picked[2], picked[3]))
    my_tokens = [tokens0.reshape(seq_len, D), tokens1.reshape(seq_len, D)]
    projected[0] = forward(0)
    heads_out[0], lse[0] = mix(0)
    grads0 = swap(after(picked[2], tokens1, projected[0]))
    projected[1] = forward(1, lse[0])
    heads_out[1], lse[1] = mix(1, grads0)
    grads1 = swap(after(picked[3], grads0, projected[1]))
    my_grads = [grads0.reshape(seq_len, D), grads1.reshape(seq_len, D)]

    res0, res1, gh0, gh1, hid0, hid1, feed_small, *wide_grads = feed(
        plain, my_sizes, piece_rows, grad_rows, my_tokens, my_passes, heads_out, my_grads, table, gain_two,
        wide_pieces, D + 2 * FF,
    )
    grad_heads, grad_hidden = (gh0, gh1), (hid0, hid1)
    steps = len(plan.orders[0])

    wide_owned = lax.psum_scatter(wide_grads[0], axes, scatter_dimension=0, tiled=True).astype(f32)
    result0 = send_back(res0)
    grad_parts[0] = mix_back(0)
    result1 = send_back(res1, result0, grad_parts[0])
    entry0, small0 = forward_back(0)
    grad_parts[1] = mix_back(1, entry0)
    moved0 = send_back(entry0, result1, grad_parts[1])
    head_grads = project_weight(
        plan, after(my_sizes, result1), grad_rows, my_tokens, my_passes, grad_parts, table, gain_one
    )
    if plan.paired:
        head_state = [tuple(head_grads[0:2]), tuple(head_grads[2:4])]
        head_state = plan.reduce_step(head_state, 0)
    else:
        head_owned = lax.psum_scatter(head_grads[0], axes, scatter_dimension=0, tiled=True).astype(f32)
        head_state = head_owned
    entry1, small1 = forward_back(1, head_state)
    moved1 = send_back(entry1, moved0)
    squares = jnp.sum(feed_small[8:].reshape(3, 8 * D), axis=1)
    counted = jnp.sum(my_sizes).astype(f32)
    last_row = jnp.zeros((1, D), f32).at[0, :3].set(squares).at[0, 3].set(counted)
    small = small0 + small1
    totals = jnp.concatenate(
        [
            small[8 : 8 + PASSES],
            jnp.sum(small[:8], axis=0, keepdims=True),
            jnp.sum(feed_small[:8], axis=0, keepdims=True),
            last_row,
        ],
        axis=0,
    )
    if plan.paired:
        for step in range(len(plan.orders[0])):
            totals = totals + plan.exchange(after(totals, head_state), *plan.orders[0][step])
            if step > 0:
                head_state = plan.reduce_step(head_state, step, *([moved0] if step == 2 else []))
        head_owned = jnp.concatenate(head_state, axis=1)
    else:
        totals = lax.psum(totals, axes)
    results, entries = (result0, result1), (moved0, moved1)

    root_squares = jnp.sqrt(totals[7, :3] / (totals[7, 3] * D))

    grad_expand = wide_owned[:, D : D + FF].reshape(row_count, CHUNKS, D).transpose(0, 2, 1)
    return (
        settle(back_index, results[0], results[1]),
        settle(back_index, entries[0], entries[1]),
        totals[:PASSES],
        totals[PASSES],
        head_owned,
        wide_owned[:, :D],
        totals[PASSES + 1],
        grad_expand.reshape(row_count, FF),
        wide_owned[:, D + FF :].reshape(row_count * CHUNKS, D),
        root_squares,
    )


def solution(mesh):
    groups = mesh.shape["dp"]
    weight_spec = P(("dp", "fsdp"), None)
    block_spec = P("fsdp", "dp", None)
    in_specs = (
        block_spec,
        P("fsdp", None),
        P("fsdp", None),
        P("dp", "fsdp", None),
        P(),
        P(),
        weight_spec,
        weight_spec,
        P(),
        weight_spec,
        weight_spec,
        block_spec,
    )
    out_specs = (
        block_spec,
        block_spec,
        P(),
        P(),
        weight_spec,
        weight_spec,
        P(),
        weight_spec,
        weight_spec,
        P(),
    )
    body = functools.partial(per_device, groups, groups * mesh.shape["fsdp"])
    return jax.shard_map(body, mesh=mesh, in_specs=in_specs, out_specs=out_specs, check_vma=False)
```

```python
import math
import functools

import jax
import jax.numpy as jnp
from jax import lax
from jax.experimental import pallas as pl
from jax.experimental.pallas import tpu as pltpu
from jax.sharding import PartitionSpec as P

D = 768
HEADS = 12
HEAD = 64
FF = 3072
PASSES = 5
EPS = 1e-05
ROWS = 256
CHUNKS = FF // D
VMEM_MOST = 64000 * 1024

f32 = jnp.float32
bf16 = jnp.bfloat16


def dot_nn(a, b):
    return lax.dot_general(a, b, (((1,), (0,)), ((), ())), preferred_element_type=f32)


def dot_nt(a, b):
    return lax.dot_general(a, b, (((1,), (1,)), ((), ())), preferred_element_type=f32)


def dot_tn(a, b):
    return lax.dot_general(a, b, (((0,), (0,)), ((), ())), preferred_element_type=f32)


def params(**more):
    return pltpu.CompilerParams(vmem_limit_bytes=VMEM_MOST, **more)


def normalized(values):
    centred = values - jnp.mean(values, axis=-1, keepdims=True)
    spread = jnp.mean(centred * centred, axis=-1, keepdims=True)
    scale = lax.rsqrt(spread + EPS)
    return centred * scale, scale


def norm_back(grad_unit, unit, scale):
    first = jnp.mean(grad_unit, axis=-1, keepdims=True)
    second = jnp.mean(grad_unit * unit, axis=-1, keepdims=True)
    return scale * (grad_unit - first - unit * second)


def onehot_rows(pass_row):
    ids = lax.broadcasted_iota(jnp.int32, (8, pass_row.shape[-1]), 0)
    return (ids == pass_row).astype(f32).astype(bf16)


def fold_rows(values):
    rows, width = values.shape
    return jnp.sum(values.reshape(rows // 8, 8, width), axis=0)


def last_block(length):
    return lax.div(length + (ROWS - 1), ROWS) - 1


def bits_of(count):
    return count.bit_length() - 1


class Plan:
    def __init__(self, groups, sharers, rows, allowed=True):
        self.groups, self.sharers, self.rows = groups, sharers, rows
        self.count = groups * sharers
        self.paired = allowed and rows % 8 == 0 and self.count & (self.count - 1) == 0 and sharers >= 4 and groups >= 2
        over_dp = [("dp", bit) for bit in range(bits_of(groups))]
        over_x = [("fsdp", bit) for bit in range(1, bits_of(sharers))]
        self.gather_dp = over_dp[::-1]
        self.gather_fsdp = over_x[::-1] + [("fsdp", 0)]
        self.orders = (
            [("fsdp", 0)] + over_x + over_dp,
            [("fsdp", 0)] + over_dp[:1] + over_x + over_dp[1:],
        )

    def size(self, axis):
        return self.groups if axis == "dp" else self.sharers

    def exchange(self, values, axis, bit):
        pairs = [(i, i ^ (1 << bit)) for i in range(self.size(axis))]
        return lax.ppermute(values, axis, pairs)

    def gather_far(self, shard):
        held = shard[None]
        for axis, bit in self.gather_dp[:-1]:
            held = jnp.concatenate([held, self.exchange(held, axis, bit)], axis=0)
        return held

    def gather_near(self, held):
        axis, bit = self.gather_dp[-1]
        return jnp.concatenate([held, self.exchange(held, axis, bit)], axis=0)

    def gather_x(self, held):
        pieces = {0: held}
        for axis, bit in self.gather_fsdp[:-1]:
            for name in list(pieces):
                pieces[name | (1 << bit)] = self.exchange(pieces[name], axis, bit)
        return pieces

    def gather_core(self, pieces, *gate):
        axis, bit = self.gather_fsdp[-1]
        found = dict(pieces)
        for name in pieces:
            found[name | (1 << bit)] = self.exchange(after(pieces[name], gate), axis, bit)
        return tuple(found[name] for name in range(self.sharers))

    def piece_rows(self, dp, fsdp):
        found = []
        for f in range(self.sharers):
            for n in range(self.groups):
                rel = sum(((n >> k) & 1) << bit for k, (axis, bit) in enumerate(self.gather_dp))
                found.append(((dp ^ rel) * self.sharers + (fsdp ^ f)) * self.rows)
        return jnp.stack(found).astype(jnp.int32)

    def grad_rows(self, dp, fsdp):
        found = []
        for order in self.orders:
            for place in range(self.count):
                rel = {"dp": 0, "fsdp": 0}
                for k, (axis, bit) in enumerate(order):
                    rel[axis] |= ((place >> (len(order) - 1 - k)) & 1) << bit
                found.append(((dp ^ rel["dp"]) * self.sharers + (fsdp ^ rel["fsdp"])) * self.rows)
        return jnp.stack(found).astype(jnp.int32)

    def reduce_step(self, state, step, *gate):
        others = []
        for (keep, send), order in zip(state, self.orders):
            others.append(self.exchange(after(send, gate), *order[step]))
        last = step == len(self.orders[0]) - 1
        found = []
        for (keep, send), other in zip(state, others):
            found.append((keep.astype(f32) + other.astype(f32))[0] if last else merge(keep, other))
        return found


def merge_kernel(keep0, keep1, other0, other1, keep_ref, send_ref):
    send_ref[...] = (keep1[...].astype(f32) + other1[...].astype(f32)).astype(bf16)
    keep_ref[...] = (keep0[...].astype(f32) + other0[...].astype(f32)).astype(bf16)


def merge(keep, other):
    blocks, rows, width = keep.shape
    half = blocks // 2
    steps = min(half, 4)
    shape = (half // steps, rows, width)
    early = pl.BlockSpec(shape, lambda b: (b, 0, 0))
    late = pl.BlockSpec(shape, lambda b: (b + steps, 0, 0))
    out = jax.ShapeDtypeStruct((half, rows, width), bf16)
    return pl.pallas_call(
        merge_kernel,
        grid=(steps,),
        in_specs=[early, late, early, late],
        out_specs=[early, early],
        out_shape=[out, out],
        compiler_params=params(),
        cost_estimate=pl.CostEstimate(flops=keep.size, bytes_accessed=6 * keep.size, transcendentals=0),
        name="merge",
    )(keep, keep, other, other)


def load_weight(plan, rows_ref, pieces, weight_ref, sem_ref):
    if not plan.paired:
        copies = [pltpu.make_async_copy(pieces[0], weight_ref, sem_ref)]
    else:
        copies = []
        for f in range(plan.sharers):
            for n in range(plan.groups):
                at = pl.multiple_of(rows_ref[f * plan.groups + n], 8)
                target = weight_ref.at[pl.ds(at, plan.rows), :]
                copies.append(pltpu.make_async_copy(pieces[f].at[n], target, sem_ref))
    for copy in copies:
        copy.start()
    for copy in copies:
        copy.wait()


def grad_shapes(plan, width):
    if not plan.paired:
        return [jax.ShapeDtypeStruct((D, width), bf16)]
    half = plan.count // 2
    cut = first_part(width)
    return [jax.ShapeDtypeStruct((half, plan.rows, w), bf16) for w in (cut, cut, width - cut, width - cut)]


def first_part(width):
    step = grad_step(width)
    return (width // step + 1) // 2 * step


def grad_step(width):
    return D if width % D == 0 and width // D > 3 else D // 2


def stage_shape(plan, width):
    step = grad_step(width)
    return (2, plan.count, plan.rows, step) if plan.paired else (2, D, step)


def store_grads(plan, rows_ref, acc_ref, outs, stage_ref, sem_ref):
    width = acc_ref.shape[1]
    step = grad_step(width)
    cut = first_part(width)
    half = plan.count // 2
    waiting = []
    for n in range(width // step):
        slot = n % 2
        cols = slice(n * step, (n + 1) * step)
        if len(waiting) == 2:
            for copy in waiting.pop(0):
                copy.wait()
        if not plan.paired:
            stage_ref[slot] = acc_ref[:, cols].astype(bf16)
            copies = [pltpu.make_async_copy(stage_ref.at[slot], outs[0].at[:, cols], sem_ref.at[slot])]
        else:
            late = n * step >= cut
            base = plan.count if late else 0
            start = n * step - (cut if late else 0)

            def fill(place, carry):
                at = pl.multiple_of(rows_ref[base + place], 8)
                stage_ref[slot, place] = acc_ref[pl.ds(at, plan.rows), cols].astype(bf16)
                return carry

            lax.fori_loop(0, plan.count, fill, 0)
            keep, send = outs[2:4] if late else outs[0:2]
            there = slice(start, start + step)
            copies = [
                pltpu.make_async_copy(stage_ref.at[slot, 0:half], keep.at[:, :, there], sem_ref.at[slot]),
                pltpu.make_async_copy(stage_ref.at[slot, half:], send.at[:, :, there], sem_ref.at[slot]),
            ]
        for copy in copies:
            copy.start()
        waiting.append(copies)
    for copies in waiting:
        for copy in copies:
            copy.wait()


def project_kernel(plan, len_ref, row_ref, tok_ref, pass_ref, table_ref, gain_ref, *rest):
    pieces, (out_ref, w_ref, sem_ref) = rest[:-3], rest[-3:]

    @pl.when(pl.program_id(0) == 0)
    def load():
        load_weight(plan, row_ref, pieces, w_ref, sem_ref)

    @pl.when(pl.program_id(0) <= last_block(len_ref[0]))
    def work():
        hot = onehot_rows(pass_ref[0])
        entry = tok_ref[...].astype(f32) + dot_tn(hot, table_ref[...])
        unit, unused = normalized(entry)
        normed = (unit * gain_ref[...]).astype(bf16)
        for part in range(3):
            out_ref[part] = dot_nn(normed, w_ref[:, part * D : (part + 1) * D]).astype(bf16)


def project(plan, length, piece_rows, tokens, pass_rows, table, gain, pieces):
    rows = tokens.shape[0]
    at = lambda b, n, r: (jnp.minimum(b, last_block(n[0])), 0)
    return pl.pallas_call(
        functools.partial(project_kernel, plan),
        grid_spec=pltpu.PrefetchScalarGridSpec(
            num_scalar_prefetch=2,
            grid=(rows // ROWS,),
            in_specs=[
                pl.BlockSpec((ROWS, D), at),
                pl.BlockSpec((1, 1, ROWS), lambda b, n, r: at(b, n, r) + (0,)),
                pl.BlockSpec((8, D), lambda b, n, r: (0, 0)),
                pl.BlockSpec((1, D), lambda b, n, r: (0, 0)),
            ]
            + [pl.BlockSpec(memory_space=pl.ANY)] * len(pieces),
            out_specs=pl.BlockSpec((3, ROWS, D), lambda b, n, r: (0,) + at(b, n, r)),
            scratch_shapes=[pltpu.VMEM((D, 3 * D), bf16), pltpu.SemaphoreType.DMA],
        ),
        out_shape=jax.ShapeDtypeStruct((3, rows, D), bf16),
        compiler_params=params(),
        cost_estimate=pl.CostEstimate(
            flops=2 * rows * D * 3 * D, bytes_accessed=rows * D * 8 + D * D * 6, transcendentals=0
        ),
        name="project",
    )(length, piece_rows, tokens, pass_rows, table, gain, *pieces)


def attend_kernel(len_ref, p_ref, out_ref, lse_ref):
    blocks = p_ref.shape[1] // ROWS
    lane = lax.broadcasted_iota(jnp.int32, (ROWS, 128), 1)
    first_head = lane < HEAD
    here = lax.broadcasted_iota(jnp.int32, (ROWS, ROWS), 0)
    there = lax.broadcasted_iota(jnp.int32, (ROWS, ROWS), 1)
    allowed = there <= here
    for i in range(blocks):
        rows = slice(i * ROWS, (i + 1) * ROWS)

        @pl.when(i * ROWS < len_ref[0])
        def work():
            query = p_ref[0, rows, :] * jnp.asarray(1.0 / math.sqrt(HEAD), bf16)
            found = []
            for head in range(2):
                mine = first_head if head == 0 else jnp.logical_not(first_head)
                q = jnp.where(mine, query, jnp.zeros_like(query))
                diag = dot_nt(q, p_ref[1, rows, :])
                diag = jnp.where(allowed, diag, -1e30)
                largest = jnp.max(diag, axis=-1, keepdims=True)
                if i > 0:
                    before = dot_nt(q, p_ref[1, : i * ROWS, :])
                    largest = jnp.maximum(largest, jnp.max(before, axis=-1, keepdims=True))
                diag = jnp.exp(diag - largest)
                total = jnp.sum(diag, axis=-1, keepdims=True)
                out = dot_nn(diag.astype(bf16), p_ref[2, rows, :])
                if i > 0:
                    before = jnp.exp(before - largest)
                    total = total + jnp.sum(before, axis=-1, keepdims=True)
                    out = out + dot_nn(before.astype(bf16), p_ref[2, : i * ROWS, :])
                found.append(out * (1.0 / total))
                lse = jnp.broadcast_to(largest + jnp.log(total), (ROWS, 128))
                lse_ref[0, head : head + 1, rows] = lse.T[0:1]
            out_ref[rows, :] = jnp.where(first_head, found[0], found[1]).astype(bf16)


def attend(length, projected):
    rows = projected.shape[1]
    pairs = HEADS // 2
    return pl.pallas_call(
        attend_kernel,
        grid_spec=pltpu.PrefetchScalarGridSpec(
            num_scalar_prefetch=1,
            grid=(pairs,),
            in_specs=[pl.BlockSpec((3, rows, 128), lambda h, n: (0, 0, h))],
            out_specs=[
                pl.BlockSpec((rows, 128), lambda h, n: (0, h)),
                pl.BlockSpec((1, 8, rows), lambda h, n: (h, 0, 0)),
            ],
        ),
        out_shape=[
            jax.ShapeDtypeStruct((rows, D), bf16),
            jax.ShapeDtypeStruct((pairs, 8, rows), f32),
        ],
        compiler_params=params(),
        cost_estimate=pl.CostEstimate(
            flops=2 * rows * rows * D, bytes_accessed=rows * D * 8, transcendentals=HEADS * rows * rows // 2
        ),
        name="attend",
    )(length, projected)


def attend_back_kernel(len_ref, p_ref, o_ref, g_ref, lse_ref, out_ref, dk_ref, dv_ref, kz_ref, vz_ref, kt_ref):
    blocks = p_ref.shape[1] // ROWS
    scaling = 1.0 / math.sqrt(HEAD)
    lane = lax.broadcasted_iota(jnp.int32, (ROWS, 128), 1)
    first_head = lane < HEAD
    row8 = lax.broadcasted_iota(jnp.int32, (8, 128), 0)
    lane8 = lax.broadcasted_iota(jnp.int32, (8, 128), 1)
    chooser = (lax.div(lane8, HEAD) == row8).astype(f32)
    key_at = lax.broadcasted_iota(jnp.int32, (2, ROWS, ROWS), 1)
    row_at = lax.broadcasted_iota(jnp.int32, (2, ROWS, ROWS), 2)
    allowed = (key_at <= row_at).reshape(2 * ROWS, ROWS)
    for i in range(blocks):
        rows = slice(i * ROWS, (i + 1) * ROWS)
        two = slice(2 * i * ROWS, 2 * (i + 1) * ROWS)

        @pl.when(i * ROWS < len_ref[0])
        def work():
            dk_ref[two, :] = jnp.zeros((2 * ROWS, 128), f32)
            dv_ref[two, :] = jnp.zeros((2 * ROWS, 128), f32)
            key, value = p_ref[1, rows, :], p_ref[2, rows, :]
            zero = jnp.zeros_like(key)
            k2 = jnp.concatenate([jnp.where(first_head, key, zero), jnp.where(first_head, zero, key)], axis=0)
            kz_ref[two, :] = k2
            kt_ref[:, two] = k2.T
            vz_ref[two, :] = jnp.concatenate([jnp.where(first_head, value, zero), jnp.where(first_head, zero, value)], axis=0)
            query = p_ref[0, rows, :] * jnp.asarray(scaling, bf16)
            grad = g_ref[rows, :]
            product = grad.astype(f32) * o_ref[rows, :].astype(f32)
            delta = lax.dot_general(chooser, product, (((1,), (1,)), ((), ())), precision=lax.Precision.HIGHEST, preferred_element_type=f32)
            def both(a, b):
                return jnp.concatenate([jnp.broadcast_to(a, (ROWS, ROWS)), jnp.broadcast_to(b, (ROWS, ROWS))], axis=0)
            lse2 = both(lse_ref[0, 0:1, rows], lse_ref[0, 1:2, rows])
            delta2 = both(delta[0:1], delta[1:2])
            dqt = jnp.zeros((128, ROWS), f32)
            for j in range(i + 1):
                cols = slice(2 * j * ROWS, 2 * (j + 1) * ROWS)
                prob = jnp.exp(dot_nt(kz_ref[cols, :], query) - lse2)
                if i == j:
                    prob = jnp.where(allowed, prob, 0.0)
                ds = (prob * (dot_nt(vz_ref[cols, :], grad) - delta2)).astype(bf16)
                dv_ref[cols, :] += dot_nn(prob.astype(bf16), grad)
                dk_ref[cols, :] += dot_nn(ds, query)
                dqt = dqt + dot_nn(kt_ref[:, cols], ds)
            out_ref[0, rows, :] = (dqt * scaling).T.astype(bf16)
    for i in range(blocks):
        rows = slice(i * ROWS, (i + 1) * ROWS)
        a = slice(2 * i * ROWS, (2 * i + 1) * ROWS); b = slice((2 * i + 1) * ROWS, 2 * (i + 1) * ROWS)

        @pl.when(i * ROWS < len_ref[0])
        def finish():
            out_ref[1, rows, :] = jnp.where(first_head, dk_ref[a, :], dk_ref[b, :]).astype(bf16)
            out_ref[2, rows, :] = jnp.where(first_head, dv_ref[a, :], dv_ref[b, :]).astype(bf16)


def attend_back(length, which, first, projected, heads_out, grad_heads, lse, before=None):
    rows = projected.shape[1]
    pairs = HEADS // 2
    at = lambda h: h + (0 if first else pairs // 2)
    in_specs = [
        pl.BlockSpec((3, rows, 128), lambda h, n: (0, 0, at(h))),
        pl.BlockSpec((rows, 128), lambda h, n: (0, at(h))),
        pl.BlockSpec((None, rows, 128), lambda h, n: (which, 0, at(h))),
        pl.BlockSpec((1, 8, rows), lambda h, n: (at(h), 0, 0)),
    ]
    operands = [length, projected, heads_out, grad_heads, lse]
    if first:
        kernel = attend_back_kernel
    else:
        kernel = lambda n, p, o, g, l, unused, *rest: attend_back_kernel(n, p, o, g, l, *rest)
        in_specs.append(pl.BlockSpec(memory_space=pl.ANY))
        operands.append(before)
    return pl.pallas_call(
        kernel,
        grid_spec=pltpu.PrefetchScalarGridSpec(
            num_scalar_prefetch=1,
            grid=(pairs // 2,),
            in_specs=in_specs,
            out_specs=pl.BlockSpec((3, rows, 128), lambda h, n: (0, 0, at(h))),
            scratch_shapes=[
                pltpu.VMEM((2 * rows, 128), f32),
                pltpu.VMEM((2 * rows, 128), f32),
                pltpu.VMEM((2 * rows, 128), bf16),
                pltpu.VMEM((2 * rows, 128), bf16),
                pltpu.VMEM((128, 2 * rows), bf16),
            ],
        ),
        out_shape=jax.ShapeDtypeStruct((3, rows, D), bf16),
        input_output_aliases={} if first else {5: 0},
        compiler_params=params(),
        cost_estimate=pl.CostEstimate(
            flops=3 * rows * rows * D, bytes_accessed=rows * D * 8, transcendentals=HEADS * rows * rows // 4
        ),
        name="attend_back",
    )(*operands)


def feed_kernel(plan, len_ref, row_ref, *refs):
    tok0, tok1, pass0, pass1, ho0, ho1, cot, table_ref, gain_ref = refs[:9]
    many = plan.sharers if plan.paired else 1
    grad_ref, pieces, refs = refs[9], refs[10 : 10 + many], refs[10 + many :]
    res, gh, hid, small_ref = refs[:4]
    outs, (w_ref, acc_ref, stage_ref, sem_ref) = refs[4:-4], refs[-4:]
    b = pl.program_id(0)
    many0 = last_block(len_ref[0]) + 1
    many1 = last_block(len_ref[1]) + 1
    early = b < many0

    @pl.when(b == 0)
    def clear():
        load_weight(plan, row_ref, pieces, w_ref, sem_ref.at[0])
        acc_ref[...] = jnp.zeros_like(acc_ref)
        small_ref[...] = jnp.zeros_like(small_ref)

    @pl.when(b < many0 + many1)
    def block():
        hot = onehot_rows(jnp.where(early, pass0[0], pass1[0]))
        entry = jnp.where(early, tok0[...], tok1[...]).astype(f32) + dot_tn(hot, table_ref[...])
        at = jnp.where(early, b, b - many0) * ROWS + lax.broadcasted_iota(jnp.int32, (ROWS, 1), 0)
        live = at < jnp.where(early, len_ref[0], len_ref[1])
        heads = jnp.where(early, ho0[...], ho1[...])
        attention = dot_nn(heads, w_ref[:, 0:D])
        hidden = entry + attention
        unit, scale = normalized(hidden)
        gain = gain_ref[...]
        normed = (unit * gain).astype(bf16)
        grad_feed = jnp.where(live, cot[...].reshape(ROWS, D).astype(f32), 0.0).astype(bf16)
        feed = jnp.zeros((ROWS, D), f32)
        grad_normed = jnp.zeros((ROWS, D), f32)
        for k in range(CHUNKS):
            up = slice(D + k * D, D + (k + 1) * D)
            down = slice(D + FF + k * D, D + FF + (k + 1) * D)
            x = dot_nn(normed, w_ref[:, up])
            grad_act = dot_nt(grad_feed, w_ref[:, down])
            c0 = math.sqrt(2.0 / math.pi)
            square = x * x
            bent = jnp.tanh(x * (c0 + (c0 * 0.044715) * square))
            half = 0.5 + 0.5 * bent
            slope = half + (0.5 * x) * (1.0 - bent * bent) * (c0 + (3.0 * c0 * 0.044715) * square)
            act = (x * half).astype(bf16)
            grad_x = (slope * grad_act).astype(bf16)
            feed = feed + dot_nn(act, w_ref[:, down])
            grad_normed = grad_normed + dot_nt(grad_x, w_ref[:, up])
            acc_ref[:, up] += dot_tn(normed, grad_x)
            acc_ref[:, down] += dot_tn(act, grad_feed)
        res[...] = jnp.where(live, hidden + feed, 0.0).astype(bf16).reshape(res.shape)
        small_ref[0:8] += fold_rows(grad_normed * unit)
        small_ref[8:16] += fold_rows(jnp.where(live, entry * entry, 0.0))
        small_ref[16:24] += fold_rows(jnp.where(live, attention * attention, 0.0))
        small_ref[24:32] += fold_rows(jnp.where(live, feed * feed, 0.0))
        grad_hidden = grad_feed.astype(f32) + norm_back(grad_normed * gain, unit, scale)
        hid[...] = grad_hidden
        grad_attention = grad_hidden.astype(bf16)
        acc_ref[:, 0:D] += dot_tn(heads, grad_attention)
        gh[...] = dot_nt(grad_attention, w_ref[:, 0:D]).astype(bf16)

    @pl.when(b == pl.num_programs(0) - 1)
    def finish():
        store_grads(plan, grad_ref, acc_ref, outs, stage_ref, sem_ref)


def feed(plan, part, lengths, piece_rows, grad_rows, tokens, pass_rows, heads_out, cotangent, table, gain, pieces, width):
    rows = tokens[0].shape[0]
    per = ROWS // part

    def at0(b, n, r):
        return jnp.minimum(b, last_block(n[0])), 0

    def at1(b, n, r):
        return jnp.clip(b - last_block(n[0]) - 1, 0, last_block(n[1])), 0

    def both(b, n, r):
        early = b <= last_block(n[0])
        return jnp.where(early, b, at1(b, n, r)[0]), jnp.where(early, 0, 1)

    row0 = pl.BlockSpec((ROWS, D), at0)
    row1 = pl.BlockSpec((ROWS, D), at1)
    pas0 = pl.BlockSpec((1, 1, ROWS), lambda *a: at0(*a) + (0,))
    pas1 = pl.BlockSpec((1, 1, ROWS), lambda *a: at1(*a) + (0,))
    dealt = pl.BlockSpec((per, 1, part, D), lambda *a: both(*a) + (0, 0))
    local = pl.BlockSpec((None, ROWS, D), lambda *a: both(*a)[::-1] + (0,))
    grads = grad_shapes(plan, width)
    anywhere = pl.BlockSpec(memory_space=pl.ANY)
    return pl.pallas_call(
        functools.partial(feed_kernel, plan),
        grid_spec=pltpu.PrefetchScalarGridSpec(
            num_scalar_prefetch=2,
            grid=(2 * rows // ROWS,),
            in_specs=[
                row0, row1, pas0, pas1, row0, row1, dealt,
                pl.BlockSpec((8, D), lambda *a: (0, 0)),
                pl.BlockSpec((1, D), lambda *a: (0, 0)),
                pl.BlockSpec(memory_space=pltpu.SMEM),
            ]
            + [anywhere] * len(pieces),
            out_specs=[dealt, local, local, pl.BlockSpec((32, D), lambda *a: (0, 0))] + [anywhere] * len(grads),
            scratch_shapes=[
                pltpu.VMEM((D, width), bf16),
                pltpu.VMEM((D, width), f32),
                pltpu.VMEM(stage_shape(plan, width), bf16),
                pltpu.SemaphoreType.DMA((2,)),
            ],
        ),
        out_shape=[
            jax.ShapeDtypeStruct(cotangent.shape, bf16),
            jax.ShapeDtypeStruct((2, rows, D), bf16),
            jax.ShapeDtypeStruct((2, rows, D), f32),
            jax.ShapeDtypeStruct((32, D), f32),
        ]
        + grads,
        compiler_params=params(),
        cost_estimate=pl.CostEstimate(
            flops=2 * 6 * rows * D * width, bytes_accessed=2 * rows * D * 14 + D * width * 4, transcendentals=2 * rows * FF
        ),
        name="feed",
    )(lengths, piece_rows, tokens[0], tokens[1], pass_rows[0], pass_rows[1], heads_out[0], heads_out[1],
      cotangent, table, gain, grad_rows, *pieces)


def project_back_kernel(plan, weight, rows_back, final, len_ref, row_ref, grad_ref, tok_ref, pass_ref, g_ref, *rest):
    rest = list(rest)
    hid_ref = rest.pop(0) if rows_back else None
    table_ref, gain_ref = rest.pop(0), rest.pop(0)
    before_ref = rest.pop(0) if final else None
    many = plan.sharers if plan.paired else 1
    pieces = [rest.pop(0) for n in range(many)] if rows_back else []
    if rows_back:
        out_ref, small_ref = rest.pop(0), rest.pop(0)
    if weight and not final:
        acc_ref = rest.pop(0)
    outs = [rest.pop(0) for shape in grad_shapes(plan, 3 * D)] if final else []
    if rows_back:
        w_ref = rest.pop(0)
    if final:
        acc_ref, stage_ref = rest.pop(0), rest.pop(0)
    sem_ref = rest.pop(0)
    b = pl.program_id(0)

    @pl.when(b == 0)
    def clear():
        if rows_back:
            load_weight(plan, row_ref, pieces, w_ref, sem_ref.at[0])
            small_ref[...] = jnp.zeros_like(small_ref)
        if weight:
            acc_ref[...] = before_ref[...] if final else jnp.zeros_like(acc_ref)

    @pl.when(b <= last_block(len_ref[0]))
    def work():
        hot = onehot_rows(pass_ref[0])
        entry = tok_ref[...].astype(f32) + dot_tn(hot, table_ref[...])
        unit, scale = normalized(entry)
        gain = gain_ref[...]
        if weight:
            normed = (unit * gain).astype(bf16)
            for part in range(3):
                acc_ref[:, part * D : (part + 1) * D] += dot_tn(normed, g_ref[part])
        if rows_back:
            grad_normed = jnp.zeros((ROWS, D), f32)
            for part in range(3):
                grad_normed = grad_normed + dot_nt(g_ref[part], w_ref[:, part * D : (part + 1) * D])
            small_ref[0:8] += fold_rows(grad_normed * unit)
            grad_entry = hid_ref[...] + norm_back(grad_normed * gain, unit, scale)
            high = grad_entry.astype(bf16)
            out_ref[...] = high
            rest_one = grad_entry - high.astype(f32)
            low = rest_one.astype(bf16)
            lower = (rest_one - low.astype(f32)).astype(bf16)
            small_ref[8:16] += dot_nn(hot, high) + dot_nn(hot, low) + dot_nn(hot, lower)

    if final:
        @pl.when(b == pl.num_programs(0) - 1)
        def finish():
            store_grads(plan, grad_ref, acc_ref, outs, stage_ref, sem_ref)


def project_back(
    plan, weight, rows_back, which, length, piece_rows, grad_rows, tokens, pass_rows, grads, grad_hidden, table, gain,
    pieces, before=None,
):
    rows = tokens.shape[0]
    final = before is not None
    at = lambda b, n, r, g: (jnp.minimum(b, last_block(n[0])), 0)
    row = pl.BlockSpec((ROWS, D), at)
    anywhere = pl.BlockSpec(memory_space=pl.ANY)
    in_specs = [
        row,
        pl.BlockSpec((1, 1, ROWS), lambda *a: at(*a) + (0,)),
        pl.BlockSpec((3, ROWS, D), lambda *a: (0,) + at(*a)),
    ]
    operands = [length, piece_rows, grad_rows, tokens, pass_rows, grads]
    if rows_back:
        in_specs.append(pl.BlockSpec((None, ROWS, D), lambda *a: (which,) + at(*a)))
        operands.append(grad_hidden)
    in_specs += [pl.BlockSpec((8, D), lambda *a: (0, 0)), pl.BlockSpec((1, D), lambda *a: (0, 0))]
    operands += [table, gain]
    out_shape, out_specs, scratch = [], [], []
    if final:
        in_specs.append(pl.BlockSpec((D, 3 * D), lambda *a: (0, 0), pipeline_mode=pl.Buffered(1)))
        operands.append(before)
    if rows_back:
        in_specs += [anywhere] * len(pieces)
        operands += pieces
        out_shape += [jax.ShapeDtypeStruct((rows, D), bf16), jax.ShapeDtypeStruct((16, D), f32)]
        out_specs += [row, pl.BlockSpec((16, D), lambda *a: (0, 0))]
        scratch.append(pltpu.VMEM((D, 3 * D), bf16))
    if weight and not final:
        out_shape.append(jax.ShapeDtypeStruct((D, 3 * D), f32))
        out_specs.append(pl.BlockSpec((D, 3 * D), lambda *a: (0, 0)))
    if final:
        shapes = grad_shapes(plan, 3 * D)
        out_shape += shapes
        out_specs += [anywhere] * len(shapes)
        scratch += [pltpu.VMEM((D, 3 * D), f32), pltpu.VMEM(stage_shape(plan, 3 * D), bf16)]
    return pl.pallas_call(
        functools.partial(project_back_kernel, plan, weight, rows_back, final),
        grid_spec=pltpu.PrefetchScalarGridSpec(
            num_scalar_prefetch=3,
            grid=(rows // ROWS,),
            in_specs=in_specs,
            out_specs=out_specs,
            scratch_shapes=scratch + [pltpu.SemaphoreType.DMA((2,))],
        ),
        out_shape=out_shape,
        compiler_params=params(),
        cost_estimate=pl.CostEstimate(
            flops=2 * (weight + rows_back) * rows * D * 3 * D, bytes_accessed=rows * D * 14 + D * D * 6, transcendentals=0
        ),
        name="project_back",
    )(*operands)


def pick_kernel(index_ref, in_ref, out_ref, sem_ref):
    copies = [
        pltpu.make_async_copy(in_ref.at[index_ref[n]], out_ref.at[n], sem_ref) for n in range(out_ref.shape[0])
    ]
    for copy in copies:
        copy.start()
    for copy in copies:
        copy.wait()


def pick(index, blocks):
    shape = index.shape + blocks.shape[1:]
    return pl.pallas_call(
        pick_kernel,
        grid_spec=pltpu.PrefetchScalarGridSpec(
            num_scalar_prefetch=1,
            grid=(1,),
            in_specs=[pl.BlockSpec(memory_space=pl.ANY)],
            out_specs=pl.BlockSpec(shape, lambda b, n: (0, 0, 0)),
            scratch_shapes=[pltpu.SemaphoreType.DMA],
        ),
        out_shape=jax.ShapeDtypeStruct(shape, blocks.dtype),
        compiler_params=params(),
        cost_estimate=pl.CostEstimate(flops=0, bytes_accessed=4 * math.prod(shape), transcendentals=0),
        name="pick",
    )(index, blocks)


def settle_kernel(index_ref, *refs):
    arrays, out_ref = refs[:-1], refs[-1]
    first = pl.program_id(0) * out_ref.shape[0]
    rows = out_ref.shape[1]
    at = lax.broadcasted_iota(jnp.int32, (rows, 1), 0)
    for n in range(out_ref.shape[0]):
        live = at < index_ref[2, first + n]
        source, late = index_ref[1, first + n], index_ref[0, first + n]
        if len(arrays) == 1:
            found = arrays[0][2 * source + late]
        else:
            found = jnp.where(late == 0, arrays[0][source], arrays[1][source])
        out_ref[n] = jnp.where(live, found.astype(f32), 0.0)


def settle(index, *arrays):
    many = index.shape[1]
    step = 4
    shape = arrays[0].shape
    whole = pl.BlockSpec(shape, lambda b, n: (0, 0, 0), pipeline_mode=pl.Buffered(1))
    return pl.pallas_call(
        settle_kernel,
        grid_spec=pltpu.PrefetchScalarGridSpec(
            num_scalar_prefetch=1,
            grid=(many // step,),
            in_specs=[whole] * len(arrays),
            out_specs=pl.BlockSpec((step,) + shape[1:], lambda b, n: (b, 0, 0)),
        ),
        out_shape=jax.ShapeDtypeStruct((many,) + shape[1:], f32),
        compiler_params=params(),
        cost_estimate=pl.CostEstimate(flops=0, bytes_accessed=6 * many * math.prod(shape[1:]), transcendentals=0),
        name="settle",
    )(index, *arrays)


def after(values, *others):
    return lax.optimization_barrier((values, others))[0]


def swap(blocks):
    return lax.all_to_all(blocks, "dp", split_axis=0, concat_axis=0, tiled=True)


def per_device(
    groups,
    width_all,
    tokens,
    passes,
    lengths,
    dealing,
    pass_table,
    gain_first,
    to_heads,
    from_heads,
    gain_second,
    expand,
    shrink,
    cotangent,
):
    axes = ("dp", "fsdp")
    slots, part, unused_width = tokens.shape
    seq_len = part * groups
    order = jnp.arange(slots, dtype=jnp.int32)
    here = lax.axis_index("dp")
    ordering = dealing[0, 0]
    sizes = lengths[0]

    ahead = (sizes[None, :] > sizes[:, None]) | (
        (sizes[None, :] == sizes[:, None]) & (order[None, :] < order[:, None])
    )
    rank = jnp.sum(ahead.astype(jnp.int32), axis=1)
    ranked = jnp.sum(jnp.where(rank[None, :] == order[:, None], order[None, :], 0), axis=1)
    place = jnp.sum(jnp.where(ordering[None, :] == order[:, None], order[None, :], 0), axis=1)
    early_seqs = ranked[:groups]
    late_seqs = ranked[groups:][::-1]
    from_early = jnp.sum(jnp.where(early_seqs[:, None] == order[None, :], place[None, :], 0), axis=1)
    from_late = jnp.sum(jnp.where(late_seqs[:, None] == order[None, :], place[None, :], 0), axis=1)
    slot_rank = jnp.sum(jnp.where(ordering[:, None] == order[None, :], rank[None, :], 0), axis=1)
    slot_size = jnp.sum(jnp.where(ordering[:, None] == order[None, :], sizes[None, :], 0), axis=1)
    is_late = (slot_rank >= groups).astype(jnp.int32)
    source = jnp.where(is_late == 1, slots - 1 - slot_rank, slot_rank)
    back_index = jnp.stack([is_late, source, slot_size - here * part])
    my_seqs = jnp.stack([early_seqs[here], late_seqs[here]])
    my_sizes = jnp.sum(jnp.where(my_seqs[:, None] == order[None, :], sizes[None, :], 0), axis=1)

    row_count = to_heads.shape[0]
    narrow = jnp.concatenate(
        [
            from_heads,
            expand.reshape(row_count, D, CHUNKS).transpose(0, 2, 1).reshape(row_count, FF),
            shrink.reshape(row_count, CHUNKS * D),
        ],
        axis=1,
    )
    plan = Plan(groups, width_all // groups, row_count)
    fsdp_here = lax.axis_index("fsdp")
    if plan.paired:
        held = plan.gather_far(jnp.concatenate([to_heads, narrow], axis=1))
        head_pieces = plan.gather_core(plan.gather_x(plan.gather_near(held[:, :, : 3 * D])))
        wide_near = plan.gather_near(held[:, :, 3 * D :])
        piece_rows = plan.piece_rows(here, fsdp_here)
        grad_rows = plan.grad_rows(here, fsdp_here)
    else:
        held = to_heads
        head_pieces = (lax.all_gather(to_heads, axes, axis=0, tiled=True),)
        wide_near = wide_pieces = (lax.all_gather(narrow, axes, axis=0, tiled=True),)
        piece_rows = grad_rows = jnp.zeros((1,), jnp.int32)

    my_passes = [passes[my_seqs[m]].reshape(seq_len // ROWS, 1, ROWS) for m in range(2)]
    one_size = [my_sizes[m : m + 1] for m in range(2)]
    table = jnp.zeros((8, D), bf16).at[:PASSES].set(pass_table)
    gain_one = gain_first.astype(f32).reshape(1, D)
    gain_two = gain_second.astype(f32).reshape(1, D)

    def forward(m, *gate):
        return project(
            plan, after(one_size[m], gate), piece_rows, my_tokens[m], my_passes[m], table, gain_one, head_pieces
        )

    def mix(m, *gate):
        return attend(after(one_size[m], gate), projected[m])

    def mix_back(m, before, *gate):
        return attend_back(
            after(one_size[m], gate), m, before is None, projected[m], heads_out[m], grad_heads, lse[m], before
        )

    def back(m, weight, rows_back, *gate, before=None):
        return project_back(
            plan, weight, rows_back, m, after(one_size[m], gate), piece_rows, grad_rows, my_tokens[m], my_passes[m],
            grad_parts[m], grad_hidden, table, gain_one, head_pieces, before,
        )

    def send_back(rows, *gate):
        return swap(after(rows, gate).reshape(groups, part, D))

    pairs_index = jnp.stack([from_early, from_late], axis=1).reshape(slots)
    picked = [pick(from_early, tokens), pick(from_late, tokens), pick(pairs_index, cotangent)]
    projected, heads_out, lse, grad_parts = [None, None], [None, None], [None, None], [None, None]
    tokens0 = swap(after(picked[0], held))
    tokens1 = swap(after(picked[1], tokens0, picked[2]))
    my_tokens = [tokens0.reshape(seq_len, D), tokens1.reshape(seq_len, D)]
    projected[0] = forward(0)
    my_grads = swap(after(picked[2].reshape(groups, 2, part, D), tokens1, projected[0]))
    heads_out[0], lse[0] = mix(0, wide_near)
    if plan.paired:
        wide_x = plan.gather_x(wide_near)
    projected[1] = forward(1, lse[0])
    if plan.paired:
        wide_pieces = plan.gather_core(wide_x, projected[1])
    heads_out[1], lse[1] = mix(1)

    res, grad_heads, grad_hidden, feed_small, *wide_grads = feed(
        plan, part, my_sizes, piece_rows, grad_rows, my_tokens, my_passes, heads_out, my_grads, table, gain_two,
        wide_pieces, D + 2 * FF,
    )

    def begin(grads):
        if not plan.paired:
            return lax.psum_scatter(grads[0], axes, scatter_dimension=0, tiled=True).astype(f32)
        return [tuple(grads[0:2]), tuple(grads[2:4])]

    def advance(state, step, *gate):
        return plan.reduce_step(state, step, gate) if plan.paired else state

    steps = len(plan.orders[0])
    wide0 = begin(wide_grads)
    result = swap(res)
    some = mix_back(0, None)
    wide1 = advance(wide0, 0)
    grad_parts[0] = mix_back(0, some, wide1)
    entry0, small0, head_sum = back(0, True, True)
    wide2 = advance(wide1, 1, some)
    some = mix_back(1, None, entry0, wide2)
    wide3 = advance(wide2, 2, entry0)
    grad_parts[1] = mix_back(1, some, result, wide3)
    moved0 = send_back(entry0, result, some)
    wide4 = advance(wide3, 3, some)
    entry1, small1 = back(1, False, True, wide4)
    moved1 = send_back(entry1, moved0)
    head_grads = back(1, True, False, entry1, moved0, before=head_sum)
    wide_state = wide4
    for step in range(4, steps):
        wide_state = advance(wide_state, step, entry1)
    head_state = begin(head_grads)
    squares = jnp.sum(feed_small[8:].reshape(3, 8 * D), axis=1)
    counted = jnp.sum(my_sizes).astype(f32)
    last_row = jnp.zeros((1, D), f32).at[0, :3].set(squares).at[0, 3].set(counted)
    small = small0 + small1
    totals = jnp.concatenate(
        [
            small[8 : 8 + PASSES],
            jnp.sum(small[:8], axis=0, keepdims=True),
            jnp.sum(feed_small[:8], axis=0, keepdims=True),
            last_row,
        ],
        axis=0,
    )
    if plan.paired:
        for step in range(steps):
            totals = totals + plan.exchange(after(totals, head_state), *plan.orders[0][step])
            head_state = plan.reduce_step(head_state, step, *([moved1] if step == 3 else []))
        wide_owned, head_owned = [jnp.concatenate(state, axis=1) for state in (wide_state, head_state)]
    else:
        totals = lax.psum(totals, axes)
        wide_owned, head_owned = wide_state, head_state

    root_squares = jnp.sqrt(totals[7, :3] / (totals[7, 3] * D))

    grad_expand = wide_owned[:, D : D + FF].reshape(row_count, CHUNKS, D).transpose(0, 2, 1)
    return (
        settle(back_index, result.reshape(slots, part, D)),
        settle(back_index, moved0, moved1),
        totals[:PASSES],
        totals[PASSES],
        head_owned,
        wide_owned[:, :D],
        totals[PASSES + 1],
        grad_expand.reshape(row_count, FF),
        wide_owned[:, D + FF :].reshape(row_count * CHUNKS, D),
        root_squares,
    )


def solution(mesh):
    groups = mesh.shape["dp"]
    weight_spec = P(("dp", "fsdp"), None)
    block_spec = P("fsdp", "dp", None)
    in_specs = (
        block_spec,
        P("fsdp", None),
        P("fsdp", None),
        P("dp", "fsdp", None),
        P(),
        P(),
        weight_spec,
        weight_spec,
        P(),
        weight_spec,
        weight_spec,
        block_spec,
    )
    out_specs = (
        block_spec,
        block_spec,
        P(),
        P(),
        weight_spec,
        weight_spec,
        P(),
        weight_spec,
        weight_spec,
        P(),
    )
    body = functools.partial(per_device, groups, groups * mesh.shape["fsdp"])
    return jax.shard_map(body, mesh=mesh, in_specs=in_specs, out_specs=out_specs, check_vma=False)
```

```python
import math
import functools

import jax
import jax.numpy as jnp
from jax import lax
from jax.experimental import pallas as pl
from jax.experimental.pallas import tpu as pltpu
from jax.sharding import PartitionSpec as P

D = 768
HEADS = 12
HEAD = 64
FF = 3072
PASSES = 5
EPS = 1e-05
ROWS = 256
CHUNKS = FF // D
VMEM_MOST = 64000 * 1024

f32 = jnp.float32
bf16 = jnp.bfloat16


def dot_nn(a, b):
    return lax.dot_general(a, b, (((1,), (0,)), ((), ())), preferred_element_type=f32)


def dot_nt(a, b):
    return lax.dot_general(a, b, (((1,), (1,)), ((), ())), preferred_element_type=f32)


def dot_tn(a, b):
    return lax.dot_general(a, b, (((0,), (0,)), ((), ())), preferred_element_type=f32)


def params(**more):
    return pltpu.CompilerParams(vmem_limit_bytes=VMEM_MOST, **more)


def normalized(values):
    centred = values - jnp.mean(values, axis=-1, keepdims=True)
    spread = jnp.mean(centred * centred, axis=-1, keepdims=True)
    scale = lax.rsqrt(spread + EPS)
    return centred * scale, scale


def norm_back(grad_unit, unit, scale):
    first = jnp.mean(grad_unit, axis=-1, keepdims=True)
    second = jnp.mean(grad_unit * unit, axis=-1, keepdims=True)
    return scale * (grad_unit - first - unit * second)


def onehot_rows(pass_row):
    ids = lax.broadcasted_iota(jnp.int32, (8, pass_row.shape[-1]), 0)
    return (ids == pass_row).astype(f32).astype(bf16)


def fold_rows(values):
    rows, width = values.shape
    return jnp.sum(values.reshape(rows // 8, 8, width), axis=0)


def last_block(length):
    return lax.div(length + (ROWS - 1), ROWS) - 1


def bits_of(count):
    return count.bit_length() - 1


class Plan:
    def __init__(self, groups, sharers, rows):
        self.groups, self.sharers, self.rows = groups, sharers, rows
        self.count = groups * sharers
        self.paired = rows % 8 == 0 and self.count & (self.count - 1) == 0 and sharers >= 4 and groups >= 4
        core, *over_x = [1 << bit for bit in range(bits_of(sharers))]
        near, *far = [sharers << bit for bit in range(bits_of(groups))]
        self.core, self.over_x, self.near, self.far = core, over_x, near, far[::-1]
        self.wide_orders = ([[core], over_x, [near], far], [[core], [near], over_x, far])
        self.head_orders = ([[core], over_x + [near], far],)

    def exchange(self, values, bits):
        pairs = [(i, i ^ bits) for i in range(self.count)]
        return lax.ppermute(values, ("dp", "fsdp"), pairs)

    def gather(self, held, masks):
        for bits in masks:
            held = jnp.concatenate([held, self.exchange(held, bits)], axis=0)
        return held

    def gather_x(self, held):
        pieces = {0: held}
        for bits in self.over_x[::-1]:
            for name in list(pieces):
                pieces[name | bits] = self.exchange(pieces[name], bits)
        return pieces

    def gather_core(self, pieces, *gate):
        found = dict(pieces)
        for name in pieces:
            found[name | self.core] = self.exchange(after(pieces[name], gate), self.core)
        return tuple(found[name] for name in range(self.sharers))

    def piece_rows(self, here):
        masks = self.far + [self.near]
        found = []
        for f in range(self.sharers):
            for n in range(self.groups):
                rel = f | ways_bits(masks, n)
                found.append((here ^ rel) * self.rows)
        return jnp.stack(found).astype(jnp.int32)

    def grad_rows(self, here, orders):
        found = []
        for order in orders:
            for place in range(self.count):
                rel, left = 0, self.count
                for masks in order:
                    left >>= len(masks)
                    rel |= ways_bits(masks, (place // left) % (1 << len(masks)))
                found.append((here ^ rel) * self.rows)
        return jnp.stack(found).astype(jnp.int32)

    def reduce_stage(self, states, orders, stage, gate=(), late=()):
        sums = []
        for ways, order in zip(states, orders):
            sums.append(
                [after(ways[0], late)]
                + [
                    self.exchange(after(ways[n], gate), ways_bits(order[stage], n))
                    for n in range(1, len(ways))
                ]
            )
        if stage == len(orders[0]) - 1:
            return [sum(part.astype(f32) for part in parts)[0] for parts in sums]
        return [merge(parts, 1 << len(order[stage + 1])) for parts, order in zip(sums, orders)]


def ways_bits(masks, way):
    return sum(bits for n, bits in enumerate(masks) if (way >> n) & 1)


def merge_kernel(many, ways, *refs):
    ins, outs = refs[: many * ways], refs[many * ways :]
    for way in range(ways):
        total = ins[way][...].astype(f32)
        for n in range(1, many):
            total = total + ins[n * ways + way][...].astype(f32)
        outs[way][...] = total.astype(bf16)


def merge(parts, ways):
    blocks, rows, width = parts[0].shape
    share = blocks // ways
    steps = min(share, 4)
    shape = (share // steps, rows, width)

    def view(way):
        return pl.BlockSpec(shape, lambda b: (b + way * steps, 0, 0))

    out = jax.ShapeDtypeStruct((share, rows, width), bf16)
    return pl.pallas_call(
        functools.partial(merge_kernel, len(parts), ways),
        grid=(steps,),
        in_specs=[view(way) for part in parts for way in range(ways)],
        out_specs=[pl.BlockSpec(shape, lambda b: (b, 0, 0))] * ways,
        out_shape=[out] * ways,
        compiler_params=params(),
        cost_estimate=pl.CostEstimate(
            flops=len(parts) * parts[0].size, bytes_accessed=(2 + 2 * len(parts)) * parts[0].size, transcendentals=0
        ),
        name="merge",
    )(*[part for part in parts for way in range(ways)])


def load_weight(plan, rows_ref, pieces, weight_ref, sem_ref):
    if not plan.paired:
        copies = [pltpu.make_async_copy(pieces[0], weight_ref, sem_ref)]
    else:
        copies = []
        for f in range(plan.sharers):
            for n in range(plan.groups):
                at = pl.multiple_of(rows_ref[f * plan.groups + n], 8)
                target = weight_ref.at[pl.ds(at, plan.rows), :]
                copies.append(pltpu.make_async_copy(pieces[f].at[n], target, sem_ref))
    for copy in copies:
        copy.start()
    for copy in copies:
        copy.wait()


def grad_shapes(plan, width, orders):
    if not plan.paired:
        return [jax.ShapeDtypeStruct((D, width), bf16)]
    half = plan.count // 2
    cut = first_part(width, orders)
    return [jax.ShapeDtypeStruct((half, plan.rows, w), bf16) for w in (cut, cut, width - cut, width - cut) if w > 0]


def first_part(width, orders):
    return (width // D + 1) // 2 * D if len(orders) == 2 else width


def stage_shape(plan):
    return (2, plan.count, plan.rows, D) if plan.paired else (2, D, D)


def store_grads(plan, orders, rows_ref, acc_ref, outs, stage_ref, sem_ref):
    width, step = acc_ref.shape[1], D
    cut = first_part(width, orders)
    half = plan.count // 2
    waiting = []
    for n in range(width // step):
        slot = n % 2
        cols = slice(n * step, (n + 1) * step)
        if len(waiting) == 2:
            for copy in waiting.pop(0):
                copy.wait()
        if not plan.paired:
            stage_ref[slot] = acc_ref[:, cols].astype(bf16)
            copies = [pltpu.make_async_copy(stage_ref.at[slot], outs[0].at[:, cols], sem_ref.at[slot])]
        else:
            late = n * step >= cut
            base = plan.count if late else 0
            start = n * step - (cut if late else 0)

            def fill(place, carry):
                at = pl.multiple_of(rows_ref[base + place], 8)
                stage_ref[slot, place] = acc_ref[pl.ds(at, plan.rows), cols].astype(bf16)
                return carry

            lax.fori_loop(0, plan.count, fill, 0, unroll=2)
            keep, send = outs[2:4] if late else outs[0:2]
            there = slice(start, start + step)
            copies = [
                pltpu.make_async_copy(stage_ref.at[slot, 0:half], keep.at[:, :, there], sem_ref.at[slot]),
                pltpu.make_async_copy(stage_ref.at[slot, half:], send.at[:, :, there], sem_ref.at[slot]),
            ]
        for copy in copies:
            copy.start()
        waiting.append(copies)
    for copies in waiting:
        for copy in copies:
            copy.wait()


def project_kernel(plan, len_ref, row_ref, tok_ref, pass_ref, table_ref, gain_ref, *rest):
    pieces, (out_ref, w_ref, sem_ref) = rest[:-3], rest[-3:]

    @pl.when(pl.program_id(0) == 0)
    def load():
        load_weight(plan, row_ref, pieces, w_ref, sem_ref)

    @pl.when(pl.program_id(0) <= last_block(len_ref[0]))
    def work():
        hot = onehot_rows(pass_ref[0])
        entry = tok_ref[...].astype(f32) + dot_tn(hot, table_ref[...])
        unit, unused = normalized(entry)
        normed = (unit * gain_ref[...]).astype(bf16)
        for part in range(3):
            out_ref[part] = dot_nn(normed, w_ref[:, part * D : (part + 1) * D]).astype(bf16)


def project(plan, length, piece_rows, tokens, pass_rows, table, gain, pieces):
    rows = tokens.shape[0]
    at = lambda b, n, r: (jnp.minimum(b, last_block(n[0])), 0)
    return pl.pallas_call(
        functools.partial(project_kernel, plan),
        grid_spec=pltpu.PrefetchScalarGridSpec(
            num_scalar_prefetch=2,
            grid=(rows // ROWS,),
            in_specs=[
                pl.BlockSpec((ROWS, D), at),
                pl.BlockSpec((1, 1, ROWS), lambda b, n, r: at(b, n, r) + (0,)),
                pl.BlockSpec((8, D), lambda b, n, r: (0, 0)),
                pl.BlockSpec((1, D), lambda b, n, r: (0, 0)),
            ]
            + [pl.BlockSpec(memory_space=pl.ANY)] * len(pieces),
            out_specs=pl.BlockSpec((3, ROWS, D), lambda b, n, r: (0,) + at(b, n, r)),
            scratch_shapes=[pltpu.VMEM((D, 3 * D), bf16), pltpu.SemaphoreType.DMA],
        ),
        out_shape=jax.ShapeDtypeStruct((3, rows, D), bf16),
        compiler_params=params(),
        cost_estimate=pl.CostEstimate(
            flops=2 * rows * D * 3 * D, bytes_accessed=rows * D * 8 + D * D * 6, transcendentals=0
        ),
        name="project",
    )(length, piece_rows, tokens, pass_rows, table, gain, *pieces)


def attend_kernel(len_ref, p_ref, out_ref, lse_ref):
    blocks = p_ref.shape[1] // ROWS
    lane = lax.broadcasted_iota(jnp.int32, (ROWS, 128), 1)
    first_head = lane < HEAD
    here = lax.broadcasted_iota(jnp.int32, (ROWS, ROWS), 0)
    there = lax.broadcasted_iota(jnp.int32, (ROWS, ROWS), 1)
    allowed = there <= here
    for i in range(blocks):
        rows = slice(i * ROWS, (i + 1) * ROWS)

        @pl.when(i * ROWS < len_ref[0])
        def work():
            query = p_ref[0, rows, :] * jnp.asarray(1.0 / math.sqrt(HEAD), bf16)
            found = []
            for head in range(2):
                mine = first_head if head == 0 else jnp.logical_not(first_head)
                q = jnp.where(mine, query, jnp.zeros_like(query))
                diag = dot_nt(q, p_ref[1, rows, :])
                diag = jnp.where(allowed, diag, -1e30)
                largest = jnp.max(diag, axis=-1, keepdims=True)
                if i > 0:
                    before = dot_nt(q, p_ref[1, : i * ROWS, :])
                    largest = jnp.maximum(largest, jnp.max(before, axis=-1, keepdims=True))
                diag = jnp.exp(diag - largest)
                total = jnp.sum(diag, axis=-1, keepdims=True)
                out = dot_nn(diag.astype(bf16), p_ref[2, rows, :])
                if i > 0:
                    before = jnp.exp(before - largest)
                    total = total + jnp.sum(before, axis=-1, keepdims=True)
                    out = out + dot_nn(before.astype(bf16), p_ref[2, : i * ROWS, :])
                found.append(out * (1.0 / total))
                lse = jnp.broadcast_to(largest + jnp.log(total), (ROWS, 128))
                lse_ref[0, head : head + 1, rows] = lse.T[0:1]
            out_ref[rows, :] = jnp.where(first_head, found[0], found[1]).astype(bf16)


def attend(length, projected):
    rows = projected.shape[1]
    pairs = HEADS // 2
    return pl.pallas_call(
        attend_kernel,
        grid_spec=pltpu.PrefetchScalarGridSpec(
            num_scalar_prefetch=1,
            grid=(pairs,),
            in_specs=[pl.BlockSpec((3, rows, 128), lambda h, n: (0, 0, h))],
            out_specs=[
                pl.BlockSpec((rows, 128), lambda h, n: (0, h)),
                pl.BlockSpec((1, 8, rows), lambda h, n: (h, 0, 0)),
            ],
        ),
        out_shape=[
            jax.ShapeDtypeStruct((rows, D), bf16),
            jax.ShapeDtypeStruct((pairs, 8, rows), f32),
        ],
        compiler_params=params(),
        cost_estimate=pl.CostEstimate(
            flops=2 * rows * rows * D, bytes_accessed=rows * D * 8, transcendentals=HEADS * rows * rows // 2
        ),
        name="attend",
    )(length, projected)


def attend_back_kernel(len_ref, p_ref, o_ref, g_ref, lse_ref, out_ref, dk_ref, dv_ref, kz_ref, vz_ref, kt_ref):
    blocks = p_ref.shape[1] // ROWS
    scaling = 1.0 / math.sqrt(HEAD)
    lane = lax.broadcasted_iota(jnp.int32, (ROWS, 128), 1)
    first_head = lane < HEAD
    row8 = lax.broadcasted_iota(jnp.int32, (8, 128), 0)
    lane8 = lax.broadcasted_iota(jnp.int32, (8, 128), 1)
    chooser = (lax.div(lane8, HEAD) == row8).astype(f32)
    key_at = lax.broadcasted_iota(jnp.int32, (2, ROWS, ROWS), 1)
    row_at = lax.broadcasted_iota(jnp.int32, (2, ROWS, ROWS), 2)
    allowed = (key_at <= row_at).reshape(2 * ROWS, ROWS)
    for i in range(blocks):
        rows = slice(i * ROWS, (i + 1) * ROWS)
        two = slice(2 * i * ROWS, 2 * (i + 1) * ROWS)

        @pl.when(i * ROWS < len_ref[0])
        def work():
            dk_ref[two, :] = jnp.zeros((2 * ROWS, 128), f32)
            dv_ref[two, :] = jnp.zeros((2 * ROWS, 128), f32)
            key, value = p_ref[1, rows, :], p_ref[2, rows, :]
            zero = jnp.zeros_like(key)
            k2 = jnp.concatenate([jnp.where(first_head, key, zero), jnp.where(first_head, zero, key)], axis=0)
            kz_ref[two, :] = k2
            kt_ref[:, two] = k2.T
            vz_ref[two, :] = jnp.concatenate([jnp.where(first_head, value, zero), jnp.where(first_head, zero, value)], axis=0)
            query = p_ref[0, rows, :] * jnp.asarray(scaling, bf16)
            grad = g_ref[rows, :]
            product = grad.astype(f32) * o_ref[rows, :].astype(f32)
            delta = lax.dot_general(chooser, product, (((1,), (1,)), ((), ())), precision=lax.Precision.HIGHEST, preferred_element_type=f32)
            def both(a, b):
                return jnp.concatenate([jnp.broadcast_to(a, (ROWS, ROWS)), jnp.broadcast_to(b, (ROWS, ROWS))], axis=0)
            lse2 = both(lse_ref[0, 0:1, rows], lse_ref[0, 1:2, rows])
            delta2 = both(delta[0:1], delta[1:2])
            dqt = jnp.zeros((128, ROWS), f32)
            for j in range(i + 1):
                cols = slice(2 * j * ROWS, 2 * (j + 1) * ROWS)
                prob = jnp.exp(dot_nt(kz_ref[cols, :], query) - lse2)
                if i == j:
                    prob = jnp.where(allowed, prob, 0.0)
                ds = (prob * (dot_nt(vz_ref[cols, :], grad) - delta2)).astype(bf16)
                dv_ref[cols, :] += dot_nn(prob.astype(bf16), grad)
                dk_ref[cols, :] += dot_nn(ds, query)
                dqt = dqt + dot_nn(kt_ref[:, cols], ds)
            out_ref[0, rows, :] = (dqt * scaling).T.astype(bf16)
    for i in range(blocks):
        rows = slice(i * ROWS, (i + 1) * ROWS)
        a = slice(2 * i * ROWS, (2 * i + 1) * ROWS); b = slice((2 * i + 1) * ROWS, 2 * (i + 1) * ROWS)

        @pl.when(i * ROWS < len_ref[0])
        def finish():
            out_ref[1, rows, :] = jnp.where(first_head, dk_ref[a, :], dk_ref[b, :]).astype(bf16)
            out_ref[2, rows, :] = jnp.where(first_head, dv_ref[a, :], dv_ref[b, :]).astype(bf16)


def blank_kernel(ready_ref, out_ref):
    pass


def blank(ready, shape):
    return pl.pallas_call(
        blank_kernel,
        in_specs=[pl.BlockSpec(memory_space=pltpu.SMEM)],
        out_specs=pl.BlockSpec(memory_space=pl.ANY),
        out_shape=shape,
        name="blank",
    )(ready)


def attend_back(choice, projected, heads_out, grad_heads, lse, before):
    rows = projected.shape[1]
    pairs = HEADS // 2
    cols = lambda h, n: (0, n[2] + h)
    blocks = lambda h, n: (0, 0, n[2] + h)

    def kernel(n, p, o, g, l, unused, *rest):
        attend_back_kernel(n, p, o, g, l, *rest)

    return pl.pallas_call(
        kernel,
        grid_spec=pltpu.PrefetchScalarGridSpec(
            num_scalar_prefetch=1,
            grid=(pairs // 2,),
            in_specs=[
                pl.BlockSpec((3, rows, 128), blocks),
                pl.BlockSpec((rows, 128), cols),
                pl.BlockSpec((None, rows, 128), lambda h, n: (n[1], 0, n[2] + h)),
                pl.BlockSpec((1, 8, rows), lambda h, n: (n[2] + h, 0, 0)),
                pl.BlockSpec(memory_space=pl.ANY),
            ],
            out_specs=pl.BlockSpec((3, rows, 128), blocks),
            scratch_shapes=[
                pltpu.VMEM((2 * rows, 128), f32),
                pltpu.VMEM((2 * rows, 128), f32),
                pltpu.VMEM((2 * rows, 128), bf16),
                pltpu.VMEM((2 * rows, 128), bf16),
                pltpu.VMEM((128, 2 * rows), bf16),
            ],
        ),
        out_shape=jax.ShapeDtypeStruct((3, rows, D), bf16),
        input_output_aliases={5: 0},
        compiler_params=params(),
        cost_estimate=pl.CostEstimate(
            flops=3 * rows * rows * D, bytes_accessed=rows * D * 8, transcendentals=HEADS * rows * rows // 4
        ),
        name="attend_back",
    )(choice, projected, heads_out, grad_heads, lse, before)


def feed_kernel(plan, len_ref, row_ref, *refs):
    tok0, tok1, pass0, pass1, ho0, ho1, cot, table_ref, gain_ref = refs[:9]
    many = plan.sharers if plan.paired else 1
    grad_ref, pieces, refs = refs[9], refs[10 : 10 + many], refs[10 + many :]
    res, gh, hid, small_ref = refs[:4]
    outs, (w_ref, acc_ref, stage_ref, sem_ref) = refs[4:-4], refs[-4:]
    b = pl.program_id(0)
    many0 = last_block(len_ref[0]) + 1
    many1 = last_block(len_ref[1]) + 1
    early = b < many0

    @pl.when(b == 0)
    def clear():
        load_weight(plan, row_ref, pieces, w_ref, sem_ref.at[0])
        acc_ref[...] = jnp.zeros_like(acc_ref)
        small_ref[...] = jnp.zeros_like(small_ref)

    @pl.when(b < many0 + many1)
    def block():
        hot = onehot_rows(jnp.where(early, pass0[0], pass1[0]))
        entry = jnp.where(early, tok0[...], tok1[...]).astype(f32) + dot_tn(hot, table_ref[...])
        at = jnp.where(early, b, b - many0) * ROWS + lax.broadcasted_iota(jnp.int32, (ROWS, 1), 0)
        live = at < jnp.where(early, len_ref[0], len_ref[1])
        heads = jnp.where(early, ho0[...], ho1[...])
        attention = dot_nn(heads, w_ref[:, 0:D])
        hidden = entry + attention
        unit, scale = normalized(hidden)
        gain = gain_ref[...]
        normed = (unit * gain).astype(bf16)
        grad_feed = jnp.where(live, cot[...].reshape(ROWS, D).astype(f32), 0.0).astype(bf16)
        feed = jnp.zeros((ROWS, D), f32)
        grad_normed = jnp.zeros((ROWS, D), f32)
        for k in range(CHUNKS):
            up = slice(D + k * D, D + (k + 1) * D)
            down = slice(D + FF + k * D, D + FF + (k + 1) * D)
            x = dot_nn(normed, w_ref[:, up])
            grad_act = dot_nt(grad_feed, w_ref[:, down])
            c0 = math.sqrt(2.0 / math.pi)
            square = x * x
            bent = jnp.tanh(x * (c0 + (c0 * 0.044715) * square))
            half = 0.5 + 0.5 * bent
            slope = half + (0.5 * x) * (1.0 - bent * bent) * (c0 + (3.0 * c0 * 0.044715) * square)
            act = (x * half).astype(bf16)
            grad_x = (slope * grad_act).astype(bf16)
            feed = feed + dot_nn(act, w_ref[:, down])
            grad_normed = grad_normed + dot_nt(grad_x, w_ref[:, up])
            acc_ref[:, up] += dot_tn(normed, grad_x)
            acc_ref[:, down] += dot_tn(act, grad_feed)
        res[...] = jnp.where(live, hidden + feed, 0.0).astype(bf16).reshape(res.shape)
        small_ref[0:8] += fold_rows(grad_normed * unit)
        small_ref[8:16] += fold_rows(jnp.where(live, entry * entry, 0.0))
        small_ref[16:24] += fold_rows(jnp.where(live, attention * attention, 0.0))
        small_ref[24:32] += fold_rows(jnp.where(live, feed * feed, 0.0))
        grad_hidden = grad_feed.astype(f32) + norm_back(grad_normed * gain, unit, scale)
        hid[...] = grad_hidden
        grad_attention = grad_hidden.astype(bf16)
        acc_ref[:, 0:D] += dot_tn(heads, grad_attention)
        gh[...] = dot_nt(grad_attention, w_ref[:, 0:D]).astype(bf16)

    @pl.when(b == pl.num_programs(0) - 1)
    def finish():
        store_grads(plan, plan.wide_orders, grad_ref, acc_ref, outs, stage_ref, sem_ref)


def feed(plan, part, lengths, piece_rows, grad_rows, tokens, pass_rows, heads_out, cotangent, table, gain, pieces, width):
    rows = tokens[0].shape[0]
    per = ROWS // part

    def at0(b, n, r):
        return jnp.minimum(b, last_block(n[0])), 0

    def at1(b, n, r):
        return jnp.clip(b - last_block(n[0]) - 1, 0, last_block(n[1])), 0

    def both(b, n, r):
        early = b <= last_block(n[0])
        return jnp.where(early, b, at1(b, n, r)[0]), jnp.where(early, 0, 1)

    row0 = pl.BlockSpec((ROWS, D), at0)
    row1 = pl.BlockSpec((ROWS, D), at1)
    pas0 = pl.BlockSpec((1, 1, ROWS), lambda *a: at0(*a) + (0,))
    pas1 = pl.BlockSpec((1, 1, ROWS), lambda *a: at1(*a) + (0,))
    dealt = pl.BlockSpec((per, 1, part, D), lambda *a: both(*a) + (0, 0))
    local = pl.BlockSpec((None, ROWS, D), lambda *a: both(*a)[::-1] + (0,))
    grads = grad_shapes(plan, width, plan.wide_orders)
    anywhere = pl.BlockSpec(memory_space=pl.ANY)
    return pl.pallas_call(
        functools.partial(feed_kernel, plan),
        grid_spec=pltpu.PrefetchScalarGridSpec(
            num_scalar_prefetch=2,
            grid=(2 * rows // ROWS,),
            in_specs=[
                row0, row1, pas0, pas1, row0, row1, dealt,
                pl.BlockSpec((8, D), lambda *a: (0, 0)),
                pl.BlockSpec((1, D), lambda *a: (0, 0)),
                pl.BlockSpec(memory_space=pltpu.SMEM),
            ]
            + [anywhere] * len(pieces),
            out_specs=[dealt, local, local, pl.BlockSpec((32, D), lambda *a: (0, 0))] + [anywhere] * len(grads),
            scratch_shapes=[
                pltpu.VMEM((D, width), bf16),
                pltpu.VMEM((D, width), f32),
                pltpu.VMEM(stage_shape(plan), bf16),
                pltpu.SemaphoreType.DMA((2,)),
            ],
        ),
        out_shape=[
            jax.ShapeDtypeStruct(cotangent.shape, bf16),
            jax.ShapeDtypeStruct((2, rows, D), bf16),
            jax.ShapeDtypeStruct((2, rows, D), f32),
            jax.ShapeDtypeStruct((32, D), f32),
        ]
        + grads,
        compiler_params=params(),
        cost_estimate=pl.CostEstimate(
            flops=2 * 6 * rows * D * width, bytes_accessed=2 * rows * D * 14 + D * width * 4, transcendentals=2 * rows * FF
        ),
        name="feed",
    )(lengths, piece_rows, tokens[0], tokens[1], pass_rows[0], pass_rows[1], heads_out[0], heads_out[1],
      cotangent, table, gain, grad_rows, *pieces)


def project_back_kernel(plan, weight, rows_back, final, len_ref, row_ref, grad_ref, tok_ref, pass_ref, g_ref, *rest):
    rest = list(rest)
    hid_ref = rest.pop(0) if rows_back else None
    table_ref, gain_ref = rest.pop(0), rest.pop(0)
    before_ref = rest.pop(0) if final else None
    many = plan.sharers if plan.paired else 1
    pieces = [rest.pop(0) for n in range(many)] if rows_back else []
    if rows_back:
        out_ref, small_ref = rest.pop(0), rest.pop(0)
    if weight and not final:
        acc_ref = rest.pop(0)
    outs = [rest.pop(0) for shape in grad_shapes(plan, 3 * D, plan.head_orders)] if final else []
    if rows_back:
        w_ref = rest.pop(0)
    if final:
        acc_ref, stage_ref = rest.pop(0), rest.pop(0)
    sem_ref = rest.pop(0)
    b = pl.program_id(0)

    @pl.when(b == 0)
    def clear():
        if rows_back:
            load_weight(plan, row_ref, pieces, w_ref, sem_ref.at[0])
            small_ref[...] = jnp.zeros_like(small_ref)
        if weight:
            acc_ref[...] = before_ref[...] if final else jnp.zeros_like(acc_ref)

    @pl.when(b <= last_block(len_ref[0]))
    def work():
        hot = onehot_rows(pass_ref[0])
        entry = tok_ref[...].astype(f32) + dot_tn(hot, table_ref[...])
        unit, scale = normalized(entry)
        gain = gain_ref[...]
        if weight:
            normed = (unit * gain).astype(bf16)
            for part in range(3):
                acc_ref[:, part * D : (part + 1) * D] += dot_tn(normed, g_ref[part])
        if rows_back:
            grad_normed = jnp.zeros((ROWS, D), f32)
            for part in range(3):
                grad_normed = grad_normed + dot_nt(g_ref[part], w_ref[:, part * D : (part + 1) * D])
            small_ref[0:8] += fold_rows(grad_normed * unit)
            grad_entry = hid_ref[...] + norm_back(grad_normed * gain, unit, scale)
            high = grad_entry.astype(bf16)
            out_ref[...] = high
            rest_one = grad_entry - high.astype(f32)
            low = rest_one.astype(bf16)
            lower = (rest_one - low.astype(f32)).astype(bf16)
            small_ref[8:16] += dot_nn(hot, high) + dot_nn(hot, low) + dot_nn(hot, lower)

    if final:
        @pl.when(b == pl.num_programs(0) - 1)
        def finish():
            store_grads(plan, plan.head_orders, grad_ref, acc_ref, outs, stage_ref, sem_ref)


def project_back(
    plan, weight, rows_back, which, length, piece_rows, grad_rows, tokens, pass_rows, grads, grad_hidden, table, gain,
    pieces, before=None,
):
    rows = tokens.shape[0]
    final = before is not None
    at = lambda b, n, r, g: (jnp.minimum(b, last_block(n[0])), 0)
    row = pl.BlockSpec((ROWS, D), at)
    anywhere = pl.BlockSpec(memory_space=pl.ANY)
    in_specs = [
        row,
        pl.BlockSpec((1, 1, ROWS), lambda *a: at(*a) + (0,)),
        pl.BlockSpec((3, ROWS, D), lambda *a: (0,) + at(*a)),
    ]
    operands = [length, piece_rows, grad_rows, tokens, pass_rows, grads]
    if rows_back:
        in_specs.append(pl.BlockSpec((None, ROWS, D), lambda *a: (which,) + at(*a)))
        operands.append(grad_hidden)
    in_specs += [pl.BlockSpec((8, D), lambda *a: (0, 0)), pl.BlockSpec((1, D), lambda *a: (0, 0))]
    operands += [table, gain]
    out_shape, out_specs, scratch = [], [], []
    if final:
        in_specs.append(pl.BlockSpec((D, 3 * D), lambda *a: (0, 0), pipeline_mode=pl.Buffered(1)))
        operands.append(before)
    if rows_back:
        in_specs += [anywhere] * len(pieces)
        operands += pieces
        out_shape += [jax.ShapeDtypeStruct((rows, D), bf16), jax.ShapeDtypeStruct((16, D), f32)]
        out_specs += [row, pl.BlockSpec((16, D), lambda *a: (0, 0))]
        scratch.append(pltpu.VMEM((D, 3 * D), bf16))
    if weight and not final:
        out_shape.append(jax.ShapeDtypeStruct((D, 3 * D), f32))
        out_specs.append(pl.BlockSpec((D, 3 * D), lambda *a: (0, 0)))
    if final:
        shapes = grad_shapes(plan, 3 * D, plan.head_orders)
        out_shape += shapes
        out_specs += [anywhere] * len(shapes)
        scratch += [pltpu.VMEM((D, 3 * D), f32), pltpu.VMEM(stage_shape(plan), bf16)]
    return pl.pallas_call(
        functools.partial(project_back_kernel, plan, weight, rows_back, final),
        grid_spec=pltpu.PrefetchScalarGridSpec(
            num_scalar_prefetch=3,
            grid=(rows // ROWS,),
            in_specs=in_specs,
            out_specs=out_specs,
            scratch_shapes=scratch + [pltpu.SemaphoreType.DMA((2,))],
        ),
        out_shape=out_shape,
        compiler_params=params(),
        cost_estimate=pl.CostEstimate(
            flops=2 * (weight + rows_back) * rows * D * 3 * D, bytes_accessed=rows * D * 14 + D * D * 6, transcendentals=0
        ),
        name="project_back",
    )(*operands)


def pick_kernel(index_ref, in_ref, out_ref, sem_ref):
    copies = [
        pltpu.make_async_copy(in_ref.at[index_ref[n]], out_ref.at[n], sem_ref) for n in range(out_ref.shape[0])
    ]
    for copy in copies:
        copy.start()
    for copy in copies:
        copy.wait()


def pick(index, blocks):
    shape = index.shape + blocks.shape[1:]
    return pl.pallas_call(
        pick_kernel,
        grid_spec=pltpu.PrefetchScalarGridSpec(
            num_scalar_prefetch=1,
            grid=(1,),
            in_specs=[pl.BlockSpec(memory_space=pl.ANY)],
            out_specs=pl.BlockSpec(shape, lambda b, n: (0, 0, 0)),
            scratch_shapes=[pltpu.SemaphoreType.DMA],
        ),
        out_shape=jax.ShapeDtypeStruct(shape, blocks.dtype),
        compiler_params=params(),
        cost_estimate=pl.CostEstimate(flops=0, bytes_accessed=4 * math.prod(shape), transcendentals=0),
        name="pick",
    )(index, blocks)


def settle_kernel(index_ref, *refs):
    arrays, out_ref = refs[:-1], refs[-1]
    first = pl.program_id(0) * out_ref.shape[0]
    rows = out_ref.shape[1]
    at = lax.broadcasted_iota(jnp.int32, (rows, 1), 0)
    for n in range(out_ref.shape[0]):
        live = at < index_ref[2, first + n]
        source, late = index_ref[1, first + n], index_ref[0, first + n]
        if len(arrays) == 1:
            found = arrays[0][2 * source + late]
        else:
            found = jnp.where(late == 0, arrays[0][source], arrays[1][source])
        out_ref[n] = jnp.where(live, found.astype(f32), 0.0)


def settle(index, *arrays):
    many = index.shape[1]
    step = 4
    shape = arrays[0].shape
    whole = pl.BlockSpec(shape, lambda b, n: (0, 0, 0), pipeline_mode=pl.Buffered(1))
    return pl.pallas_call(
        settle_kernel,
        grid_spec=pltpu.PrefetchScalarGridSpec(
            num_scalar_prefetch=1,
            grid=(many // step,),
            in_specs=[whole] * len(arrays),
            out_specs=pl.BlockSpec((step,) + shape[1:], lambda b, n: (b, 0, 0)),
        ),
        out_shape=jax.ShapeDtypeStruct((many,) + shape[1:], f32),
        compiler_params=params(),
        cost_estimate=pl.CostEstimate(flops=0, bytes_accessed=6 * many * math.prod(shape[1:]), transcendentals=0),
        name="settle",
    )(index, *arrays)


def after(values, *others):
    return lax.optimization_barrier((values, others))[0]


def swap(blocks):
    return lax.all_to_all(blocks, "dp", split_axis=0, concat_axis=0, tiled=True)


def per_device(
    groups,
    width_all,
    tokens,
    passes,
    lengths,
    dealing,
    pass_table,
    gain_first,
    to_heads,
    from_heads,
    gain_second,
    expand,
    shrink,
    cotangent,
):
    axes = ("dp", "fsdp")
    slots, part, unused_width = tokens.shape
    seq_len = part * groups
    order = jnp.arange(slots, dtype=jnp.int32)
    here = lax.axis_index("dp")
    ordering = dealing[0, 0]
    sizes = lengths[0]

    ahead = (sizes[None, :] > sizes[:, None]) | (
        (sizes[None, :] == sizes[:, None]) & (order[None, :] < order[:, None])
    )
    rank = jnp.sum(ahead.astype(jnp.int32), axis=1)
    ranked = jnp.sum(jnp.where(rank[None, :] == order[:, None], order[None, :], 0), axis=1)
    place = jnp.sum(jnp.where(ordering[None, :] == order[:, None], order[None, :], 0), axis=1)
    early_seqs = ranked[:groups]
    late_seqs = ranked[groups:][::-1]
    from_early = jnp.sum(jnp.where(early_seqs[:, None] == order[None, :], place[None, :], 0), axis=1)
    from_late = jnp.sum(jnp.where(late_seqs[:, None] == order[None, :], place[None, :], 0), axis=1)
    slot_rank = jnp.sum(jnp.where(ordering[:, None] == order[None, :], rank[None, :], 0), axis=1)
    slot_size = jnp.sum(jnp.where(ordering[:, None] == order[None, :], sizes[None, :], 0), axis=1)
    is_late = (slot_rank >= groups).astype(jnp.int32)
    source = jnp.where(is_late == 1, slots - 1 - slot_rank, slot_rank)
    back_index = jnp.stack([is_late, source, slot_size - here * part])
    my_seqs = jnp.stack([early_seqs[here], late_seqs[here]])
    my_sizes = jnp.sum(jnp.where(my_seqs[:, None] == order[None, :], sizes[None, :], 0), axis=1)

    row_count = to_heads.shape[0]
    narrow = jnp.concatenate(
        [
            from_heads,
            expand.reshape(row_count, D, CHUNKS).transpose(0, 2, 1).reshape(row_count, FF),
            shrink.reshape(row_count, CHUNKS * D),
        ],
        axis=1,
    )
    plan = Plan(groups, width_all // groups, row_count)
    index_here = here * (width_all // groups) + lax.axis_index("fsdp")
    my_passes = [passes[my_seqs[m]].reshape(seq_len // ROWS, 1, ROWS) for m in range(2)]
    one_size = [my_sizes[m : m + 1] for m in range(2)]
    table = jnp.zeros((8, D), bf16).at[:PASSES].set(pass_table)
    gain_one = gain_first.astype(f32).reshape(1, D)
    gain_two = gain_second.astype(f32).reshape(1, D)

    pairs_index = jnp.stack([from_early, from_late], axis=1).reshape(slots)
    picked = [pick(from_early, tokens), pick(from_late, tokens), pick(pairs_index, cotangent)]
    if plan.paired:
        piece_rows = plan.piece_rows(index_here)
        wide_rows = plan.grad_rows(index_here, plan.wide_orders)
        head_rows = plan.grad_rows(index_here, plan.head_orders)
        head_far = plan.gather(to_heads[None], plan.far)
        tokens0 = swap(after(picked[0], head_far, my_passes, one_size, piece_rows, table, gain_one, narrow))
        head_near = plan.gather(head_far, [plan.near])
        head_x = plan.gather_x(head_near)
        head_pieces = plan.gather_core(head_x)
        wide_one = plan.gather(after(narrow, head_near)[None], plan.far[:1])
        tokens1 = swap(after(picked[1], tokens0, picked[2], wide_one, head_x))
        wide_far = plan.gather(wide_one, plan.far[1:])
    else:
        piece_rows = wide_rows = head_rows = jnp.zeros((1,), jnp.int32)
        head_pieces = (lax.all_gather(to_heads, axes, axis=0, tiled=True),)
        wide_pieces = (lax.all_gather(narrow, axes, axis=0, tiled=True),)
        tokens0 = swap(picked[0])
        tokens1 = swap(after(picked[1], tokens0))

    def forward(m, *gate):
        return project(
            plan, after(one_size[m], gate), piece_rows, my_tokens[m], my_passes[m], table, gain_one, head_pieces
        )

    def mix(m, *gate):
        return attend(after(one_size[m], gate), projected[m])

    def mix_back(m, first, before, *gate):
        choice = jnp.stack([my_sizes[m], jnp.int32(m), jnp.int32(first)])
        return attend_back(after(choice, gate), projected[m], heads_out[m], grad_heads, lse[m], before)

    def back(m, weight, rows_back, *gate, before=None):
        return project_back(
            plan, weight, rows_back, m, after(one_size[m], gate), piece_rows, head_rows, my_tokens[m], my_passes[m],
            grad_parts[m], grad_hidden, table, gain_one, head_pieces, before,
        )

    def send_back(rows, *gate):
        return swap(after(rows, gate).reshape(groups, part, D))

    projected, heads_out, lse, grad_parts = [None, None], [None, None], [None, None], [None, None]
    my_tokens = [tokens0.reshape(seq_len, D), tokens1.reshape(seq_len, D)]
    projected[0] = forward(0)
    my_grads = swap(after(picked[2].reshape(groups, 2, part, D), tokens1, projected[0]))
    heads_out[0], lse[0] = mix(0)
    if plan.paired:
        wide_near = plan.gather(wide_far, [plan.near])
    projected[1] = forward(1, lse[0])
    if plan.paired:
        wide_x = plan.gather_x(wide_near)
    heads_out[1], lse[1] = mix(1)
    if plan.paired:
        wide_pieces = plan.gather_core(wide_x, lse[1])

    res, grad_heads, grad_hidden, feed_small, *wide_grads = feed(
        plan, part, my_sizes, piece_rows, wide_rows, my_tokens, my_passes, heads_out, my_grads, table, gain_two,
        wide_pieces, D + 2 * FF,
    )

    def begin(grads):
        if not plan.paired:
            return lax.psum_scatter(grads[0], axes, scatter_dimension=0, tiled=True).astype(f32)
        return [grads[n : n + 2] for n in range(0, len(grads), 2)]

    def advance(state, stage, gate, late):
        return plan.reduce_stage(state, plan.wide_orders, stage, (gate,), (late,)) if plan.paired else state

    half = HEADS // 4
    space = jax.ShapeDtypeStruct((3, seq_len, D), bf16)
    wide0 = begin(wide_grads)
    result = swap(res)
    some = mix_back(0, 0, blank(one_size[0], space))
    wide1 = advance(wide0, 0, (), some)
    grad_parts[0] = mix_back(0, half, some, wide1)
    entry0, small0, head_sum = back(0, True, True)
    wide2 = advance(wide1, 1, some, entry0)
    moved0 = send_back(entry0, result)
    some = mix_back(1, 0, blank(one_size[1], space), entry0, wide2, result)
    wide3 = advance(wide2, 2, entry0, some)
    grad_parts[1] = mix_back(1, half, some, wide3)
    entry1, small1 = back(1, False, True)
    wide_owned = advance(wide3, 3, some, entry1)
    moved1 = send_back(entry1, moved0)
    head_grads = back(1, True, False, entry1, moved0, before=head_sum)
    head_state = begin(head_grads)
    squares = jnp.sum(feed_small[8:].reshape(3, 8 * D), axis=1)
    counted = jnp.sum(my_sizes).astype(f32)
    last_row = jnp.zeros((1, D), f32).at[0, :3].set(squares).at[0, 3].set(counted)
    small = small0 + small1
    totals = jnp.concatenate(
        [
            small[8 : 8 + PASSES],
            jnp.sum(small[:8], axis=0, keepdims=True),
            jnp.sum(feed_small[:8], axis=0, keepdims=True),
            last_row,
        ],
        axis=0,
    )
    if plan.paired:
        stages = plan.head_orders[0]
        for n in range(len(stages)):
            for bits in stages[n]:
                totals = totals + plan.exchange(after(totals, head_state), bits)
            head_state = plan.reduce_stage(
                head_state, plan.head_orders, n, (wide_owned,) if n == 0 else (), (moved1,) if n == 1 else ()
            )
        wide_owned, head_owned = jnp.concatenate(wide_owned, axis=1), head_state[0]
    else:
        totals = lax.psum(totals, axes)
        head_owned = head_state
    root_squares = jnp.sqrt(totals[7, :3] / (totals[7, 3] * D))

    grad_expand = wide_owned[:, D : D + FF].reshape(row_count, CHUNKS, D).transpose(0, 2, 1)
    return (
        settle(back_index, result.reshape(slots, part, D)),
        settle(back_index, moved0, moved1),
        totals[:PASSES],
        totals[PASSES],
        head_owned,
        wide_owned[:, :D],
        totals[PASSES + 1],
        grad_expand.reshape(row_count, FF),
        wide_owned[:, D + FF :].reshape(row_count * CHUNKS, D),
        root_squares,
    )


def solution(mesh):
    groups = mesh.shape["dp"]
    weight_spec = P(("dp", "fsdp"), None)
    block_spec = P("fsdp", "dp", None)
    in_specs = (
        block_spec,
        P("fsdp", None),
        P("fsdp", None),
        P("dp", "fsdp", None),
        P(),
        P(),
        weight_spec,
        weight_spec,
        P(),
        weight_spec,
        weight_spec,
        block_spec,
    )
    out_specs = (
        block_spec,
        block_spec,
        P(),
        P(),
        weight_spec,
        weight_spec,
        P(),
        weight_spec,
        weight_spec,
        P(),
    )
    body = functools.partial(per_device, groups, groups * mesh.shape["fsdp"])
    return jax.shard_map(body, mesh=mesh, in_specs=in_specs, out_specs=out_specs, check_vma=False)
```

```python
import math
import functools

import jax
import jax.numpy as jnp
from jax import lax
from jax.experimental import pallas as pl
from jax.experimental.pallas import tpu as pltpu
from jax.sharding import PartitionSpec as P

D = 768
HEADS = 12
HEAD = 64
FF = 3072
PASSES = 5
EPS = 1e-05
ROWS = 256
CHUNKS = FF // D
VMEM_MOST = 64000 * 1024

f32 = jnp.float32
bf16 = jnp.bfloat16


def dot_nn(a, b):
    return lax.dot_general(a, b, (((1,), (0,)), ((), ())), preferred_element_type=f32)


def dot_nt(a, b):
    return lax.dot_general(a, b, (((1,), (1,)), ((), ())), preferred_element_type=f32)


def dot_tn(a, b):
    return lax.dot_general(a, b, (((0,), (0,)), ((), ())), preferred_element_type=f32)


def params(**more):
    return pltpu.CompilerParams(vmem_limit_bytes=VMEM_MOST, **more)


def normalized(values):
    centred = values - jnp.mean(values, axis=-1, keepdims=True)
    spread = jnp.mean(centred * centred, axis=-1, keepdims=True)
    scale = lax.rsqrt(spread + EPS)
    return centred * scale, scale


def norm_back(grad_unit, unit, scale):
    first = jnp.mean(grad_unit, axis=-1, keepdims=True)
    second = jnp.mean(grad_unit * unit, axis=-1, keepdims=True)
    return scale * (grad_unit - first - unit * second)


def onehot_rows(pass_row):
    ids = lax.broadcasted_iota(jnp.int32, (8, pass_row.shape[-1]), 0)
    return (ids == pass_row).astype(f32).astype(bf16)


def fold_rows(values):
    rows, width = values.shape
    return jnp.sum(values.reshape(rows // 8, 8, width), axis=0)


def last_block(length):
    return lax.div(length + (ROWS - 1), ROWS) - 1


def bits_of(count):
    return count.bit_length() - 1


class Plan:
    def __init__(self, groups, sharers, rows):
        self.groups, self.sharers, self.rows = groups, sharers, rows
        self.count = groups * sharers
        self.paired = rows % 8 == 0 and self.count & (self.count - 1) == 0 and sharers >= 4 and groups >= 4
        core, *over_x = [1 << bit for bit in range(bits_of(sharers))]
        near, *far = [sharers << bit for bit in range(bits_of(groups))]
        self.core, self.over_x, self.near, self.far = core, over_x, near, far[::-1]
        self.wide_orders = ([[core], over_x, [near], far], [[core], [near], over_x, far])
        self.head_orders = ([[core], over_x + [near], far],)

    def exchange(self, values, bits):
        pairs = [(i, i ^ bits) for i in range(self.count)]
        return lax.ppermute(values, ("dp", "fsdp"), pairs)

    def gather(self, held, masks):
        for bits in masks:
            held = jnp.concatenate([held, self.exchange(held, bits)], axis=0)
        return held

    def gather_x(self, held, *gate):
        pieces = {0: held}
        for bits in self.over_x[::-1]:
            for name in list(pieces):
                pieces[name | bits] = self.exchange(after(pieces[name], gate), bits)
        return pieces

    def gather_near(self, pieces, gate=(), late=()):
        return {
            name: jnp.concatenate([after(held, late), self.exchange(after(held, gate), self.near)], axis=0)
            for name, held in pieces.items()
        }

    def gather_core(self, pieces, *gate):
        found = dict(pieces)
        for name in pieces:
            found[name | self.core] = self.exchange(after(pieces[name], gate), self.core)
        return tuple(found[name] for name in range(self.sharers))

    def piece_rows(self, here):
        masks = self.far + [self.near]
        found = []
        for f in range(self.sharers):
            for n in range(self.groups):
                rel = f | ways_bits(masks, n)
                found.append((here ^ rel) * self.rows)
        return jnp.stack(found).astype(jnp.int32)

    def grad_rows(self, here, orders):
        found = []
        for order in orders:
            for place in range(self.count):
                rel, left = 0, self.count
                for masks in order:
                    left >>= len(masks)
                    rel |= ways_bits(masks, (place // left) % (1 << len(masks)))
                found.append((here ^ rel) * self.rows)
        return jnp.stack(found).astype(jnp.int32)

    def reduce_stage(self, states, orders, stage, gate=(), late=()):
        sums = []
        for ways, order in zip(states, orders):
            sums.append(
                [after(ways[0], late)]
                + [
                    self.exchange(after(ways[n], gate), ways_bits(order[stage], n))
                    for n in range(1, len(ways))
                ]
            )
        if stage == len(orders[0]) - 1:
            return [sum(part.astype(f32) for part in parts)[0] for parts in sums]
        return [merge(parts, 1 << len(order[stage + 1])) for parts, order in zip(sums, orders)]


def ways_bits(masks, way):
    return sum(bits for n, bits in enumerate(masks) if (way >> n) & 1)


def merge_kernel(many, ways, *refs):
    ins, outs = refs[: many * ways], refs[many * ways :]
    for way in range(ways):
        total = ins[way][...].astype(f32)
        for n in range(1, many):
            total = total + ins[n * ways + way][...].astype(f32)
        outs[way][...] = total.astype(bf16)


def merge(parts, ways):
    blocks, rows, width = parts[0].shape
    share = blocks // ways
    steps = min(share, 4)
    shape = (share // steps, rows, width)

    def view(way):
        return pl.BlockSpec(shape, lambda b: (b + way * steps, 0, 0))

    out = jax.ShapeDtypeStruct((share, rows, width), bf16)
    return pl.pallas_call(
        functools.partial(merge_kernel, len(parts), ways),
        grid=(steps,),
        in_specs=[view(way) for part in parts for way in range(ways)],
        out_specs=[pl.BlockSpec(shape, lambda b: (b, 0, 0))] * ways,
        out_shape=[out] * ways,
        compiler_params=params(),
        cost_estimate=pl.CostEstimate(
            flops=len(parts) * parts[0].size, bytes_accessed=(2 + 2 * len(parts)) * parts[0].size, transcendentals=0
        ),
        name="merge",
    )(*[part for part in parts for way in range(ways)])


def load_weight(plan, rows_ref, pieces, weight_ref, sem_ref):
    copies = []
    if not plan.paired:
        copies.append(pltpu.make_async_copy(pieces[0], weight_ref, sem_ref))
    first = 0
    for k in range(0, len(pieces) if plan.paired else 0, plan.sharers):
        width = pieces[k].shape[-1]
        for f in range(plan.sharers):
            for n in range(plan.groups):
                at = pl.multiple_of(rows_ref[f * plan.groups + n], 8)
                target = weight_ref.at[pl.ds(at, plan.rows), first : first + width]
                copies.append(pltpu.make_async_copy(pieces[k + f].at[n], target, sem_ref))
        first += width
    for copy in copies:
        copy.start()
    for copy in copies:
        copy.wait()


def grad_shapes(plan, width, orders):
    if not plan.paired:
        return [jax.ShapeDtypeStruct((D, width), bf16)]
    half = plan.count // 2
    cut = first_part(width, orders)
    return [jax.ShapeDtypeStruct((half, plan.rows, w), bf16) for w in (cut, cut, width - cut, width - cut) if w > 0]


def first_part(width, orders):
    return (width // D + 1) // 2 * D if len(orders) == 2 else width


def stage_shape(plan):
    return (2, plan.count, plan.rows, D) if plan.paired else (2, D, D)


def store_grads(plan, orders, rows_ref, acc_ref, outs, stage_ref, sem_ref):
    width, step = acc_ref.shape[1], D
    cut = first_part(width, orders)
    half = plan.count // 2
    waiting = []
    for n in range(width // step):
        slot = n % 2
        cols = slice(n * step, (n + 1) * step)
        if len(waiting) == 2:
            for copy in waiting.pop(0):
                copy.wait()
        if not plan.paired:
            stage_ref[slot] = acc_ref[:, cols].astype(bf16)
            copies = [pltpu.make_async_copy(stage_ref.at[slot], outs[0].at[:, cols], sem_ref.at[slot])]
        else:
            late = n * step >= cut
            base = plan.count if late else 0
            start = n * step - (cut if late else 0)

            def fill(place, carry):
                at = pl.multiple_of(rows_ref[base + place], 8)
                stage_ref[slot, place] = acc_ref[pl.ds(at, plan.rows), cols].astype(bf16)
                return carry

            lax.fori_loop(0, plan.count, fill, 0, unroll=2)
            keep, send = outs[2:4] if late else outs[0:2]
            there = slice(start, start + step)
            copies = [
                pltpu.make_async_copy(stage_ref.at[slot, 0:half], keep.at[:, :, there], sem_ref.at[slot]),
                pltpu.make_async_copy(stage_ref.at[slot, half:], send.at[:, :, there], sem_ref.at[slot]),
            ]
        for copy in copies:
            copy.start()
        waiting.append(copies)
    for copies in waiting:
        for copy in copies:
            copy.wait()


def project_kernel(plan, len_ref, row_ref, tok_ref, pass_ref, table_ref, gain_ref, *rest):
    pieces, (out_ref, w_ref, sem_ref) = rest[:-3], rest[-3:]

    @pl.when(pl.program_id(0) == 0)
    def load():
        load_weight(plan, row_ref, pieces, w_ref, sem_ref)

    @pl.when(pl.program_id(0) <= last_block(len_ref[0]))
    def work():
        hot = onehot_rows(pass_ref[0])
        entry = tok_ref[...].astype(f32) + dot_tn(hot, table_ref[...])
        unit, unused = normalized(entry)
        normed = (unit * gain_ref[...]).astype(bf16)
        for part in range(3):
            out_ref[part] = dot_nn(normed, w_ref[:, part * D : (part + 1) * D]).astype(bf16)


def project(plan, length, piece_rows, tokens, pass_rows, table, gain, pieces):
    rows = tokens.shape[0]
    at = lambda b, n, r: (jnp.minimum(b, last_block(n[0])), 0)
    return pl.pallas_call(
        functools.partial(project_kernel, plan),
        grid_spec=pltpu.PrefetchScalarGridSpec(
            num_scalar_prefetch=2,
            grid=(rows // ROWS,),
            in_specs=[
                pl.BlockSpec((ROWS, D), at),
                pl.BlockSpec((1, 1, ROWS), lambda b, n, r: at(b, n, r) + (0,)),
                pl.BlockSpec((8, D), lambda b, n, r: (0, 0)),
                pl.BlockSpec((1, D), lambda b, n, r: (0, 0)),
            ]
            + [pl.BlockSpec(memory_space=pl.ANY)] * len(pieces),
            out_specs=pl.BlockSpec((3, ROWS, D), lambda b, n, r: (0,) + at(b, n, r)),
            scratch_shapes=[pltpu.VMEM((D, 3 * D), bf16), pltpu.SemaphoreType.DMA],
        ),
        out_shape=jax.ShapeDtypeStruct((3, rows, D), bf16),
        compiler_params=params(),
        cost_estimate=pl.CostEstimate(
            flops=2 * rows * D * 3 * D, bytes_accessed=rows * D * 8 + D * D * 6, transcendentals=0
        ),
        name="project",
    )(length, piece_rows, tokens, pass_rows, table, gain, *pieces)


def attend_kernel(len_ref, p_ref, out_ref, lse_ref):
    blocks = p_ref.shape[1] // ROWS
    lane = lax.broadcasted_iota(jnp.int32, (ROWS, 128), 1)
    first_head = lane < HEAD
    here = lax.broadcasted_iota(jnp.int32, (ROWS, ROWS), 0)
    there = lax.broadcasted_iota(jnp.int32, (ROWS, ROWS), 1)
    allowed = there <= here
    for i in range(blocks):
        rows = slice(i * ROWS, (i + 1) * ROWS)

        @pl.when(i * ROWS < len_ref[0])
        def work():
            query = p_ref[0, rows, :] * jnp.asarray(1.0 / math.sqrt(HEAD), bf16)
            found = []
            for head in range(2):
                mine = first_head if head == 0 else jnp.logical_not(first_head)
                q = jnp.where(mine, query, jnp.zeros_like(query))
                diag = dot_nt(q, p_ref[1, rows, :])
                diag = jnp.where(allowed, diag, -1e30)
                largest = jnp.max(diag, axis=-1, keepdims=True)
                if i > 0:
                    before = dot_nt(q, p_ref[1, : i * ROWS, :])
                    largest = jnp.maximum(largest, jnp.max(before, axis=-1, keepdims=True))
                diag = jnp.exp(diag - largest)
                total = jnp.sum(diag, axis=-1, keepdims=True)
                out = dot_nn(diag.astype(bf16), p_ref[2, rows, :])
                if i > 0:
                    before = jnp.exp(before - largest)
                    total = total + jnp.sum(before, axis=-1, keepdims=True)
                    out = out + dot_nn(before.astype(bf16), p_ref[2, : i * ROWS, :])
                found.append(out * (1.0 / total))
                lse = jnp.broadcast_to(largest + jnp.log(total), (ROWS, 128))
                lse_ref[0, head : head + 1, rows] = lse.T[0:1]
            out_ref[rows, :] = jnp.where(first_head, found[0], found[1]).astype(bf16)


def attend(length, projected):
    rows = projected.shape[1]
    pairs = HEADS // 2
    return pl.pallas_call(
        attend_kernel,
        grid_spec=pltpu.PrefetchScalarGridSpec(
            num_scalar_prefetch=1,
            grid=(pairs,),
            in_specs=[pl.BlockSpec((3, rows, 128), lambda h, n: (0, 0, h))],
            out_specs=[
                pl.BlockSpec((rows, 128), lambda h, n: (0, h)),
                pl.BlockSpec((1, 8, rows), lambda h, n: (h, 0, 0)),
            ],
        ),
        out_shape=[
            jax.ShapeDtypeStruct((rows, D), bf16),
            jax.ShapeDtypeStruct((pairs, 8, rows), f32),
        ],
        compiler_params=params(),
        cost_estimate=pl.CostEstimate(
            flops=2 * rows * rows * D, bytes_accessed=rows * D * 8, transcendentals=HEADS * rows * rows // 2
        ),
        name="attend",
    )(length, projected)


def attend_back_kernel(len_ref, p_ref, o_ref, g_ref, lse_ref, out_ref, dk_ref, dv_ref, kz_ref, vz_ref, kt_ref):
    blocks = p_ref.shape[1] // ROWS
    scaling = 1.0 / math.sqrt(HEAD)
    lane = lax.broadcasted_iota(jnp.int32, (ROWS, 128), 1)
    first_head = lane < HEAD
    row8 = lax.broadcasted_iota(jnp.int32, (8, 128), 0)
    lane8 = lax.broadcasted_iota(jnp.int32, (8, 128), 1)
    chooser = (lax.div(lane8, HEAD) == row8).astype(f32)
    key_at = lax.broadcasted_iota(jnp.int32, (2, ROWS, ROWS), 1)
    row_at = lax.broadcasted_iota(jnp.int32, (2, ROWS, ROWS), 2)
    allowed = (key_at <= row_at).reshape(2 * ROWS, ROWS)
    for i in range(blocks):
        rows = slice(i * ROWS, (i + 1) * ROWS)
        two = slice(2 * i * ROWS, 2 * (i + 1) * ROWS)

        @pl.when(i * ROWS < len_ref[0])
        def work():
            dk_ref[two, :] = jnp.zeros((2 * ROWS, 128), f32)
            dv_ref[two, :] = jnp.zeros((2 * ROWS, 128), f32)
            key, value = p_ref[1, rows, :], p_ref[2, rows, :]
            zero = jnp.zeros_like(key)
            k2 = jnp.concatenate([jnp.where(first_head, key, zero), jnp.where(first_head, zero, key)], axis=0)
            kz_ref[two, :] = k2
            kt_ref[:, two] = k2.T
            vz_ref[two, :] = jnp.concatenate([jnp.where(first_head, value, zero), jnp.where(first_head, zero, value)], axis=0)
            query = p_ref[0, rows, :] * jnp.asarray(scaling, bf16)
            grad = g_ref[rows, :]
            product = grad.astype(f32) * o_ref[rows, :].astype(f32)
            delta = lax.dot_general(chooser, product, (((1,), (1,)), ((), ())), precision=lax.Precision.HIGHEST, preferred_element_type=f32)
            def both(a, b):
                return jnp.concatenate([jnp.broadcast_to(a, (ROWS, ROWS)), jnp.broadcast_to(b, (ROWS, ROWS))], axis=0)
            lse2 = both(lse_ref[0, 0:1, rows], lse_ref[0, 1:2, rows])
            delta2 = both(delta[0:1], delta[1:2])
            dqt = jnp.zeros((128, ROWS), f32)
            for j in range(i + 1):
                cols = slice(2 * j * ROWS, 2 * (j + 1) * ROWS)
                prob = jnp.exp(dot_nt(kz_ref[cols, :], query) - lse2)
                if i == j:
                    prob = jnp.where(allowed, prob, 0.0)
                ds = (prob * (dot_nt(vz_ref[cols, :], grad) - delta2)).astype(bf16)
                dv_ref[cols, :] += dot_nn(prob.astype(bf16), grad)
                dk_ref[cols, :] += dot_nn(ds, query)
                dqt = dqt + dot_nn(kt_ref[:, cols], ds)
            out_ref[0, rows, :] = (dqt * scaling).T.astype(bf16)
    for i in range(blocks):
        rows = slice(i * ROWS, (i + 1) * ROWS)
        a = slice(2 * i * ROWS, (2 * i + 1) * ROWS); b = slice((2 * i + 1) * ROWS, 2 * (i + 1) * ROWS)

        @pl.when(i * ROWS < len_ref[0])
        def finish():
            out_ref[1, rows, :] = jnp.where(first_head, dk_ref[a, :], dk_ref[b, :]).astype(bf16)
            out_ref[2, rows, :] = jnp.where(first_head, dv_ref[a, :], dv_ref[b, :]).astype(bf16)


def blank_kernel(ready_ref, out_ref):
    pass


def blank(ready, shape):
    return pl.pallas_call(
        blank_kernel,
        in_specs=[pl.BlockSpec(memory_space=pltpu.SMEM)],
        out_specs=pl.BlockSpec(memory_space=pl.ANY),
        out_shape=shape,
        name="blank",
    )(ready)


def attend_back(choice, projected, heads_out, grad_heads, lse, before):
    rows = projected.shape[1]
    pairs = HEADS // 2
    cols = lambda h, n: (0, n[2] + h)
    blocks = lambda h, n: (0, 0, n[2] + h)

    def kernel(n, p, o, g, l, unused, *rest):
        attend_back_kernel(n, p, o, g, l, *rest)

    return pl.pallas_call(
        kernel,
        grid_spec=pltpu.PrefetchScalarGridSpec(
            num_scalar_prefetch=1,
            grid=(pairs // 2,),
            in_specs=[
                pl.BlockSpec((3, rows, 128), blocks),
                pl.BlockSpec((rows, 128), cols),
                pl.BlockSpec((None, rows, 128), lambda h, n: (n[1], 0, n[2] + h)),
                pl.BlockSpec((1, 8, rows), lambda h, n: (n[2] + h, 0, 0)),
                pl.BlockSpec(memory_space=pl.ANY),
            ],
            out_specs=pl.BlockSpec((3, rows, 128), blocks),
            scratch_shapes=[
                pltpu.VMEM((2 * rows, 128), f32),
                pltpu.VMEM((2 * rows, 128), f32),
                pltpu.VMEM((2 * rows, 128), bf16),
                pltpu.VMEM((2 * rows, 128), bf16),
                pltpu.VMEM((128, 2 * rows), bf16),
            ],
        ),
        out_shape=jax.ShapeDtypeStruct((3, rows, D), bf16),
        input_output_aliases={5: 0},
        compiler_params=params(),
        cost_estimate=pl.CostEstimate(
            flops=3 * rows * rows * D, bytes_accessed=rows * D * 8, transcendentals=HEADS * rows * rows // 4
        ),
        name="attend_back",
    )(choice, projected, heads_out, grad_heads, lse, before)


def feed_kernel(plan, len_ref, row_ref, *refs):
    tok0, tok1, pass0, pass1, ho0, ho1, cot, table_ref, gain_ref = refs[:9]
    many = 2 * plan.sharers if plan.paired else 1
    grad_ref, pieces, refs = refs[9], refs[10 : 10 + many], refs[10 + many :]
    res, gh, hid, small_ref = refs[:4]
    outs, (w_ref, acc_ref, sums_ref, stage_ref, sem_ref) = refs[4:-5], refs[-5:]
    b = pl.program_id(0)
    many0 = last_block(len_ref[0]) + 1
    many1 = last_block(len_ref[1]) + 1
    early = b < many0

    @pl.when(b == 0)
    def clear():
        load_weight(plan, row_ref, pieces, w_ref, sem_ref.at[0])
        acc_ref[...] = jnp.zeros_like(acc_ref)
        sums_ref[...] = jnp.zeros_like(sums_ref)

    @pl.when(b < many0 + many1)
    def block():
        hot = onehot_rows(jnp.where(early, pass0[0], pass1[0]))
        entry = jnp.where(early, tok0[...], tok1[...]).astype(f32) + dot_tn(hot, table_ref[...])
        at = jnp.where(early, b, b - many0) * ROWS + lax.broadcasted_iota(jnp.int32, (ROWS, 1), 0)
        live = at < jnp.where(early, len_ref[0], len_ref[1])
        heads = jnp.where(early, ho0[...], ho1[...])
        attention = dot_nn(heads, w_ref[:, 0:D])
        hidden = entry + attention
        unit, scale = normalized(hidden)
        gain = gain_ref[...]
        normed = (unit * gain).astype(bf16)
        grad_feed = jnp.where(live, cot[...].reshape(ROWS, D).astype(f32), 0.0).astype(bf16)
        feed = jnp.zeros((ROWS, D), f32)
        grad_normed = jnp.zeros((ROWS, D), f32)
        for k in range(CHUNKS):
            up = slice(D + k * D, D + (k + 1) * D)
            down = slice(D + FF + k * D, D + FF + (k + 1) * D)
            x = dot_nn(normed, w_ref[:, up])
            grad_act = dot_nt(grad_feed, w_ref[:, down])
            c0 = math.sqrt(2.0 / math.pi)
            square = x * x
            bent = jnp.tanh(x * (c0 + (c0 * 0.044715) * square))
            half = 0.5 + 0.5 * bent
            slope = half + (0.5 * x) * (1.0 - bent * bent) * (c0 + (3.0 * c0 * 0.044715) * square)
            act = (x * half).astype(bf16)
            grad_x = (slope * grad_act).astype(bf16)
            feed = feed + dot_nn(act, w_ref[:, down])
            grad_normed = grad_normed + dot_nt(grad_x, w_ref[:, up])
            acc_ref[:, up] += dot_tn(normed, grad_x)
            acc_ref[:, down] += dot_tn(act, grad_feed)
        res[...] = jnp.where(live, hidden + feed, 0.0).astype(bf16).reshape(res.shape)
        sums_ref[0:8] += fold_rows(grad_normed * unit)
        sums_ref[8:16] += fold_rows(jnp.where(live, entry * entry, 0.0))
        sums_ref[16:24] += fold_rows(jnp.where(live, attention * attention, 0.0))
        sums_ref[24:32] += fold_rows(jnp.where(live, feed * feed, 0.0))
        grad_hidden = grad_feed.astype(f32) + norm_back(grad_normed * gain, unit, scale)
        hid[...] = grad_hidden
        grad_attention = grad_hidden.astype(bf16)
        acc_ref[:, 0:D] += dot_tn(heads, grad_attention)
        gh[...] = dot_nt(grad_attention, w_ref[:, 0:D]).astype(bf16)

    @pl.when(b == pl.num_programs(0) - 1)
    def finish():
        counted = (len_ref[0] + len_ref[1]).astype(f32)
        small_ref[...] = jnp.full(small_ref.shape, counted, f32)
        for n in range(4):
            small_ref[n : n + 1] = jnp.sum(sums_ref[8 * n : 8 * n + 8], axis=0, keepdims=True)
        store_grads(plan, plan.wide_orders, grad_ref, acc_ref, outs, stage_ref, sem_ref)


def feed(plan, part, lengths, piece_rows, grad_rows, tokens, pass_rows, heads_out, cotangent, table, gain, pieces, width):
    rows = tokens[0].shape[0]
    per = ROWS // part

    def at0(b, n, r):
        return jnp.minimum(b, last_block(n[0])), 0

    def at1(b, n, r):
        return jnp.clip(b - last_block(n[0]) - 1, 0, last_block(n[1])), 0

    def both(b, n, r):
        early = b <= last_block(n[0])
        return jnp.where(early, b, at1(b, n, r)[0]), jnp.where(early, 0, 1)

    row0 = pl.BlockSpec((ROWS, D), at0)
    row1 = pl.BlockSpec((ROWS, D), at1)
    pas0 = pl.BlockSpec((1, 1, ROWS), lambda *a: at0(*a) + (0,))
    pas1 = pl.BlockSpec((1, 1, ROWS), lambda *a: at1(*a) + (0,))
    dealt = pl.BlockSpec((per, 1, part, D), lambda *a: both(*a) + (0, 0))
    local = pl.BlockSpec((None, ROWS, D), lambda *a: both(*a)[::-1] + (0,))
    grads = grad_shapes(plan, width, plan.wide_orders)
    anywhere = pl.BlockSpec(memory_space=pl.ANY)
    return pl.pallas_call(
        functools.partial(feed_kernel, plan),
        grid_spec=pltpu.PrefetchScalarGridSpec(
            num_scalar_prefetch=2,
            grid=(2 * rows // ROWS,),
            in_specs=[
                row0, row1, pas0, pas1, row0, row1, dealt,
                pl.BlockSpec((8, D), lambda *a: (0, 0)),
                pl.BlockSpec((1, D), lambda *a: (0, 0)),
                pl.BlockSpec(memory_space=pltpu.SMEM),
            ]
            + [anywhere] * len(pieces),
            out_specs=[dealt, local, local, pl.BlockSpec((8, D), lambda *a: (0, 0))] + [anywhere] * len(grads),
            scratch_shapes=[
                pltpu.VMEM((D, width), bf16),
                pltpu.VMEM((D, width), f32),
                pltpu.VMEM((32, D), f32),
                pltpu.VMEM(stage_shape(plan), bf16),
                pltpu.SemaphoreType.DMA((2,)),
            ],
        ),
        out_shape=[
            jax.ShapeDtypeStruct(cotangent.shape, bf16),
            jax.ShapeDtypeStruct((2, rows, D), bf16),
            jax.ShapeDtypeStruct((2, rows, D), f32),
            jax.ShapeDtypeStruct((8, D), f32),
        ]
        + grads,
        compiler_params=params(),
        cost_estimate=pl.CostEstimate(
            flops=2 * 6 * rows * D * width, bytes_accessed=2 * rows * D * 14 + D * width * 4, transcendentals=2 * rows * FF
        ),
        name="feed",
    )(lengths, piece_rows, tokens[0], tokens[1], pass_rows[0], pass_rows[1], heads_out[0], heads_out[1],
      cotangent, table, gain, grad_rows, *pieces)


def project_back_kernel(plan, weight, rows_back, final, len_ref, row_ref, grad_ref, tok_ref, pass_ref, g_ref, *rest):
    rest = list(rest)
    hid_ref = rest.pop(0) if rows_back else None
    table_ref, gain_ref = rest.pop(0), rest.pop(0)
    before_ref = rest.pop(0) if final else None
    many = plan.sharers if plan.paired else 1
    pieces = [rest.pop(0) for n in range(many)] if rows_back else []
    if rows_back:
        out_ref, small_ref = rest.pop(0), rest.pop(0)
    if weight and not final:
        acc_ref = rest.pop(0)
    outs = [rest.pop(0) for shape in grad_shapes(plan, 3 * D, plan.head_orders)] if final else []
    if rows_back:
        w_ref, sums_ref = rest.pop(0), rest.pop(0)
    if final:
        acc_ref, stage_ref = rest.pop(0), rest.pop(0)
    sem_ref = rest.pop(0)
    b = pl.program_id(0)

    @pl.when(b == 0)
    def clear():
        if rows_back:
            load_weight(plan, row_ref, pieces, w_ref, sem_ref.at[0])
            sums_ref[...] = jnp.zeros_like(sums_ref)
        if weight:
            acc_ref[...] = before_ref[...] if final else jnp.zeros_like(acc_ref)

    @pl.when(b <= last_block(len_ref[0]))
    def work():
        hot = onehot_rows(pass_ref[0])
        entry = tok_ref[...].astype(f32) + dot_tn(hot, table_ref[...])
        unit, scale = normalized(entry)
        gain = gain_ref[...]
        if weight:
            normed = (unit * gain).astype(bf16)
            for part in range(3):
                acc_ref[:, part * D : (part + 1) * D] += dot_tn(normed, g_ref[part])
        if rows_back:
            grad_normed = jnp.zeros((ROWS, D), f32)
            for part in range(3):
                grad_normed = grad_normed + dot_nt(g_ref[part], w_ref[:, part * D : (part + 1) * D])
            sums_ref[0:8] += fold_rows(grad_normed * unit)
            grad_entry = hid_ref[...] + norm_back(grad_normed * gain, unit, scale)
            high = grad_entry.astype(bf16)
            out_ref[...] = high
            rest_one = grad_entry - high.astype(f32)
            low = rest_one.astype(bf16)
            lower = (rest_one - low.astype(f32)).astype(bf16)
            sums_ref[8:16] += dot_nn(hot, high) + dot_nn(hot, low) + dot_nn(hot, lower)

    if rows_back:
        @pl.when(b == pl.num_programs(0) - 1)
        def sums():
            small_ref[...] = sums_ref[8:16]
            small_ref[PASSES : PASSES + 1] = jnp.sum(sums_ref[0:8], axis=0, keepdims=True)

    if final:
        @pl.when(b == pl.num_programs(0) - 1)
        def finish():
            store_grads(plan, plan.head_orders, grad_ref, acc_ref, outs, stage_ref, sem_ref)


def project_back(
    plan, weight, rows_back, which, length, piece_rows, grad_rows, tokens, pass_rows, grads, grad_hidden, table, gain,
    pieces, before=None,
):
    rows = tokens.shape[0]
    final = before is not None
    at = lambda b, n, r, g: (jnp.minimum(b, last_block(n[0])), 0)
    row = pl.BlockSpec((ROWS, D), at)
    anywhere = pl.BlockSpec(memory_space=pl.ANY)
    in_specs = [
        row,
        pl.BlockSpec((1, 1, ROWS), lambda *a: at(*a) + (0,)),
        pl.BlockSpec((3, ROWS, D), lambda *a: (0,) + at(*a)),
    ]
    operands = [length, piece_rows, grad_rows, tokens, pass_rows, grads]
    if rows_back:
        in_specs.append(pl.BlockSpec((None, ROWS, D), lambda *a: (which,) + at(*a)))
        operands.append(grad_hidden)
    in_specs += [pl.BlockSpec((8, D), lambda *a: (0, 0)), pl.BlockSpec((1, D), lambda *a: (0, 0))]
    operands += [table, gain]
    out_shape, out_specs, scratch = [], [], []
    if final:
        in_specs.append(pl.BlockSpec((D, 3 * D), lambda *a: (0, 0), pipeline_mode=pl.Buffered(1)))
        operands.append(before)
    if rows_back:
        in_specs += [anywhere] * len(pieces)
        operands += pieces
        out_shape += [jax.ShapeDtypeStruct((rows, D), bf16), jax.ShapeDtypeStruct((8, D), f32)]
        out_specs += [row, pl.BlockSpec((8, D), lambda *a: (0, 0))]
        scratch += [pltpu.VMEM((D, 3 * D), bf16), pltpu.VMEM((16, D), f32)]
    if weight and not final:
        out_shape.append(jax.ShapeDtypeStruct((D, 3 * D), f32))
        out_specs.append(pl.BlockSpec((D, 3 * D), lambda *a: (0, 0)))
    if final:
        shapes = grad_shapes(plan, 3 * D, plan.head_orders)
        out_shape += shapes
        out_specs += [anywhere] * len(shapes)
        scratch += [pltpu.VMEM((D, 3 * D), f32), pltpu.VMEM(stage_shape(plan), bf16)]
    return pl.pallas_call(
        functools.partial(project_back_kernel, plan, weight, rows_back, final),
        grid_spec=pltpu.PrefetchScalarGridSpec(
            num_scalar_prefetch=3,
            grid=(rows // ROWS,),
            in_specs=in_specs,
            out_specs=out_specs,
            scratch_shapes=scratch + [pltpu.SemaphoreType.DMA((2,))],
        ),
        out_shape=out_shape,
        compiler_params=params(),
        cost_estimate=pl.CostEstimate(
            flops=2 * (weight + rows_back) * rows * D * 3 * D, bytes_accessed=rows * D * 14 + D * D * 6, transcendentals=0
        ),
        name="project_back",
    )(*operands)


def pick_kernel(index_ref, in_ref, out_ref, sem_ref):
    copies = [
        pltpu.make_async_copy(in_ref.at[index_ref[n]], out_ref.at[n], sem_ref) for n in range(out_ref.shape[0])
    ]
    for copy in copies:
        copy.start()
    for copy in copies:
        copy.wait()


def pick(index, blocks):
    shape = index.shape + blocks.shape[1:]
    return pl.pallas_call(
        pick_kernel,
        grid_spec=pltpu.PrefetchScalarGridSpec(
            num_scalar_prefetch=1,
            grid=(1,),
            in_specs=[pl.BlockSpec(memory_space=pl.ANY)],
            out_specs=pl.BlockSpec(shape, lambda b, n: (0, 0, 0)),
            scratch_shapes=[pltpu.SemaphoreType.DMA],
        ),
        out_shape=jax.ShapeDtypeStruct(shape, blocks.dtype),
        compiler_params=params(),
        cost_estimate=pl.CostEstimate(flops=0, bytes_accessed=4 * math.prod(shape), transcendentals=0),
        name="pick",
    )(index, blocks)


def settle_kernel(index_ref, *refs):
    arrays, out_ref = refs[:-1], refs[-1]
    first = pl.program_id(0) * out_ref.shape[0]
    rows = out_ref.shape[1]
    at = lax.broadcasted_iota(jnp.int32, (rows, 1), 0)
    for n in range(out_ref.shape[0]):
        live = at < index_ref[2, first + n]
        source, late = index_ref[1, first + n], index_ref[0, first + n]
        if len(arrays) == 1:
            found = arrays[0][2 * source + late]
        else:
            found = jnp.where(late == 0, arrays[0][source], arrays[1][source])
        out_ref[n] = jnp.where(live, found.astype(f32), 0.0)


def settle(index, *arrays):
    many = index.shape[1]
    step = 4
    shape = arrays[0].shape
    whole = pl.BlockSpec(shape, lambda b, n: (0, 0, 0), pipeline_mode=pl.Buffered(1))
    return pl.pallas_call(
        settle_kernel,
        grid_spec=pltpu.PrefetchScalarGridSpec(
            num_scalar_prefetch=1,
            grid=(many // step,),
            in_specs=[whole] * len(arrays),
            out_specs=pl.BlockSpec((step,) + shape[1:], lambda b, n: (b, 0, 0)),
        ),
        out_shape=jax.ShapeDtypeStruct((many,) + shape[1:], f32),
        compiler_params=params(),
        cost_estimate=pl.CostEstimate(flops=0, bytes_accessed=6 * many * math.prod(shape[1:]), transcendentals=0),
        name="settle",
    )(index, *arrays)


def after(values, *others):
    return lax.optimization_barrier((values, others))[0]


def swap(blocks):
    return lax.all_to_all(blocks, "dp", split_axis=0, concat_axis=0, tiled=True)


def per_device(
    groups,
    width_all,
    tokens,
    passes,
    lengths,
    dealing,
    pass_table,
    gain_first,
    to_heads,
    from_heads,
    gain_second,
    expand,
    shrink,
    cotangent,
):
    axes = ("dp", "fsdp")
    slots, part, unused_width = tokens.shape
    seq_len = part * groups
    order = jnp.arange(slots, dtype=jnp.int32)
    here = lax.axis_index("dp")
    ordering = dealing[0, 0]
    sizes = lengths[0]

    ahead = (sizes[None, :] > sizes[:, None]) | (
        (sizes[None, :] == sizes[:, None]) & (order[None, :] < order[:, None])
    )
    rank = jnp.sum(ahead.astype(jnp.int32), axis=1)
    ranked = jnp.sum(jnp.where(rank[None, :] == order[:, None], order[None, :], 0), axis=1)
    place = jnp.sum(jnp.where(ordering[None, :] == order[:, None], order[None, :], 0), axis=1)
    early_seqs = ranked[:groups]
    late_seqs = ranked[groups:][::-1]
    from_early = jnp.sum(jnp.where(early_seqs[:, None] == order[None, :], place[None, :], 0), axis=1)
    from_late = jnp.sum(jnp.where(late_seqs[:, None] == order[None, :], place[None, :], 0), axis=1)
    slot_rank = jnp.sum(jnp.where(ordering[:, None] == order[None, :], rank[None, :], 0), axis=1)
    slot_size = jnp.sum(jnp.where(ordering[:, None] == order[None, :], sizes[None, :], 0), axis=1)
    is_late = (slot_rank >= groups).astype(jnp.int32)
    source = jnp.where(is_late == 1, slots - 1 - slot_rank, slot_rank)
    back_index = jnp.stack([is_late, source, slot_size - here * part])
    my_seqs = jnp.stack([early_seqs[here], late_seqs[here]])
    my_sizes = jnp.sum(jnp.where(my_seqs[:, None] == order[None, :], sizes[None, :], 0), axis=1)

    row_count = to_heads.shape[0]
    narrow = jnp.concatenate(
        [
            from_heads,
            expand.reshape(row_count, D, CHUNKS).transpose(0, 2, 1).reshape(row_count, FF),
            shrink.reshape(row_count, CHUNKS * D),
        ],
        axis=1,
    )
    plan = Plan(groups, width_all // groups, row_count)
    index_here = here * (width_all // groups) + lax.axis_index("fsdp")
    my_passes = [passes[my_seqs[m]].reshape(seq_len // ROWS, 1, ROWS) for m in range(2)]
    one_size = [my_sizes[m : m + 1] for m in range(2)]
    table = jnp.zeros((8, D), bf16).at[:PASSES].set(pass_table)
    gain_one = gain_first.astype(f32).reshape(1, D)
    gain_two = gain_second.astype(f32).reshape(1, D)

    pairs_index = jnp.stack([from_early, from_late], axis=1).reshape(slots)
    picked = [pick(from_early, tokens), pick(from_late, tokens), pick(pairs_index, cotangent)]
    if plan.paired:
        piece_rows = plan.piece_rows(index_here)
        wide_rows = plan.grad_rows(index_here, plan.wide_orders)
        head_rows = plan.grad_rows(index_here, plan.head_orders)
        head_near = plan.gather(to_heads[None], plan.far + [plan.near])
        ready = (my_passes, one_size, piece_rows, table, gain_one, narrow)
        tokens0 = swap(after(picked[0], head_near, ready))
        head_pieces = plan.gather_core(plan.gather_x(head_near))
        tokens1 = swap(after(picked[1], tokens0, picked[2], head_pieces))
    else:
        piece_rows = wide_rows = head_rows = jnp.zeros((1,), jnp.int32)
        head_pieces = (lax.all_gather(to_heads, axes, axis=0, tiled=True),)
        wide_pieces = (lax.all_gather(narrow, axes, axis=0, tiled=True),)
        tokens0 = swap(picked[0])
        tokens1 = swap(after(picked[1], tokens0))

    def forward(m, *gate):
        return project(
            plan, after(one_size[m], gate), piece_rows, my_tokens[m], my_passes[m], table, gain_one, head_pieces
        )

    def mix(m, *gate):
        return attend(after(one_size[m], gate), projected[m])

    def mix_back(m, first, before, *gate):
        choice = jnp.stack([my_sizes[m], jnp.int32(m), jnp.int32(first)])
        return attend_back(after(choice, gate), projected[m], heads_out[m], grad_heads, lse[m], before)

    def back(m, weight, rows_back, *gate, before=None):
        return project_back(
            plan, weight, rows_back, m, after(one_size[m], gate), piece_rows, head_rows, my_tokens[m], my_passes[m],
            grad_parts[m], grad_hidden, table, gain_one, head_pieces, before,
        )

    def send_back(rows, *gate):
        return swap(after(rows, gate).reshape(groups, part, D))

    projected, heads_out, lse, grad_parts = [None, None], [None, None], [None, None], [None, None]
    my_tokens = [tokens0.reshape(seq_len, D), tokens1.reshape(seq_len, D)]
    projected[0] = forward(0)
    heads_out[0], lse[0] = mix(0)
    if plan.paired:
        wide_one = plan.gather(after(narrow, projected[0])[None], plan.far[:1])
        wide_far = plan.gather(after(wide_one, lse[0]), plan.far[1:])
    else:
        wide_one = wide_far = wide_pieces
    projected[1] = forward(1, lse[0], wide_one)
    my_grads = swap(after(picked[2].reshape(groups, 2, part, D), tokens1, projected[1], wide_far))
    heads_out[1], lse[1] = mix(1, wide_far)
    if plan.paired:
        cut = first_part(wide_far.shape[-1], plan.wide_orders)
        first = plan.gather_near({0: wide_far[:, :, :cut]}, (), lse[1])
        second = plan.gather_x(wide_far[:, :, cut:])
        first = plan.gather_x(first[0])
        second = plan.gather_near(second, lse[1])
        wide_pieces = plan.gather_core(first) + plan.gather_core(second)

    res, grad_heads, grad_hidden, feed_small, *wide_grads = feed(
        plan, part, my_sizes, piece_rows, wide_rows, my_tokens, my_passes, heads_out, my_grads, table, gain_two,
        wide_pieces, D + 2 * FF,
    )

    def begin(grads):
        if not plan.paired:
            return lax.psum_scatter(grads[0], axes, scatter_dimension=0, tiled=True).astype(f32)
        return [grads[n : n + 2] for n in range(0, len(grads), 2)]

    def advance(state, stage, gate, late):
        return plan.reduce_stage(state, plan.wide_orders, stage, (gate,), (late,)) if plan.paired else state

    half = HEADS // 4
    space = jax.ShapeDtypeStruct((3, seq_len, D), bf16)
    wide0 = begin(wide_grads)
    result = swap(res)
    some = mix_back(0, 0, blank(one_size[0], space))
    wide1 = advance(wide0, 0, (), some)
    grad_parts[0] = mix_back(0, half, some, wide1)
    entry0, small0, head_sum = back(0, True, True)
    wide2 = advance(wide1, 1, some, entry0)
    moved0 = send_back(entry0, result)
    some = mix_back(1, 0, blank(one_size[1], space), entry0, wide2, result)
    wide3 = advance(wide2, 2, entry0, some)
    grad_parts[1] = mix_back(1, half, some, wide3)
    entry1, small1 = back(1, False, True)
    wide_owned = advance(wide3, 3, some, entry1)
    moved1 = send_back(entry1, moved0)
    head_grads = back(1, True, False, entry1, moved0, before=head_sum)
    head_state = begin(head_grads)
    totals = jnp.concatenate([small0 + small1, feed_small], axis=0)
    if plan.paired:
        stages = plan.head_orders[0]
        for n in range(len(stages)):
            mine, masks = after(totals, head_state), stages[n]
            found = [mine] + [plan.exchange(mine, ways_bits(masks, way)) for way in range(1, 1 << len(masks))]
            while len(found) > 1:
                found = [found[k] + found[k + 1] for k in range(0, len(found), 2)]
            totals = found[0]
            head_state = plan.reduce_stage(
                head_state, plan.head_orders, n, (wide_owned,) if n == 0 else (), (moved1,) if n == 1 else ()
            )
        wide_owned, head_owned = jnp.concatenate(wide_owned, axis=1), head_state[0]
    else:
        totals = lax.psum(totals, axes)
        head_owned = head_state
    root_squares = jnp.sqrt(jnp.sum(totals[9:12], axis=1) / (totals[12, 0] * D))

    grad_expand = wide_owned[:, D : D + FF].reshape(row_count, CHUNKS, D).transpose(0, 2, 1)
    return (
        settle(back_index, result.reshape(slots, part, D)),
        settle(back_index, moved0, moved1),
        totals[:PASSES],
        totals[PASSES],
        head_owned,
        wide_owned[:, :D],
        totals[8],
        grad_expand.reshape(row_count, FF),
        wide_owned[:, D + FF :].reshape(row_count * CHUNKS, D),
        root_squares,
    )


def solution(mesh):
    groups = mesh.shape["dp"]
    weight_spec = P(("dp", "fsdp"), None)
    block_spec = P("fsdp", "dp", None)
    in_specs = (
        block_spec,
        P("fsdp", None),
        P("fsdp", None),
        P("dp", "fsdp", None),
        P(),
        P(),
        weight_spec,
        weight_spec,
        P(),
        weight_spec,
        weight_spec,
        block_spec,
    )
    out_specs = (
        block_spec,
        block_spec,
        P(),
        P(),
        weight_spec,
        weight_spec,
        P(),
        weight_spec,
        weight_spec,
        P(),
    )
    body = functools.partial(per_device, groups, groups * mesh.shape["fsdp"])
    return jax.shard_map(body, mesh=mesh, in_specs=in_specs, out_specs=out_specs, check_vma=False)
```

```python
import math
import functools

import jax
import jax.numpy as jnp
from jax import lax
from jax.experimental import pallas as pl
from jax.experimental.pallas import tpu as pltpu
from jax.sharding import PartitionSpec as P

D = 768
HEADS = 12
HEAD = 64
FF = 3072
PASSES = 5
EPS = 1e-05
ROWS = 256
CHUNKS = FF // D
VMEM_MOST = 64000 * 1024

f32 = jnp.float32
bf16 = jnp.bfloat16


def dot_nn(a, b):
    return lax.dot_general(a, b, (((1,), (0,)), ((), ())), preferred_element_type=f32)


def dot_nt(a, b):
    return lax.dot_general(a, b, (((1,), (1,)), ((), ())), preferred_element_type=f32)


def dot_tn(a, b):
    return lax.dot_general(a, b, (((0,), (0,)), ((), ())), preferred_element_type=f32)


def params(**more):
    return pltpu.CompilerParams(vmem_limit_bytes=VMEM_MOST, **more)


def normalized(values):
    centred = values - jnp.mean(values, axis=-1, keepdims=True)
    spread = jnp.mean(centred * centred, axis=-1, keepdims=True)
    scale = lax.rsqrt(spread + EPS)
    return centred * scale, scale


def norm_back(grad_unit, unit, scale):
    first = jnp.mean(grad_unit, axis=-1, keepdims=True)
    second = jnp.mean(grad_unit * unit, axis=-1, keepdims=True)
    return scale * (grad_unit - first - unit * second)


def onehot_rows(pass_row):
    ids = lax.broadcasted_iota(jnp.int32, (8, pass_row.shape[-1]), 0)
    return (ids == pass_row).astype(f32).astype(bf16)


def fold_rows(values):
    rows, width = values.shape
    return jnp.sum(values.reshape(rows // 8, 8, width), axis=0)


def last_block(length):
    return lax.div(length + (ROWS - 1), ROWS) - 1


def bits_of(count):
    return count.bit_length() - 1


class Plan:
    def __init__(self, groups, sharers, rows):
        self.groups, self.sharers, self.rows = groups, sharers, rows
        self.count = groups * sharers
        self.paired = rows % 8 == 0 and self.count & (self.count - 1) == 0 and sharers >= 4 and groups >= 4
        core, *over_x = [1 << bit for bit in range(bits_of(sharers))]
        near, *far = [sharers << bit for bit in range(bits_of(groups))]
        self.core, self.over_x, self.near, self.far = core, over_x, near, far[::-1]
        self.wide_orders = ([[core], over_x, [near], far], [[core], [near], over_x, far])
        self.head_orders = ([[core], over_x + [near], far],)

    def exchange(self, values, bits):
        pairs = [(i, i ^ bits) for i in range(self.count)]
        return lax.ppermute(values, ("dp", "fsdp"), pairs)

    def gather(self, held, masks, gate=(), late=()):
        for bits in masks:
            held = jnp.concatenate([after(held, late), self.exchange(after(held, gate), bits)], axis=0)
        return held

    def gather_x(self, held, *gate):
        pieces = {0: held}
        for bits in self.over_x[::-1]:
            for name in list(pieces):
                pieces[name | bits] = self.exchange(after(pieces[name], gate), bits)
        return pieces

    def gather_near(self, pieces, gate=(), late=()):
        return {name: self.gather(held, [self.near], gate, late) for name, held in pieces.items()}

    def gather_core(self, pieces, *gate):
        found = dict(pieces)
        for name in pieces:
            found[name | self.core] = self.exchange(after(pieces[name], gate), self.core)
        return tuple(found[name] for name in range(self.sharers))

    def piece_rows(self, here):
        masks = self.far + [self.near]
        found = []
        for f in range(self.sharers):
            for n in range(self.groups):
                rel = f | ways_bits(masks, n)
                found.append((here ^ rel) * self.rows)
        return jnp.stack(found).astype(jnp.int32)

    def grad_rows(self, here, orders):
        found = []
        for order in orders:
            for place in range(self.count):
                rel, left = 0, self.count
                for masks in order:
                    left >>= len(masks)
                    rel |= ways_bits(masks, (place // left) % (1 << len(masks)))
                found.append((here ^ rel) * self.rows)
        return jnp.stack(found).astype(jnp.int32)

    def total_stage(self, values, masks, gate=(), late=()):
        found = [after(values, late)]
        found += [self.exchange(after(values, gate), ways_bits(masks, way)) for way in range(1, 1 << len(masks))]
        while len(found) > 1:
            found = [found[k] + found[k + 1] for k in range(0, len(found), 2)]
        return found[0]

    def reduce_stage(self, states, orders, stage, gate=(), late=()):
        sums = []
        for ways, order in zip(states, orders):
            sums.append(
                [after(ways[0], late)]
                + [
                    self.exchange(after(ways[n], gate), ways_bits(order[stage], n))
                    for n in range(1, len(ways))
                ]
            )
        if stage == len(orders[0]) - 1:
            return [sum(part.astype(f32) for part in parts)[0] for parts in sums]
        ways = 1 << len(orders[0][stage + 1])
        if stage == len(orders[0]) - 2:
            return [merge(sums, ways)]
        return [merge([parts], ways) for parts in sums]


def ways_bits(masks, way):
    return sum(bits for n, bits in enumerate(masks) if (way >> n) & 1)


def merge_kernel(widths, many, ways, *refs):
    ins, outs = refs[: len(widths) * many * ways], refs[len(widths) * many * ways :]
    for way in range(ways):
        first = 0
        for k, width in enumerate(widths):
            views = [ins[(k * many + n) * ways + way] for n in range(many)]
            total = views[0][...].astype(f32)
            for view in views[1:]:
                total = total + view[...].astype(f32)
            outs[way][:, :, first : first + width] = total.astype(bf16)
            first += width


def merge(groups, ways):
    blocks, rows, unused = groups[0][0].shape
    widths = [parts[0].shape[2] for parts in groups]
    share = blocks // ways
    steps = min(share, 4)

    def view(way, width):
        return pl.BlockSpec((share // steps, rows, width), lambda b: (b + way * steps, 0, 0))

    out = jax.ShapeDtypeStruct((share, rows, sum(widths)), bf16)
    many = len(groups[0])
    size = blocks * rows * sum(widths)
    return pl.pallas_call(
        functools.partial(merge_kernel, widths, many, ways),
        grid=(steps,),
        in_specs=[view(way, width) for width in widths for n in range(many) for way in range(ways)],
        out_specs=[view(0, sum(widths))] * ways,
        out_shape=[out] * ways,
        compiler_params=params(),
        cost_estimate=pl.CostEstimate(flops=many * size, bytes_accessed=(2 + 2 * many) * size, transcendentals=0),
        name="merge",
    )(*[part for parts in groups for part in parts for way in range(ways)])


def load_weight(plan, rows_ref, pieces, weight_ref, sem_ref):
    copies = []
    if not plan.paired:
        copies.append(pltpu.make_async_copy(pieces[0], weight_ref, sem_ref))
    first = 0
    for k in range(0, len(pieces) if plan.paired else 0, plan.sharers):
        width = pieces[k].shape[-1]
        for f in range(plan.sharers):
            for n in range(plan.groups):
                at = pl.multiple_of(rows_ref[f * plan.groups + n], 8)
                target = weight_ref.at[pl.ds(at, plan.rows), first : first + width]
                copies.append(pltpu.make_async_copy(pieces[k + f].at[n], target, sem_ref))
        first += width
    for copy in copies:
        copy.start()
    for copy in copies:
        copy.wait()


def grad_shapes(plan, width, orders):
    if not plan.paired:
        return [jax.ShapeDtypeStruct((D, width), bf16)]
    half = plan.count // 2
    cut = first_part(width, orders)
    return [jax.ShapeDtypeStruct((half, plan.rows, w), bf16) for w in (cut, cut, width - cut, width - cut) if w > 0]


def first_part(width, orders):
    return (width // D + 1) // 2 * D if len(orders) == 2 else width


def stage_shape(plan):
    return (2, plan.count, plan.rows, D) if plan.paired else (2, D, D)


def store_grads(plan, orders, rows_ref, acc_ref, outs, stage_ref, sem_ref):
    width, step = acc_ref.shape[1], D
    cut = first_part(width, orders)
    half = plan.count // 2
    waiting = []
    for n in range(width // step):
        slot = n % 2
        cols = slice(n * step, (n + 1) * step)
        if len(waiting) == 2:
            for copy in waiting.pop(0):
                copy.wait()
        if not plan.paired:
            stage_ref[slot] = acc_ref[:, cols].astype(bf16)
            copies = [pltpu.make_async_copy(stage_ref.at[slot], outs[0].at[:, cols], sem_ref.at[slot])]
        else:
            late = n * step >= cut
            base = plan.count if late else 0
            start = n * step - (cut if late else 0)

            def fill(place, carry):
                at = pl.multiple_of(rows_ref[base + place], 8)
                stage_ref[slot, place] = acc_ref[pl.ds(at, plan.rows), cols].astype(bf16)
                return carry

            lax.fori_loop(0, plan.count, fill, 0, unroll=2)
            keep, send = outs[2:4] if late else outs[0:2]
            there = slice(start, start + step)
            copies = [
                pltpu.make_async_copy(stage_ref.at[slot, 0:half], keep.at[:, :, there], sem_ref.at[slot]),
                pltpu.make_async_copy(stage_ref.at[slot, half:], send.at[:, :, there], sem_ref.at[slot]),
            ]
        for copy in copies:
            copy.start()
        waiting.append(copies)
    for copies in waiting:
        for copy in copies:
            copy.wait()


def project_kernel(plan, len_ref, row_ref, tok_ref, pass_ref, table_ref, gain_ref, *rest):
    pieces, (out_ref, w_ref, sem_ref) = rest[:-3], rest[-3:]

    @pl.when(pl.program_id(0) == 0)
    def load():
        load_weight(plan, row_ref, pieces, w_ref, sem_ref)

    @pl.when(pl.program_id(0) <= last_block(len_ref[0]))
    def work():
        hot = onehot_rows(pass_ref[0])
        entry = tok_ref[...].astype(f32) + dot_tn(hot, table_ref[...])
        unit, unused = normalized(entry)
        normed = (unit * gain_ref[...]).astype(bf16)
        for part in range(3):
            out_ref[part] = dot_nn(normed, w_ref[:, part * D : (part + 1) * D]).astype(bf16)


def project(plan, length, piece_rows, tokens, pass_rows, table, gain, pieces):
    rows = tokens.shape[0]
    at = lambda b, n, r: (jnp.minimum(b, last_block(n[0])), 0)
    return pl.pallas_call(
        functools.partial(project_kernel, plan),
        grid_spec=pltpu.PrefetchScalarGridSpec(
            num_scalar_prefetch=2,
            grid=(rows // ROWS,),
            in_specs=[
                pl.BlockSpec((ROWS, D), at),
                pl.BlockSpec((1, 1, ROWS), lambda b, n, r: at(b, n, r) + (0,)),
                pl.BlockSpec((8, D), lambda b, n, r: (0, 0)),
                pl.BlockSpec((1, D), lambda b, n, r: (0, 0)),
            ]
            + [pl.BlockSpec(memory_space=pl.ANY)] * len(pieces),
            out_specs=pl.BlockSpec((3, ROWS, D), lambda b, n, r: (0,) + at(b, n, r)),
            scratch_shapes=[pltpu.VMEM((D, 3 * D), bf16), pltpu.SemaphoreType.DMA],
        ),
        out_shape=jax.ShapeDtypeStruct((3, rows, D), bf16),
        compiler_params=params(),
        cost_estimate=pl.CostEstimate(
            flops=2 * rows * D * 3 * D, bytes_accessed=rows * D * 8 + D * D * 6, transcendentals=0
        ),
        name="project",
    )(length, piece_rows, tokens, pass_rows, table, gain, *pieces)


def attend_kernel(len_ref, p_ref, out_ref, lse_ref):
    blocks = p_ref.shape[1] // ROWS
    lane = lax.broadcasted_iota(jnp.int32, (ROWS, 128), 1)
    first_head = lane < HEAD
    here = lax.broadcasted_iota(jnp.int32, (ROWS, ROWS), 0)
    there = lax.broadcasted_iota(jnp.int32, (ROWS, ROWS), 1)
    allowed = there <= here
    for i in range(blocks):
        rows = slice(i * ROWS, (i + 1) * ROWS)

        @pl.when(i * ROWS < len_ref[0])
        def work():
            query = p_ref[0, rows, :] * jnp.asarray(1.0 / math.sqrt(HEAD), bf16)
            found = []
            for head in range(2):
                mine = first_head if head == 0 else jnp.logical_not(first_head)
                q = jnp.where(mine, query, jnp.zeros_like(query))
                diag = dot_nt(q, p_ref[1, rows, :])
                diag = jnp.where(allowed, diag, -1e30)
                largest = jnp.max(diag, axis=-1, keepdims=True)
                if i > 0:
                    before = dot_nt(q, p_ref[1, : i * ROWS, :])
                    largest = jnp.maximum(largest, jnp.max(before, axis=-1, keepdims=True))
                diag = jnp.exp(diag - largest)
                total = jnp.sum(diag, axis=-1, keepdims=True)
                out = dot_nn(diag.astype(bf16), p_ref[2, rows, :])
                if i > 0:
                    before = jnp.exp(before - largest)
                    total = total + jnp.sum(before, axis=-1, keepdims=True)
                    out = out + dot_nn(before.astype(bf16), p_ref[2, : i * ROWS, :])
                found.append(out * (1.0 / total))
                lse = jnp.broadcast_to(largest + jnp.log(total), (ROWS, 128))
                lse_ref[0, head : head + 1, rows] = lse.T[0:1]
            out_ref[rows, :] = jnp.where(first_head, found[0], found[1]).astype(bf16)


def attend(length, projected):
    rows = projected.shape[1]
    pairs = HEADS // 2
    return pl.pallas_call(
        attend_kernel,
        grid_spec=pltpu.PrefetchScalarGridSpec(
            num_scalar_prefetch=1,
            grid=(pairs,),
            in_specs=[pl.BlockSpec((3, rows, 128), lambda h, n: (0, 0, h))],
            out_specs=[
                pl.BlockSpec((rows, 128), lambda h, n: (0, h)),
                pl.BlockSpec((1, 8, rows), lambda h, n: (h, 0, 0)),
            ],
        ),
        out_shape=[
            jax.ShapeDtypeStruct((rows, D), bf16),
            jax.ShapeDtypeStruct((pairs, 8, rows), f32),
        ],
        compiler_params=params(),
        cost_estimate=pl.CostEstimate(
            flops=2 * rows * rows * D, bytes_accessed=rows * D * 8, transcendentals=HEADS * rows * rows // 2
        ),
        name="attend",
    )(length, projected)


def attend_back_kernel(len_ref, p_ref, o_ref, g_ref, lse_ref, out_ref, dk_ref, dv_ref, kz_ref, vz_ref, kt_ref):
    blocks = p_ref.shape[1] // ROWS
    scaling = 1.0 / math.sqrt(HEAD)
    lane = lax.broadcasted_iota(jnp.int32, (ROWS, 128), 1)
    first_head = lane < HEAD
    row8 = lax.broadcasted_iota(jnp.int32, (8, 128), 0)
    lane8 = lax.broadcasted_iota(jnp.int32, (8, 128), 1)
    chooser = (lax.div(lane8, HEAD) == row8).astype(f32)
    key_at = lax.broadcasted_iota(jnp.int32, (2, ROWS, ROWS), 1)
    row_at = lax.broadcasted_iota(jnp.int32, (2, ROWS, ROWS), 2)
    allowed = (key_at <= row_at).reshape(2 * ROWS, ROWS)
    for i in range(blocks):
        rows = slice(i * ROWS, (i + 1) * ROWS)
        two = slice(2 * i * ROWS, 2 * (i + 1) * ROWS)

        @pl.when(i * ROWS < len_ref[0])
        def work():
            dk_ref[two, :] = jnp.zeros((2 * ROWS, 128), f32)
            dv_ref[two, :] = jnp.zeros((2 * ROWS, 128), f32)
            key, value = p_ref[1, rows, :], p_ref[2, rows, :]
            zero = jnp.zeros_like(key)
            k2 = jnp.concatenate([jnp.where(first_head, key, zero), jnp.where(first_head, zero, key)], axis=0)
            kz_ref[two, :] = k2
            kt_ref[:, two] = k2.T
            vz_ref[two, :] = jnp.concatenate([jnp.where(first_head, value, zero), jnp.where(first_head, zero, value)], axis=0)
            query = p_ref[0, rows, :] * jnp.asarray(scaling, bf16)
            grad = g_ref[rows, :]
            product = grad.astype(f32) * o_ref[rows, :].astype(f32)
            delta = lax.dot_general(chooser, product, (((1,), (1,)), ((), ())), precision=lax.Precision.HIGHEST, preferred_element_type=f32)
            def both(a, b):
                return jnp.concatenate([jnp.broadcast_to(a, (ROWS, ROWS)), jnp.broadcast_to(b, (ROWS, ROWS))], axis=0)
            lse2 = both(lse_ref[0, 0:1, rows], lse_ref[0, 1:2, rows])
            delta2 = both(delta[0:1], delta[1:2])
            dqt = jnp.zeros((128, ROWS), f32)
            for j in range(i + 1):
                cols = slice(2 * j * ROWS, 2 * (j + 1) * ROWS)
                prob = jnp.exp(dot_nt(kz_ref[cols, :], query) - lse2)
                if i == j:
                    prob = jnp.where(allowed, prob, 0.0)
                ds = (prob * (dot_nt(vz_ref[cols, :], grad) - delta2)).astype(bf16)
                dv_ref[cols, :] += dot_nn(prob.astype(bf16), grad)
                dk_ref[cols, :] += dot_nn(ds, query)
                dqt = dqt + dot_nn(kt_ref[:, cols], ds)
            out_ref[0, rows, :] = (dqt * scaling).T.astype(bf16)
    for i in range(blocks):
        rows = slice(i * ROWS, (i + 1) * ROWS)
        a = slice(2 * i * ROWS, (2 * i + 1) * ROWS); b = slice((2 * i + 1) * ROWS, 2 * (i + 1) * ROWS)

        @pl.when(i * ROWS < len_ref[0])
        def finish():
            out_ref[1, rows, :] = jnp.where(first_head, dk_ref[a, :], dk_ref[b, :]).astype(bf16)
            out_ref[2, rows, :] = jnp.where(first_head, dv_ref[a, :], dv_ref[b, :]).astype(bf16)


def blank_kernel(ready_ref, out_ref):
    pass


def blank(ready, shape):
    return pl.pallas_call(
        blank_kernel,
        in_specs=[pl.BlockSpec(memory_space=pltpu.SMEM)],
        out_specs=pl.BlockSpec(memory_space=pl.ANY),
        out_shape=shape,
        name="blank",
    )(ready)


def attend_back(choice, projected, heads_out, grad_heads, lse, before):
    rows = projected.shape[1]
    pairs = HEADS // 2
    cols = lambda h, n: (0, n[2] + h)
    blocks = lambda h, n: (0, 0, n[2] + h)

    def kernel(n, p, o, g, l, unused, *rest):
        attend_back_kernel(n, p, o, g, l, *rest)

    return pl.pallas_call(
        kernel,
        grid_spec=pltpu.PrefetchScalarGridSpec(
            num_scalar_prefetch=1,
            grid=(pairs // 2,),
            in_specs=[
                pl.BlockSpec((3, rows, 128), blocks),
                pl.BlockSpec((rows, 128), cols),
                pl.BlockSpec((None, rows, 128), lambda h, n: (n[1], 0, n[2] + h)),
                pl.BlockSpec((1, 8, rows), lambda h, n: (n[2] + h, 0, 0)),
                pl.BlockSpec(memory_space=pl.ANY),
            ],
            out_specs=pl.BlockSpec((3, rows, 128), blocks),
            scratch_shapes=[
                pltpu.VMEM((2 * rows, 128), f32),
                pltpu.VMEM((2 * rows, 128), f32),
                pltpu.VMEM((2 * rows, 128), bf16),
                pltpu.VMEM((2 * rows, 128), bf16),
                pltpu.VMEM((128, 2 * rows), bf16),
            ],
        ),
        out_shape=jax.ShapeDtypeStruct((3, rows, D), bf16),
        input_output_aliases={5: 0},
        compiler_params=params(),
        cost_estimate=pl.CostEstimate(
            flops=3 * rows * rows * D, bytes_accessed=rows * D * 8, transcendentals=HEADS * rows * rows // 4
        ),
        name="attend_back",
    )(choice, projected, heads_out, grad_heads, lse, before)


def feed_kernel(plan, len_ref, row_ref, *refs):
    tok0, tok1, pass0, pass1, ho0, ho1, cot, table_ref, gain_ref = refs[:9]
    many = 2 * plan.sharers if plan.paired else 1
    grad_ref, pieces, refs = refs[9], refs[10 : 10 + many], refs[10 + many :]
    res, gh, hid, small_ref = refs[:4]
    outs, (w_ref, acc_ref, sums_ref, stage_ref, sem_ref) = refs[4:-5], refs[-5:]
    b = pl.program_id(0)
    many0 = last_block(len_ref[0]) + 1
    many1 = last_block(len_ref[1]) + 1
    early = b < many0

    @pl.when(b == 0)
    def clear():
        load_weight(plan, row_ref, pieces, w_ref, sem_ref.at[0])
        acc_ref[...] = jnp.zeros_like(acc_ref)
        sums_ref[...] = jnp.zeros_like(sums_ref)

    @pl.when(b < many0 + many1)
    def block():
        hot = onehot_rows(jnp.where(early, pass0[0], pass1[0]))
        entry = jnp.where(early, tok0[...], tok1[...]).astype(f32) + dot_tn(hot, table_ref[...])
        at = jnp.where(early, b, b - many0) * ROWS + lax.broadcasted_iota(jnp.int32, (ROWS, 1), 0)
        live = at < jnp.where(early, len_ref[0], len_ref[1])
        heads = jnp.where(early, ho0[...], ho1[...])
        attention = dot_nn(heads, w_ref[:, 0:D])
        hidden = entry + attention
        unit, scale = normalized(hidden)
        gain = gain_ref[...]
        normed = (unit * gain).astype(bf16)
        grad_feed = jnp.where(live, cot[...].reshape(ROWS, D).astype(f32), 0.0).astype(bf16)
        feed = jnp.zeros((ROWS, D), f32)
        grad_normed = jnp.zeros((ROWS, D), f32)
        for k in range(CHUNKS):
            up = slice(D + k * D, D + (k + 1) * D)
            down = slice(D + FF + k * D, D + FF + (k + 1) * D)
            x = dot_nn(normed, w_ref[:, up])
            grad_act = dot_nt(grad_feed, w_ref[:, down])
            c0 = math.sqrt(2.0 / math.pi)
            square = x * x
            bent = jnp.tanh(x * (c0 + (c0 * 0.044715) * square))
            half = 0.5 + 0.5 * bent
            slope = half + (0.5 * x) * (1.0 - bent * bent) * (c0 + (3.0 * c0 * 0.044715) * square)
            act = (x * half).astype(bf16)
            grad_x = (slope * grad_act).astype(bf16)
            feed = feed + dot_nn(act, w_ref[:, down])
            grad_normed = grad_normed + dot_nt(grad_x, w_ref[:, up])
            acc_ref[:, up] += dot_tn(normed, grad_x)
            acc_ref[:, down] += dot_tn(act, grad_feed)
        res[...] = jnp.where(live, hidden + feed, 0.0).astype(bf16).reshape(res.shape)
        sums_ref[0:8] += fold_rows(grad_normed * unit)
        sums_ref[8:16] += fold_rows(jnp.where(live, entry * entry, 0.0))
        sums_ref[16:24] += fold_rows(jnp.where(live, attention * attention, 0.0))
        sums_ref[24:32] += fold_rows(jnp.where(live, feed * feed, 0.0))
        grad_hidden = grad_feed.astype(f32) + norm_back(grad_normed * gain, unit, scale)
        hid[...] = grad_hidden
        grad_attention = grad_hidden.astype(bf16)
        acc_ref[:, 0:D] += dot_tn(heads, grad_attention)
        gh[...] = dot_nt(grad_attention, w_ref[:, 0:D]).astype(bf16)

    @pl.when(b == pl.num_programs(0) - 1)
    def finish():
        counted = (len_ref[0] + len_ref[1]).astype(f32)
        small_ref[...] = jnp.full(small_ref.shape, counted, f32)
        for n in range(4):
            small_ref[n : n + 1] = jnp.sum(sums_ref[8 * n : 8 * n + 8], axis=0, keepdims=True)
        store_grads(plan, plan.wide_orders, grad_ref, acc_ref, outs, stage_ref, sem_ref)


def feed(plan, part, lengths, piece_rows, grad_rows, tokens, pass_rows, heads_out, cotangent, table, gain, pieces, width):
    rows = tokens[0].shape[0]
    per = ROWS // part

    def at0(b, n, r):
        return jnp.minimum(b, last_block(n[0])), 0

    def at1(b, n, r):
        return jnp.clip(b - last_block(n[0]) - 1, 0, last_block(n[1])), 0

    def both(b, n, r):
        early = b <= last_block(n[0])
        return jnp.where(early, b, at1(b, n, r)[0]), jnp.where(early, 0, 1)

    row0 = pl.BlockSpec((ROWS, D), at0)
    row1 = pl.BlockSpec((ROWS, D), at1)
    pas0 = pl.BlockSpec((1, 1, ROWS), lambda *a: at0(*a) + (0,))
    pas1 = pl.BlockSpec((1, 1, ROWS), lambda *a: at1(*a) + (0,))
    dealt = pl.BlockSpec((per, 1, part, D), lambda *a: both(*a) + (0, 0))
    local = pl.BlockSpec((None, ROWS, D), lambda *a: both(*a)[::-1] + (0,))
    grads = grad_shapes(plan, width, plan.wide_orders)
    anywhere = pl.BlockSpec(memory_space=pl.ANY)
    return pl.pallas_call(
        functools.partial(feed_kernel, plan),
        grid_spec=pltpu.PrefetchScalarGridSpec(
            num_scalar_prefetch=2,
            grid=(2 * rows // ROWS,),
            in_specs=[
                row0, row1, pas0, pas1, row0, row1, dealt,
                pl.BlockSpec((8, D), lambda *a: (0, 0)),
                pl.BlockSpec((1, D), lambda *a: (0, 0)),
                pl.BlockSpec(memory_space=pltpu.SMEM),
            ]
            + [anywhere] * len(pieces),
            out_specs=[dealt, local, local, pl.BlockSpec((8, D), lambda *a: (0, 0))] + [anywhere] * len(grads),
            scratch_shapes=[
                pltpu.VMEM((D, width), bf16),
                pltpu.VMEM((D, width), f32),
                pltpu.VMEM((32, D), f32),
                pltpu.VMEM(stage_shape(plan), bf16),
                pltpu.SemaphoreType.DMA((2,)),
            ],
        ),
        out_shape=[
            jax.ShapeDtypeStruct(cotangent.shape, bf16),
            jax.ShapeDtypeStruct((2, rows, D), bf16),
            jax.ShapeDtypeStruct((2, rows, D), f32),
            jax.ShapeDtypeStruct((8, D), f32),
        ]
        + grads,
        compiler_params=params(),
        cost_estimate=pl.CostEstimate(
            flops=2 * 6 * rows * D * width, bytes_accessed=2 * rows * D * 14 + D * width * 4, transcendentals=2 * rows * FF
        ),
        name="feed",
    )(lengths, piece_rows, tokens[0], tokens[1], pass_rows[0], pass_rows[1], heads_out[0], heads_out[1],
      cotangent, table, gain, grad_rows, *pieces)


def project_back_kernel(plan, weight, rows_back, final, len_ref, row_ref, grad_ref, tok_ref, pass_ref, g_ref, *rest):
    rest = list(rest)
    hid_ref = rest.pop(0) if rows_back else None
    table_ref, gain_ref = rest.pop(0), rest.pop(0)
    before_ref = rest.pop(0) if final else None
    many = plan.sharers if plan.paired else 1
    pieces = [rest.pop(0) for n in range(many)] if rows_back else []
    if rows_back:
        out_ref, small_ref = rest.pop(0), rest.pop(0)
    if weight and not final:
        acc_ref = rest.pop(0)
    outs = [rest.pop(0) for shape in grad_shapes(plan, 3 * D, plan.head_orders)] if final else []
    if rows_back:
        w_ref, sums_ref = rest.pop(0), rest.pop(0)
    if final:
        acc_ref, stage_ref = rest.pop(0), rest.pop(0)
    sem_ref = rest.pop(0)
    b = pl.program_id(0)

    @pl.when(b == 0)
    def clear():
        if rows_back:
            load_weight(plan, row_ref, pieces, w_ref, sem_ref.at[0])
            sums_ref[...] = jnp.zeros_like(sums_ref)
        if weight:
            acc_ref[...] = before_ref[...] if final else jnp.zeros_like(acc_ref)

    @pl.when(b <= last_block(len_ref[0]))
    def work():
        hot = onehot_rows(pass_ref[0])
        entry = tok_ref[...].astype(f32) + dot_tn(hot, table_ref[...])
        unit, scale = normalized(entry)
        gain = gain_ref[...]
        if weight:
            normed = (unit * gain).astype(bf16)
            for part in range(3):
                acc_ref[:, part * D : (part + 1) * D] += dot_tn(normed, g_ref[part])
        if rows_back:
            grad_normed = jnp.zeros((ROWS, D), f32)
            for part in range(3):
                grad_normed = grad_normed + dot_nt(g_ref[part], w_ref[:, part * D : (part + 1) * D])
            sums_ref[0:8] += fold_rows(grad_normed * unit)
            grad_entry = hid_ref[...] + norm_back(grad_normed * gain, unit, scale)
            high = grad_entry.astype(bf16)
            out_ref[...] = high
            rest_one = grad_entry - high.astype(f32)
            low = rest_one.astype(bf16)
            lower = (rest_one - low.astype(f32)).astype(bf16)
            sums_ref[8:16] += dot_nn(hot, high) + dot_nn(hot, low) + dot_nn(hot, lower)

    if rows_back:
        @pl.when(b == pl.num_programs(0) - 1)
        def sums():
            small_ref[...] = sums_ref[8:16]
            small_ref[PASSES : PASSES + 1] = jnp.sum(sums_ref[0:8], axis=0, keepdims=True)

    if final:
        @pl.when(b == pl.num_programs(0) - 1)
        def finish():
            store_grads(plan, plan.head_orders, grad_ref, acc_ref, outs, stage_ref, sem_ref)


def project_back(
    plan, weight, rows_back, which, length, piece_rows, grad_rows, tokens, pass_rows, grads, grad_hidden, table, gain,
    pieces, before=None,
):
    rows = tokens.shape[0]
    final = before is not None
    at = lambda b, n, r, g: (jnp.minimum(b, last_block(n[0])), 0)
    row = pl.BlockSpec((ROWS, D), at)
    anywhere = pl.BlockSpec(memory_space=pl.ANY)
    in_specs = [
        row,
        pl.BlockSpec((1, 1, ROWS), lambda *a: at(*a) + (0,)),
        pl.BlockSpec((3, ROWS, D), lambda *a: (0,) + at(*a)),
    ]
    operands = [length, piece_rows, grad_rows, tokens, pass_rows, grads]
    if rows_back:
        in_specs.append(pl.BlockSpec((None, ROWS, D), lambda *a: (which,) + at(*a)))
        operands.append(grad_hidden)
    in_specs += [pl.BlockSpec((8, D), lambda *a: (0, 0)), pl.BlockSpec((1, D), lambda *a: (0, 0))]
    operands += [table, gain]
    out_shape, out_specs, scratch = [], [], []
    if final:
        in_specs.append(pl.BlockSpec((D, 3 * D), lambda *a: (0, 0), pipeline_mode=pl.Buffered(1)))
        operands.append(before)
    if rows_back:
        in_specs += [anywhere] * len(pieces)
        operands += pieces
        out_shape += [jax.ShapeDtypeStruct((rows, D), bf16), jax.ShapeDtypeStruct((8, D), f32)]
        out_specs += [row, pl.BlockSpec((8, D), lambda *a: (0, 0))]
        scratch += [pltpu.VMEM((D, 3 * D), bf16), pltpu.VMEM((16, D), f32)]
    if weight and not final:
        out_shape.append(jax.ShapeDtypeStruct((D, 3 * D), f32))
        out_specs.append(pl.BlockSpec((D, 3 * D), lambda *a: (0, 0)))
    if final:
        shapes = grad_shapes(plan, 3 * D, plan.head_orders)
        out_shape += shapes
        out_specs += [anywhere] * len(shapes)
        scratch += [pltpu.VMEM((D, 3 * D), f32), pltpu.VMEM(stage_shape(plan), bf16)]
    return pl.pallas_call(
        functools.partial(project_back_kernel, plan, weight, rows_back, final),
        grid_spec=pltpu.PrefetchScalarGridSpec(
            num_scalar_prefetch=3,
            grid=(rows // ROWS,),
            in_specs=in_specs,
            out_specs=out_specs,
            scratch_shapes=scratch + [pltpu.SemaphoreType.DMA((2,))],
        ),
        out_shape=out_shape,
        compiler_params=params(),
        cost_estimate=pl.CostEstimate(
            flops=2 * (weight + rows_back) * rows * D * 3 * D, bytes_accessed=rows * D * 14 + D * D * 6, transcendentals=0
        ),
        name="project_back",
    )(*operands)


def pick_kernel(index_ref, in_ref, out_ref, sem_ref):
    copies = [
        pltpu.make_async_copy(in_ref.at[index_ref[n]], out_ref.at[n], sem_ref) for n in range(out_ref.shape[0])
    ]
    for copy in copies:
        copy.start()
    for copy in copies:
        copy.wait()


def pick(index, blocks):
    shape = index.shape + blocks.shape[1:]
    return pl.pallas_call(
        pick_kernel,
        grid_spec=pltpu.PrefetchScalarGridSpec(
            num_scalar_prefetch=1,
            grid=(1,),
            in_specs=[pl.BlockSpec(memory_space=pl.ANY)],
            out_specs=pl.BlockSpec(shape, lambda b, n: (0, 0, 0)),
            scratch_shapes=[pltpu.SemaphoreType.DMA],
        ),
        out_shape=jax.ShapeDtypeStruct(shape, blocks.dtype),
        compiler_params=params(),
        cost_estimate=pl.CostEstimate(flops=0, bytes_accessed=4 * math.prod(shape), transcendentals=0),
        name="pick",
    )(index, blocks)


def settle_kernel(index_ref, *refs):
    arrays, out_ref = refs[:-1], refs[-1]
    first = pl.program_id(0) * out_ref.shape[0]
    rows = out_ref.shape[1]
    at = lax.broadcasted_iota(jnp.int32, (rows, 1), 0)
    for n in range(out_ref.shape[0]):
        live = at < index_ref[2, first + n]
        source, late = index_ref[1, first + n], index_ref[0, first + n]
        if len(arrays) == 1:
            found = arrays[0][2 * source + late]
        else:
            found = jnp.where(late == 0, arrays[0][source], arrays[1][source])
        out_ref[n] = jnp.where(live, found.astype(f32), 0.0)


def settle(index, *arrays):
    many = index.shape[1]
    step = 4
    shape = arrays[0].shape
    whole = pl.BlockSpec(shape, lambda b, n: (0, 0, 0), pipeline_mode=pl.Buffered(1))
    return pl.pallas_call(
        settle_kernel,
        grid_spec=pltpu.PrefetchScalarGridSpec(
            num_scalar_prefetch=1,
            grid=(many // step,),
            in_specs=[whole] * len(arrays),
            out_specs=pl.BlockSpec((step,) + shape[1:], lambda b, n: (b, 0, 0)),
        ),
        out_shape=jax.ShapeDtypeStruct((many,) + shape[1:], f32),
        compiler_params=params(),
        cost_estimate=pl.CostEstimate(flops=0, bytes_accessed=6 * many * math.prod(shape[1:]), transcendentals=0),
        name="settle",
    )(index, *arrays)


def after(values, *others):
    return lax.optimization_barrier((values, others))[0]


def swap(blocks):
    return lax.all_to_all(blocks, "dp", split_axis=0, concat_axis=0, tiled=True)


def per_device(
    groups,
    width_all,
    tokens,
    passes,
    lengths,
    dealing,
    pass_table,
    gain_first,
    to_heads,
    from_heads,
    gain_second,
    expand,
    shrink,
    cotangent,
):
    axes = ("dp", "fsdp")
    slots, part, unused_width = tokens.shape
    seq_len = part * groups
    order = jnp.arange(slots, dtype=jnp.int32)
    here = lax.axis_index("dp")
    ordering = dealing[0, 0]
    sizes = lengths[0]

    ahead = (sizes[None, :] > sizes[:, None]) | (
        (sizes[None, :] == sizes[:, None]) & (order[None, :] < order[:, None])
    )
    rank = jnp.sum(ahead.astype(jnp.int32), axis=1)
    ranked = jnp.sum(jnp.where(rank[None, :] == order[:, None], order[None, :], 0), axis=1)
    place = jnp.sum(jnp.where(ordering[None, :] == order[:, None], order[None, :], 0), axis=1)
    early_seqs = ranked[:groups]
    late_seqs = ranked[groups:][::-1]
    from_early = jnp.sum(jnp.where(early_seqs[:, None] == order[None, :], place[None, :], 0), axis=1)
    from_late = jnp.sum(jnp.where(late_seqs[:, None] == order[None, :], place[None, :], 0), axis=1)
    slot_rank = jnp.sum(jnp.where(ordering[:, None] == order[None, :], rank[None, :], 0), axis=1)
    slot_size = jnp.sum(jnp.where(ordering[:, None] == order[None, :], sizes[None, :], 0), axis=1)
    is_late = (slot_rank >= groups).astype(jnp.int32)
    source = jnp.where(is_late == 1, slots - 1 - slot_rank, slot_rank)
    back_index = jnp.stack([is_late, source, slot_size - here * part])
    my_seqs = jnp.stack([early_seqs[here], late_seqs[here]])
    my_sizes = jnp.sum(jnp.where(my_seqs[:, None] == order[None, :], sizes[None, :], 0), axis=1)

    row_count = to_heads.shape[0]
    narrow = jnp.concatenate(
        [
            from_heads,
            expand.reshape(row_count, D, CHUNKS).transpose(0, 2, 1).reshape(row_count, FF),
            shrink.reshape(row_count, CHUNKS * D),
        ],
        axis=1,
    )
    plan = Plan(groups, width_all // groups, row_count)
    index_here = here * (width_all // groups) + lax.axis_index("fsdp")
    my_passes = [passes[my_seqs[m]].reshape(seq_len // ROWS, 1, ROWS) for m in range(2)]
    one_size = [my_sizes[m : m + 1] for m in range(2)]
    table = jnp.zeros((8, D), bf16).at[:PASSES].set(pass_table)
    gain_one = gain_first.astype(f32).reshape(1, D)
    gain_two = gain_second.astype(f32).reshape(1, D)

    pairs_index = jnp.stack([from_early, from_late], axis=1).reshape(slots)
    picked = [pick(from_early, tokens), pick(from_late, tokens), pick(pairs_index, cotangent)]
    if plan.paired:
        piece_rows = plan.piece_rows(index_here)
        wide_rows = plan.grad_rows(index_here, plan.wide_orders)
        head_rows = plan.grad_rows(index_here, plan.head_orders)
        head_far = plan.gather(to_heads[None], plan.far)
        head_near = plan.gather(head_far, [plan.near])
        wide_one = plan.gather(after(narrow, head_far)[None], plan.far[:1])
        ready = (my_passes, one_size, piece_rows, table, gain_one)
        tokens0 = swap(after(picked[0], head_near, wide_one, ready))
        head_pieces = plan.gather_core(plan.gather_x(head_near))
    else:
        piece_rows = wide_rows = head_rows = jnp.zeros((1,), jnp.int32)
        head_pieces = (lax.all_gather(to_heads, axes, axis=0, tiled=True),)
        wide_pieces = (lax.all_gather(narrow, axes, axis=0, tiled=True),)
        tokens0 = swap(picked[0])
        wide_far = wide_pieces

    def forward(m, *gate):
        return project(
            plan, after(one_size[m], gate), piece_rows, my_tokens[m], my_passes[m], table, gain_one, head_pieces
        )

    def mix(m, *gate):
        return attend(after(one_size[m], gate), projected[m])

    def mix_back(m, first, before, *gate):
        choice = jnp.stack([my_sizes[m], jnp.int32(m), jnp.int32(first)])
        return attend_back(after(choice, gate), projected[m], heads_out[m], grad_heads, lse[m], before)

    def back(m, weight, rows_back, *gate, before=None):
        return project_back(
            plan, weight, rows_back, m, after(one_size[m], gate), piece_rows, head_rows, my_tokens[m], my_passes[m],
            grad_parts[m], grad_hidden, table, gain_one, head_pieces, before,
        )

    def send_back(rows, *gate):
        return swap(after(rows, gate).reshape(groups, part, D))

    projected, heads_out, lse, grad_parts = [None, None], [None, None], [None, None], [None, None]
    my_tokens = [tokens0.reshape(seq_len, D)]
    projected[0] = forward(0)
    if plan.paired:
        wide_far = plan.gather(wide_one, plan.far[1:], head_pieces, projected[0])
        cut = first_part(wide_far.shape[-1], plan.wide_orders)
    tokens1 = swap(after(picked[1], tokens0, picked[2], wide_far))
    my_tokens.append(tokens1.reshape(seq_len, D))
    heads_out[0], lse[0] = mix(0, wide_far)
    if plan.paired:
        first = plan.gather_near({0: wide_far[:, :, :cut]}, (), lse[0])
        second = plan.gather_x(wide_far[:, :, cut:], ())
        ready = (first, second)
    else:
        ready = ()
    my_grads = swap(after(picked[2].reshape(groups, 2, part, D), tokens1, lse[0], ready))
    projected[1] = forward(1, lse[0])
    if plan.paired:
        first = plan.gather_x(first[0])
        second = plan.gather_near(second, lse[0], projected[1])
    heads_out[1], lse[1] = mix(1)
    if plan.paired:
        wide_pieces = plan.gather_core(first, lse[1]) + plan.gather_core(second, lse[1])

    res, grad_heads, grad_hidden, feed_small, *wide_grads = feed(
        plan, part, my_sizes, piece_rows, wide_rows, my_tokens, my_passes, heads_out, my_grads, table, gain_two,
        wide_pieces, D + 2 * FF,
    )

    def begin(grads):
        if not plan.paired:
            return lax.psum_scatter(grads[0], axes, scatter_dimension=0, tiled=True).astype(f32)
        return [grads[n : n + 2] for n in range(0, len(grads), 2)]

    def advance(state, stage, gate, late):
        return plan.reduce_stage(state, plan.wide_orders, stage, (gate,), (late,)) if plan.paired else state

    half = HEADS // 4
    space = jax.ShapeDtypeStruct((3, seq_len, D), bf16)
    wide0 = begin(wide_grads)
    result = swap(res)
    some = mix_back(0, 0, blank(one_size[0], space))
    wide1 = advance(wide0, 0, (), some)
    grad_parts[0] = mix_back(0, half, some, wide1)
    entry0, small0, head_sum = back(0, True, True)
    wide2 = advance(wide1, 1, some, entry0)
    moved0 = send_back(entry0, result)
    some = mix_back(1, 0, blank(one_size[1], space), entry0, wide2, result)
    wide3 = advance(wide2, 2, entry0, some)
    grad_parts[1] = mix_back(1, half, some, wide3)
    entry1, small1 = back(1, False, True)
    wide_owned = advance(wide3, 3, some, entry1)
    moved1 = send_back(entry1, moved0, wide_owned)
    totals = jnp.concatenate([small0 + small1, feed_small], axis=0)
    head_grads = back(1, True, False, entry1, moved0, before=head_sum)
    output = settle(after(back_index, head_grads[:1]), result.reshape(slots, part, D))
    head_state = begin(head_grads)
    if plan.paired:
        orders = plan.head_orders
        totals = plan.total_stage(totals, orders[0][0], (), head_grads[:1])
        head_state = plan.reduce_stage(head_state, orders, 0, (wide_owned,), (output,))
        totals = plan.total_stage(totals, orders[0][1])
        head_state = plan.reduce_stage(head_state, orders, 1, (totals,), (moved1,))
        totals = plan.total_stage(totals, orders[0][2], (head_state,))
        head_owned = plan.reduce_stage(head_state, orders, 2)[0]
        wide_owned = wide_owned[0]
    else:
        totals = lax.psum(totals, axes)
        head_owned = head_state
    root_squares = jnp.sqrt(jnp.sum(totals[9:12], axis=1) / (totals[12, 0] * D))

    grad_expand = wide_owned[:, D : D + FF].reshape(row_count, CHUNKS, D).transpose(0, 2, 1)
    return (
        output,
        settle(back_index, moved0, moved1),
        totals[:PASSES],
        totals[PASSES],
        head_owned,
        wide_owned[:, :D],
        totals[8],
        grad_expand.reshape(row_count, FF),
        wide_owned[:, D + FF :].reshape(row_count * CHUNKS, D),
        root_squares,
    )


def solution(mesh):
    groups = mesh.shape["dp"]
    weight_spec = P(("dp", "fsdp"), None)
    block_spec = P("fsdp", "dp", None)
    in_specs = (
        block_spec,
        P("fsdp", None),
        P("fsdp", None),
        P("dp", "fsdp", None),
        P(),
        P(),
        weight_spec,
        weight_spec,
        P(),
        weight_spec,
        weight_spec,
        block_spec,
    )
    out_specs = (
        block_spec,
        block_spec,
        P(),
        P(),
        weight_spec,
        weight_spec,
        P(),
        weight_spec,
        weight_spec,
        P(),
    )
    body = functools.partial(per_device, groups, groups * mesh.shape["fsdp"])
    return jax.shard_map(body, mesh=mesh, in_specs=in_specs, out_specs=out_specs, check_vma=False)
```

```python
import math
import functools

import jax
import jax.numpy as jnp
from jax import lax
from jax.experimental import pallas as pl
from jax.experimental.pallas import tpu as pltpu
from jax.sharding import PartitionSpec as P

D = 768
HEADS = 12
HEAD = 64
FF = 3072
PASSES = 5
EPS = 1e-05
ROWS = 256
CHUNKS = FF // D
VMEM_MOST = 64000 * 1024

f32 = jnp.float32
bf16 = jnp.bfloat16


def dot_nn(a, b):
    return lax.dot_general(a, b, (((1,), (0,)), ((), ())), preferred_element_type=f32)


def dot_nt(a, b):
    return lax.dot_general(a, b, (((1,), (1,)), ((), ())), preferred_element_type=f32)


def dot_tn(a, b):
    return lax.dot_general(a, b, (((0,), (0,)), ((), ())), preferred_element_type=f32)


def params(**more):
    return pltpu.CompilerParams(vmem_limit_bytes=VMEM_MOST, **more)


def normalized(values):
    centred = values - jnp.mean(values, axis=-1, keepdims=True)
    spread = jnp.mean(centred * centred, axis=-1, keepdims=True)
    scale = lax.rsqrt(spread + EPS)
    return centred * scale, scale


def norm_back(grad_unit, unit, scale):
    first = jnp.mean(grad_unit, axis=-1, keepdims=True)
    second = jnp.mean(grad_unit * unit, axis=-1, keepdims=True)
    return scale * (grad_unit - first - unit * second)


def onehot_rows(pass_row):
    ids = lax.broadcasted_iota(jnp.int32, (8, pass_row.shape[-1]), 0)
    return (ids == pass_row).astype(f32).astype(bf16)


def fold_rows(values):
    rows, width = values.shape
    return jnp.sum(values.reshape(rows // 8, 8, width), axis=0)


def last_block(length):
    return lax.div(length + (ROWS - 1), ROWS) - 1


def bits_of(count):
    return count.bit_length() - 1


class Plan:
    def __init__(self, groups, sharers, rows):
        self.groups, self.sharers, self.rows = groups, sharers, rows
        self.count = groups * sharers
        self.paired = rows % 8 == 0 and self.count & (self.count - 1) == 0 and sharers >= 4 and groups >= 4
        core, *over_x = [1 << bit for bit in range(bits_of(sharers))]
        near, *far = [sharers << bit for bit in range(bits_of(groups))]
        self.core, self.over_x, self.near, self.far = core, over_x, near, far[::-1]
        self.wide_orders = ([[core], over_x, [near], far], [[core], [near], over_x, far])
        self.head_orders = ([[core], over_x + [near], far],)

    def exchange(self, values, bits):
        pairs = [(i, i ^ bits) for i in range(self.count)]
        return lax.ppermute(values, ("dp", "fsdp"), pairs)

    def gather(self, held, masks, gate=(), late=()):
        for bits in masks:
            held = jnp.concatenate([after(held, late), self.exchange(after(held, gate), bits)], axis=0)
        return held

    def gather_x(self, held, *gate):
        pieces = {0: held}
        for bits in self.over_x[::-1]:
            for name in list(pieces):
                pieces[name | bits] = self.exchange(after(pieces[name], gate), bits)
        return pieces

    def gather_near(self, pieces, gate=(), late=()):
        return {name: self.gather(held, [self.near], gate, late) for name, held in pieces.items()}

    def gather_core(self, pieces, *gate):
        found = dict(pieces)
        for name in pieces:
            found[name | self.core] = self.exchange(after(pieces[name], gate), self.core)
        return tuple(found[name] for name in range(self.sharers))

    def piece_rows(self, here):
        masks = self.far + [self.near]
        found = []
        for f in range(self.sharers):
            for n in range(self.groups):
                rel = f | ways_bits(masks, n)
                found.append((here ^ rel) * self.rows)
        return jnp.stack(found).astype(jnp.int32)

    def grad_rows(self, here, orders):
        found = []
        for order in orders:
            for place in range(self.count):
                rel, left = 0, self.count
                for masks in order:
                    left >>= len(masks)
                    rel |= ways_bits(masks, (place // left) % (1 << len(masks)))
                found.append((here ^ rel) * self.rows)
        return jnp.stack(found).astype(jnp.int32)

    def total_stage(self, values, masks, gate=(), late=()):
        found = [after(values, late)]
        found += [self.exchange(after(values, gate), ways_bits(masks, way)) for way in range(1, 1 << len(masks))]
        while len(found) > 1:
            found = [found[k] + found[k + 1] for k in range(0, len(found), 2)]
        return found[0]

    def reduce_stage(self, states, orders, stage, gate=(), late=()):
        sums = []
        for ways, order in zip(states, orders):
            sums.append(
                [after(ways[0], late)]
                + [
                    self.exchange(after(ways[n], gate), ways_bits(order[stage], n))
                    for n in range(1, len(ways))
                ]
            )
        if stage == len(orders[0]) - 1:
            return [sum(part.astype(f32) for part in parts)[0] for parts in sums]
        ways = 1 << len(orders[0][stage + 1])
        if stage == len(orders[0]) - 2:
            return [merge(sums, ways)]
        return [merge([parts], ways) for parts in sums]


def ways_bits(masks, way):
    return sum(bits for n, bits in enumerate(masks) if (way >> n) & 1)


def merge_kernel(widths, many, ways, *refs):
    ins, outs = refs[: len(widths) * many * ways], refs[len(widths) * many * ways :]
    for way in range(ways):
        first = 0
        for k, width in enumerate(widths):
            views = [ins[(k * many + n) * ways + way] for n in range(many)]
            total = views[0][...].astype(f32)
            for view in views[1:]:
                total = total + view[...].astype(f32)
            outs[way][:, :, first : first + width] = total.astype(bf16)
            first += width


def merge(groups, ways):
    blocks, rows, unused = groups[0][0].shape
    widths = [parts[0].shape[2] for parts in groups]
    share = blocks // ways
    steps = min(share, 4)

    def view(way, width):
        return pl.BlockSpec((share // steps, rows, width), lambda b: (b + way * steps, 0, 0))

    out = jax.ShapeDtypeStruct((share, rows, sum(widths)), bf16)
    many = len(groups[0])
    size = blocks * rows * sum(widths)
    return pl.pallas_call(
        functools.partial(merge_kernel, widths, many, ways),
        grid=(steps,),
        in_specs=[view(way, width) for width in widths for n in range(many) for way in range(ways)],
        out_specs=[view(0, sum(widths))] * ways,
        out_shape=[out] * ways,
        compiler_params=params(),
        cost_estimate=pl.CostEstimate(flops=many * size, bytes_accessed=(2 + 2 * many) * size, transcendentals=0),
        name="merge",
    )(*[part for parts in groups for part in parts for way in range(ways)])


def load_weight(plan, rows_ref, pieces, weight_ref, sem_ref):
    copies = []
    if not plan.paired:
        copies.append(pltpu.make_async_copy(pieces[0], weight_ref, sem_ref))
    first = 0
    for k in range(0, len(pieces) if plan.paired else 0, plan.sharers):
        width = pieces[k].shape[-1]
        for f in range(plan.sharers):
            for n in range(plan.groups):
                at = pl.multiple_of(rows_ref[f * plan.groups + n], 8)
                target = weight_ref.at[pl.ds(at, plan.rows), first : first + width]
                copies.append(pltpu.make_async_copy(pieces[k + f].at[n], target, sem_ref))
        first += width
    for copy in copies:
        copy.start()
    for copy in copies:
        copy.wait()


def grad_shapes(plan, width, orders):
    if not plan.paired:
        return [jax.ShapeDtypeStruct((D, width), bf16)]
    half = plan.count // 2
    cut = first_part(width, orders)
    return [jax.ShapeDtypeStruct((half, plan.rows, w), bf16) for w in (cut, cut, width - cut, width - cut) if w > 0]


def first_part(width, orders):
    return (width // D + 1) // 2 * D if len(orders) == 2 else width


def stage_shape(plan):
    return (2, plan.count, plan.rows, D) if plan.paired else (2, D, D)


def store_grads(plan, orders, rows_ref, acc_ref, outs, stage_ref, sem_ref):
    width, step = acc_ref.shape[1], D
    cut = first_part(width, orders)
    half = plan.count // 2
    waiting = []
    for n in range(width // step):
        slot = n % 2
        cols = slice(n * step, (n + 1) * step)
        if len(waiting) == 2:
            for copy in waiting.pop(0):
                copy.wait()
        if not plan.paired:
            stage_ref[slot] = acc_ref[:, cols].astype(bf16)
            copies = [pltpu.make_async_copy(stage_ref.at[slot], outs[0].at[:, cols], sem_ref.at[slot])]
        else:
            late = n * step >= cut
            base = plan.count if late else 0
            start = n * step - (cut if late else 0)

            def fill(place, carry):
                at = pl.multiple_of(rows_ref[base + place], 8)
                stage_ref[slot, place] = acc_ref[pl.ds(at, plan.rows), cols].astype(bf16)
                return carry

            lax.fori_loop(0, plan.count, fill, 0, unroll=2)
            keep, send = outs[2:4] if late else outs[0:2]
            there = slice(start, start + step)
            copies = [
                pltpu.make_async_copy(stage_ref.at[slot, 0:half], keep.at[:, :, there], sem_ref.at[slot]),
                pltpu.make_async_copy(stage_ref.at[slot, half:], send.at[:, :, there], sem_ref.at[slot]),
            ]
        for copy in copies:
            copy.start()
        waiting.append(copies)
    for copies in waiting:
        for copy in copies:
            copy.wait()


def project_kernel(plan, len_ref, row_ref, tok_ref, pass_ref, table_ref, gain_ref, *rest):
    pieces, (out_ref, w_ref, sem_ref) = rest[:-3], rest[-3:]

    @pl.when(pl.program_id(0) == 0)
    def load():
        load_weight(plan, row_ref, pieces, w_ref, sem_ref)

    @pl.when(pl.program_id(0) <= last_block(len_ref[0]))
    def work():
        hot = onehot_rows(pass_ref[0])
        entry = tok_ref[...].reshape(ROWS, D).astype(f32) + dot_tn(hot, table_ref[...])
        unit, unused = normalized(entry)
        normed = (unit * gain_ref[...]).astype(bf16)
        for part in range(3):
            out_ref[part] = dot_nn(normed, w_ref[:, part * D : (part + 1) * D]).astype(bf16)


def dealt_spec(part, at):
    return pl.BlockSpec((ROWS // part, 1, part, D), lambda *a: at(*a) + (0, 0))


def project(plan, which, length, piece_rows, tokens, pass_rows, table, gain, pieces):
    part = tokens.shape[2]
    rows = tokens.shape[0] * part
    at = lambda b, n, r: (jnp.minimum(b, last_block(n[0])), 0)
    return pl.pallas_call(
        functools.partial(project_kernel, plan),
        grid_spec=pltpu.PrefetchScalarGridSpec(
            num_scalar_prefetch=2,
            grid=(rows // ROWS,),
            in_specs=[
                dealt_spec(part, lambda *a: (at(*a)[0], which)),
                pl.BlockSpec((1, 1, ROWS), lambda b, n, r: at(b, n, r) + (0,)),
                pl.BlockSpec((8, D), lambda b, n, r: (0, 0)),
                pl.BlockSpec((1, D), lambda b, n, r: (0, 0)),
            ]
            + [pl.BlockSpec(memory_space=pl.ANY)] * len(pieces),
            out_specs=pl.BlockSpec((3, ROWS, D), lambda b, n, r: (0,) + at(b, n, r)),
            scratch_shapes=[pltpu.VMEM((D, 3 * D), bf16), pltpu.SemaphoreType.DMA],
        ),
        out_shape=jax.ShapeDtypeStruct((3, rows, D), bf16),
        compiler_params=params(),
        cost_estimate=pl.CostEstimate(
            flops=2 * rows * D * 3 * D, bytes_accessed=rows * D * 8 + D * D * 6, transcendentals=0
        ),
        name="project",
    )(length, piece_rows, tokens, pass_rows, table, gain, *pieces)


def attend_kernel(len_ref, p_ref, out_ref, lse_ref):
    blocks = p_ref.shape[1] // ROWS
    lane = lax.broadcasted_iota(jnp.int32, (ROWS, 128), 1)
    first_head = lane < HEAD
    here = lax.broadcasted_iota(jnp.int32, (ROWS, ROWS), 0)
    there = lax.broadcasted_iota(jnp.int32, (ROWS, ROWS), 1)
    allowed = there <= here
    for i in range(blocks):
        rows = slice(i * ROWS, (i + 1) * ROWS)

        @pl.when(i * ROWS < len_ref[0])
        def work():
            query = p_ref[0, rows, :] * jnp.asarray(1.0 / math.sqrt(HEAD), bf16)
            found = []
            for head in range(2):
                mine = first_head if head == 0 else jnp.logical_not(first_head)
                q = jnp.where(mine, query, jnp.zeros_like(query))
                diag = dot_nt(q, p_ref[1, rows, :])
                diag = jnp.where(allowed, diag, -1e30)
                largest = jnp.max(diag, axis=-1, keepdims=True)
                if i > 0:
                    before = dot_nt(q, p_ref[1, : i * ROWS, :])
                    largest = jnp.maximum(largest, jnp.max(before, axis=-1, keepdims=True))
                diag = jnp.exp(diag - largest)
                total = jnp.sum(diag, axis=-1, keepdims=True)
                out = dot_nn(diag.astype(bf16), p_ref[2, rows, :])
                if i > 0:
                    before = jnp.exp(before - largest)
                    total = total + jnp.sum(before, axis=-1, keepdims=True)
                    out = out + dot_nn(before.astype(bf16), p_ref[2, : i * ROWS, :])
                found.append(out * (1.0 / total))
                lse = jnp.broadcast_to(largest + jnp.log(total), (ROWS, 128))
                lse_ref[0, head : head + 1, rows] = lse.T[0:1]
            out_ref[rows, :] = jnp.where(first_head, found[0], found[1]).astype(bf16)


def attend(length, projected):
    rows = projected.shape[1]
    pairs = HEADS // 2
    return pl.pallas_call(
        attend_kernel,
        grid_spec=pltpu.PrefetchScalarGridSpec(
            num_scalar_prefetch=1,
            grid=(pairs,),
            in_specs=[pl.BlockSpec((3, rows, 128), lambda h, n: (0, 0, h))],
            out_specs=[
                pl.BlockSpec((rows, 128), lambda h, n: (0, h)),
                pl.BlockSpec((1, 8, rows), lambda h, n: (h, 0, 0)),
            ],
        ),
        out_shape=[
            jax.ShapeDtypeStruct((rows, D), bf16),
            jax.ShapeDtypeStruct((pairs, 8, rows), f32),
        ],
        compiler_params=params(),
        cost_estimate=pl.CostEstimate(
            flops=2 * rows * rows * D, bytes_accessed=rows * D * 8, transcendentals=HEADS * rows * rows // 2
        ),
        name="attend",
    )(length, projected)


def attend_back_kernel(len_ref, p_ref, o_ref, g_ref, lse_ref, out_ref, dk_ref, dv_ref, kz_ref, vz_ref, kt_ref):
    blocks = p_ref.shape[1] // ROWS
    scaling = 1.0 / math.sqrt(HEAD)
    lane = lax.broadcasted_iota(jnp.int32, (ROWS, 128), 1)
    first_head = lane < HEAD
    row8 = lax.broadcasted_iota(jnp.int32, (8, 128), 0)
    lane8 = lax.broadcasted_iota(jnp.int32, (8, 128), 1)
    chooser = (lax.div(lane8, HEAD) == row8).astype(f32)
    key_at = lax.broadcasted_iota(jnp.int32, (2, ROWS, ROWS), 1)
    row_at = lax.broadcasted_iota(jnp.int32, (2, ROWS, ROWS), 2)
    allowed = (key_at <= row_at).reshape(2 * ROWS, ROWS)
    for i in range(blocks):
        rows = slice(i * ROWS, (i + 1) * ROWS)
        two = slice(2 * i * ROWS, 2 * (i + 1) * ROWS)

        @pl.when(i * ROWS < len_ref[0])
        def work():
            dk_ref[two, :] = jnp.zeros((2 * ROWS, 128), f32)
            dv_ref[two, :] = jnp.zeros((2 * ROWS, 128), f32)
            key, value = p_ref[1, rows, :], p_ref[2, rows, :]
            zero = jnp.zeros_like(key)
            k2 = jnp.concatenate([jnp.where(first_head, key, zero), jnp.where(first_head, zero, key)], axis=0)
            kz_ref[two, :] = k2
            kt_ref[:, two] = k2.T
            vz_ref[two, :] = jnp.concatenate([jnp.where(first_head, value, zero), jnp.where(first_head, zero, value)], axis=0)
            query = p_ref[0, rows, :] * jnp.asarray(scaling, bf16)
            grad = g_ref[rows, :]
            product = grad.astype(f32) * o_ref[rows, :].astype(f32)
            delta = lax.dot_general(chooser, product, (((1,), (1,)), ((), ())), precision=lax.Precision.HIGHEST, preferred_element_type=f32)
            def both(a, b):
                return jnp.concatenate([jnp.broadcast_to(a, (ROWS, ROWS)), jnp.broadcast_to(b, (ROWS, ROWS))], axis=0)
            lse2 = both(lse_ref[0, 0:1, rows], lse_ref[0, 1:2, rows])
            delta2 = both(delta[0:1], delta[1:2])
            dqt = jnp.zeros((128, ROWS), f32)
            for j in range(i + 1):
                cols = slice(2 * j * ROWS, 2 * (j + 1) * ROWS)
                prob = jnp.exp(dot_nt(kz_ref[cols, :], query) - lse2)
                if i == j:
                    prob = jnp.where(allowed, prob, 0.0)
                ds = (prob * (dot_nt(vz_ref[cols, :], grad) - delta2)).astype(bf16)
                dv_ref[cols, :] += dot_nn(prob.astype(bf16), grad)
                dk_ref[cols, :] += dot_nn(ds, query)
                dqt = dqt + dot_nn(kt_ref[:, cols], ds)
            out_ref[0, rows, :] = (dqt * scaling).T.astype(bf16)
    for i in range(blocks):
        rows = slice(i * ROWS, (i + 1) * ROWS)
        a = slice(2 * i * ROWS, (2 * i + 1) * ROWS); b = slice((2 * i + 1) * ROWS, 2 * (i + 1) * ROWS)

        @pl.when(i * ROWS < len_ref[0])
        def finish():
            out_ref[1, rows, :] = jnp.where(first_head, dk_ref[a, :], dk_ref[b, :]).astype(bf16)
            out_ref[2, rows, :] = jnp.where(first_head, dv_ref[a, :], dv_ref[b, :]).astype(bf16)


def blank_kernel(ready_ref, out_ref):
    pass


def blank(ready, shape):
    return pl.pallas_call(
        blank_kernel,
        in_specs=[pl.BlockSpec(memory_space=pltpu.SMEM)],
        out_specs=pl.BlockSpec(memory_space=pl.ANY),
        out_shape=shape,
        name="blank",
    )(ready)


def attend_back(choice, projected, heads_out, grad_heads, lse, before):
    rows = projected.shape[1]
    pairs = HEADS // 2
    cols = lambda h, n: (0, n[2] + h)
    blocks = lambda h, n: (0, 0, n[2] + h)

    def kernel(n, p, o, g, l, unused, *rest):
        attend_back_kernel(n, p, o, g, l, *rest)

    return pl.pallas_call(
        kernel,
        grid_spec=pltpu.PrefetchScalarGridSpec(
            num_scalar_prefetch=1,
            grid=(pairs // 2,),
            in_specs=[
                pl.BlockSpec((3, rows, 128), blocks),
                pl.BlockSpec((rows, 128), cols),
                pl.BlockSpec((None, rows, 128), lambda h, n: (n[1], 0, n[2] + h)),
                pl.BlockSpec((1, 8, rows), lambda h, n: (n[2] + h, 0, 0)),
                pl.BlockSpec(memory_space=pl.ANY),
            ],
            out_specs=pl.BlockSpec((3, rows, 128), blocks),
            scratch_shapes=[
                pltpu.VMEM((2 * rows, 128), f32),
                pltpu.VMEM((2 * rows, 128), f32),
                pltpu.VMEM((2 * rows, 128), bf16),
                pltpu.VMEM((2 * rows, 128), bf16),
                pltpu.VMEM((128, 2 * rows), bf16),
            ],
        ),
        out_shape=jax.ShapeDtypeStruct((3, rows, D), bf16),
        input_output_aliases={5: 0},
        compiler_params=params(),
        cost_estimate=pl.CostEstimate(
            flops=3 * rows * rows * D, bytes_accessed=rows * D * 8, transcendentals=HEADS * rows * rows // 4
        ),
        name="attend_back",
    )(choice, projected, heads_out, grad_heads, lse, before)


def feed_kernel(plan, len_ref, row_ref, *refs):
    tok, pass0, pass1, ho0, ho1, cot, table_ref, gain_ref = refs[:8]
    many = plan.sharers if plan.paired else 1
    grad_ref, pieces, refs = refs[8], refs[9 : 9 + many], refs[9 + many :]
    res, gh, hid, small_ref = refs[:4]
    outs, (w_ref, acc_ref, sums_ref, stage_ref, sem_ref) = refs[4:-5], refs[-5:]
    b = pl.program_id(0)
    many0 = last_block(len_ref[0]) + 1
    many1 = last_block(len_ref[1]) + 1
    early = b < many0

    @pl.when(b == 0)
    def clear():
        load_weight(plan, row_ref, pieces, w_ref, sem_ref.at[0])
        acc_ref[...] = jnp.zeros_like(acc_ref)
        sums_ref[...] = jnp.zeros_like(sums_ref)

    @pl.when(b < many0 + many1)
    def block():
        hot = onehot_rows(jnp.where(early, pass0[0], pass1[0]))
        entry = tok[...].reshape(ROWS, D).astype(f32) + dot_tn(hot, table_ref[...])
        at = jnp.where(early, b, b - many0) * ROWS + lax.broadcasted_iota(jnp.int32, (ROWS, 1), 0)
        live = at < jnp.where(early, len_ref[0], len_ref[1])
        heads = jnp.where(early, ho0[...], ho1[...])
        attention = dot_nn(heads, w_ref[:, 0:D])
        hidden = entry + attention
        unit, scale = normalized(hidden)
        gain = gain_ref[...]
        normed = (unit * gain).astype(bf16)
        grad_feed = jnp.where(live, cot[...].reshape(ROWS, D).astype(f32), 0.0).astype(bf16)
        feed = jnp.zeros((ROWS, D), f32)
        grad_normed = jnp.zeros((ROWS, D), f32)
        for k in range(CHUNKS):
            up = slice(D + k * D, D + (k + 1) * D)
            down = slice(D + FF + k * D, D + FF + (k + 1) * D)
            x = dot_nn(normed, w_ref[:, up])
            grad_act = dot_nt(grad_feed, w_ref[:, down])
            c0 = math.sqrt(2.0 / math.pi)
            square = x * x
            bent = jnp.tanh(x * (c0 + (c0 * 0.044715) * square))
            half = 0.5 + 0.5 * bent
            slope = half + (0.5 * x) * (1.0 - bent * bent) * (c0 + (3.0 * c0 * 0.044715) * square)
            act = (x * half).astype(bf16)
            grad_x = (slope * grad_act).astype(bf16)
            feed = feed + dot_nn(act, w_ref[:, down])
            grad_normed = grad_normed + dot_nt(grad_x, w_ref[:, up])
            acc_ref[:, up] += dot_tn(normed, grad_x)
            acc_ref[:, down] += dot_tn(act, grad_feed)
        res[...] = jnp.where(live, hidden + feed, 0.0).astype(bf16).reshape(res.shape)
        sums_ref[0:8] += fold_rows(grad_normed * unit)
        sums_ref[8:16] += fold_rows(jnp.where(live, entry * entry, 0.0))
        sums_ref[16:24] += fold_rows(jnp.where(live, attention * attention, 0.0))
        sums_ref[24:32] += fold_rows(jnp.where(live, feed * feed, 0.0))
        grad_hidden = grad_feed.astype(f32) + norm_back(grad_normed * gain, unit, scale)
        hid[...] = grad_hidden
        grad_attention = grad_hidden.astype(bf16)
        acc_ref[:, 0:D] += dot_tn(heads, grad_attention)
        gh[...] = dot_nt(grad_attention, w_ref[:, 0:D]).astype(bf16)

    @pl.when(b == pl.num_programs(0) - 1)
    def finish():
        counted = (len_ref[0] + len_ref[1]).astype(f32)
        small_ref[...] = jnp.full(small_ref.shape, counted, f32)
        for n in range(4):
            small_ref[n : n + 1] = jnp.sum(sums_ref[8 * n : 8 * n + 8], axis=0, keepdims=True)
        store_grads(plan, plan.wide_orders, grad_ref, acc_ref, outs, stage_ref, sem_ref)


def feed(plan, lengths, piece_rows, grad_rows, tokens, pass_rows, heads_out, cotangent, table, gain, pieces, width):
    part = tokens.shape[2]
    rows = tokens.shape[0] * part

    def at0(b, n, r):
        return jnp.minimum(b, last_block(n[0])), 0

    def at1(b, n, r):
        return jnp.clip(b - last_block(n[0]) - 1, 0, last_block(n[1])), 0

    def both(b, n, r):
        early = b <= last_block(n[0])
        return jnp.where(early, b, at1(b, n, r)[0]), jnp.where(early, 0, 1)

    row0 = pl.BlockSpec((ROWS, D), at0)
    row1 = pl.BlockSpec((ROWS, D), at1)
    pas0 = pl.BlockSpec((1, 1, ROWS), lambda *a: at0(*a) + (0,))
    pas1 = pl.BlockSpec((1, 1, ROWS), lambda *a: at1(*a) + (0,))
    dealt = dealt_spec(part, both)
    local = pl.BlockSpec((None, ROWS, D), lambda *a: both(*a)[::-1] + (0,))
    grads = grad_shapes(plan, width, plan.wide_orders)
    anywhere = pl.BlockSpec(memory_space=pl.ANY)
    return pl.pallas_call(
        functools.partial(feed_kernel, plan),
        grid_spec=pltpu.PrefetchScalarGridSpec(
            num_scalar_prefetch=2,
            grid=(2 * rows // ROWS,),
            in_specs=[
                dealt, pas0, pas1, row0, row1, dealt,
                pl.BlockSpec((8, D), lambda *a: (0, 0)),
                pl.BlockSpec((1, D), lambda *a: (0, 0)),
                pl.BlockSpec(memory_space=pltpu.SMEM),
            ]
            + [anywhere] * len(pieces),
            out_specs=[dealt, local, local, pl.BlockSpec((8, D), lambda *a: (0, 0))] + [anywhere] * len(grads),
            scratch_shapes=[
                pltpu.VMEM((D, width), bf16),
                pltpu.VMEM((D, width), f32),
                pltpu.VMEM((32, D), f32),
                pltpu.VMEM(stage_shape(plan), bf16),
                pltpu.SemaphoreType.DMA((2,)),
            ],
        ),
        out_shape=[
            jax.ShapeDtypeStruct(cotangent.shape, bf16),
            jax.ShapeDtypeStruct((2, rows, D), bf16),
            jax.ShapeDtypeStruct((2, rows, D), f32),
            jax.ShapeDtypeStruct((8, D), f32),
        ]
        + grads,
        compiler_params=params(),
        cost_estimate=pl.CostEstimate(
            flops=2 * 6 * rows * D * width, bytes_accessed=2 * rows * D * 14 + D * width * 4, transcendentals=2 * rows * FF
        ),
        name="feed",
    )(lengths, piece_rows, tokens, pass_rows[0], pass_rows[1], heads_out[0], heads_out[1],
      cotangent, table, gain, grad_rows, *pieces)


def project_back_kernel(plan, weight, rows_back, final, len_ref, row_ref, grad_ref, tok_ref, pass_ref, g_ref, *rest):
    rest = list(rest)
    hid_ref = rest.pop(0) if rows_back else None
    table_ref, gain_ref = rest.pop(0), rest.pop(0)
    before_ref = rest.pop(0) if final else None
    many = plan.sharers if plan.paired else 1
    pieces = [rest.pop(0) for n in range(many)] if rows_back else []
    if rows_back:
        out_ref, small_ref = rest.pop(0), rest.pop(0)
    if weight and not final:
        acc_ref = rest.pop(0)
    outs = [rest.pop(0) for shape in grad_shapes(plan, 3 * D, plan.head_orders)] if final else []
    if rows_back:
        w_ref, sums_ref = rest.pop(0), rest.pop(0)
    if final:
        acc_ref, stage_ref = rest.pop(0), rest.pop(0)
    sem_ref = rest.pop(0)
    b = pl.program_id(0)

    @pl.when(b == 0)
    def clear():
        if rows_back:
            load_weight(plan, row_ref, pieces, w_ref, sem_ref.at[0])
            sums_ref[...] = jnp.zeros_like(sums_ref)
        if weight:
            acc_ref[...] = before_ref[...] if final else jnp.zeros_like(acc_ref)

    @pl.when(b <= last_block(len_ref[0]))
    def work():
        hot = onehot_rows(pass_ref[0])
        entry = tok_ref[...].reshape(ROWS, D).astype(f32) + dot_tn(hot, table_ref[...])
        unit, scale = normalized(entry)
        gain = gain_ref[...]
        if weight:
            normed = (unit * gain).astype(bf16)
            for part in range(3):
                acc_ref[:, part * D : (part + 1) * D] += dot_tn(normed, g_ref[part])
        if rows_back:
            grad_normed = jnp.zeros((ROWS, D), f32)
            for part in range(3):
                grad_normed = grad_normed + dot_nt(g_ref[part], w_ref[:, part * D : (part + 1) * D])
            sums_ref[0:8] += fold_rows(grad_normed * unit)
            grad_entry = hid_ref[...] + norm_back(grad_normed * gain, unit, scale)
            high = grad_entry.astype(bf16)
            out_ref[...] = high
            rest_one = grad_entry - high.astype(f32)
            low = rest_one.astype(bf16)
            lower = (rest_one - low.astype(f32)).astype(bf16)
            sums_ref[8:16] += dot_nn(hot, high) + dot_nn(hot, low) + dot_nn(hot, lower)

    if rows_back:
        @pl.when(b == pl.num_programs(0) - 1)
        def sums():
            small_ref[...] = sums_ref[8:16]
            small_ref[PASSES : PASSES + 1] = jnp.sum(sums_ref[0:8], axis=0, keepdims=True)

    if final:
        @pl.when(b == pl.num_programs(0) - 1)
        def finish():
            store_grads(plan, plan.head_orders, grad_ref, acc_ref, outs, stage_ref, sem_ref)


def project_back(
    plan, weight, rows_back, which, length, piece_rows, grad_rows, tokens, pass_rows, grads, grad_hidden, table, gain,
    pieces, before=None,
):
    part = tokens.shape[2]
    rows = tokens.shape[0] * part
    final = before is not None
    at = lambda b, n, r, g: (jnp.minimum(b, last_block(n[0])), 0)
    row = pl.BlockSpec((ROWS, D), at)
    anywhere = pl.BlockSpec(memory_space=pl.ANY)
    in_specs = [
        dealt_spec(part, lambda *a: (at(*a)[0], which)),
        pl.BlockSpec((1, 1, ROWS), lambda *a: at(*a) + (0,)),
        pl.BlockSpec((3, ROWS, D), lambda *a: (0,) + at(*a)),
    ]
    operands = [length, piece_rows, grad_rows, tokens, pass_rows, grads]
    if rows_back:
        in_specs.append(pl.BlockSpec((None, ROWS, D), lambda *a: (which,) + at(*a)))
        operands.append(grad_hidden)
    in_specs += [pl.BlockSpec((8, D), lambda *a: (0, 0)), pl.BlockSpec((1, D), lambda *a: (0, 0))]
    operands += [table, gain]
    out_shape, out_specs, scratch = [], [], []
    if final:
        in_specs.append(pl.BlockSpec((D, 3 * D), lambda *a: (0, 0), pipeline_mode=pl.Buffered(1)))
        operands.append(before)
    if rows_back:
        in_specs += [anywhere] * len(pieces)
        operands += pieces
        out_shape += [jax.ShapeDtypeStruct((rows, D), bf16), jax.ShapeDtypeStruct((8, D), f32)]
        out_specs += [row, pl.BlockSpec((8, D), lambda *a: (0, 0))]
        scratch += [pltpu.VMEM((D, 3 * D), bf16), pltpu.VMEM((16, D), f32)]
    if weight and not final:
        out_shape.append(jax.ShapeDtypeStruct((D, 3 * D), f32))
        out_specs.append(pl.BlockSpec((D, 3 * D), lambda *a: (0, 0)))
    if final:
        shapes = grad_shapes(plan, 3 * D, plan.head_orders)
        out_shape += shapes
        out_specs += [anywhere] * len(shapes)
        scratch += [pltpu.VMEM((D, 3 * D), f32), pltpu.VMEM(stage_shape(plan), bf16)]
    return pl.pallas_call(
        functools.partial(project_back_kernel, plan, weight, rows_back, final),
        grid_spec=pltpu.PrefetchScalarGridSpec(
            num_scalar_prefetch=3,
            grid=(rows // ROWS,),
            in_specs=in_specs,
            out_specs=out_specs,
            scratch_shapes=scratch + [pltpu.SemaphoreType.DMA((2,))],
        ),
        out_shape=out_shape,
        compiler_params=params(),
        cost_estimate=pl.CostEstimate(
            flops=2 * (weight + rows_back) * rows * D * 3 * D, bytes_accessed=rows * D * 14 + D * D * 6, transcendentals=0
        ),
        name="project_back",
    )(*operands)


def pick_kernel(index_ref, in_ref, out_ref, sem_ref):
    copies = [
        pltpu.make_async_copy(in_ref.at[index_ref[n]], out_ref.at[n], sem_ref) for n in range(out_ref.shape[0])
    ]
    for copy in copies:
        copy.start()
    for copy in copies:
        copy.wait()


def pick(index, blocks):
    shape = index.shape + blocks.shape[1:]
    return pl.pallas_call(
        pick_kernel,
        grid_spec=pltpu.PrefetchScalarGridSpec(
            num_scalar_prefetch=1,
            grid=(1,),
            in_specs=[pl.BlockSpec(memory_space=pl.ANY)],
            out_specs=pl.BlockSpec(shape, lambda b, n: (0, 0, 0)),
            scratch_shapes=[pltpu.SemaphoreType.DMA],
        ),
        out_shape=jax.ShapeDtypeStruct(shape, blocks.dtype),
        compiler_params=params(),
        cost_estimate=pl.CostEstimate(flops=0, bytes_accessed=4 * math.prod(shape), transcendentals=0),
        name="pick",
    )(index, blocks)


def settle_kernel(index_ref, *refs):
    arrays, out_ref = refs[:-1], refs[-1]
    first = pl.program_id(0) * out_ref.shape[0]
    rows = out_ref.shape[1]
    at = lax.broadcasted_iota(jnp.int32, (rows, 1), 0)
    for n in range(out_ref.shape[0]):
        live = at < index_ref[2, first + n]
        source, late = index_ref[1, first + n], index_ref[0, first + n]
        if len(arrays) == 1:
            found = arrays[0][2 * source + late]
        else:
            found = jnp.where(late == 0, arrays[0][source], arrays[1][source])
        out_ref[n] = jnp.where(live, found.astype(f32), 0.0)


def settle(index, *arrays):
    many = index.shape[1]
    step = 4
    shape = arrays[0].shape
    whole = pl.BlockSpec(shape, lambda b, n: (0, 0, 0), pipeline_mode=pl.Buffered(1))
    return pl.pallas_call(
        settle_kernel,
        grid_spec=pltpu.PrefetchScalarGridSpec(
            num_scalar_prefetch=1,
            grid=(many // step,),
            in_specs=[whole] * len(arrays),
            out_specs=pl.BlockSpec((step,) + shape[1:], lambda b, n: (b, 0, 0)),
        ),
        out_shape=jax.ShapeDtypeStruct((many,) + shape[1:], f32),
        compiler_params=params(),
        cost_estimate=pl.CostEstimate(flops=0, bytes_accessed=6 * many * math.prod(shape[1:]), transcendentals=0),
        name="settle",
    )(index, *arrays)


def after(values, *others):
    return lax.optimization_barrier((values, others))[0]


def swap(blocks):
    return lax.all_to_all(blocks, "dp", split_axis=0, concat_axis=0, tiled=True)


def per_device(
    groups,
    width_all,
    tokens,
    passes,
    lengths,
    dealing,
    pass_table,
    gain_first,
    to_heads,
    from_heads,
    gain_second,
    expand,
    shrink,
    cotangent,
):
    axes = ("dp", "fsdp")
    slots, part, unused_width = tokens.shape
    seq_len = part * groups
    order = jnp.arange(slots, dtype=jnp.int32)
    here = lax.axis_index("dp")
    ordering = dealing[0, 0]
    sizes = lengths[0]

    ahead = (sizes[None, :] > sizes[:, None]) | (
        (sizes[None, :] == sizes[:, None]) & (order[None, :] < order[:, None])
    )
    rank = jnp.sum(ahead.astype(jnp.int32), axis=1)
    ranked = jnp.sum(jnp.where(rank[None, :] == order[:, None], order[None, :], 0), axis=1)
    place = jnp.sum(jnp.where(ordering[None, :] == order[:, None], order[None, :], 0), axis=1)
    early_seqs = ranked[:groups]
    late_seqs = ranked[groups:][::-1]
    from_early = jnp.sum(jnp.where(early_seqs[:, None] == order[None, :], place[None, :], 0), axis=1)
    from_late = jnp.sum(jnp.where(late_seqs[:, None] == order[None, :], place[None, :], 0), axis=1)
    slot_rank = jnp.sum(jnp.where(ordering[:, None] == order[None, :], rank[None, :], 0), axis=1)
    slot_size = jnp.sum(jnp.where(ordering[:, None] == order[None, :], sizes[None, :], 0), axis=1)
    is_late = (slot_rank >= groups).astype(jnp.int32)
    source = jnp.where(is_late == 1, slots - 1 - slot_rank, slot_rank)
    back_index = jnp.stack([is_late, source, slot_size - here * part])
    my_seqs = jnp.stack([early_seqs[here], late_seqs[here]])
    my_sizes = jnp.sum(jnp.where(my_seqs[:, None] == order[None, :], sizes[None, :], 0), axis=1)

    row_count = to_heads.shape[0]
    narrow = jnp.concatenate(
        [
            from_heads,
            expand.reshape(row_count, D, CHUNKS).transpose(0, 2, 1).reshape(row_count, FF),
            shrink.reshape(row_count, CHUNKS * D),
        ],
        axis=1,
    )
    plan = Plan(groups, width_all // groups, row_count)
    index_here = here * (width_all // groups) + lax.axis_index("fsdp")
    my_passes = [passes[my_seqs[m]].reshape(seq_len // ROWS, 1, ROWS) for m in range(2)]
    one_size = [my_sizes[m : m + 1] for m in range(2)]
    table = jnp.zeros((8, D), bf16).at[:PASSES].set(pass_table)
    gain_one = gain_first.astype(f32).reshape(1, D)
    gain_two = gain_second.astype(f32).reshape(1, D)

    pairs_index = jnp.stack([from_early, from_late], axis=1).reshape(slots)
    picked = [pick(pairs_index, blocks).reshape(groups, 2, part, D) for blocks in (tokens, cotangent)]
    if plan.paired:
        piece_rows = plan.piece_rows(index_here)
        wide_rows = plan.grad_rows(index_here, plan.wide_orders)
        head_rows = plan.grad_rows(index_here, plan.head_orders)
        head_far = plan.gather(to_heads[None], plan.far)
        head_near = plan.gather(head_far, [plan.near])
        wide_far = plan.gather(after(narrow, head_far)[None], plan.far)
        ready = (my_passes, one_size, piece_rows, table, gain_one)
        my_tokens = swap(after(picked[0], head_near, wide_far, ready))
        head_pieces = plan.gather_core(plan.gather_x(head_near))
        wide_near = plan.gather(wide_far, [plan.near], (), (head_pieces, my_tokens))
        wide_x = plan.gather_x(wide_near)
    else:
        piece_rows = wide_rows = head_rows = jnp.zeros((1,), jnp.int32)
        head_pieces = (lax.all_gather(to_heads, axes, axis=0, tiled=True),)
        wide_pieces = (lax.all_gather(narrow, axes, axis=0, tiled=True),)
        my_tokens = swap(picked[0])
        wide_near = ()
    my_grads = swap(after(picked[1], my_tokens, wide_near))

    def forward(m, *gate):
        return project(
            plan, m, after(one_size[m], gate), piece_rows, my_tokens, my_passes[m], table, gain_one, head_pieces
        )

    def mix(m, *gate):
        return attend(after(one_size[m], gate), projected[m])

    def mix_back(m, first, before, *gate):
        choice = jnp.stack([my_sizes[m], jnp.int32(m), jnp.int32(first)])
        return attend_back(after(choice, gate), projected[m], heads_out[m], grad_heads, lse[m], before)

    def back(m, weight, rows_back, *gate, before=None):
        return project_back(
            plan, weight, rows_back, m, after(one_size[m], gate), piece_rows, head_rows, my_tokens, my_passes[m],
            grad_parts[m], grad_hidden, table, gain_one, head_pieces, before,
        )

    def send_back(rows, *gate):
        return swap(after(rows, gate).reshape(groups, part, D))

    projected, heads_out, lse, grad_parts = [None, None], [None, None], [None, None], [None, None]
    projected[0] = forward(0)
    heads_out[0], lse[0] = mix(0)
    projected[1] = forward(1, lse[0])
    if plan.paired:
        wide_pieces = plan.gather_core(wide_x, projected[1])
    heads_out[1], lse[1] = mix(1)

    res, grad_heads, grad_hidden, feed_small, *wide_grads = feed(
        plan, my_sizes, piece_rows, wide_rows, my_tokens, my_passes, heads_out, my_grads, table, gain_two,
        wide_pieces, D + 2 * FF,
    )

    def begin(grads):
        if not plan.paired:
            return lax.psum_scatter(grads[0], axes, scatter_dimension=0, tiled=True).astype(f32)
        return [grads[n : n + 2] for n in range(0, len(grads), 2)]

    def advance(state, stage, gate, late):
        return plan.reduce_stage(state, plan.wide_orders, stage, (gate,), (late,)) if plan.paired else state

    half = HEADS // 4
    space = jax.ShapeDtypeStruct((3, seq_len, D), bf16)
    wide0 = begin(wide_grads)
    some = mix_back(0, 0, blank(one_size[0], space))
    wide1 = advance(wide0, 0, (), some)
    result = swap(after(res, wide1))
    grad_parts[0] = mix_back(0, half, some, wide1)
    entry0, small0, head_sum = back(0, True, True)
    wide2 = advance(wide1, 1, some, entry0)
    some = mix_back(1, 0, blank(one_size[1], space), entry0, wide2)
    wide3 = advance(wide2, 2, entry0, some)
    grad_parts[1] = mix_back(1, half, some, wide3)
    wide_owned = advance(wide3, 3, some, grad_parts[1])
    moved0 = send_back(entry0, result, wide_owned)
    head_grads = back(1, True, False, grad_parts[1], wide_owned, before=head_sum)
    head_state = begin(head_grads)
    head_next = plan.reduce_stage(head_state, plan.head_orders, 0) if plan.paired else head_state
    entry1, small1 = back(1, False, True, head_next)
    moved1 = send_back(entry1, moved0, wide_owned)
    totals = jnp.concatenate([small0 + small1, feed_small], axis=0)
    if plan.paired:
        orders = plan.head_orders
        head_state = plan.reduce_stage(head_next, orders, 1, (), (entry1,))
        totals = plan.total_stage(totals, orders[0][0])
        totals = plan.total_stage(totals, orders[0][1], (head_state,))
        totals = plan.total_stage(totals, orders[0][2])
        head_owned = plan.reduce_stage(head_state, orders, 2)[0]
        wide_owned = wide_owned[0]
    else:
        totals = lax.psum(totals, axes)
        head_owned = head_state
    output = settle(after(back_index, head_state), result.reshape(slots, part, D))
    root_squares = jnp.sqrt(jnp.sum(totals[9:12], axis=1) / (totals[12, 0] * D))

    grad_expand = wide_owned[:, D : D + FF].reshape(row_count, CHUNKS, D).transpose(0, 2, 1)
    return (
        output,
        settle(back_index, moved0, moved1),
        totals[:PASSES],
        totals[PASSES],
        head_owned,
        wide_owned[:, :D],
        totals[8],
        grad_expand.reshape(row_count, FF),
        wide_owned[:, D + FF :].reshape(row_count * CHUNKS, D),
        root_squares,
    )


def solution(mesh):
    groups = mesh.shape["dp"]
    weight_spec = P(("dp", "fsdp"), None)
    block_spec = P("fsdp", "dp", None)
    in_specs = (
        block_spec,
        P("fsdp", None),
        P("fsdp", None),
        P("dp", "fsdp", None),
        P(),
        P(),
        weight_spec,
        weight_spec,
        P(),
        weight_spec,
        weight_spec,
        block_spec,
    )
    out_specs = (
        block_spec,
        block_spec,
        P(),
        P(),
        weight_spec,
        weight_spec,
        P(),
        weight_spec,
        weight_spec,
        P(),
    )
    body = functools.partial(per_device, groups, groups * mesh.shape["fsdp"])
    return jax.shard_map(body, mesh=mesh, in_specs=in_specs, out_specs=out_specs, check_vma=False)
```

```python
import math
import functools

import jax
import jax.numpy as jnp
from jax import lax
from jax.experimental import pallas as pl
from jax.experimental.pallas import tpu as pltpu
from jax.sharding import PartitionSpec as P

D = 768
HEADS = 12
HEAD = 64
FF = 3072
PASSES = 5
EPS = 1e-05
ROWS = 256
CHUNKS = FF // D
VMEM_MOST = 64000 * 1024

f32 = jnp.float32
bf16 = jnp.bfloat16


def dot_nn(a, b):
    return lax.dot_general(a, b, (((1,), (0,)), ((), ())), preferred_element_type=f32)


def dot_nt(a, b):
    return lax.dot_general(a, b, (((1,), (1,)), ((), ())), preferred_element_type=f32)


def dot_tn(a, b):
    return lax.dot_general(a, b, (((0,), (0,)), ((), ())), preferred_element_type=f32)


def params(**more):
    return pltpu.CompilerParams(vmem_limit_bytes=VMEM_MOST, **more)


def normalized(values):
    centred = values - jnp.mean(values, axis=-1, keepdims=True)
    spread = jnp.mean(centred * centred, axis=-1, keepdims=True)
    scale = lax.rsqrt(spread + EPS)
    return centred * scale, scale


def norm_back(grad_unit, unit, scale):
    first = jnp.mean(grad_unit, axis=-1, keepdims=True)
    second = jnp.mean(grad_unit * unit, axis=-1, keepdims=True)
    return scale * (grad_unit - first - unit * second)


def onehot_rows(pass_row):
    ids = lax.broadcasted_iota(jnp.int32, (8, pass_row.shape[-1]), 0)
    return (ids == pass_row).astype(f32).astype(bf16)


def fold_rows(values):
    rows, width = values.shape
    return jnp.sum(values.reshape(rows // 8, 8, width), axis=0)


def last_block(length):
    return lax.div(length + (ROWS - 1), ROWS) - 1


def bits_of(count):
    return count.bit_length() - 1


class Plan:
    def __init__(self, groups, sharers, rows):
        self.groups, self.sharers, self.rows = groups, sharers, rows
        self.count = groups * sharers
        self.paired = rows % 8 == 0 and self.count & (self.count - 1) == 0 and sharers >= 4 and groups >= 4
        core, *over_x = [1 << bit for bit in range(bits_of(sharers))]
        near, *far = [sharers << bit for bit in range(bits_of(groups))]
        self.core, self.over_x, self.near, self.far = core, over_x, near, far[::-1]
        self.wide_orders = ([[core], over_x, [near], far], [[core], [near], over_x, far])
        self.head_orders = ([[core], over_x + [near], far],)

    def exchange(self, values, bits):
        pairs = [(i, i ^ bits) for i in range(self.count)]
        return lax.ppermute(values, ("dp", "fsdp"), pairs)

    def gather(self, held, masks, gate=(), late=()):
        for bits in masks:
            held = jnp.concatenate([after(held, late), self.exchange(after(held, gate), bits)], axis=0)
        return held

    def gather_x(self, held, *gate):
        pieces = {0: held}
        for bits in self.over_x[::-1]:
            for name in list(pieces):
                pieces[name | bits] = self.exchange(after(pieces[name], gate), bits)
        return pieces

    def gather_near(self, pieces, gate=(), late=()):
        return {name: self.gather(held, [self.near], gate, late) for name, held in pieces.items()}

    def gather_core(self, pieces, *gate):
        found = dict(pieces)
        for name in pieces:
            found[name | self.core] = self.exchange(after(pieces[name], gate), self.core)
        return tuple(found[name] for name in range(self.sharers))

    def piece_rows(self, here):
        masks = self.far + [self.near]
        found = []
        for f in range(self.sharers):
            for n in range(self.groups):
                rel = f | ways_bits(masks, n)
                found.append((here ^ rel) * self.rows)
        return jnp.stack(found).astype(jnp.int32)

    def grad_rows(self, here, orders):
        found = []
        for order in orders:
            for place in range(self.count):
                rel, left = 0, self.count
                for masks in order:
                    left >>= len(masks)
                    rel |= ways_bits(masks, (place // left) % (1 << len(masks)))
                found.append((here ^ rel) * self.rows)
        return jnp.stack(found).astype(jnp.int32)

    def total_stage(self, values, masks, gate=(), late=()):
        found = [after(values, late)]
        found += [self.exchange(after(values, gate), ways_bits(masks, way)) for way in range(1, 1 << len(masks))]
        while len(found) > 1:
            found = [found[k] + found[k + 1] for k in range(0, len(found), 2)]
        return found[0]

    def reduce_stage(self, states, orders, stage, gate=(), late=()):
        sums = []
        for ways, order in zip(states, orders):
            sums.append(
                [after(ways[0], late)]
                + [
                    self.exchange(after(ways[n], gate), ways_bits(order[stage], n))
                    for n in range(1, len(ways))
                ]
            )
        if stage == len(orders[0]) - 1:
            return [sum(part.astype(f32) for part in parts)[0] for parts in sums]
        ways = 1 << len(orders[0][stage + 1])
        if stage == len(orders[0]) - 2:
            return [merge(sums, ways)]
        return [merge([parts], ways) for parts in sums]


def ways_bits(masks, way):
    return sum(bits for n, bits in enumerate(masks) if (way >> n) & 1)


def merge_kernel(widths, many, ways, *refs):
    ins, outs = refs[: len(widths) * many * ways], refs[len(widths) * many * ways :]
    for way in range(ways):
        first = 0
        for k, width in enumerate(widths):
            views = [ins[(k * many + n) * ways + way] for n in range(many)]
            total = views[0][...].astype(f32)
            for view in views[1:]:
                total = total + view[...].astype(f32)
            outs[way][:, :, first : first + width] = total.astype(bf16)
            first += width


def merge(groups, ways):
    blocks, rows, unused = groups[0][0].shape
    widths = [parts[0].shape[2] for parts in groups]
    share = blocks // ways
    steps = min(share, 4)

    def view(way, width):
        return pl.BlockSpec((share // steps, rows, width), lambda b: (b + way * steps, 0, 0))

    out = jax.ShapeDtypeStruct((share, rows, sum(widths)), bf16)
    many = len(groups[0])
    size = blocks * rows * sum(widths)
    return pl.pallas_call(
        functools.partial(merge_kernel, widths, many, ways),
        grid=(steps,),
        in_specs=[view(way, width) for width in widths for n in range(many) for way in range(ways)],
        out_specs=[view(0, sum(widths))] * ways,
        out_shape=[out] * ways,
        compiler_params=params(),
        cost_estimate=pl.CostEstimate(flops=many * size, bytes_accessed=(2 + 2 * many) * size, transcendentals=0),
        name="merge",
    )(*[part for parts in groups for part in parts for way in range(ways)])


def load_weight(plan, rows_ref, pieces, weight_ref, sem_ref):
    copies = []
    if not plan.paired:
        copies.append(pltpu.make_async_copy(pieces[0], weight_ref, sem_ref))
    first = 0
    for k in range(0, len(pieces) if plan.paired else 0, plan.sharers):
        width = pieces[k].shape[-1]
        for f in range(plan.sharers):
            for n in range(plan.groups):
                at = pl.multiple_of(rows_ref[f * plan.groups + n], 8)
                target = weight_ref.at[pl.ds(at, plan.rows), first : first + width]
                copies.append(pltpu.make_async_copy(pieces[k + f].at[n], target, sem_ref))
        first += width
    for copy in copies:
        copy.start()
    for copy in copies:
        copy.wait()


def grad_shapes(plan, width, orders):
    if not plan.paired:
        return [jax.ShapeDtypeStruct((D, width), bf16)]
    half = plan.count // 2
    cut = first_part(width, orders)
    return [jax.ShapeDtypeStruct((half, plan.rows, w), bf16) for w in (cut, cut, width - cut, width - cut) if w > 0]


def first_part(width, orders):
    return (width // D + 1) // 2 * D if len(orders) == 2 else width


def stage_shape(plan):
    return (2, plan.count, plan.rows, D) if plan.paired else (2, D, D)


def store_grads(plan, orders, rows_ref, acc_ref, outs, stage_ref, sem_ref):
    width, step = acc_ref.shape[1], D
    cut = first_part(width, orders)
    half = plan.count // 2
    waiting = []
    for n in range(width // step):
        slot = n % 2
        cols = slice(n * step, (n + 1) * step)
        if len(waiting) == 2:
            for copy in waiting.pop(0):
                copy.wait()
        if not plan.paired:
            stage_ref[slot] = acc_ref[:, cols].astype(bf16)
            copies = [pltpu.make_async_copy(stage_ref.at[slot], outs[0].at[:, cols], sem_ref.at[slot])]
        else:
            late = n * step >= cut
            base = plan.count if late else 0
            start = n * step - (cut if late else 0)

            def fill(place, carry):
                at = pl.multiple_of(rows_ref[base + place], 8)
                stage_ref[slot, place] = acc_ref[pl.ds(at, plan.rows), cols].astype(bf16)
                return carry

            lax.fori_loop(0, plan.count, fill, 0, unroll=2)
            keep, send = outs[2:4] if late else outs[0:2]
            there = slice(start, start + step)
            copies = [
                pltpu.make_async_copy(stage_ref.at[slot, 0:half], keep.at[:, :, there], sem_ref.at[slot]),
                pltpu.make_async_copy(stage_ref.at[slot, half:], send.at[:, :, there], sem_ref.at[slot]),
            ]
        for copy in copies:
            copy.start()
        waiting.append(copies)
    for copies in waiting:
        for copy in copies:
            copy.wait()


def project_kernel(plan, len_ref, row_ref, tok_ref, pass_ref, table_ref, gain_ref, *rest):
    pieces, (out_ref, w_ref, sem_ref) = rest[:-3], rest[-3:]

    @pl.when(pl.program_id(0) == 0)
    def load():
        load_weight(plan, row_ref, pieces, w_ref, sem_ref)

    @pl.when(pl.program_id(0) <= last_block(len_ref[0]))
    def work():
        hot = onehot_rows(pass_ref[0])
        entry = tok_ref[...].astype(f32) + dot_tn(hot, table_ref[...])
        unit, unused = normalized(entry)
        normed = (unit * gain_ref[...]).astype(bf16)
        for part in range(3):
            out_ref[part] = dot_nn(normed, w_ref[:, part * D : (part + 1) * D]).astype(bf16)


def project(plan, length, piece_rows, tokens, pass_rows, table, gain, pieces):
    rows = tokens.shape[0]
    at = lambda b, n, r: (jnp.minimum(b, last_block(n[0])), 0)
    return pl.pallas_call(
        functools.partial(project_kernel, plan),
        grid_spec=pltpu.PrefetchScalarGridSpec(
            num_scalar_prefetch=2,
            grid=(rows // ROWS,),
            in_specs=[
                pl.BlockSpec((ROWS, D), at),
                pl.BlockSpec((1, 1, ROWS), lambda b, n, r: at(b, n, r) + (0,)),
                pl.BlockSpec((8, D), lambda b, n, r: (0, 0)),
                pl.BlockSpec((1, D), lambda b, n, r: (0, 0)),
            ]
            + [pl.BlockSpec(memory_space=pl.ANY)] * len(pieces),
            out_specs=pl.BlockSpec((3, ROWS, D), lambda b, n, r: (0,) + at(b, n, r)),
            scratch_shapes=[pltpu.VMEM((D, 3 * D), bf16), pltpu.SemaphoreType.DMA],
        ),
        out_shape=jax.ShapeDtypeStruct((3, rows, D), bf16),
        compiler_params=params(),
        cost_estimate=pl.CostEstimate(
            flops=2 * rows * D * 3 * D, bytes_accessed=rows * D * 8 + D * D * 6, transcendentals=0
        ),
        name="project",
    )(length, piece_rows, tokens, pass_rows, table, gain, *pieces)


def attend_kernel(len_ref, p_ref, out_ref, lse_ref):
    blocks = p_ref.shape[1] // ROWS
    lane = lax.broadcasted_iota(jnp.int32, (ROWS, 128), 1)
    first_head = lane < HEAD
    here = lax.broadcasted_iota(jnp.int32, (ROWS, ROWS), 0)
    there = lax.broadcasted_iota(jnp.int32, (ROWS, ROWS), 1)
    allowed = there <= here
    for i in range(blocks):
        rows = slice(i * ROWS, (i + 1) * ROWS)

        @pl.when(i * ROWS < len_ref[0])
        def work():
            query = p_ref[0, rows, :] * jnp.asarray(1.0 / math.sqrt(HEAD), bf16)
            found = []
            for head in range(2):
                mine = first_head if head == 0 else jnp.logical_not(first_head)
                q = jnp.where(mine, query, jnp.zeros_like(query))
                diag = dot_nt(q, p_ref[1, rows, :])
                diag = jnp.where(allowed, diag, -1e30)
                largest = jnp.max(diag, axis=-1, keepdims=True)
                if i > 0:
                    before = dot_nt(q, p_ref[1, : i * ROWS, :])
                    largest = jnp.maximum(largest, jnp.max(before, axis=-1, keepdims=True))
                diag = jnp.exp(diag - largest)
                total = jnp.sum(diag, axis=-1, keepdims=True)
                out = dot_nn(diag.astype(bf16), p_ref[2, rows, :])
                if i > 0:
                    before = jnp.exp(before - largest)
                    total = total + jnp.sum(before, axis=-1, keepdims=True)
                    out = out + dot_nn(before.astype(bf16), p_ref[2, : i * ROWS, :])
                found.append(out * (1.0 / total))
                lse = jnp.broadcast_to(largest + jnp.log(total), (ROWS, 128))
                lse_ref[0, head : head + 1, rows] = lse.T[0:1]
            out_ref[rows, :] = jnp.where(first_head, found[0], found[1]).astype(bf16)


def attend(length, projected):
    rows = projected.shape[1]
    pairs = HEADS // 2
    return pl.pallas_call(
        attend_kernel,
        grid_spec=pltpu.PrefetchScalarGridSpec(
            num_scalar_prefetch=1,
            grid=(pairs,),
            in_specs=[pl.BlockSpec((3, rows, 128), lambda h, n: (0, 0, h))],
            out_specs=[
                pl.BlockSpec((rows, 128), lambda h, n: (0, h)),
                pl.BlockSpec((1, 8, rows), lambda h, n: (h, 0, 0)),
            ],
        ),
        out_shape=[
            jax.ShapeDtypeStruct((rows, D), bf16),
            jax.ShapeDtypeStruct((pairs, 8, rows), f32),
        ],
        compiler_params=params(),
        cost_estimate=pl.CostEstimate(
            flops=2 * rows * rows * D, bytes_accessed=rows * D * 8, transcendentals=HEADS * rows * rows // 2
        ),
        name="attend",
    )(length, projected)


def attend_back_kernel(len_ref, p_ref, o_ref, g_ref, lse_ref, out_ref, dk_ref, dv_ref, kz_ref, vz_ref, kt_ref):
    blocks = p_ref.shape[1] // ROWS
    scaling = 1.0 / math.sqrt(HEAD)
    lane = lax.broadcasted_iota(jnp.int32, (ROWS, 128), 1)
    first_head = lane < HEAD
    row8 = lax.broadcasted_iota(jnp.int32, (8, 128), 0)
    lane8 = lax.broadcasted_iota(jnp.int32, (8, 128), 1)
    chooser = (lax.div(lane8, HEAD) == row8).astype(f32)
    key_at = lax.broadcasted_iota(jnp.int32, (2, ROWS, ROWS), 1)
    row_at = lax.broadcasted_iota(jnp.int32, (2, ROWS, ROWS), 2)
    allowed = (key_at <= row_at).reshape(2 * ROWS, ROWS)
    for i in range(blocks):
        rows = slice(i * ROWS, (i + 1) * ROWS)
        two = slice(2 * i * ROWS, 2 * (i + 1) * ROWS)

        @pl.when(i * ROWS < len_ref[0])
        def work():
            dk_ref[two, :] = jnp.zeros((2 * ROWS, 128), f32)
            dv_ref[two, :] = jnp.zeros((2 * ROWS, 128), f32)
            key, value = p_ref[1, rows, :], p_ref[2, rows, :]
            zero = jnp.zeros_like(key)
            k2 = jnp.concatenate([jnp.where(first_head, key, zero), jnp.where(first_head, zero, key)], axis=0)
            kz_ref[two, :] = k2
            kt_ref[:, two] = k2.T
            vz_ref[two, :] = jnp.concatenate([jnp.where(first_head, value, zero), jnp.where(first_head, zero, value)], axis=0)
            query = p_ref[0, rows, :] * jnp.asarray(scaling, bf16)
            grad = g_ref[rows, :]
            product = grad.astype(f32) * o_ref[rows, :].astype(f32)
            delta = lax.dot_general(chooser, product, (((1,), (1,)), ((), ())), precision=lax.Precision.HIGHEST, preferred_element_type=f32)
            def both(a, b):
                return jnp.concatenate([jnp.broadcast_to(a, (ROWS, ROWS)), jnp.broadcast_to(b, (ROWS, ROWS))], axis=0)
            lse2 = both(lse_ref[0, 0:1, rows], lse_ref[0, 1:2, rows])
            delta2 = both(delta[0:1], delta[1:2])
            dqt = jnp.zeros((128, ROWS), f32)
            for j in range(i + 1):
                cols = slice(2 * j * ROWS, 2 * (j + 1) * ROWS)
                prob = jnp.exp(dot_nt(kz_ref[cols, :], query) - lse2)
                if i == j:
                    prob = jnp.where(allowed, prob, 0.0)
                ds = (prob * (dot_nt(vz_ref[cols, :], grad) - delta2)).astype(bf16)
                dv_ref[cols, :] += dot_nn(prob.astype(bf16), grad)
                dk_ref[cols, :] += dot_nn(ds, query)
                dqt = dqt + dot_nn(kt_ref[:, cols], ds)
            out_ref[0, rows, :] = (dqt * scaling).T.astype(bf16)
    for i in range(blocks):
        rows = slice(i * ROWS, (i + 1) * ROWS)
        a = slice(2 * i * ROWS, (2 * i + 1) * ROWS); b = slice((2 * i + 1) * ROWS, 2 * (i + 1) * ROWS)

        @pl.when(i * ROWS < len_ref[0])
        def finish():
            out_ref[1, rows, :] = jnp.where(first_head, dk_ref[a, :], dk_ref[b, :]).astype(bf16)
            out_ref[2, rows, :] = jnp.where(first_head, dv_ref[a, :], dv_ref[b, :]).astype(bf16)


def blank_kernel(ready_ref, out_ref):
    pass


def blank(ready, shape):
    return pl.pallas_call(
        blank_kernel,
        in_specs=[pl.BlockSpec(memory_space=pltpu.SMEM)],
        out_specs=pl.BlockSpec(memory_space=pl.ANY),
        out_shape=shape,
        name="blank",
    )(ready)


def attend_back(choice, projected, heads_out, grad_heads, lse, before):
    rows = projected.shape[1]
    pairs = HEADS // 2
    cols = lambda h, n: (0, n[2] + h)
    blocks = lambda h, n: (0, 0, n[2] + h)

    def kernel(n, p, o, g, l, unused, *rest):
        attend_back_kernel(n, p, o, g, l, *rest)

    return pl.pallas_call(
        kernel,
        grid_spec=pltpu.PrefetchScalarGridSpec(
            num_scalar_prefetch=1,
            grid=(pairs // 2,),
            in_specs=[
                pl.BlockSpec((3, rows, 128), blocks),
                pl.BlockSpec((rows, 128), cols),
                pl.BlockSpec((None, rows, 128), lambda h, n: (n[1], 0, n[2] + h)),
                pl.BlockSpec((1, 8, rows), lambda h, n: (n[2] + h, 0, 0)),
                pl.BlockSpec(memory_space=pl.ANY),
            ],
            out_specs=pl.BlockSpec((3, rows, 128), blocks),
            scratch_shapes=[
                pltpu.VMEM((2 * rows, 128), f32),
                pltpu.VMEM((2 * rows, 128), f32),
                pltpu.VMEM((2 * rows, 128), bf16),
                pltpu.VMEM((2 * rows, 128), bf16),
                pltpu.VMEM((128, 2 * rows), bf16),
            ],
        ),
        out_shape=jax.ShapeDtypeStruct((3, rows, D), bf16),
        input_output_aliases={5: 0},
        compiler_params=params(),
        cost_estimate=pl.CostEstimate(
            flops=3 * rows * rows * D, bytes_accessed=rows * D * 8, transcendentals=HEADS * rows * rows // 4
        ),
        name="attend_back",
    )(choice, projected, heads_out, grad_heads, lse, before)


def feed_kernel(plan, len_ref, row_ref, *refs):
    tok0, tok1, pass0, pass1, ho0, ho1, cot, table_ref, gain_ref = refs[:9]
    many = 2 * plan.sharers if plan.paired else 1
    grad_ref, pieces, refs = refs[9], refs[10 : 10 + many], refs[10 + many :]
    res, gh, hid, small_ref = refs[:4]
    outs, (w_ref, acc_ref, sums_ref, stage_ref, sem_ref) = refs[4:-5], refs[-5:]
    b = pl.program_id(0)
    many0 = last_block(len_ref[0]) + 1
    many1 = last_block(len_ref[1]) + 1
    early = b < many0

    @pl.when(b == 0)
    def clear():
        load_weight(plan, row_ref, pieces, w_ref, sem_ref.at[0])
        acc_ref[...] = jnp.zeros_like(acc_ref)
        sums_ref[...] = jnp.zeros_like(sums_ref)

    @pl.when(b < many0 + many1)
    def block():
        hot = onehot_rows(jnp.where(early, pass0[0], pass1[0]))
        entry = jnp.where(early, tok0[...], tok1[...]).astype(f32) + dot_tn(hot, table_ref[...])
        at = jnp.where(early, b, b - many0) * ROWS + lax.broadcasted_iota(jnp.int32, (ROWS, 1), 0)
        live = at < jnp.where(early, len_ref[0], len_ref[1])
        heads = jnp.where(early, ho0[...], ho1[...])
        attention = dot_nn(heads, w_ref[:, 0:D])
        hidden = entry + attention
        unit, scale = normalized(hidden)
        gain = gain_ref[...]
        normed = (unit * gain).astype(bf16)
        grad_feed = jnp.where(live, cot[...].reshape(ROWS, D).astype(f32), 0.0).astype(bf16)
        feed = jnp.zeros((ROWS, D), f32)
        grad_normed = jnp.zeros((ROWS, D), f32)
        for k in range(CHUNKS):
            up = slice(D + k * D, D + (k + 1) * D)
            down = slice(D + FF + k * D, D + FF + (k + 1) * D)
            x = dot_nn(normed, w_ref[:, up])
            grad_act = dot_nt(grad_feed, w_ref[:, down])
            c0 = math.sqrt(2.0 / math.pi)
            square = x * x
            bent = jnp.tanh(x * (c0 + (c0 * 0.044715) * square))
            half = 0.5 + 0.5 * bent
            slope = half + (0.5 * x) * (1.0 - bent * bent) * (c0 + (3.0 * c0 * 0.044715) * square)
            act = (x * half).astype(bf16)
            grad_x = (slope * grad_act).astype(bf16)
            feed = feed + dot_nn(act, w_ref[:, down])
            grad_normed = grad_normed + dot_nt(grad_x, w_ref[:, up])
            acc_ref[:, up] += dot_tn(normed, grad_x)
            acc_ref[:, down] += dot_tn(act, grad_feed)
        res[...] = jnp.where(live, hidden + feed, 0.0).astype(bf16).reshape(res.shape)
        sums_ref[0:8] += fold_rows(grad_normed * unit)
        sums_ref[8:16] += fold_rows(jnp.where(live, entry * entry, 0.0))
        sums_ref[16:24] += fold_rows(jnp.where(live, attention * attention, 0.0))
        sums_ref[24:32] += fold_rows(jnp.where(live, feed * feed, 0.0))
        grad_hidden = grad_feed.astype(f32) + norm_back(grad_normed * gain, unit, scale)
        hid[...] = grad_hidden
        grad_attention = grad_hidden.astype(bf16)
        acc_ref[:, 0:D] += dot_tn(heads, grad_attention)
        gh[...] = dot_nt(grad_attention, w_ref[:, 0:D]).astype(bf16)

    @pl.when(b == pl.num_programs(0) - 1)
    def finish():
        counted = (len_ref[0] + len_ref[1]).astype(f32)
        small_ref[...] = jnp.full(small_ref.shape, counted, f32)
        for n in range(4):
            small_ref[n : n + 1] = jnp.sum(sums_ref[8 * n : 8 * n + 8], axis=0, keepdims=True)
        store_grads(plan, plan.wide_orders, grad_ref, acc_ref, outs, stage_ref, sem_ref)


def feed(plan, part, lengths, piece_rows, grad_rows, tokens, pass_rows, heads_out, cotangent, table, gain, pieces, width):
    rows = tokens[0].shape[0]
    per = ROWS // part

    def at0(b, n, r):
        return jnp.minimum(b, last_block(n[0])), 0

    def at1(b, n, r):
        return jnp.clip(b - last_block(n[0]) - 1, 0, last_block(n[1])), 0

    def both(b, n, r):
        early = b <= last_block(n[0])
        return jnp.where(early, b, at1(b, n, r)[0]), jnp.where(early, 0, 1)

    row0 = pl.BlockSpec((ROWS, D), at0)
    row1 = pl.BlockSpec((ROWS, D), at1)
    pas0 = pl.BlockSpec((1, 1, ROWS), lambda *a: at0(*a) + (0,))
    pas1 = pl.BlockSpec((1, 1, ROWS), lambda *a: at1(*a) + (0,))
    dealt = pl.BlockSpec((per, 1, part, D), lambda *a: both(*a) + (0, 0))
    local = pl.BlockSpec((None, ROWS, D), lambda *a: both(*a)[::-1] + (0,))
    grads = grad_shapes(plan, width, plan.wide_orders)
    anywhere = pl.BlockSpec(memory_space=pl.ANY)
    return pl.pallas_call(
        functools.partial(feed_kernel, plan),
        grid_spec=pltpu.PrefetchScalarGridSpec(
            num_scalar_prefetch=2,
            grid=(2 * rows // ROWS,),
            in_specs=[
                row0, row1, pas0, pas1, row0, row1, dealt,
                pl.BlockSpec((8, D), lambda *a: (0, 0)),
                pl.BlockSpec((1, D), lambda *a: (0, 0)),
                pl.BlockSpec(memory_space=pltpu.SMEM),
            ]
            + [anywhere] * len(pieces),
            out_specs=[dealt, local, local, pl.BlockSpec((8, D), lambda *a: (0, 0))] + [anywhere] * len(grads),
            scratch_shapes=[
                pltpu.VMEM((D, width), bf16),
                pltpu.VMEM((D, width), f32),
                pltpu.VMEM((32, D), f32),
                pltpu.VMEM(stage_shape(plan), bf16),
                pltpu.SemaphoreType.DMA((2,)),
            ],
        ),
        out_shape=[
            jax.ShapeDtypeStruct(cotangent.shape, bf16),
            jax.ShapeDtypeStruct((2, rows, D), bf16),
            jax.ShapeDtypeStruct((2, rows, D), f32),
            jax.ShapeDtypeStruct((8, D), f32),
        ]
        + grads,
        compiler_params=params(),
        cost_estimate=pl.CostEstimate(
            flops=2 * 6 * rows * D * width, bytes_accessed=2 * rows * D * 14 + D * width * 4, transcendentals=2 * rows * FF
        ),
        name="feed",
    )(lengths, piece_rows, tokens[0], tokens[1], pass_rows[0], pass_rows[1], heads_out[0], heads_out[1],
      cotangent, table, gain, grad_rows, *pieces)


def project_back_kernel(plan, weight, rows_back, final, len_ref, row_ref, grad_ref, tok_ref, pass_ref, g_ref, *rest):
    rest = list(rest)
    hid_ref = rest.pop(0) if rows_back else None
    table_ref, gain_ref = rest.pop(0), rest.pop(0)
    before_ref = rest.pop(0) if final else None
    many = plan.sharers if plan.paired else 1
    pieces = [rest.pop(0) for n in range(many)] if rows_back else []
    if rows_back:
        out_ref, small_ref = rest.pop(0), rest.pop(0)
    if weight and not final:
        acc_ref = rest.pop(0)
    outs = [rest.pop(0) for shape in grad_shapes(plan, 3 * D, plan.head_orders)] if final else []
    if rows_back:
        w_ref, sums_ref = rest.pop(0), rest.pop(0)
    if final:
        acc_ref, stage_ref = rest.pop(0), rest.pop(0)
    sem_ref = rest.pop(0)
    b = pl.program_id(0)

    @pl.when(b == 0)
    def clear():
        if rows_back:
            load_weight(plan, row_ref, pieces, w_ref, sem_ref.at[0])
            sums_ref[...] = jnp.zeros_like(sums_ref)
        if weight:
            acc_ref[...] = before_ref[...] if final else jnp.zeros_like(acc_ref)

    @pl.when(b <= last_block(len_ref[0]))
    def work():
        hot = onehot_rows(pass_ref[0])
        entry = tok_ref[...].astype(f32) + dot_tn(hot, table_ref[...])
        unit, scale = normalized(entry)
        gain = gain_ref[...]
        if weight:
            normed = (unit * gain).astype(bf16)
            for part in range(3):
                acc_ref[:, part * D : (part + 1) * D] += dot_tn(normed, g_ref[part])
        if rows_back:
            grad_normed = jnp.zeros((ROWS, D), f32)
            for part in range(3):
                grad_normed = grad_normed + dot_nt(g_ref[part], w_ref[:, part * D : (part + 1) * D])
            sums_ref[0:8] += fold_rows(grad_normed * unit)
            grad_entry = hid_ref[...] + norm_back(grad_normed * gain, unit, scale)
            high = grad_entry.astype(bf16)
            out_ref[...] = high
            rest_one = grad_entry - high.astype(f32)
            low = rest_one.astype(bf16)
            lower = (rest_one - low.astype(f32)).astype(bf16)
            sums_ref[8:16] += dot_nn(hot, high) + dot_nn(hot, low) + dot_nn(hot, lower)

    if rows_back:
        @pl.when(b == pl.num_programs(0) - 1)
        def sums():
            small_ref[...] = sums_ref[8:16]
            small_ref[PASSES : PASSES + 1] = jnp.sum(sums_ref[0:8], axis=0, keepdims=True)

    if final:
        @pl.when(b == pl.num_programs(0) - 1)
        def finish():
            store_grads(plan, plan.head_orders, grad_ref, acc_ref, outs, stage_ref, sem_ref)


def project_back(
    plan, weight, rows_back, which, length, piece_rows, grad_rows, tokens, pass_rows, grads, grad_hidden, table, gain,
    pieces, before=None,
):
    rows = tokens.shape[0]
    final = before is not None
    at = lambda b, n, r, g: (jnp.minimum(b, last_block(n[0])), 0)
    row = pl.BlockSpec((ROWS, D), at)
    anywhere = pl.BlockSpec(memory_space=pl.ANY)
    in_specs = [
        row,
        pl.BlockSpec((1, 1, ROWS), lambda *a: at(*a) + (0,)),
        pl.BlockSpec((3, ROWS, D), lambda *a: (0,) + at(*a)),
    ]
    operands = [length, piece_rows, grad_rows, tokens, pass_rows, grads]
    if rows_back:
        in_specs.append(pl.BlockSpec((None, ROWS, D), lambda *a: (which,) + at(*a)))
        operands.append(grad_hidden)
    in_specs += [pl.BlockSpec((8, D), lambda *a: (0, 0)), pl.BlockSpec((1, D), lambda *a: (0, 0))]
    operands += [table, gain]
    out_shape, out_specs, scratch = [], [], []
    if final:
        in_specs.append(pl.BlockSpec((D, 3 * D), lambda *a: (0, 0), pipeline_mode=pl.Buffered(1)))
        operands.append(before)
    if rows_back:
        in_specs += [anywhere] * len(pieces)
        operands += pieces
        out_shape += [jax.ShapeDtypeStruct((rows, D), bf16), jax.ShapeDtypeStruct((8, D), f32)]
        out_specs += [row, pl.BlockSpec((8, D), lambda *a: (0, 0))]
        scratch += [pltpu.VMEM((D, 3 * D), bf16), pltpu.VMEM((16, D), f32)]
    if weight and not final:
        out_shape.append(jax.ShapeDtypeStruct((D, 3 * D), f32))
        out_specs.append(pl.BlockSpec((D, 3 * D), lambda *a: (0, 0)))
    if final:
        shapes = grad_shapes(plan, 3 * D, plan.head_orders)
        out_shape += shapes
        out_specs += [anywhere] * len(shapes)
        scratch += [pltpu.VMEM((D, 3 * D), f32), pltpu.VMEM(stage_shape(plan), bf16)]
    return pl.pallas_call(
        functools.partial(project_back_kernel, plan, weight, rows_back, final),
        grid_spec=pltpu.PrefetchScalarGridSpec(
            num_scalar_prefetch=3,
            grid=(rows // ROWS,),
            in_specs=in_specs,
            out_specs=out_specs,
            scratch_shapes=scratch + [pltpu.SemaphoreType.DMA((2,))],
        ),
        out_shape=out_shape,
        compiler_params=params(),
        cost_estimate=pl.CostEstimate(
            flops=2 * (weight + rows_back) * rows * D * 3 * D, bytes_accessed=rows * D * 14 + D * D * 6, transcendentals=0
        ),
        name="project_back",
    )(*operands)


def pick_kernel(index_ref, in_ref, out_ref, sem_ref):
    copies = [
        pltpu.make_async_copy(in_ref.at[index_ref[n]], out_ref.at[n], sem_ref) for n in range(out_ref.shape[0])
    ]
    for copy in copies:
        copy.start()
    for copy in copies:
        copy.wait()


def pick(index, blocks):
    shape = index.shape + blocks.shape[1:]
    return pl.pallas_call(
        pick_kernel,
        grid_spec=pltpu.PrefetchScalarGridSpec(
            num_scalar_prefetch=1,
            grid=(1,),
            in_specs=[pl.BlockSpec(memory_space=pl.ANY)],
            out_specs=pl.BlockSpec(shape, lambda b, n: (0, 0, 0)),
            scratch_shapes=[pltpu.SemaphoreType.DMA],
        ),
        out_shape=jax.ShapeDtypeStruct(shape, blocks.dtype),
        compiler_params=params(),
        cost_estimate=pl.CostEstimate(flops=0, bytes_accessed=4 * math.prod(shape), transcendentals=0),
        name="pick",
    )(index, blocks)


def settle_kernel(index_ref, *refs):
    arrays, out_ref = refs[:-1], refs[-1]
    first = pl.program_id(0) * out_ref.shape[0]
    rows = out_ref.shape[1]
    at = lax.broadcasted_iota(jnp.int32, (rows, 1), 0)
    for n in range(out_ref.shape[0]):
        live = at < index_ref[2, first + n]
        source, late = index_ref[1, first + n], index_ref[0, first + n]
        if len(arrays) == 1:
            found = arrays[0][2 * source + late]
        else:
            found = jnp.where(late == 0, arrays[0][source], arrays[1][source])
        out_ref[n] = jnp.where(live, found.astype(f32), 0.0)


def settle(index, *arrays):
    many = index.shape[1]
    step = 4
    shape = arrays[0].shape
    whole = pl.BlockSpec(shape, lambda b, n: (0, 0, 0), pipeline_mode=pl.Buffered(1))
    return pl.pallas_call(
        settle_kernel,
        grid_spec=pltpu.PrefetchScalarGridSpec(
            num_scalar_prefetch=1,
            grid=(many // step,),
            in_specs=[whole] * len(arrays),
            out_specs=pl.BlockSpec((step,) + shape[1:], lambda b, n: (b, 0, 0)),
        ),
        out_shape=jax.ShapeDtypeStruct((many,) + shape[1:], f32),
        compiler_params=params(),
        cost_estimate=pl.CostEstimate(flops=0, bytes_accessed=6 * many * math.prod(shape[1:]), transcendentals=0),
        name="settle",
    )(index, *arrays)


def after(values, *others):
    return lax.optimization_barrier((values, others))[0]


def swap(blocks):
    return lax.all_to_all(blocks, "dp", split_axis=0, concat_axis=0, tiled=True)


def per_device(
    groups,
    width_all,
    tokens,
    passes,
    lengths,
    dealing,
    pass_table,
    gain_first,
    to_heads,
    from_heads,
    gain_second,
    expand,
    shrink,
    cotangent,
):
    axes = ("dp", "fsdp")
    slots, part, unused_width = tokens.shape
    seq_len = part * groups
    order = jnp.arange(slots, dtype=jnp.int32)
    here = lax.axis_index("dp")
    ordering = dealing[0, 0]
    sizes = lengths[0]

    ahead = (sizes[None, :] > sizes[:, None]) | (
        (sizes[None, :] == sizes[:, None]) & (order[None, :] < order[:, None])
    )
    rank = jnp.sum(ahead.astype(jnp.int32), axis=1)
    ranked = jnp.sum(jnp.where(rank[None, :] == order[:, None], order[None, :], 0), axis=1)
    place = jnp.sum(jnp.where(ordering[None, :] == order[:, None], order[None, :], 0), axis=1)
    early_seqs = ranked[:groups]
    late_seqs = ranked[groups:][::-1]
    from_early = jnp.sum(jnp.where(early_seqs[:, None] == order[None, :], place[None, :], 0), axis=1)
    from_late = jnp.sum(jnp.where(late_seqs[:, None] == order[None, :], place[None, :], 0), axis=1)
    slot_rank = jnp.sum(jnp.where(ordering[:, None] == order[None, :], rank[None, :], 0), axis=1)
    slot_size = jnp.sum(jnp.where(ordering[:, None] == order[None, :], sizes[None, :], 0), axis=1)
    is_late = (slot_rank >= groups).astype(jnp.int32)
    source = jnp.where(is_late == 1, slots - 1 - slot_rank, slot_rank)
    back_index = jnp.stack([is_late, source, slot_size - here * part])
    my_seqs = jnp.stack([early_seqs[here], late_seqs[here]])
    my_sizes = jnp.sum(jnp.where(my_seqs[:, None] == order[None, :], sizes[None, :], 0), axis=1)

    row_count = to_heads.shape[0]
    narrow = jnp.concatenate(
        [
            from_heads,
            expand.reshape(row_count, D, CHUNKS).transpose(0, 2, 1).reshape(row_count, FF),
            shrink.reshape(row_count, CHUNKS * D),
        ],
        axis=1,
    )
    plan = Plan(groups, width_all // groups, row_count)
    index_here = here * (width_all // groups) + lax.axis_index("fsdp")
    my_passes = [passes[my_seqs[m]].reshape(seq_len // ROWS, 1, ROWS) for m in range(2)]
    one_size = [my_sizes[m : m + 1] for m in range(2)]
    table = jnp.zeros((8, D), bf16).at[:PASSES].set(pass_table)
    gain_one = gain_first.astype(f32).reshape(1, D)
    gain_two = gain_second.astype(f32).reshape(1, D)

    pairs_index = jnp.stack([from_early, from_late], axis=1).reshape(slots)
    picked = [pick(from_early, tokens), pick(from_late, tokens), pick(pairs_index, cotangent)]
    if plan.paired:
        piece_rows = plan.piece_rows(index_here)
        wide_rows = plan.grad_rows(index_here, plan.wide_orders)
        head_rows = plan.grad_rows(index_here, plan.head_orders)
        head_far = plan.gather(to_heads[None], plan.far)
        head_near = plan.gather(head_far, [plan.near])
        wide_one = plan.gather(after(narrow, head_far)[None], plan.far[:1])
        ready = (my_passes, one_size, piece_rows, table, gain_one)
        tokens0 = swap(after(picked[0], head_far, ready))
        head_pieces = plan.gather_core(plan.gather_x(head_near))
    else:
        piece_rows = wide_rows = head_rows = jnp.zeros((1,), jnp.int32)
        head_pieces = (lax.all_gather(to_heads, axes, axis=0, tiled=True),)
        wide_pieces = (lax.all_gather(narrow, axes, axis=0, tiled=True),)
        tokens0 = swap(picked[0])
        wide_far = wide_pieces

    def forward(m, *gate):
        return project(
            plan, after(one_size[m], gate), piece_rows, my_tokens[m], my_passes[m], table, gain_one, head_pieces
        )

    def mix(m, *gate):
        return attend(after(one_size[m], gate), projected[m])

    half = HEADS // 4
    choices = {
        (m, first): jnp.stack([my_sizes[m], jnp.int32(m), jnp.int32(first)]) for m in range(2) for first in (0, half)
    }

    def mix_back(m, first, before, *gate):
        return attend_back(after(choices[m, first], gate), projected[m], heads_out[m], grad_heads, lse[m], before)

    def back(m, weight, rows_back, *gate, before=None):
        return project_back(
            plan, weight, rows_back, m, after(one_size[m], gate), piece_rows, head_rows, my_tokens[m], my_passes[m],
            grad_parts[m], grad_hidden, table, gain_one, head_pieces, before,
        )

    def send_back(rows, *gate):
        return swap(after(rows, gate).reshape(groups, part, D))

    projected, heads_out, lse, grad_parts = [None, None], [None, None], [None, None], [None, None]
    my_tokens = [tokens0.reshape(seq_len, D)]
    projected[0] = forward(0)
    if plan.paired:
        wide_far = plan.gather(wide_one, plan.far[1:], head_pieces, projected[0])
        cut = first_part(wide_far.shape[-1], plan.wide_orders)
    tokens1 = swap(after(picked[1], tokens0, picked[2], wide_far))
    my_tokens.append(tokens1.reshape(seq_len, D))
    heads_out[0], lse[0] = mix(0, wide_far)
    if plan.paired:
        first = plan.gather_near({0: wide_far[:, :, :cut]}, (), lse[0])
        second = plan.gather_x(wide_far[:, :, cut:], ())
        ready = (first, second)
    else:
        ready = ()
    my_grads = swap(after(picked[2].reshape(groups, 2, part, D), tokens1, lse[0], ready))
    projected[1] = forward(1, lse[0])
    if plan.paired:
        first = plan.gather_x(first[0])
        second = plan.gather_near(second, lse[0], projected[1])
    heads_out[1], lse[1] = mix(1)
    if plan.paired:
        wide_pieces = plan.gather_core(first, lse[1]) + plan.gather_core(second, lse[1])

    res, grad_heads, grad_hidden, feed_small, *wide_grads = feed(
        plan, part, after(my_sizes, choices), piece_rows, wide_rows, my_tokens, my_passes, heads_out, my_grads, table, gain_two,
        wide_pieces, D + 2 * FF,
    )

    def begin(grads):
        if not plan.paired:
            return lax.psum_scatter(grads[0], axes, scatter_dimension=0, tiled=True).astype(f32)
        return [grads[n : n + 2] for n in range(0, len(grads), 2)]

    def advance(state, stage, gate, late):
        return plan.reduce_stage(state, plan.wide_orders, stage, (gate,), (late,)) if plan.paired else state

    space = jax.ShapeDtypeStruct((3, seq_len, D), bf16)
    wide0 = begin(wide_grads)
    result = swap(res)
    some = mix_back(0, 0, blank(one_size[0], space))
    wide1 = advance(wide0, 0, (), some)
    grad_parts[0] = mix_back(0, half, some, wide1)
    entry0, small0, head_sum = back(0, True, True)
    wide2 = advance(wide1, 1, some, entry0)
    moved0 = send_back(entry0, result)
    some = mix_back(1, 0, blank(one_size[1], space), entry0, wide2, result)
    wide3 = advance(wide2, 2, entry0, some)
    grad_parts[1] = mix_back(1, half, some, wide3)
    entry1, small1 = back(1, False, True)
    wide_owned = advance(wide3, 3, some, entry1)
    moved1 = send_back(entry1, moved0, wide_owned)
    totals = jnp.concatenate([small0 + small1, feed_small], axis=0)
    head_grads = back(1, True, False, entry1, moved0, before=head_sum)
    head_state = begin(head_grads)
    if plan.paired:
        orders = plan.head_orders
        totals = plan.total_stage(totals, orders[0][0], (), head_grads[:1])
        head_state = plan.reduce_stage(head_state, orders, 0, (wide_owned,))
    output = settle(after(back_index, head_state), result.reshape(slots, part, D))
    grad_tokens = settle(after(back_index, output), moved0, moved1)
    if plan.paired:
        totals = plan.total_stage(totals, orders[0][1])
        head_state = plan.reduce_stage(head_state, orders, 1, (totals,), (output, grad_tokens))
        totals = plan.total_stage(totals, orders[0][2], (head_state,))
        head_owned = plan.reduce_stage(head_state, orders, 2)[0]
        wide_owned = wide_owned[0]
    else:
        totals = lax.psum(totals, axes)
        head_owned = head_state
    root_squares = jnp.sqrt(jnp.sum(totals[9:12], axis=1) / (totals[12, 0] * D))

    grad_expand = wide_owned[:, D : D + FF].reshape(row_count, CHUNKS, D).transpose(0, 2, 1)
    return (
        output,
        grad_tokens,
        totals[:PASSES],
        totals[PASSES],
        head_owned,
        wide_owned[:, :D],
        totals[8],
        grad_expand.reshape(row_count, FF),
        wide_owned[:, D + FF :].reshape(row_count * CHUNKS, D),
        root_squares,
    )


def solution(mesh):
    groups = mesh.shape["dp"]
    weight_spec = P(("dp", "fsdp"), None)
    block_spec = P("fsdp", "dp", None)
    in_specs = (
        block_spec,
        P("fsdp", None),
        P("fsdp", None),
        P("dp", "fsdp", None),
        P(),
        P(),
        weight_spec,
        weight_spec,
        P(),
        weight_spec,
        weight_spec,
        block_spec,
    )
    out_specs = (
        block_spec,
        block_spec,
        P(),
        P(),
        weight_spec,
        weight_spec,
        P(),
        weight_spec,
        weight_spec,
        P(),
    )
    body = functools.partial(per_device, groups, groups * mesh.shape["fsdp"])
    return jax.shard_map(body, mesh=mesh, in_specs=in_specs, out_specs=out_specs, check_vma=False)
```

```python
import math
import functools

import jax
import jax.numpy as jnp
from jax import lax
from jax.experimental import pallas as pl
from jax.experimental.pallas import tpu as pltpu
from jax.sharding import PartitionSpec as P

D = 768
HEADS = 12
HEAD = 64
FF = 3072
PASSES = 5
EPS = 1e-05
ROWS = 256
CHUNKS = FF // D
VMEM_MOST = 64000 * 1024

f32 = jnp.float32
bf16 = jnp.bfloat16


def dot_nn(a, b):
    return lax.dot_general(a, b, (((1,), (0,)), ((), ())), preferred_element_type=f32)


def dot_nt(a, b):
    return lax.dot_general(a, b, (((1,), (1,)), ((), ())), preferred_element_type=f32)


def dot_tn(a, b):
    return lax.dot_general(a, b, (((0,), (0,)), ((), ())), preferred_element_type=f32)


def params(**more):
    return pltpu.CompilerParams(vmem_limit_bytes=VMEM_MOST, **more)


def normalized(values):
    centred = values - jnp.mean(values, axis=-1, keepdims=True)
    spread = jnp.mean(centred * centred, axis=-1, keepdims=True)
    scale = lax.rsqrt(spread + EPS)
    return centred * scale, scale


def norm_back(grad_unit, unit, scale):
    first = jnp.mean(grad_unit, axis=-1, keepdims=True)
    second = jnp.mean(grad_unit * unit, axis=-1, keepdims=True)
    return scale * (grad_unit - first - unit * second)


def onehot_rows(pass_row):
    ids = lax.broadcasted_iota(jnp.int32, (8, pass_row.shape[-1]), 0)
    return (ids == pass_row).astype(f32).astype(bf16)


def fold_rows(values):
    rows, width = values.shape
    return jnp.sum(values.reshape(rows // 8, 8, width), axis=0)


def last_block(length):
    return lax.div(length + (ROWS - 1), ROWS) - 1


def bits_of(count):
    return count.bit_length() - 1


class Plan:
    def __init__(self, groups, sharers, rows):
        self.groups, self.sharers, self.rows = groups, sharers, rows
        self.count = groups * sharers
        self.paired = rows % 8 == 0 and self.count & (self.count - 1) == 0 and sharers >= 4 and groups >= 4
        core, *over_x = [1 << bit for bit in range(bits_of(sharers))]
        near, *far = [sharers << bit for bit in range(bits_of(groups))]
        self.core, self.over_x, self.near, self.far = core, over_x, near, far[::-1]
        self.wide_orders = ([[core], over_x, [near], far], [[core], [near], over_x, far])
        self.head_orders = ([[core], over_x + [near], far],)

    def exchange(self, values, bits):
        pairs = [(i, i ^ bits) for i in range(self.count)]
        return lax.ppermute(values, ("dp", "fsdp"), pairs)

    def gather(self, held, masks, gate=(), late=()):
        for bits in masks:
            held = jnp.concatenate([after(held, late), self.exchange(after(held, gate), bits)], axis=0)
        return held

    def gather_x(self, held, *gate):
        pieces = {0: held}
        for bits in self.over_x[::-1]:
            for name in list(pieces):
                pieces[name | bits] = self.exchange(after(pieces[name], gate), bits)
        return pieces

    def gather_near(self, pieces, gate=(), late=()):
        return {name: self.gather(held, [self.near], gate, late) for name, held in pieces.items()}

    def gather_core(self, pieces, *gate):
        found = dict(pieces)
        for name in pieces:
            found[name | self.core] = self.exchange(after(pieces[name], gate), self.core)
        return tuple(found[name] for name in range(self.sharers))

    def piece_rows(self, here):
        masks = self.far + [self.near]
        found = []
        for f in range(self.sharers):
            for n in range(self.groups):
                rel = f | ways_bits(masks, n)
                found.append((here ^ rel) * self.rows)
        return jnp.stack(found).astype(jnp.int32)

    def grad_rows(self, here, orders):
        found = []
        for order in orders:
            for place in range(self.count):
                rel, left = 0, self.count
                for masks in order:
                    left >>= len(masks)
                    rel |= ways_bits(masks, (place // left) % (1 << len(masks)))
                found.append((here ^ rel) * self.rows)
        return jnp.stack(found).astype(jnp.int32)

    def total_stage(self, values, masks, gate=(), late=()):
        found = [after(values, late)]
        found += [self.exchange(after(values, gate), ways_bits(masks, way)) for way in range(1, 1 << len(masks))]
        while len(found) > 1:
            found = [found[k] + found[k + 1] for k in range(0, len(found), 2)]
        return found[0]

    def reduce_stage(self, states, orders, stage, gate=(), late=()):
        sums = []
        for ways, order in zip(states, orders):
            sums.append(
                [after(ways[0], late)]
                + [
                    self.exchange(after(ways[n], gate), ways_bits(order[stage], n))
                    for n in range(1, len(ways))
                ]
            )
        if stage == len(orders[0]) - 1:
            return [sum(part.astype(f32) for part in parts)[0] for parts in sums]
        ways = 1 << len(orders[0][stage + 1])
        if stage == len(orders[0]) - 2:
            return [merge(sums, ways)]
        return [merge([parts], ways) for parts in sums]


def ways_bits(masks, way):
    return sum(bits for n, bits in enumerate(masks) if (way >> n) & 1)


def merge_kernel(widths, many, ways, *refs):
    ins, outs = refs[: len(widths) * many * ways], refs[len(widths) * many * ways :]
    for way in range(ways):
        first = 0
        for k, width in enumerate(widths):
            views = [ins[(k * many + n) * ways + way] for n in range(many)]
            total = views[0][...].astype(f32)
            for view in views[1:]:
                total = total + view[...].astype(f32)
            outs[way][:, :, first : first + width] = total.astype(bf16)
            first += width


def merge(groups, ways):
    blocks, rows, unused = groups[0][0].shape
    widths = [parts[0].shape[2] for parts in groups]
    share = blocks // ways
    steps = min(share, 4)

    def view(way, width):
        return pl.BlockSpec((share // steps, rows, width), lambda b: (b + way * steps, 0, 0))

    out = jax.ShapeDtypeStruct((share, rows, sum(widths)), bf16)
    many = len(groups[0])
    size = blocks * rows * sum(widths)
    return pl.pallas_call(
        functools.partial(merge_kernel, widths, many, ways),
        grid=(steps,),
        in_specs=[view(way, width) for width in widths for n in range(many) for way in range(ways)],
        out_specs=[view(0, sum(widths))] * ways,
        out_shape=[out] * ways,
        compiler_params=params(),
        cost_estimate=pl.CostEstimate(flops=many * size, bytes_accessed=(2 + 2 * many) * size, transcendentals=0),
        name="merge",
    )(*[part for parts in groups for part in parts for way in range(ways)])


def weight_copies(plan, rows_ref, pieces, weight_ref, sem_ref):
    if not plan.paired:
        return [pltpu.make_async_copy(pieces[0], weight_ref, sem_ref)]
    copies, first = [], 0
    for k in range(0, len(pieces), plan.sharers):
        width = pieces[k].shape[-1]
        for f in range(plan.sharers):
            for n in range(plan.groups):
                at = pl.multiple_of(rows_ref[f * plan.groups + n], 8)
                target = weight_ref.at[pl.ds(at, plan.rows), first : first + width]
                copies.append(pltpu.make_async_copy(pieces[k + f].at[n], target, sem_ref))
        first += width
    return copies


def load_weight(plan, rows_ref, pieces, weight_ref, sem_ref, *cleared):
    copies = weight_copies(plan, rows_ref, pieces, weight_ref, sem_ref)
    for copy in copies:
        copy.start()
    for ref in cleared:
        ref[...] = jnp.zeros_like(ref)
    for copy in copies:
        copy.wait()


def grad_shapes(plan, width, orders):
    if not plan.paired:
        return [jax.ShapeDtypeStruct((D, width), bf16)]
    half = plan.count // 2
    cut = first_part(width, orders)
    return [jax.ShapeDtypeStruct((half, plan.rows, w), bf16) for w in (cut, cut, width - cut, width - cut) if w > 0]


def first_part(width, orders):
    return (width // D + 1) // 2 * D if len(orders) == 2 else width


def stage_shape(plan):
    return (2, plan.count, plan.rows, D) if plan.paired else (2, D, D)


def store_grads(plan, orders, rows_ref, acc_ref, outs, stage_ref, sem_ref):
    width, step = acc_ref.shape[1], D
    cut = first_part(width, orders)
    half = plan.count // 2
    waiting = []
    for n in range(width // step):
        slot = n % 2
        cols = slice(n * step, (n + 1) * step)
        if len(waiting) == 2:
            for copy in waiting.pop(0):
                copy.wait()
        if not plan.paired:
            stage_ref[slot] = acc_ref[:, cols].astype(bf16)
            copies = [pltpu.make_async_copy(stage_ref.at[slot], outs[0].at[:, cols], sem_ref.at[slot])]
        else:
            late = n * step >= cut
            base = plan.count if late else 0
            start = n * step - (cut if late else 0)

            def fill(place, carry):
                at = pl.multiple_of(rows_ref[base + place], 8)
                stage_ref[slot, place] = acc_ref[pl.ds(at, plan.rows), cols].astype(bf16)
                return carry

            lax.fori_loop(0, plan.count, fill, 0, unroll=8)
            keep, send = outs[2:4] if late else outs[0:2]
            there = slice(start, start + step)
            copies = [
                pltpu.make_async_copy(stage_ref.at[slot, 0:half], keep.at[:, :, there], sem_ref.at[slot]),
                pltpu.make_async_copy(stage_ref.at[slot, half:], send.at[:, :, there], sem_ref.at[slot]),
            ]
        for copy in copies:
            copy.start()
        waiting.append(copies)
    for copies in waiting:
        for copy in copies:
            copy.wait()


def project_kernel(plan, len_ref, row_ref, tok_ref, pass_ref, table_ref, gain_ref, *rest):
    pieces, (out_ref, w_ref, sem_ref) = rest[:-3], rest[-3:]

    @pl.when(pl.program_id(0) == 0)
    def load():
        load_weight(plan, row_ref, pieces, w_ref, sem_ref)

    @pl.when(pl.program_id(0) <= last_block(len_ref[0]))
    def work():
        hot = onehot_rows(pass_ref[0])
        entry = tok_ref[...].astype(f32) + dot_tn(hot, table_ref[...])
        unit, unused = normalized(entry)
        normed = (unit * gain_ref[...]).astype(bf16)
        for part in range(3):
            out_ref[part] = dot_nn(normed, w_ref[:, part * D : (part + 1) * D]).astype(bf16)


def project(plan, length, piece_rows, tokens, pass_rows, table, gain, pieces):
    rows = tokens.shape[0]
    at = lambda b, n, r: (jnp.minimum(b, last_block(n[0])), 0)
    return pl.pallas_call(
        functools.partial(project_kernel, plan),
        grid_spec=pltpu.PrefetchScalarGridSpec(
            num_scalar_prefetch=2,
            grid=(rows // ROWS,),
            in_specs=[
                pl.BlockSpec((ROWS, D), at),
                pl.BlockSpec((1, 1, ROWS), lambda b, n, r: at(b, n, r) + (0,)),
                pl.BlockSpec((8, D), lambda b, n, r: (0, 0)),
                pl.BlockSpec((1, D), lambda b, n, r: (0, 0)),
            ]
            + [pl.BlockSpec(memory_space=pl.ANY)] * len(pieces),
            out_specs=pl.BlockSpec((3, ROWS, D), lambda b, n, r: (0,) + at(b, n, r)),
            scratch_shapes=[pltpu.VMEM((D, 3 * D), bf16), pltpu.SemaphoreType.DMA],
        ),
        out_shape=jax.ShapeDtypeStruct((3, rows, D), bf16),
        compiler_params=params(),
        cost_estimate=pl.CostEstimate(
            flops=2 * rows * D * 3 * D, bytes_accessed=rows * D * 8 + D * D * 6, transcendentals=0
        ),
        name="project",
    )(length, piece_rows, tokens, pass_rows, table, gain, *pieces)


def attend_kernel(len_ref, p_ref, out_ref, lse_ref):
    blocks = p_ref.shape[1] // ROWS
    lane = lax.broadcasted_iota(jnp.int32, (ROWS, 128), 1)
    first_head = lane < HEAD
    here = lax.broadcasted_iota(jnp.int32, (ROWS, ROWS), 0)
    there = lax.broadcasted_iota(jnp.int32, (ROWS, ROWS), 1)
    allowed = there <= here
    for i in range(blocks):
        rows = slice(i * ROWS, (i + 1) * ROWS)

        @pl.when(i * ROWS < len_ref[0])
        def work():
            query = p_ref[0, rows, :] * jnp.asarray(1.0 / math.sqrt(HEAD), bf16)
            found = []
            for head in range(2):
                mine = first_head if head == 0 else jnp.logical_not(first_head)
                q = jnp.where(mine, query, jnp.zeros_like(query))
                diag = dot_nt(q, p_ref[1, rows, :])
                diag = jnp.where(allowed, diag, -1e30)
                largest = jnp.max(diag, axis=-1, keepdims=True)
                if i > 0:
                    before = dot_nt(q, p_ref[1, : i * ROWS, :])
                    largest = jnp.maximum(largest, jnp.max(before, axis=-1, keepdims=True))
                diag = jnp.exp(diag - largest)
                total = jnp.sum(diag, axis=-1, keepdims=True)
                out = dot_nn(diag.astype(bf16), p_ref[2, rows, :])
                if i > 0:
                    before = jnp.exp(before - largest)
                    total = total + jnp.sum(before, axis=-1, keepdims=True)
                    out = out + dot_nn(before.astype(bf16), p_ref[2, : i * ROWS, :])
                found.append(out * (1.0 / total))
                lse = jnp.broadcast_to(largest + jnp.log(total), (ROWS, 128))
                lse_ref[0, head : head + 1, rows] = lse.T[0:1]
            out_ref[rows, :] = jnp.where(first_head, found[0], found[1]).astype(bf16)


def attend(length, projected):
    rows = projected.shape[1]
    pairs = HEADS // 2
    return pl.pallas_call(
        attend_kernel,
        grid_spec=pltpu.PrefetchScalarGridSpec(
            num_scalar_prefetch=1,
            grid=(pairs,),
            in_specs=[pl.BlockSpec((3, rows, 128), lambda h, n: (0, 0, h))],
            out_specs=[
                pl.BlockSpec((rows, 128), lambda h, n: (0, h)),
                pl.BlockSpec((1, 8, rows), lambda h, n: (h, 0, 0)),
            ],
        ),
        out_shape=[
            jax.ShapeDtypeStruct((rows, D), bf16),
            jax.ShapeDtypeStruct((pairs, 8, rows), f32),
        ],
        compiler_params=params(),
        cost_estimate=pl.CostEstimate(
            flops=2 * rows * rows * D, bytes_accessed=rows * D * 8, transcendentals=HEADS * rows * rows // 2
        ),
        name="attend",
    )(length, projected)


def attend_back_kernel(len_ref, p_ref, o_ref, g_ref, lse_ref, out_ref, dk_ref, dv_ref, kz_ref, vz_ref, kt_ref):
    blocks = p_ref.shape[1] // ROWS
    scaling = 1.0 / math.sqrt(HEAD)
    lane = lax.broadcasted_iota(jnp.int32, (ROWS, 128), 1)
    first_head = lane < HEAD
    row8 = lax.broadcasted_iota(jnp.int32, (8, 128), 0)
    lane8 = lax.broadcasted_iota(jnp.int32, (8, 128), 1)
    chooser = (lax.div(lane8, HEAD) == row8).astype(f32)
    key_at = lax.broadcasted_iota(jnp.int32, (2, ROWS, ROWS), 1)
    row_at = lax.broadcasted_iota(jnp.int32, (2, ROWS, ROWS), 2)
    allowed = (key_at <= row_at).reshape(2 * ROWS, ROWS)
    for i in range(blocks):
        rows = slice(i * ROWS, (i + 1) * ROWS)
        two = slice(2 * i * ROWS, 2 * (i + 1) * ROWS)

        @pl.when(i * ROWS < len_ref[0])
        def work():
            dk_ref[two, :] = jnp.zeros((2 * ROWS, 128), f32)
            dv_ref[two, :] = jnp.zeros((2 * ROWS, 128), f32)
            key, value = p_ref[1, rows, :], p_ref[2, rows, :]
            zero = jnp.zeros_like(key)
            k2 = jnp.concatenate([jnp.where(first_head, key, zero), jnp.where(first_head, zero, key)], axis=0)
            kz_ref[two, :] = k2
            kt_ref[:, two] = k2.T
            vz_ref[two, :] = jnp.concatenate([jnp.where(first_head, value, zero), jnp.where(first_head, zero, value)], axis=0)
            query = p_ref[0, rows, :] * jnp.asarray(scaling, bf16)
            grad = g_ref[rows, :]
            product = grad.astype(f32) * o_ref[rows, :].astype(f32)
            delta = lax.dot_general(chooser, product, (((1,), (1,)), ((), ())), precision=lax.Precision.HIGHEST, preferred_element_type=f32)
            def both(a, b):
                return jnp.concatenate([jnp.broadcast_to(a, (ROWS, ROWS)), jnp.broadcast_to(b, (ROWS, ROWS))], axis=0)
            lse2 = both(lse_ref[0, 0:1, rows], lse_ref[0, 1:2, rows])
            delta2 = both(delta[0:1], delta[1:2])
            dqt = jnp.zeros((128, ROWS), f32)
            for j in range(i + 1):
                cols = slice(2 * j * ROWS, 2 * (j + 1) * ROWS)
                prob = jnp.exp(dot_nt(kz_ref[cols, :], query) - lse2)
                if i == j:
                    prob = jnp.where(allowed, prob, 0.0)
                ds = (prob * (dot_nt(vz_ref[cols, :], grad) - delta2)).astype(bf16)
                dv_ref[cols, :] += dot_nn(prob.astype(bf16), grad)
                dk_ref[cols, :] += dot_nn(ds, query)
                dqt = dqt + dot_nn(kt_ref[:, cols], ds)
            out_ref[0, rows, :] = (dqt * scaling).T.astype(bf16)
    for i in range(blocks):
        rows = slice(i * ROWS, (i + 1) * ROWS)
        a = slice(2 * i * ROWS, (2 * i + 1) * ROWS); b = slice((2 * i + 1) * ROWS, 2 * (i + 1) * ROWS)

        @pl.when(i * ROWS < len_ref[0])
        def finish():
            out_ref[1, rows, :] = jnp.where(first_head, dk_ref[a, :], dk_ref[b, :]).astype(bf16)
            out_ref[2, rows, :] = jnp.where(first_head, dv_ref[a, :], dv_ref[b, :]).astype(bf16)


def blank_kernel(ready_ref, out_ref):
    pass


def blank(ready, shape):
    return pl.pallas_call(
        blank_kernel,
        in_specs=[pl.BlockSpec(memory_space=pltpu.SMEM)],
        out_specs=pl.BlockSpec(memory_space=pl.ANY),
        out_shape=shape,
        name="blank",
    )(ready)


def attend_back(choice, share, projected, heads_out, grad_heads, lse, before):
    rows = projected.shape[1]
    cols = lambda h, n: (0, n[2] + h)
    blocks = lambda h, n: (0, 0, n[2] + h)

    def kernel(n, p, o, g, l, unused, *rest):
        attend_back_kernel(n, p, o, g, l, *rest)

    return pl.pallas_call(
        kernel,
        grid_spec=pltpu.PrefetchScalarGridSpec(
            num_scalar_prefetch=1,
            grid=(share,),
            in_specs=[
                pl.BlockSpec((3, rows, 128), blocks),
                pl.BlockSpec((rows, 128), cols),
                pl.BlockSpec((None, rows, 128), lambda h, n: (n[1], 0, n[2] + h)),
                pl.BlockSpec((1, 8, rows), lambda h, n: (n[2] + h, 0, 0)),
                pl.BlockSpec(memory_space=pl.ANY),
            ],
            out_specs=pl.BlockSpec((3, rows, 128), blocks),
            scratch_shapes=[
                pltpu.VMEM((2 * rows, 128), f32),
                pltpu.VMEM((2 * rows, 128), f32),
                pltpu.VMEM((2 * rows, 128), bf16),
                pltpu.VMEM((2 * rows, 128), bf16),
                pltpu.VMEM((128, 2 * rows), bf16),
            ],
        ),
        out_shape=jax.ShapeDtypeStruct((3, rows, D), bf16),
        input_output_aliases={5: 0},
        compiler_params=params(),
        cost_estimate=pl.CostEstimate(
            flops=share * rows * rows * D, bytes_accessed=share * rows * D * 3, transcendentals=share * rows * rows
        ),
        name="attend_back",
    )(choice, projected, heads_out, grad_heads, lse, before)


def feed_kernel(plan, len_ref, row_ref, *refs):
    tok0, tok1, pass0, pass1, ho0, ho1, cot, table_ref, gain_ref = refs[:9]
    many = 2 * plan.sharers if plan.paired else 1
    grad_ref, pieces, refs = refs[9], refs[10 : 10 + many], refs[10 + many :]
    res, gh, hid, small_ref = refs[:4]
    outs, (w_ref, acc_ref, sums_ref, stage_ref, sem_ref) = refs[4:-5], refs[-5:]
    b = pl.program_id(0)
    many0 = last_block(len_ref[0]) + 1
    many1 = last_block(len_ref[1]) + 1
    early = b < many0

    @pl.when(b == 0)
    def clear():
        load_weight(plan, row_ref, pieces, w_ref, sem_ref.at[0], acc_ref, sums_ref)

    @pl.when(b < many0 + many1)
    def block():
        hot = onehot_rows(jnp.where(early, pass0[0], pass1[0]))
        entry = jnp.where(early, tok0[...], tok1[...]).astype(f32) + dot_tn(hot, table_ref[...])
        at = jnp.where(early, b, b - many0) * ROWS + lax.broadcasted_iota(jnp.int32, (ROWS, 1), 0)
        live = at < jnp.where(early, len_ref[0], len_ref[1])
        heads = jnp.where(early, ho0[...], ho1[...])
        attention = dot_nn(heads, w_ref[:, 0:D])
        hidden = entry + attention
        unit, scale = normalized(hidden)
        gain = gain_ref[...]
        normed = (unit * gain).astype(bf16)
        grad_feed = jnp.where(live, cot[...].reshape(ROWS, D).astype(f32), 0.0).astype(bf16)
        feed = jnp.zeros((ROWS, D), f32)
        grad_normed = jnp.zeros((ROWS, D), f32)
        for k in range(CHUNKS):
            up = slice(D + k * D, D + (k + 1) * D)
            down = slice(D + FF + k * D, D + FF + (k + 1) * D)
            x = dot_nn(normed, w_ref[:, up])
            grad_act = dot_nt(grad_feed, w_ref[:, down])
            c0 = math.sqrt(2.0 / math.pi)
            square = x * x
            bent = jnp.tanh(x * (c0 + (c0 * 0.044715) * square))
            half = 0.5 + 0.5 * bent
            slope = half + (0.5 * x) * (1.0 - bent * bent) * (c0 + (3.0 * c0 * 0.044715) * square)
            act = (x * half).astype(bf16)
            grad_x = (slope * grad_act).astype(bf16)
            feed = feed + dot_nn(act, w_ref[:, down])
            grad_normed = grad_normed + dot_nt(grad_x, w_ref[:, up])
            acc_ref[:, up] += dot_tn(normed, grad_x)
            acc_ref[:, down] += dot_tn(act, grad_feed)
        res[...] = jnp.where(live, hidden + feed, 0.0).astype(bf16).reshape(res.shape)
        sums_ref[0:8] += fold_rows(grad_normed * unit)
        sums_ref[8:16] += fold_rows(jnp.where(live, entry * entry, 0.0))
        sums_ref[16:24] += fold_rows(jnp.where(live, attention * attention, 0.0))
        sums_ref[24:32] += fold_rows(jnp.where(live, feed * feed, 0.0))
        grad_hidden = grad_feed.astype(f32) + norm_back(grad_normed * gain, unit, scale)
        hid[...] = grad_hidden
        grad_attention = grad_hidden.astype(bf16)
        acc_ref[:, 0:D] += dot_tn(heads, grad_attention)
        gh[...] = dot_nt(grad_attention, w_ref[:, 0:D]).astype(bf16)

    @pl.when(b == pl.num_programs(0) - 1)
    def finish():
        counted = (len_ref[0] + len_ref[1]).astype(f32)
        small_ref[...] = jnp.full(small_ref.shape, counted, f32)
        for n in range(4):
            small_ref[n : n + 1] = jnp.sum(sums_ref[8 * n : 8 * n + 8], axis=0, keepdims=True)
        store_grads(plan, plan.wide_orders, grad_ref, acc_ref, outs, stage_ref, sem_ref)


def feed(plan, part, lengths, piece_rows, grad_rows, tokens, pass_rows, heads_out, cotangent, table, gain, pieces, width):
    rows = tokens[0].shape[0]
    per = ROWS // part

    def at0(b, n, r):
        return jnp.minimum(b, last_block(n[0])), 0

    def at1(b, n, r):
        return jnp.clip(b - last_block(n[0]) - 1, 0, last_block(n[1])), 0

    def both(b, n, r):
        early = b <= last_block(n[0])
        return jnp.where(early, b, at1(b, n, r)[0]), jnp.where(early, 0, 1)

    row0 = pl.BlockSpec((ROWS, D), at0)
    row1 = pl.BlockSpec((ROWS, D), at1)
    pas0 = pl.BlockSpec((1, 1, ROWS), lambda *a: at0(*a) + (0,))
    pas1 = pl.BlockSpec((1, 1, ROWS), lambda *a: at1(*a) + (0,))
    dealt = pl.BlockSpec((per, 1, part, D), lambda *a: both(*a) + (0, 0))
    local = pl.BlockSpec((None, ROWS, D), lambda *a: both(*a)[::-1] + (0,))
    grads = grad_shapes(plan, width, plan.wide_orders)
    anywhere = pl.BlockSpec(memory_space=pl.ANY)
    return pl.pallas_call(
        functools.partial(feed_kernel, plan),
        grid_spec=pltpu.PrefetchScalarGridSpec(
            num_scalar_prefetch=2,
            grid=(2 * rows // ROWS,),
            in_specs=[
                row0, row1, pas0, pas1, row0, row1, dealt,
                pl.BlockSpec((8, D), lambda *a: (0, 0)),
                pl.BlockSpec((1, D), lambda *a: (0, 0)),
                pl.BlockSpec(memory_space=pltpu.SMEM),
            ]
            + [anywhere] * len(pieces),
            out_specs=[dealt, local, local, pl.BlockSpec((8, D), lambda *a: (0, 0))] + [anywhere] * len(grads),
            scratch_shapes=[
                pltpu.VMEM((D, width), bf16),
                pltpu.VMEM((D, width), f32),
                pltpu.VMEM((32, D), f32),
                pltpu.VMEM(stage_shape(plan), bf16),
                pltpu.SemaphoreType.DMA((2,)),
            ],
        ),
        out_shape=[
            jax.ShapeDtypeStruct(cotangent.shape, bf16),
            jax.ShapeDtypeStruct((2, rows, D), bf16),
            jax.ShapeDtypeStruct((2, rows, D), f32),
            jax.ShapeDtypeStruct((8, D), f32),
        ]
        + grads,
        compiler_params=params(),
        cost_estimate=pl.CostEstimate(
            flops=2 * 6 * rows * D * width, bytes_accessed=2 * rows * D * 14 + D * width * 4, transcendentals=2 * rows * FF
        ),
        name="feed",
    )(lengths, piece_rows, tokens[0], tokens[1], pass_rows[0], pass_rows[1], heads_out[0], heads_out[1],
      cotangent, table, gain, grad_rows, *pieces)


def project_back_kernel(plan, weight, rows_back, final, len_ref, row_ref, grad_ref, tok_ref, pass_ref, g_ref, *rest):
    rest = list(rest)
    hid_ref = rest.pop(0) if rows_back else None
    table_ref, gain_ref = rest.pop(0), rest.pop(0)
    before_ref = rest.pop(0) if final else None
    many = plan.sharers if plan.paired else 1
    pieces = [rest.pop(0) for n in range(many)] if rows_back else []
    if rows_back:
        out_ref, small_ref = rest.pop(0), rest.pop(0)
    if weight and not final:
        acc_ref = rest.pop(0)
    outs = [rest.pop(0) for shape in grad_shapes(plan, 3 * D, plan.head_orders)] if final else []
    if rows_back:
        w_ref, sums_ref = rest.pop(0), rest.pop(0)
    if final:
        acc_ref, stage_ref = rest.pop(0), rest.pop(0)
    sem_ref = rest.pop(0)
    b = pl.program_id(0)

    @pl.when(b == 0)
    def clear():
        if rows_back:
            load_weight(plan, row_ref, pieces, w_ref, sem_ref.at[0], sums_ref, *([acc_ref] if weight and not final else []))
        if final:
            copy = pltpu.make_async_copy(before_ref, acc_ref, sem_ref.at[0])
            copy.start()
            copy.wait()

    @pl.when(b <= last_block(len_ref[0]))
    def work():
        hot = onehot_rows(pass_ref[0])
        entry = tok_ref[...].astype(f32) + dot_tn(hot, table_ref[...])
        unit, scale = normalized(entry)
        gain = gain_ref[...]
        if weight:
            normed = (unit * gain).astype(bf16)
            for part in range(3):
                acc_ref[:, part * D : (part + 1) * D] += dot_tn(normed, g_ref[part])
        if rows_back:
            grad_normed = jnp.zeros((ROWS, D), f32)
            for part in range(3):
                grad_normed = grad_normed + dot_nt(g_ref[part], w_ref[:, part * D : (part + 1) * D])
            sums_ref[0:8] += fold_rows(grad_normed * unit)
            grad_entry = hid_ref[...] + norm_back(grad_normed * gain, unit, scale)
            high = grad_entry.astype(bf16)
            out_ref[...] = high
            rest_one = grad_entry - high.astype(f32)
            low = rest_one.astype(bf16)
            lower = (rest_one - low.astype(f32)).astype(bf16)
            sums_ref[8:16] += dot_nn(hot, high) + dot_nn(hot, low) + dot_nn(hot, lower)

    if rows_back:
        @pl.when(b == pl.num_programs(0) - 1)
        def sums():
            small_ref[...] = sums_ref[8:16]
            small_ref[PASSES : PASSES + 1] = jnp.sum(sums_ref[0:8], axis=0, keepdims=True)

    if final:
        @pl.when(b == pl.num_programs(0) - 1)
        def finish():
            store_grads(plan, plan.head_orders, grad_ref, acc_ref, outs, stage_ref, sem_ref)


def project_back(
    plan, weight, rows_back, which, length, piece_rows, grad_rows, tokens, pass_rows, grads, grad_hidden, table, gain,
    pieces, before=None,
):
    rows = tokens.shape[0]
    final = before is not None
    at = lambda b, n, r, g: (jnp.minimum(b, last_block(n[0])), 0)
    row = pl.BlockSpec((ROWS, D), at)
    anywhere = pl.BlockSpec(memory_space=pl.ANY)
    in_specs = [
        row,
        pl.BlockSpec((1, 1, ROWS), lambda *a: at(*a) + (0,)),
        pl.BlockSpec((3, ROWS, D), lambda *a: (0,) + at(*a)),
    ]
    operands = [length, piece_rows, grad_rows, tokens, pass_rows, grads]
    if rows_back:
        in_specs.append(pl.BlockSpec((None, ROWS, D), lambda *a: (which,) + at(*a)))
        operands.append(grad_hidden)
    in_specs += [pl.BlockSpec((8, D), lambda *a: (0, 0)), pl.BlockSpec((1, D), lambda *a: (0, 0))]
    operands += [table, gain]
    out_shape, out_specs, scratch = [], [], []
    if final:
        in_specs.append(anywhere)
        operands.append(before)
    if rows_back:
        in_specs += [anywhere] * len(pieces)
        operands += pieces
        out_shape += [jax.ShapeDtypeStruct((rows, D), bf16), jax.ShapeDtypeStruct((8, D), f32)]
        out_specs += [row, pl.BlockSpec((8, D), lambda *a: (0, 0))]
        scratch += [pltpu.VMEM((D, 3 * D), bf16), pltpu.VMEM((16, D), f32)]
    if weight and not final:
        out_shape.append(jax.ShapeDtypeStruct((D, 3 * D), f32))
        out_specs.append(pl.BlockSpec((D, 3 * D), lambda *a: (0, 0)))
    if final:
        shapes = grad_shapes(plan, 3 * D, plan.head_orders)
        out_shape += shapes
        out_specs += [anywhere] * len(shapes)
        scratch += [pltpu.VMEM((D, 3 * D), f32), pltpu.VMEM(stage_shape(plan), bf16)]
    return pl.pallas_call(
        functools.partial(project_back_kernel, plan, weight, rows_back, final),
        grid_spec=pltpu.PrefetchScalarGridSpec(
            num_scalar_prefetch=3,
            grid=(rows // ROWS,),
            in_specs=in_specs,
            out_specs=out_specs,
            scratch_shapes=scratch + [pltpu.SemaphoreType.DMA((2,))],
        ),
        out_shape=out_shape,
        compiler_params=params(),
        cost_estimate=pl.CostEstimate(
            flops=2 * (weight + rows_back) * rows * D * 3 * D, bytes_accessed=rows * D * 14 + D * D * 6, transcendentals=0
        ),
        name="project_back",
    )(*operands)


def pick_kernel(index_ref, in_ref, out_ref, sem_ref):
    copies = [
        pltpu.make_async_copy(in_ref.at[index_ref[n]], out_ref.at[n], sem_ref) for n in range(out_ref.shape[0])
    ]
    for copy in copies:
        copy.start()
    for copy in copies:
        copy.wait()


def pick(index, blocks):
    shape = index.shape + blocks.shape[1:]
    return pl.pallas_call(
        pick_kernel,
        grid_spec=pltpu.PrefetchScalarGridSpec(
            num_scalar_prefetch=1,
            grid=(1,),
            in_specs=[pl.BlockSpec(memory_space=pl.ANY)],
            out_specs=pl.BlockSpec(shape, lambda b, n: (0, 0, 0)),
            scratch_shapes=[pltpu.SemaphoreType.DMA],
        ),
        out_shape=jax.ShapeDtypeStruct(shape, blocks.dtype),
        compiler_params=params(),
        cost_estimate=pl.CostEstimate(flops=0, bytes_accessed=4 * math.prod(shape), transcendentals=0),
        name="pick",
    )(index, blocks)


def settle_kernel(index_ref, *refs):
    arrays, out_ref = refs[:-1], refs[-1]
    first = pl.program_id(0) * out_ref.shape[0]
    rows = out_ref.shape[1]
    at = lax.broadcasted_iota(jnp.int32, (rows, 1), 0)
    for n in range(out_ref.shape[0]):
        live = at < index_ref[2, first + n]
        source, late = index_ref[1, first + n], index_ref[0, first + n]
        if len(arrays) == 1:
            found = arrays[0][2 * source + late]
        else:
            found = jnp.where(late == 0, arrays[0][source], arrays[1][source])
        out_ref[n] = jnp.where(live, found.astype(f32), 0.0)


def settle(index, *arrays):
    many = index.shape[1]
    step = 4
    shape = arrays[0].shape
    whole = pl.BlockSpec(shape, lambda b, n: (0, 0, 0), pipeline_mode=pl.Buffered(1))
    return pl.pallas_call(
        settle_kernel,
        grid_spec=pltpu.PrefetchScalarGridSpec(
            num_scalar_prefetch=1,
            grid=(many // step,),
            in_specs=[whole] * len(arrays),
            out_specs=pl.BlockSpec((step,) + shape[1:], lambda b, n: (b, 0, 0)),
        ),
        out_shape=jax.ShapeDtypeStruct((many,) + shape[1:], f32),
        compiler_params=params(),
        cost_estimate=pl.CostEstimate(flops=0, bytes_accessed=6 * many * math.prod(shape[1:]), transcendentals=0),
        name="settle",
    )(index, *arrays)


def after(values, *others):
    return lax.optimization_barrier((values, others))[0]


def swap(blocks):
    return lax.all_to_all(blocks, "dp", split_axis=0, concat_axis=0, tiled=True)


def per_device(
    groups,
    width_all,
    tokens,
    passes,
    lengths,
    dealing,
    pass_table,
    gain_first,
    to_heads,
    from_heads,
    gain_second,
    expand,
    shrink,
    cotangent,
):
    axes = ("dp", "fsdp")
    slots, part, unused_width = tokens.shape
    seq_len = part * groups
    order = jnp.arange(slots, dtype=jnp.int32)
    here = lax.axis_index("dp")
    ordering = dealing[0, 0]
    sizes = lengths[0]

    ahead = (sizes[None, :] > sizes[:, None]) | (
        (sizes[None, :] == sizes[:, None]) & (order[None, :] < order[:, None])
    )
    rank = jnp.sum(ahead.astype(jnp.int32), axis=1)
    ranked = jnp.sum(jnp.where(rank[None, :] == order[:, None], order[None, :], 0), axis=1)
    place = jnp.sum(jnp.where(ordering[None, :] == order[:, None], order[None, :], 0), axis=1)
    early_seqs = ranked[:groups]
    late_seqs = ranked[groups:][::-1]
    from_early = jnp.sum(jnp.where(early_seqs[:, None] == order[None, :], place[None, :], 0), axis=1)
    from_late = jnp.sum(jnp.where(late_seqs[:, None] == order[None, :], place[None, :], 0), axis=1)
    slot_rank = jnp.sum(jnp.where(ordering[:, None] == order[None, :], rank[None, :], 0), axis=1)
    slot_size = jnp.sum(jnp.where(ordering[:, None] == order[None, :], sizes[None, :], 0), axis=1)
    is_late = (slot_rank >= groups).astype(jnp.int32)
    source = jnp.where(is_late == 1, slots - 1 - slot_rank, slot_rank)
    back_index = jnp.stack([is_late, source, slot_size - here * part])
    my_seqs = jnp.stack([early_seqs[here], late_seqs[here]])
    my_sizes = jnp.sum(jnp.where(my_seqs[:, None] == order[None, :], sizes[None, :], 0), axis=1)

    row_count = to_heads.shape[0]
    narrow = jnp.concatenate(
        [
            from_heads,
            expand.reshape(row_count, D, CHUNKS).transpose(0, 2, 1).reshape(row_count, FF),
            shrink.reshape(row_count, CHUNKS * D),
        ],
        axis=1,
    )
    plan = Plan(groups, width_all // groups, row_count)
    index_here = here * (width_all // groups) + lax.axis_index("fsdp")
    my_passes = [passes[my_seqs[m]].reshape(seq_len // ROWS, 1, ROWS) for m in range(2)]
    one_size = [my_sizes[m : m + 1] for m in range(2)]
    table = jnp.zeros((8, D), bf16).at[:PASSES].set(pass_table)
    gain_one = gain_first.astype(f32).reshape(1, D)
    gain_two = gain_second.astype(f32).reshape(1, D)

    pairs_index = jnp.stack([from_early, from_late], axis=1).reshape(slots)
    picked = [pick(from_early, tokens), pick(from_late, tokens), pick(pairs_index, cotangent)]
    if plan.paired:
        piece_rows = plan.piece_rows(index_here)
        wide_rows = plan.grad_rows(index_here, plan.wide_orders)
        head_rows = plan.grad_rows(index_here, plan.head_orders)
        head_far = plan.gather(to_heads[None], plan.far)
        head_near = plan.gather(head_far, [plan.near])
        wide_one = plan.gather(after(narrow, head_far)[None], plan.far[:1])
        ready = (my_passes, one_size, piece_rows, table, gain_one)
        tokens0 = swap(after(picked[0], head_near, wide_one, ready))
        head_pieces = plan.gather_core(plan.gather_x(head_near))
    else:
        piece_rows = wide_rows = head_rows = jnp.zeros((1,), jnp.int32)
        head_pieces = (lax.all_gather(to_heads, axes, axis=0, tiled=True),)
        wide_pieces = (lax.all_gather(narrow, axes, axis=0, tiled=True),)
        tokens0 = swap(picked[0])
        wide_far = wide_pieces

    def forward(m, *gate):
        return project(
            plan, after(one_size[m], gate), piece_rows, my_tokens[m], my_passes[m], table, gain_one, head_pieces
        )

    def mix(m, *gate):
        return attend(after(one_size[m], gate), projected[m])

    half = HEADS // 4
    choices = {
        (m, first): jnp.stack([my_sizes[m], jnp.int32(m), jnp.int32(first)]) for m in range(2) for first in (0, half)
    }

    def mix_back(m, first, before, *gate):
        return attend_back(after(choices[m, first], gate), half, projected[m], heads_out[m], grad_heads, lse[m], before)

    def back(m, weight, rows_back, *gate, before=None):
        return project_back(
            plan, weight, rows_back, m, after(one_size[m], gate), piece_rows, head_rows, my_tokens[m], my_passes[m],
            grad_parts[m], grad_hidden, table, gain_one, head_pieces, before,
        )

    def send_back(rows, *gate):
        return swap(after(rows, gate).reshape(groups, part, D))

    projected, heads_out, lse, grad_parts = [None, None], [None, None], [None, None], [None, None]
    my_tokens = [tokens0.reshape(seq_len, D)]
    projected[0] = forward(0)
    if plan.paired:
        wide_far = plan.gather(wide_one, plan.far[1:], head_pieces, projected[0])
        cut = first_part(wide_far.shape[-1], plan.wide_orders)
    tokens1 = swap(after(picked[1], tokens0, picked[2], wide_far))
    my_tokens.append(tokens1.reshape(seq_len, D))
    heads_out[0], lse[0] = mix(0, wide_far)
    if plan.paired:
        first = plan.gather_near({0: wide_far[:, :, :cut]}, (), lse[0])
        second = plan.gather_x(wide_far[:, :, cut:], ())
        ready = (first, second)
    else:
        ready = ()
    my_grads = swap(after(picked[2].reshape(groups, 2, part, D), tokens1, lse[0], ready))
    projected[1] = forward(1, lse[0])
    if plan.paired:
        first = plan.gather_x(first[0])
        second = plan.gather_near(second, lse[0], projected[1])
    heads_out[1], lse[1] = mix(1)
    if plan.paired:
        wide_pieces = plan.gather_core(first, lse[1]) + plan.gather_core(second, lse[1])

    res, grad_heads, grad_hidden, feed_small, *wide_grads = feed(
        plan, part, after(my_sizes, choices), piece_rows, wide_rows, my_tokens, my_passes, heads_out, my_grads, table, gain_two,
        wide_pieces, D + 2 * FF,
    )

    def begin(grads):
        if not plan.paired:
            return lax.psum_scatter(grads[0], axes, scatter_dimension=0, tiled=True).astype(f32)
        return [grads[n : n + 2] for n in range(0, len(grads), 2)]

    def advance(state, stage, gate, late):
        return plan.reduce_stage(state, plan.wide_orders, stage, (gate,), (late,)) if plan.paired else state

    space = jax.ShapeDtypeStruct((3, seq_len, D), bf16)
    wide0 = begin(wide_grads)
    result = swap(res)
    some = mix_back(0, 0, blank(one_size[0], space))
    wide1 = advance(wide0, 0, (), some)
    grad_parts[0] = mix_back(0, half, some, wide1)
    entry0, small0, head_sum = back(0, True, True)
    wide2 = advance(wide1, 1, some, entry0)
    moved0 = send_back(entry0, result)
    some = mix_back(1, 0, blank(one_size[1], space), entry0, wide2, result)
    wide3 = advance(wide2, 2, entry0, some)
    grad_parts[1] = mix_back(1, half, some, wide3)
    entry1, small1 = back(1, False, True)
    wide_owned = advance(wide3, 3, some, entry1)
    moved1 = send_back(entry1, moved0, wide_owned)
    totals = jnp.concatenate([small0 + small1, feed_small], axis=0)
    head_grads = back(1, True, False, entry1, moved0, before=head_sum)
    head_state = begin(head_grads)
    if plan.paired:
        orders = plan.head_orders
        totals = plan.total_stage(totals, orders[0][0], (), head_grads[:1])
        head_state = plan.reduce_stage(head_state, orders, 0, (wide_owned,))
    output = settle(after(back_index, head_state), result.reshape(slots, part, D))
    grad_tokens = settle(after(back_index, output), moved0, moved1)
    if plan.paired:
        totals = plan.total_stage(totals, orders[0][1])
        head_state = plan.reduce_stage(head_state, orders, 1, (totals,), (output, grad_tokens))
        totals = plan.total_stage(totals, orders[0][2], (head_state,))
        head_owned = plan.reduce_stage(head_state, orders, 2)[0]
        wide_owned = wide_owned[0]
    else:
        totals = lax.psum(totals, axes)
        head_owned = head_state
    root_squares = jnp.sqrt(jnp.sum(totals[9:12], axis=1) / (totals[12, 0] * D))

    grad_expand = wide_owned[:, D : D + FF].reshape(row_count, CHUNKS, D).transpose(0, 2, 1)
    return (
        output,
        grad_tokens,
        totals[:PASSES],
        totals[PASSES],
        head_owned,
        wide_owned[:, :D],
        totals[8],
        grad_expand.reshape(row_count, FF),
        wide_owned[:, D + FF :].reshape(row_count * CHUNKS, D),
        root_squares,
    )


def solution(mesh):
    groups = mesh.shape["dp"]
    weight_spec = P(("dp", "fsdp"), None)
    block_spec = P("fsdp", "dp", None)
    in_specs = (
        block_spec,
        P("fsdp", None),
        P("fsdp", None),
        P("dp", "fsdp", None),
        P(),
        P(),
        weight_spec,
        weight_spec,
        P(),
        weight_spec,
        weight_spec,
        block_spec,
    )
    out_specs = (
        block_spec,
        block_spec,
        P(),
        P(),
        weight_spec,
        weight_spec,
        P(),
        weight_spec,
        weight_spec,
        P(),
    )
    body = functools.partial(per_device, groups, groups * mesh.shape["fsdp"])
    return jax.shard_map(body, mesh=mesh, in_specs=in_specs, out_specs=out_specs, check_vma=False)
```

```python
import math
import functools

import jax
import jax.numpy as jnp
from jax import lax
from jax.experimental import pallas as pl
from jax.experimental.pallas import tpu as pltpu
from jax.sharding import PartitionSpec as P

D = 768
HEADS = 12
HEAD = 64
FF = 3072
PASSES = 5
EPS = 1e-05
ROWS = 256
CHUNKS = FF // D
VMEM_MOST = 64000 * 1024

f32 = jnp.float32
bf16 = jnp.bfloat16


def dot_nn(a, b):
    return lax.dot_general(a, b, (((1,), (0,)), ((), ())), preferred_element_type=f32)


def dot_nt(a, b):
    return lax.dot_general(a, b, (((1,), (1,)), ((), ())), preferred_element_type=f32)


def dot_tn(a, b):
    return lax.dot_general(a, b, (((0,), (0,)), ((), ())), preferred_element_type=f32)


def params(**more):
    return pltpu.CompilerParams(vmem_limit_bytes=VMEM_MOST, **more)


def normalized(values):
    centred = values - jnp.mean(values, axis=-1, keepdims=True)
    spread = jnp.mean(centred * centred, axis=-1, keepdims=True)
    scale = lax.rsqrt(spread + EPS)
    return centred * scale, scale


def norm_back(grad_unit, unit, scale):
    first = jnp.mean(grad_unit, axis=-1, keepdims=True)
    second = jnp.mean(grad_unit * unit, axis=-1, keepdims=True)
    return scale * (grad_unit - first - unit * second)


def onehot_rows(pass_row):
    ids = lax.broadcasted_iota(jnp.int32, (8, pass_row.shape[-1]), 0)
    return (ids == pass_row).astype(f32).astype(bf16)


def fold_rows(values):
    rows, width = values.shape
    return jnp.sum(values.reshape(rows // 8, 8, width), axis=0)


def last_block(length):
    return lax.div(length + (ROWS - 1), ROWS) - 1


def bits_of(count):
    return count.bit_length() - 1


class Plan:
    def __init__(self, groups, sharers, rows):
        self.groups, self.sharers, self.rows = groups, sharers, rows
        self.count = groups * sharers
        self.paired = rows % 8 == 0 and self.count & (self.count - 1) == 0 and sharers >= 4 and groups >= 4
        core, *over_x = [1 << bit for bit in range(bits_of(sharers))]
        near, *far = [sharers << bit for bit in range(bits_of(groups))]
        self.core, self.over_x, self.near, self.far = core, over_x, near, far[::-1]
        self.wide_orders = ([[core], over_x, [near], far], [[core], [near], over_x, far])
        self.head_orders = ([[core], over_x + [near], far],)

    def exchange(self, values, bits):
        pairs = [(i, i ^ bits) for i in range(self.count)]
        return lax.ppermute(values, ("dp", "fsdp"), pairs)

    def gather(self, held, masks, gate=(), late=()):
        for bits in masks:
            held = jnp.concatenate([after(held, late), self.exchange(after(held, gate), bits)], axis=0)
        return held

    def gather_x(self, held, *gate):
        pieces = {0: held}
        for bits in self.over_x[::-1]:
            for name in list(pieces):
                pieces[name | bits] = self.exchange(after(pieces[name], gate), bits)
        return pieces

    def gather_near(self, pieces, gate=(), late=()):
        return {name: self.gather(held, [self.near], gate, late) for name, held in pieces.items()}

    def gather_core(self, pieces, *gate):
        found = dict(pieces)
        for name in pieces:
            found[name | self.core] = self.exchange(after(pieces[name], gate), self.core)
        return tuple(found[name] for name in range(self.sharers))

    def piece_rows(self, here):
        masks = self.far + [self.near]
        found = []
        for f in range(self.sharers):
            for n in range(self.groups):
                rel = f | ways_bits(masks, n)
                found.append((here ^ rel) * self.rows)
        return jnp.stack(found).astype(jnp.int32)

    def grad_rows(self, here, orders):
        found = []
        for order in orders:
            for place in range(self.count):
                rel, left = 0, self.count
                for masks in order:
                    left >>= len(masks)
                    rel |= ways_bits(masks, (place // left) % (1 << len(masks)))
                found.append((here ^ rel) * self.rows)
        return jnp.stack(found).astype(jnp.int32)

    def total_stage(self, values, masks, gate=(), late=()):
        found = [after(values, late)]
        found += [self.exchange(after(values, gate), ways_bits(masks, way)) for way in range(1, 1 << len(masks))]
        while len(found) > 1:
            found = [found[k] + found[k + 1] for k in range(0, len(found), 2)]
        return found[0]

    def reduce_stage(self, states, orders, stage, gate=(), late=()):
        sums = []
        for ways, order in zip(states, orders):
            sums.append(
                [after(ways[0], late)]
                + [
                    self.exchange(after(ways[n], gate), ways_bits(order[stage], n))
                    for n in range(1, len(ways))
                ]
            )
        if stage == len(orders[0]) - 1:
            return [sum(part.astype(f32) for part in parts)[0] for parts in sums]
        ways = 1 << len(orders[0][stage + 1])
        if stage == len(orders[0]) - 2:
            return [merge(sums, ways)]
        return [merge([parts], ways) for parts in sums]


def ways_bits(masks, way):
    return sum(bits for n, bits in enumerate(masks) if (way >> n) & 1)


def merge_kernel(widths, many, ways, *refs):
    ins, outs = refs[: len(widths) * many * ways], refs[len(widths) * many * ways :]
    for way in range(ways):
        first = 0
        for k, width in enumerate(widths):
            views = [ins[(k * many + n) * ways + way] for n in range(many)]
            total = views[0][...].astype(f32)
            for view in views[1:]:
                total = total + view[...].astype(f32)
            outs[way][:, :, first : first + width] = total.astype(bf16)
            first += width


def merge(groups, ways):
    blocks, rows, unused = groups[0][0].shape
    widths = [parts[0].shape[2] for parts in groups]
    share = blocks // ways
    steps = min(share, 4)

    def view(way, width):
        return pl.BlockSpec((share // steps, rows, width), lambda b: (b + way * steps, 0, 0))

    out = jax.ShapeDtypeStruct((share, rows, sum(widths)), bf16)
    many = len(groups[0])
    size = blocks * rows * sum(widths)
    return pl.pallas_call(
        functools.partial(merge_kernel, widths, many, ways),
        grid=(steps,),
        in_specs=[view(way, width) for width in widths for n in range(many) for way in range(ways)],
        out_specs=[view(0, sum(widths))] * ways,
        out_shape=[out] * ways,
        compiler_params=params(),
        cost_estimate=pl.CostEstimate(flops=many * size, bytes_accessed=(2 + 2 * many) * size, transcendentals=0),
        name="merge",
    )(*[part for parts in groups for part in parts for way in range(ways)])


def weight_copies(plan, rows_ref, pieces, weight_ref, sem_ref, group):
    if not plan.paired:
        return [pltpu.make_async_copy(pieces[0], weight_ref, sem_ref.at[0])] if group == 0 else []
    mine = pieces[group * plan.sharers : (group + 1) * plan.sharers]
    if len(mine) == 0:
        return []
    first = pieces[0].shape[-1] * group
    copies = []
    for f, piece in enumerate(mine):
        for n in range(plan.groups):
            at = pl.multiple_of(rows_ref[f * plan.groups + n], 8)
            target = weight_ref.at[pl.ds(at, plan.rows), first : first + piece.shape[-1]]
            copies.append(pltpu.make_async_copy(piece.at[n], target, sem_ref.at[group]))
    return copies


def load_weight(plan, rows_ref, pieces, weight_ref, sem_ref, *cleared):
    first, second = [weight_copies(plan, rows_ref, pieces, weight_ref, sem_ref, group) for group in range(2)]
    for copy in first + second:
        copy.start()
    for ref in cleared:
        ref[...] = jnp.zeros_like(ref)
    for copy in first:
        copy.wait()


def grad_shapes(plan, width, orders):
    if not plan.paired:
        return [jax.ShapeDtypeStruct((D, width), bf16)]
    half = plan.count // 2
    cut = first_part(width, orders)
    return [jax.ShapeDtypeStruct((half, plan.rows, w), bf16) for w in (cut, cut, width - cut, width - cut) if w > 0]


def first_part(width, orders):
    return (width // D + 1) // 2 * D if len(orders) == 2 else width


def stage_shape(plan):
    return (2, plan.count, plan.rows, D) if plan.paired else (2, D, D)


def store_grads(plan, orders, rows_ref, acc_ref, outs, stage_ref, sem_ref):
    width, step = acc_ref.shape[1], D
    cut = first_part(width, orders)
    half = plan.count // 2
    waiting = []
    for n in range(width // step):
        slot = n % 2
        cols = slice(n * step, (n + 1) * step)
        if len(waiting) == 2:
            for copy in waiting.pop(0):
                copy.wait()
        if not plan.paired:
            stage_ref[slot] = acc_ref[:, cols].astype(bf16)
            copies = [pltpu.make_async_copy(stage_ref.at[slot], outs[0].at[:, cols], sem_ref.at[slot])]
        else:
            late = n * step >= cut
            base = plan.count if late else 0
            start = n * step - (cut if late else 0)

            def fill(place, carry):
                at = pl.multiple_of(rows_ref[base + place], 8)
                stage_ref[slot, place] = acc_ref[pl.ds(at, plan.rows), cols].astype(bf16)
                return carry

            lax.fori_loop(0, plan.count, fill, 0, unroll=8)
            keep, send = outs[2:4] if late else outs[0:2]
            there = slice(start, start + step)
            copies = [
                pltpu.make_async_copy(stage_ref.at[slot, 0:half], keep.at[:, :, there], sem_ref.at[slot]),
                pltpu.make_async_copy(stage_ref.at[slot, half:], send.at[:, :, there], sem_ref.at[slot]),
            ]
        for copy in copies:
            copy.start()
        waiting.append(copies)
    for copies in waiting:
        for copy in copies:
            copy.wait()


def project_kernel(plan, len_ref, row_ref, tok_ref, pass_ref, table_ref, gain_ref, *rest):
    pieces, (out_ref, w_ref, sem_ref) = rest[:-3], rest[-3:]

    @pl.when(pl.program_id(0) == 0)
    def load():
        load_weight(plan, row_ref, pieces, w_ref, sem_ref)

    @pl.when(pl.program_id(0) <= last_block(len_ref[0]))
    def work():
        hot = onehot_rows(pass_ref[0])
        entry = tok_ref[...].astype(f32) + dot_tn(hot, table_ref[...])
        unit, unused = normalized(entry)
        normed = (unit * gain_ref[...]).astype(bf16)
        for part in range(3):
            out_ref[part] = dot_nn(normed, w_ref[:, part * D : (part + 1) * D]).astype(bf16)


def project(plan, length, piece_rows, tokens, pass_rows, table, gain, pieces):
    rows = tokens.shape[0]
    at = lambda b, n, r: (jnp.minimum(b, last_block(n[0])), 0)
    return pl.pallas_call(
        functools.partial(project_kernel, plan),
        grid_spec=pltpu.PrefetchScalarGridSpec(
            num_scalar_prefetch=2,
            grid=(rows // ROWS,),
            in_specs=[
                pl.BlockSpec((ROWS, D), at),
                pl.BlockSpec((1, 1, ROWS), lambda b, n, r: at(b, n, r) + (0,)),
                pl.BlockSpec((8, D), lambda b, n, r: (0, 0)),
                pl.BlockSpec((1, D), lambda b, n, r: (0, 0)),
            ]
            + [pl.BlockSpec(memory_space=pl.ANY)] * len(pieces),
            out_specs=pl.BlockSpec((3, ROWS, D), lambda b, n, r: (0,) + at(b, n, r)),
            scratch_shapes=[pltpu.VMEM((D, 3 * D), bf16), pltpu.SemaphoreType.DMA((1,))],
        ),
        out_shape=jax.ShapeDtypeStruct((3, rows, D), bf16),
        compiler_params=params(),
        cost_estimate=pl.CostEstimate(
            flops=2 * rows * D * 3 * D, bytes_accessed=rows * D * 8 + D * D * 6, transcendentals=0
        ),
        name="project",
    )(length, piece_rows, tokens, pass_rows, table, gain, *pieces)


def attend_kernel(len_ref, p_ref, out_ref, lse_ref):
    blocks = p_ref.shape[1] // ROWS
    lane = lax.broadcasted_iota(jnp.int32, (ROWS, 128), 1)
    first_head = lane < HEAD
    here = lax.broadcasted_iota(jnp.int32, (ROWS, ROWS), 0)
    there = lax.broadcasted_iota(jnp.int32, (ROWS, ROWS), 1)
    allowed = there <= here
    for i in range(blocks):
        rows = slice(i * ROWS, (i + 1) * ROWS)

        @pl.when(i * ROWS < len_ref[0])
        def work():
            query = p_ref[0, rows, :] * jnp.asarray(1.0 / math.sqrt(HEAD), bf16)
            found = []
            for head in range(2):
                mine = first_head if head == 0 else jnp.logical_not(first_head)
                q = jnp.where(mine, query, jnp.zeros_like(query))
                diag = dot_nt(q, p_ref[1, rows, :])
                diag = jnp.where(allowed, diag, -1e30)
                largest = jnp.max(diag, axis=-1, keepdims=True)
                if i > 0:
                    before = dot_nt(q, p_ref[1, : i * ROWS, :])
                    largest = jnp.maximum(largest, jnp.max(before, axis=-1, keepdims=True))
                diag = jnp.exp(diag - largest)
                total = jnp.sum(diag, axis=-1, keepdims=True)
                out = dot_nn(diag.astype(bf16), p_ref[2, rows, :])
                if i > 0:
                    before = jnp.exp(before - largest)
                    total = total + jnp.sum(before, axis=-1, keepdims=True)
                    out = out + dot_nn(before.astype(bf16), p_ref[2, : i * ROWS, :])
                found.append(out * (1.0 / total))
                lse = jnp.broadcast_to(largest + jnp.log(total), (ROWS, 128))
                lse_ref[0, head : head + 1, rows] = lse.T[0:1]
            out_ref[rows, :] = jnp.where(first_head, found[0], found[1]).astype(bf16)


def attend(length, projected):
    rows = projected.shape[1]
    pairs = HEADS // 2
    return pl.pallas_call(
        attend_kernel,
        grid_spec=pltpu.PrefetchScalarGridSpec(
            num_scalar_prefetch=1,
            grid=(pairs,),
            in_specs=[pl.BlockSpec((3, rows, 128), lambda h, n: (0, 0, h))],
            out_specs=[
                pl.BlockSpec((rows, 128), lambda h, n: (0, h)),
                pl.BlockSpec((1, 8, rows), lambda h, n: (h, 0, 0)),
            ],
        ),
        out_shape=[
            jax.ShapeDtypeStruct((rows, D), bf16),
            jax.ShapeDtypeStruct((pairs, 8, rows), f32),
        ],
        compiler_params=params(),
        cost_estimate=pl.CostEstimate(
            flops=2 * rows * rows * D, bytes_accessed=rows * D * 8, transcendentals=HEADS * rows * rows // 2
        ),
        name="attend",
    )(length, projected)


def attend_back_kernel(len_ref, p_ref, o_ref, g_ref, lse_ref, out_ref, dk_ref, dv_ref, kz_ref, vz_ref, kt_ref):
    blocks = p_ref.shape[1] // ROWS
    scaling = 1.0 / math.sqrt(HEAD)
    lane = lax.broadcasted_iota(jnp.int32, (ROWS, 128), 1)
    first_head = lane < HEAD
    row8 = lax.broadcasted_iota(jnp.int32, (8, 128), 0)
    lane8 = lax.broadcasted_iota(jnp.int32, (8, 128), 1)
    chooser = (lax.div(lane8, HEAD) == row8).astype(f32)
    key_at = lax.broadcasted_iota(jnp.int32, (2, ROWS, ROWS), 1)
    row_at = lax.broadcasted_iota(jnp.int32, (2, ROWS, ROWS), 2)
    allowed = (key_at <= row_at).reshape(2 * ROWS, ROWS)
    for i in range(blocks):
        rows = slice(i * ROWS, (i + 1) * ROWS)
        two = slice(2 * i * ROWS, 2 * (i + 1) * ROWS)

        @pl.when(i * ROWS < len_ref[0])
        def work():
            dk_ref[two, :] = jnp.zeros((2 * ROWS, 128), f32)
            dv_ref[two, :] = jnp.zeros((2 * ROWS, 128), f32)
            key, value = p_ref[1, rows, :], p_ref[2, rows, :]
            zero = jnp.zeros_like(key)
            k2 = jnp.concatenate([jnp.where(first_head, key, zero), jnp.where(first_head, zero, key)], axis=0)
            kz_ref[two, :] = k2
            kt_ref[:, two] = k2.T
            vz_ref[two, :] = jnp.concatenate([jnp.where(first_head, value, zero), jnp.where(first_head, zero, value)], axis=0)
            query = p_ref[0, rows, :] * jnp.asarray(scaling, bf16)
            grad = g_ref[rows, :]
            product = grad.astype(f32) * o_ref[rows, :].astype(f32)
            delta = lax.dot_general(chooser, product, (((1,), (1,)), ((), ())), precision=lax.Precision.HIGHEST, preferred_element_type=f32)
            def both(a, b):
                return jnp.concatenate([jnp.broadcast_to(a, (ROWS, ROWS)), jnp.broadcast_to(b, (ROWS, ROWS))], axis=0)
            lse2 = both(lse_ref[0, 0:1, rows], lse_ref[0, 1:2, rows])
            delta2 = both(delta[0:1], delta[1:2])
            dqt = jnp.zeros((128, ROWS), f32)
            for j in range(i + 1):
                cols = slice(2 * j * ROWS, 2 * (j + 1) * ROWS)
                prob = jnp.exp(dot_nt(kz_ref[cols, :], query) - lse2)
                if i == j:
                    prob = jnp.where(allowed, prob, 0.0)
                ds = (prob * (dot_nt(vz_ref[cols, :], grad) - delta2)).astype(bf16)
                dv_ref[cols, :] += dot_nn(prob.astype(bf16), grad)
                dk_ref[cols, :] += dot_nn(ds, query)
                dqt = dqt + dot_nn(kt_ref[:, cols], ds)
            out_ref[0, rows, :] = (dqt * scaling).T.astype(bf16)
    for i in range(blocks):
        rows = slice(i * ROWS, (i + 1) * ROWS)
        a = slice(2 * i * ROWS, (2 * i + 1) * ROWS); b = slice((2 * i + 1) * ROWS, 2 * (i + 1) * ROWS)

        @pl.when(i * ROWS < len_ref[0])
        def finish():
            out_ref[1, rows, :] = jnp.where(first_head, dk_ref[a, :], dk_ref[b, :]).astype(bf16)
            out_ref[2, rows, :] = jnp.where(first_head, dv_ref[a, :], dv_ref[b, :]).astype(bf16)


def blank_kernel(ready_ref, out_ref):
    pass


def blank(ready, shape):
    return pl.pallas_call(
        blank_kernel,
        in_specs=[pl.BlockSpec(memory_space=pltpu.SMEM)],
        out_specs=pl.BlockSpec(memory_space=pl.ANY),
        out_shape=shape,
        name="blank",
    )(ready)


def attend_back(choice, share, projected, heads_out, grad_heads, lse, before):
    rows = projected.shape[1]
    cols = lambda h, n: (0, n[2] + h)
    blocks = lambda h, n: (0, 0, n[2] + h)

    def kernel(n, p, o, g, l, unused, *rest):
        attend_back_kernel(n, p, o, g, l, *rest)

    return pl.pallas_call(
        kernel,
        grid_spec=pltpu.PrefetchScalarGridSpec(
            num_scalar_prefetch=1,
            grid=(share,),
            in_specs=[
                pl.BlockSpec((3, rows, 128), blocks),
                pl.BlockSpec((rows, 128), cols),
                pl.BlockSpec((None, rows, 128), lambda h, n: (n[1], 0, n[2] + h)),
                pl.BlockSpec((1, 8, rows), lambda h, n: (n[2] + h, 0, 0)),
                pl.BlockSpec(memory_space=pl.ANY),
            ],
            out_specs=pl.BlockSpec((3, rows, 128), blocks),
            scratch_shapes=[
                pltpu.VMEM((2 * rows, 128), f32),
                pltpu.VMEM((2 * rows, 128), f32),
                pltpu.VMEM((2 * rows, 128), bf16),
                pltpu.VMEM((2 * rows, 128), bf16),
                pltpu.VMEM((128, 2 * rows), bf16),
            ],
        ),
        out_shape=jax.ShapeDtypeStruct((3, rows, D), bf16),
        input_output_aliases={5: 0},
        compiler_params=params(),
        cost_estimate=pl.CostEstimate(
            flops=share * rows * rows * D, bytes_accessed=share * rows * D * 3, transcendentals=share * rows * rows
        ),
        name="attend_back",
    )(choice, projected, heads_out, grad_heads, lse, before)


def feed_kernel(plan, len_ref, row_ref, *refs):
    tok0, tok1, pass0, pass1, ho0, ho1, cot, table_ref, gain_ref = refs[:9]
    many = 2 * plan.sharers if plan.paired else 1
    grad_ref, pieces, refs = refs[9], refs[10 : 10 + many], refs[10 + many :]
    res, gh, hid, small_ref = refs[:4]
    outs, (w_ref, acc_ref, sums_ref, stage_ref, sem_ref) = refs[4:-5], refs[-5:]
    b = pl.program_id(0)
    many0 = last_block(len_ref[0]) + 1
    many1 = last_block(len_ref[1]) + 1
    early = b < many0

    @pl.when(b == 0)
    def clear():
        load_weight(plan, row_ref, pieces, w_ref, sem_ref, acc_ref, sums_ref)

    @pl.when(b < many0 + many1)
    def block():
        hot = onehot_rows(jnp.where(early, pass0[0], pass1[0]))
        entry = jnp.where(early, tok0[...], tok1[...]).astype(f32) + dot_tn(hot, table_ref[...])
        at = jnp.where(early, b, b - many0) * ROWS + lax.broadcasted_iota(jnp.int32, (ROWS, 1), 0)
        live = at < jnp.where(early, len_ref[0], len_ref[1])
        heads = jnp.where(early, ho0[...], ho1[...])
        attention = dot_nn(heads, w_ref[:, 0:D])
        hidden = entry + attention
        unit, scale = normalized(hidden)
        gain = gain_ref[...]
        normed = (unit * gain).astype(bf16)
        grad_feed = jnp.where(live, cot[...].reshape(ROWS, D).astype(f32), 0.0).astype(bf16)
        @pl.when(b == 0)
        def rest_of_weight():
            for copy in weight_copies(plan, row_ref, pieces, w_ref, sem_ref, 1):
                copy.wait()

        feed = jnp.zeros((ROWS, D), f32)
        grad_normed = jnp.zeros((ROWS, D), f32)
        for k in range(CHUNKS):
            up = slice(D + k * D, D + (k + 1) * D)
            down = slice(D + FF + k * D, D + FF + (k + 1) * D)
            x = dot_nn(normed, w_ref[:, up])
            grad_act = dot_nt(grad_feed, w_ref[:, down])
            c0 = math.sqrt(2.0 / math.pi)
            square = x * x
            bent = jnp.tanh(x * (c0 + (c0 * 0.044715) * square))
            half = 0.5 + 0.5 * bent
            slope = half + (0.5 * x) * (1.0 - bent * bent) * (c0 + (3.0 * c0 * 0.044715) * square)
            act = (x * half).astype(bf16)
            grad_x = (slope * grad_act).astype(bf16)
            feed = feed + dot_nn(act, w_ref[:, down])
            grad_normed = grad_normed + dot_nt(grad_x, w_ref[:, up])
            acc_ref[:, up] += dot_tn(normed, grad_x)
            acc_ref[:, down] += dot_tn(act, grad_feed)
        res[...] = jnp.where(live, hidden + feed, 0.0).astype(bf16).reshape(res.shape)
        sums_ref[0:8] += fold_rows(grad_normed * unit)
        sums_ref[8:16] += fold_rows(jnp.where(live, entry * entry, 0.0))
        sums_ref[16:24] += fold_rows(jnp.where(live, attention * attention, 0.0))
        sums_ref[24:32] += fold_rows(jnp.where(live, feed * feed, 0.0))
        grad_hidden = grad_feed.astype(f32) + norm_back(grad_normed * gain, unit, scale)
        hid[...] = grad_hidden
        grad_attention = grad_hidden.astype(bf16)
        acc_ref[:, 0:D] += dot_tn(heads, grad_attention)
        gh[...] = dot_nt(grad_attention, w_ref[:, 0:D]).astype(bf16)

    @pl.when(b == pl.num_programs(0) - 1)
    def finish():
        counted = (len_ref[0] + len_ref[1]).astype(f32)
        small_ref[...] = jnp.full(small_ref.shape, counted, f32)
        for n in range(4):
            small_ref[n : n + 1] = jnp.sum(sums_ref[8 * n : 8 * n + 8], axis=0, keepdims=True)
        store_grads(plan, plan.wide_orders, grad_ref, acc_ref, outs, stage_ref, sem_ref)


def feed(plan, part, lengths, piece_rows, grad_rows, tokens, pass_rows, heads_out, cotangent, table, gain, pieces, width):
    rows = tokens[0].shape[0]
    per = ROWS // part

    def at0(b, n, r):
        return jnp.minimum(b, last_block(n[0])), 0

    def at1(b, n, r):
        return jnp.clip(b - last_block(n[0]) - 1, 0, last_block(n[1])), 0

    def both(b, n, r):
        early = b <= last_block(n[0])
        return jnp.where(early, b, at1(b, n, r)[0]), jnp.where(early, 0, 1)

    row0 = pl.BlockSpec((ROWS, D), at0)
    row1 = pl.BlockSpec((ROWS, D), at1)
    pas0 = pl.BlockSpec((1, 1, ROWS), lambda *a: at0(*a) + (0,))
    pas1 = pl.BlockSpec((1, 1, ROWS), lambda *a: at1(*a) + (0,))
    dealt = pl.BlockSpec((per, 1, part, D), lambda *a: both(*a) + (0, 0))
    local = pl.BlockSpec((None, ROWS, D), lambda *a: both(*a)[::-1] + (0,))
    grads = grad_shapes(plan, width, plan.wide_orders)
    anywhere = pl.BlockSpec(memory_space=pl.ANY)
    return pl.pallas_call(
        functools.partial(feed_kernel, plan),
        grid_spec=pltpu.PrefetchScalarGridSpec(
            num_scalar_prefetch=2,
            grid=(2 * rows // ROWS,),
            in_specs=[
                row0, row1, pas0, pas1, row0, row1, dealt,
                pl.BlockSpec((8, D), lambda *a: (0, 0)),
                pl.BlockSpec((1, D), lambda *a: (0, 0)),
                pl.BlockSpec(memory_space=pltpu.SMEM),
            ]
            + [anywhere] * len(pieces),
            out_specs=[dealt, local, local, pl.BlockSpec((8, D), lambda *a: (0, 0))] + [anywhere] * len(grads),
            scratch_shapes=[
                pltpu.VMEM((D, width), bf16),
                pltpu.VMEM((D, width), f32),
                pltpu.VMEM((32, D), f32),
                pltpu.VMEM(stage_shape(plan), bf16),
                pltpu.SemaphoreType.DMA((2,)),
            ],
        ),
        out_shape=[
            jax.ShapeDtypeStruct(cotangent.shape, bf16),
            jax.ShapeDtypeStruct((2, rows, D), bf16),
            jax.ShapeDtypeStruct((2, rows, D), f32),
            jax.ShapeDtypeStruct((8, D), f32),
        ]
        + grads,
        compiler_params=params(),
        cost_estimate=pl.CostEstimate(
            flops=2 * 6 * rows * D * width, bytes_accessed=2 * rows * D * 14 + D * width * 4, transcendentals=2 * rows * FF
        ),
        name="feed",
    )(lengths, piece_rows, tokens[0], tokens[1], pass_rows[0], pass_rows[1], heads_out[0], heads_out[1],
      cotangent, table, gain, grad_rows, *pieces)


def project_back_kernel(plan, weight, rows_back, final, len_ref, row_ref, grad_ref, tok_ref, pass_ref, g_ref, *rest):
    rest = list(rest)
    hid_ref = rest.pop(0) if rows_back else None
    table_ref, gain_ref = rest.pop(0), rest.pop(0)
    before_ref = rest.pop(0) if final else None
    many = plan.sharers if plan.paired else 1
    pieces = [rest.pop(0) for n in range(many)] if rows_back else []
    if rows_back:
        out_ref, small_ref = rest.pop(0), rest.pop(0)
    if weight and not final:
        acc_ref = rest.pop(0)
    outs = [rest.pop(0) for shape in grad_shapes(plan, 3 * D, plan.head_orders)] if final else []
    if rows_back:
        w_ref, sums_ref = rest.pop(0), rest.pop(0)
    if final:
        acc_ref, stage_ref = rest.pop(0), rest.pop(0)
    sem_ref = rest.pop(0)
    b = pl.program_id(0)

    @pl.when(b == 0)
    def clear():
        if rows_back:
            load_weight(plan, row_ref, pieces, w_ref, sem_ref, sums_ref, *([acc_ref] if weight and not final else []))
        if final:
            copy = pltpu.make_async_copy(before_ref, acc_ref, sem_ref.at[0])
            copy.start()
            copy.wait()

    @pl.when(b <= last_block(len_ref[0]))
    def work():
        hot = onehot_rows(pass_ref[0])
        entry = tok_ref[...].astype(f32) + dot_tn(hot, table_ref[...])
        unit, scale = normalized(entry)
        gain = gain_ref[...]
        if weight:
            normed = (unit * gain).astype(bf16)
            for part in range(3):
                acc_ref[:, part * D : (part + 1) * D] += dot_tn(normed, g_ref[part])
        if rows_back:
            grad_normed = jnp.zeros((ROWS, D), f32)
            for part in range(3):
                grad_normed = grad_normed + dot_nt(g_ref[part], w_ref[:, part * D : (part + 1) * D])
            sums_ref[0:8] += fold_rows(grad_normed * unit)
            grad_entry = hid_ref[...] + norm_back(grad_normed * gain, unit, scale)
            high = grad_entry.astype(bf16)
            out_ref[...] = high
            rest_one = grad_entry - high.astype(f32)
            low = rest_one.astype(bf16)
            lower = (rest_one - low.astype(f32)).astype(bf16)
            sums_ref[8:16] += dot_nn(hot, high) + dot_nn(hot, low) + dot_nn(hot, lower)

    if rows_back:
        @pl.when(b == pl.num_programs(0) - 1)
        def sums():
            small_ref[...] = sums_ref[8:16]
            small_ref[PASSES : PASSES + 1] = jnp.sum(sums_ref[0:8], axis=0, keepdims=True)

    if final:
        @pl.when(b == pl.num_programs(0) - 1)
        def finish():
            store_grads(plan, plan.head_orders, grad_ref, acc_ref, outs, stage_ref, sem_ref)


def project_back(
    plan, weight, rows_back, which, length, piece_rows, grad_rows, tokens, pass_rows, grads, grad_hidden, table, gain,
    pieces, before=None,
):
    rows = tokens.shape[0]
    final = before is not None
    at = lambda b, n, r, g: (jnp.minimum(b, last_block(n[0])), 0)
    row = pl.BlockSpec((ROWS, D), at)
    anywhere = pl.BlockSpec(memory_space=pl.ANY)
    in_specs = [
        row,
        pl.BlockSpec((1, 1, ROWS), lambda *a: at(*a) + (0,)),
        pl.BlockSpec((3, ROWS, D), lambda *a: (0,) + at(*a)),
    ]
    operands = [length, piece_rows, grad_rows, tokens, pass_rows, grads]
    if rows_back:
        in_specs.append(pl.BlockSpec((None, ROWS, D), lambda *a: (which,) + at(*a)))
        operands.append(grad_hidden)
    in_specs += [pl.BlockSpec((8, D), lambda *a: (0, 0)), pl.BlockSpec((1, D), lambda *a: (0, 0))]
    operands += [table, gain]
    out_shape, out_specs, scratch = [], [], []
    if final:
        in_specs.append(anywhere)
        operands.append(before)
    if rows_back:
        in_specs += [anywhere] * len(pieces)
        operands += pieces
        out_shape += [jax.ShapeDtypeStruct((rows, D), bf16), jax.ShapeDtypeStruct((8, D), f32)]
        out_specs += [row, pl.BlockSpec((8, D), lambda *a: (0, 0))]
        scratch += [pltpu.VMEM((D, 3 * D), bf16), pltpu.VMEM((16, D), f32)]
    if weight and not final:
        out_shape.append(jax.ShapeDtypeStruct((D, 3 * D), f32))
        out_specs.append(pl.BlockSpec((D, 3 * D), lambda *a: (0, 0)))
    if final:
        shapes = grad_shapes(plan, 3 * D, plan.head_orders)
        out_shape += shapes
        out_specs += [anywhere] * len(shapes)
        scratch += [pltpu.VMEM((D, 3 * D), f32), pltpu.VMEM(stage_shape(plan), bf16)]
    return pl.pallas_call(
        functools.partial(project_back_kernel, plan, weight, rows_back, final),
        grid_spec=pltpu.PrefetchScalarGridSpec(
            num_scalar_prefetch=3,
            grid=(rows // ROWS,),
            in_specs=in_specs,
            out_specs=out_specs,
            scratch_shapes=scratch + [pltpu.SemaphoreType.DMA((2,))],
        ),
        out_shape=out_shape,
        compiler_params=params(),
        cost_estimate=pl.CostEstimate(
            flops=2 * (weight + rows_back) * rows * D * 3 * D, bytes_accessed=rows * D * 14 + D * D * 6, transcendentals=0
        ),
        name="project_back",
    )(*operands)


def pick_kernel(index_ref, in_ref, out_ref, sem_ref):
    copies = [
        pltpu.make_async_copy(in_ref.at[index_ref[n]], out_ref.at[n], sem_ref) for n in range(out_ref.shape[0])
    ]
    for copy in copies:
        copy.start()
    for copy in copies:
        copy.wait()


def pick(index, blocks):
    shape = index.shape + blocks.shape[1:]
    return pl.pallas_call(
        pick_kernel,
        grid_spec=pltpu.PrefetchScalarGridSpec(
            num_scalar_prefetch=1,
            grid=(1,),
            in_specs=[pl.BlockSpec(memory_space=pl.ANY)],
            out_specs=pl.BlockSpec(shape, lambda b, n: (0, 0, 0)),
            scratch_shapes=[pltpu.SemaphoreType.DMA],
        ),
        out_shape=jax.ShapeDtypeStruct(shape, blocks.dtype),
        compiler_params=params(),
        cost_estimate=pl.CostEstimate(flops=0, bytes_accessed=4 * math.prod(shape), transcendentals=0),
        name="pick",
    )(index, blocks)


def settle_kernel(index_ref, *refs):
    arrays, out_ref = refs[:-1], refs[-1]
    first = pl.program_id(0) * out_ref.shape[0]
    rows = out_ref.shape[1]
    at = lax.broadcasted_iota(jnp.int32, (rows, 1), 0)
    for n in range(out_ref.shape[0]):
        live = at < index_ref[2, first + n]
        source, late = index_ref[1, first + n], index_ref[0, first + n]
        if len(arrays) == 1:
            found = arrays[0][2 * source + late]
        else:
            found = jnp.where(late == 0, arrays[0][source], arrays[1][source])
        out_ref[n] = jnp.where(live, found.astype(f32), 0.0)


def settle(index, *arrays):
    many = index.shape[1]
    step = 4
    shape = arrays[0].shape
    whole = pl.BlockSpec(shape, lambda b, n: (0, 0, 0), pipeline_mode=pl.Buffered(1))
    return pl.pallas_call(
        settle_kernel,
        grid_spec=pltpu.PrefetchScalarGridSpec(
            num_scalar_prefetch=1,
            grid=(many // step,),
            in_specs=[whole] * len(arrays),
            out_specs=pl.BlockSpec((step,) + shape[1:], lambda b, n: (b, 0, 0)),
        ),
        out_shape=jax.ShapeDtypeStruct((many,) + shape[1:], f32),
        compiler_params=params(),
        cost_estimate=pl.CostEstimate(flops=0, bytes_accessed=6 * many * math.prod(shape[1:]), transcendentals=0),
        name="settle",
    )(index, *arrays)


def after(values, *others):
    return lax.optimization_barrier((values, others))[0]


def swap(blocks):
    return lax.all_to_all(blocks, "dp", split_axis=0, concat_axis=0, tiled=True)


def per_device(
    groups,
    width_all,
    tokens,
    passes,
    lengths,
    dealing,
    pass_table,
    gain_first,
    to_heads,
    from_heads,
    gain_second,
    expand,
    shrink,
    cotangent,
):
    axes = ("dp", "fsdp")
    slots, part, unused_width = tokens.shape
    seq_len = part * groups
    order = jnp.arange(slots, dtype=jnp.int32)
    here = lax.axis_index("dp")
    ordering = dealing[0, 0]
    sizes = lengths[0]

    ahead = (sizes[None, :] > sizes[:, None]) | (
        (sizes[None, :] == sizes[:, None]) & (order[None, :] < order[:, None])
    )
    rank = jnp.sum(ahead.astype(jnp.int32), axis=1)
    ranked = jnp.sum(jnp.where(rank[None, :] == order[:, None], order[None, :], 0), axis=1)
    place = jnp.sum(jnp.where(ordering[None, :] == order[:, None], order[None, :], 0), axis=1)
    early_seqs = ranked[:groups]
    late_seqs = ranked[groups:][::-1]
    from_early = jnp.sum(jnp.where(early_seqs[:, None] == order[None, :], place[None, :], 0), axis=1)
    from_late = jnp.sum(jnp.where(late_seqs[:, None] == order[None, :], place[None, :], 0), axis=1)
    slot_rank = jnp.sum(jnp.where(ordering[:, None] == order[None, :], rank[None, :], 0), axis=1)
    slot_size = jnp.sum(jnp.where(ordering[:, None] == order[None, :], sizes[None, :], 0), axis=1)
    is_late = (slot_rank >= groups).astype(jnp.int32)
    source = jnp.where(is_late == 1, slots - 1 - slot_rank, slot_rank)
    back_index = jnp.stack([is_late, source, slot_size - here * part])
    my_seqs = jnp.stack([early_seqs[here], late_seqs[here]])
    my_sizes = jnp.sum(jnp.where(my_seqs[:, None] == order[None, :], sizes[None, :], 0), axis=1)

    row_count = to_heads.shape[0]
    narrow = jnp.concatenate(
        [
            from_heads,
            expand.reshape(row_count, D, CHUNKS).transpose(0, 2, 1).reshape(row_count, FF),
            shrink.reshape(row_count, CHUNKS * D),
        ],
        axis=1,
    )
    plan = Plan(groups, width_all // groups, row_count)
    index_here = here * (width_all // groups) + lax.axis_index("fsdp")
    my_passes = [passes[my_seqs[m]].reshape(seq_len // ROWS, 1, ROWS) for m in range(2)]
    one_size = [my_sizes[m : m + 1] for m in range(2)]
    table = jnp.zeros((8, D), bf16).at[:PASSES].set(pass_table)
    gain_one = gain_first.astype(f32).reshape(1, D)
    gain_two = gain_second.astype(f32).reshape(1, D)

    pairs_index = jnp.stack([from_early, from_late], axis=1).reshape(slots)
    picked = [pick(from_early, tokens), pick(from_late, tokens), pick(pairs_index, cotangent)]
    if plan.paired:
        piece_rows = plan.piece_rows(index_here)
        wide_rows = plan.grad_rows(index_here, plan.wide_orders)
        head_rows = plan.grad_rows(index_here, plan.head_orders)
        head_far = plan.gather(to_heads[None], plan.far)
        head_near = plan.gather(head_far, [plan.near])
        wide_one = plan.gather(after(narrow, head_far)[None], plan.far[:1])
        ready = (my_passes, one_size, piece_rows, table, gain_one)
        tokens0 = swap(after(picked[0], head_near, wide_one, ready))
        head_pieces = plan.gather_core(plan.gather_x(head_near))
    else:
        piece_rows = wide_rows = head_rows = jnp.zeros((1,), jnp.int32)
        head_pieces = (lax.all_gather(to_heads, axes, axis=0, tiled=True),)
        wide_pieces = (lax.all_gather(narrow, axes, axis=0, tiled=True),)
        tokens0 = swap(picked[0])
        wide_far = wide_pieces

    def forward(m, *gate):
        return project(
            plan, after(one_size[m], gate), piece_rows, my_tokens[m], my_passes[m], table, gain_one, head_pieces
        )

    def mix(m, *gate):
        return attend(after(one_size[m], gate), projected[m])

    half = HEADS // 4
    choices = {
        (m, first): jnp.stack([my_sizes[m], jnp.int32(m), jnp.int32(first)]) for m in range(2) for first in (0, half)
    }

    def mix_back(m, first, before, *gate):
        return attend_back(after(choices[m, first], gate), half, projected[m], heads_out[m], grad_heads, lse[m], before)

    def back(m, weight, rows_back, *gate, before=None):
        return project_back(
            plan, weight, rows_back, m, after(one_size[m], gate), piece_rows, head_rows, my_tokens[m], my_passes[m],
            grad_parts[m], grad_hidden, table, gain_one, head_pieces, before,
        )

    def send_back(rows, *gate):
        return swap(after(rows, gate).reshape(groups, part, D))

    projected, heads_out, lse, grad_parts = [None, None], [None, None], [None, None], [None, None]
    my_tokens = [tokens0.reshape(seq_len, D)]
    projected[0] = forward(0)
    if plan.paired:
        wide_far = plan.gather(wide_one, plan.far[1:], head_pieces, projected[0])
        cut = first_part(wide_far.shape[-1], plan.wide_orders)
    tokens1 = swap(after(picked[1], tokens0, picked[2], wide_far))
    my_tokens.append(tokens1.reshape(seq_len, D))
    heads_out[0], lse[0] = mix(0, wide_far)
    if plan.paired:
        first = plan.gather_near({0: wide_far[:, :, :cut]}, (), lse[0])
        second = plan.gather_x(wide_far[:, :, cut:], ())
        ready = (first, second)
    else:
        ready = ()
    my_grads = swap(after(picked[2].reshape(groups, 2, part, D), tokens1, lse[0], ready))
    projected[1] = forward(1, lse[0])
    if plan.paired:
        first = plan.gather_x(first[0])
        second = plan.gather_near(second, lse[0], projected[1])
    heads_out[1], lse[1] = mix(1)
    if plan.paired:
        wide_pieces = plan.gather_core(first, lse[1]) + plan.gather_core(second, lse[1])

    res, grad_heads, grad_hidden, feed_small, *wide_grads = feed(
        plan, part, after(my_sizes, choices), piece_rows, wide_rows, my_tokens, my_passes, heads_out, my_grads, table, gain_two,
        wide_pieces, D + 2 * FF,
    )

    def begin(grads):
        if not plan.paired:
            return lax.psum_scatter(grads[0], axes, scatter_dimension=0, tiled=True).astype(f32)
        return [grads[n : n + 2] for n in range(0, len(grads), 2)]

    def advance(state, stage, gate, late):
        return plan.reduce_stage(state, plan.wide_orders, stage, (gate,), (late,)) if plan.paired else state

    space = jax.ShapeDtypeStruct((3, seq_len, D), bf16)
    wide0 = begin(wide_grads)
    result = swap(res)
    some = mix_back(0, 0, blank(one_size[0], space))
    wide1 = advance(wide0, 0, (), some)
    grad_parts[0] = mix_back(0, half, some, wide1)
    entry0, small0, head_sum = back(0, True, True)
    wide2 = advance(wide1, 1, some, entry0)
    moved0 = send_back(entry0, result)
    some = mix_back(1, 0, blank(one_size[1], space), entry0, wide2, result)
    wide3 = advance(wide2, 2, entry0, some)
    grad_parts[1] = mix_back(1, half, some, wide3)
    entry1, small1 = back(1, False, True)
    wide_owned = advance(wide3, 3, some, entry1)
    moved1 = send_back(entry1, moved0, wide_owned)
    totals = jnp.concatenate([small0 + small1, feed_small], axis=0)
    stages = plan.head_orders[0]
    head_grads = back(1, True, False, entry1, moved0, before=head_sum)
    head_state = begin(head_grads)
    if plan.paired:
        totals = plan.total_stage(totals, stages[0], (), head_grads[:1])
        head_state = plan.reduce_stage(head_state, plan.head_orders, 0, (wide_owned,))
        wide_owned = wide_owned[0]
    output = settle(after(back_index, head_state), result.reshape(slots, part, D))
    grad_tokens = settle(after(back_index, output), moved0, moved1)
    grad_from = wide_owned[:, :D]
    grad_expand = wide_owned[:, D : D + FF].reshape(row_count, CHUNKS, D).transpose(0, 2, 1).reshape(row_count, FF)
    grad_shrink = wide_owned[:, D + FF :].reshape(row_count * CHUNKS, D)
    if plan.paired:
        totals = plan.total_stage(totals, stages[1])
        late = (output, grad_tokens, grad_from, grad_expand, grad_shrink)
        head_state = plan.reduce_stage(head_state, plan.head_orders, 1, (totals,), late)
        totals = plan.total_stage(totals, stages[2], (head_state,))
        head_owned = plan.reduce_stage(head_state, plan.head_orders, 2)[0]
    else:
        totals = lax.psum(totals, axes)
        head_owned = head_state
    root_squares = jnp.sqrt(jnp.sum(totals[9:12], axis=1) / (totals[12, 0] * D))

    return (
        output,
        grad_tokens,
        totals[:PASSES],
        totals[PASSES],
        head_owned,
        grad_from,
        totals[8],
        grad_expand,
        grad_shrink,
        root_squares,
    )


def solution(mesh):
    groups = mesh.shape["dp"]
    weight_spec = P(("dp", "fsdp"), None)
    block_spec = P("fsdp", "dp", None)
    in_specs = (
        block_spec,
        P("fsdp", None),
        P("fsdp", None),
        P("dp", "fsdp", None),
        P(),
        P(),
        weight_spec,
        weight_spec,
        P(),
        weight_spec,
        weight_spec,
        block_spec,
    )
    out_specs = (
        block_spec,
        block_spec,
        P(),
        P(),
        weight_spec,
        weight_spec,
        P(),
        weight_spec,
        weight_spec,
        P(),
    )
    body = functools.partial(per_device, groups, groups * mesh.shape["fsdp"])
    return jax.shard_map(body, mesh=mesh, in_specs=in_specs, out_specs=out_specs, check_vma=False)
```

```python
import math
import functools

import jax
import jax.numpy as jnp
from jax import lax
from jax.experimental import pallas as pl
from jax.experimental.pallas import tpu as pltpu
from jax.sharding import PartitionSpec as P

D = 768
HEADS = 12
HEAD = 64
FF = 3072
PASSES = 5
EPS = 1e-05
ROWS = 256
CHUNKS = FF // D
VMEM_MOST = 64000 * 1024

f32 = jnp.float32
bf16 = jnp.bfloat16


def dot_nn(a, b):
    return lax.dot_general(a, b, (((1,), (0,)), ((), ())), preferred_element_type=f32)


def dot_nt(a, b):
    return lax.dot_general(a, b, (((1,), (1,)), ((), ())), preferred_element_type=f32)


def dot_tn(a, b):
    return lax.dot_general(a, b, (((0,), (0,)), ((), ())), preferred_element_type=f32)


def params(**more):
    return pltpu.CompilerParams(vmem_limit_bytes=VMEM_MOST, **more)


def normalized(values):
    centred = values - jnp.mean(values, axis=-1, keepdims=True)
    spread = jnp.mean(centred * centred, axis=-1, keepdims=True)
    scale = lax.rsqrt(spread + EPS)
    return centred * scale, scale


def norm_back(grad_unit, unit, scale):
    first = jnp.mean(grad_unit, axis=-1, keepdims=True)
    second = jnp.mean(grad_unit * unit, axis=-1, keepdims=True)
    return scale * (grad_unit - first - unit * second)


def onehot_rows(pass_row):
    ids = lax.broadcasted_iota(jnp.int32, (8, pass_row.shape[-1]), 0)
    return (ids == pass_row).astype(f32).astype(bf16)


def fold_rows(values):
    rows, width = values.shape
    return jnp.sum(values.reshape(rows // 8, 8, width), axis=0)


def last_block(length):
    return lax.div(length + (ROWS - 1), ROWS) - 1


def bits_of(count):
    return count.bit_length() - 1


class Plan:
    def __init__(self, groups, sharers, rows):
        self.groups, self.sharers, self.rows = groups, sharers, rows
        self.count = groups * sharers
        self.paired = rows % 8 == 0 and self.count & (self.count - 1) == 0 and sharers >= 4 and groups >= 4
        core, *over_x = [1 << bit for bit in range(bits_of(sharers))]
        near, *far = [sharers << bit for bit in range(bits_of(groups))]
        self.core, self.over_x, self.near, self.far = core, over_x, near, far[::-1]
        self.wide_orders = ([[core], over_x, [near], far], [[core], [near], over_x, far])
        self.head_orders = ([[core], over_x + [near], far],)

    def exchange(self, values, bits):
        pairs = [(i, i ^ bits) for i in range(self.count)]
        return lax.ppermute(values, ("dp", "fsdp"), pairs)

    def gather(self, held, masks, gate=(), late=()):
        for bits in masks:
            held = jnp.concatenate([after(held, late), self.exchange(after(held, gate), bits)], axis=0)
        return held

    def gather_x(self, held, *gate):
        pieces = {0: held}
        for bits in self.over_x[::-1]:
            for name in list(pieces):
                pieces[name | bits] = self.exchange(after(pieces[name], gate), bits)
        return pieces

    def gather_near(self, pieces, gate=(), late=()):
        return {name: self.gather(held, [self.near], gate, late) for name, held in pieces.items()}

    def gather_core(self, pieces, *gate):
        found = dict(pieces)
        for name in pieces:
            found[name | self.core] = self.exchange(after(pieces[name], gate), self.core)
        return tuple(found[name] for name in range(self.sharers))

    def piece_rows(self, here):
        masks = self.far + [self.near]
        found = []
        for f in range(self.sharers):
            for n in range(self.groups):
                rel = f | ways_bits(masks, n)
                found.append((here ^ rel) * self.rows)
        return jnp.stack(found).astype(jnp.int32)

    def grad_rows(self, here, orders):
        found = []
        for order in orders:
            for place in range(self.count):
                rel, left = 0, self.count
                for masks in order:
                    left >>= len(masks)
                    rel |= ways_bits(masks, (place // left) % (1 << len(masks)))
                found.append((here ^ rel) * self.rows)
        return jnp.stack(found).astype(jnp.int32)

    def total_stage(self, values, masks, gate=(), late=()):
        found = [after(values, late)]
        found += [self.exchange(after(values, gate), ways_bits(masks, way)) for way in range(1, 1 << len(masks))]
        while len(found) > 1:
            found = [found[k] + found[k + 1] for k in range(0, len(found), 2)]
        return found[0]

    def reduce_stage(self, states, orders, stage, gate=(), late=()):
        sums = []
        for ways, order in zip(states, orders):
            sums.append(
                [after(ways[0], late)]
                + [
                    self.exchange(after(ways[n], gate), ways_bits(order[stage], n))
                    for n in range(1, len(ways))
                ]
            )
        if stage == len(orders[0]) - 1:
            return [sum(part.astype(f32) for part in parts)[0] for parts in sums]
        ways = 1 << len(orders[0][stage + 1])
        if stage == len(orders[0]) - 2:
            return [merge(sums, ways)]
        return [merge([parts], ways) for parts in sums]


def ways_bits(masks, way):
    return sum(bits for n, bits in enumerate(masks) if (way >> n) & 1)


def merge_kernel(widths, many, ways, *refs):
    ins, outs = refs[: len(widths) * many * ways], refs[len(widths) * many * ways :]
    for way in range(ways):
        first = 0
        for k, width in enumerate(widths):
            views = [ins[(k * many + n) * ways + way] for n in range(many)]
            total = views[0][...].astype(f32)
            for view in views[1:]:
                total = total + view[...].astype(f32)
            outs[way][:, :, first : first + width] = total.astype(bf16)
            first += width


def merge(groups, ways):
    blocks, rows, unused = groups[0][0].shape
    widths = [parts[0].shape[2] for parts in groups]
    share = blocks // ways
    steps = min(share, 4)

    def view(way, width):
        return pl.BlockSpec((share // steps, rows, width), lambda b: (b + way * steps, 0, 0))

    out = jax.ShapeDtypeStruct((share, rows, sum(widths)), bf16)
    many = len(groups[0])
    size = blocks * rows * sum(widths)
    return pl.pallas_call(
        functools.partial(merge_kernel, widths, many, ways),
        grid=(steps,),
        in_specs=[view(way, width) for width in widths for n in range(many) for way in range(ways)],
        out_specs=[view(0, sum(widths))] * ways,
        out_shape=[out] * ways,
        compiler_params=params(),
        cost_estimate=pl.CostEstimate(flops=many * size, bytes_accessed=(2 + 2 * many) * size, transcendentals=0),
        name="merge",
    )(*[part for parts in groups for part in parts for way in range(ways)])


def weight_copies(plan, rows_ref, pieces, weight_ref, sem_ref, group):
    if not plan.paired:
        return [pltpu.make_async_copy(pieces[0], weight_ref, sem_ref.at[0])] if group == 0 else []
    mine = pieces[group * plan.sharers : (group + 1) * plan.sharers]
    if len(mine) == 0:
        return []
    first = pieces[0].shape[-1] * group
    copies = []
    for f, piece in enumerate(mine):
        for n in range(plan.groups):
            at = pl.multiple_of(rows_ref[f * plan.groups + n], 8)
            target = weight_ref.at[pl.ds(at, plan.rows), first : first + piece.shape[-1]]
            copies.append(pltpu.make_async_copy(piece.at[n], target, sem_ref.at[group]))
    return copies


def load_weight(plan, rows_ref, pieces, weight_ref, sem_ref, *cleared):
    first, second = [weight_copies(plan, rows_ref, pieces, weight_ref, sem_ref, group) for group in range(2)]
    for copy in first + second:
        copy.start()
    for ref in cleared:
        ref[...] = jnp.zeros_like(ref)
    for copy in first:
        copy.wait()


def grad_shapes(plan, width, orders):
    if not plan.paired:
        return [jax.ShapeDtypeStruct((D, width), bf16)]
    half = plan.count // 2
    cut = first_part(width, orders)
    return [jax.ShapeDtypeStruct((half, plan.rows, w), bf16) for w in (cut, cut, width - cut, width - cut) if w > 0]


def first_part(width, orders):
    return width // D // 2 * D if len(orders) == 2 else width


def stage_shape(plan):
    return (2, plan.count, plan.rows, D) if plan.paired else (2, D, D)


def store_grads(plan, orders, rows_ref, acc_ref, outs, stage_ref, sem_ref):
    width, step = acc_ref.shape[1], D
    cut = first_part(width, orders)
    half = plan.count // 2
    waiting = []
    for n in range(width // step):
        slot = n % 2
        cols = slice(n * step, (n + 1) * step)
        if len(waiting) == 2:
            for copy in waiting.pop(0):
                copy.wait()
        if not plan.paired:
            stage_ref[slot] = acc_ref[:, cols].astype(bf16)
            copies = [pltpu.make_async_copy(stage_ref.at[slot], outs[0].at[:, cols], sem_ref.at[slot])]
        else:
            late = n * step >= cut
            base = plan.count if late else 0
            start = n * step - (cut if late else 0)

            def fill(place, carry):
                at = pl.multiple_of(rows_ref[base + place], 8)
                stage_ref[slot, place] = acc_ref[pl.ds(at, plan.rows), cols].astype(bf16)
                return carry

            lax.fori_loop(0, plan.count, fill, 0, unroll=8)
            keep, send = outs[2:4] if late else outs[0:2]
            there = slice(start, start + step)
            copies = [
                pltpu.make_async_copy(stage_ref.at[slot, 0:half], keep.at[:, :, there], sem_ref.at[slot]),
                pltpu.make_async_copy(stage_ref.at[slot, half:], send.at[:, :, there], sem_ref.at[slot]),
            ]
        for copy in copies:
            copy.start()
        waiting.append(copies)
    for copies in waiting:
        for copy in copies:
            copy.wait()


def project_kernel(plan, len_ref, row_ref, tok_ref, pass_ref, table_ref, gain_ref, *rest):
    pieces, (out_ref, w_ref, sem_ref) = rest[:-3], rest[-3:]

    @pl.when(pl.program_id(0) == 0)
    def load():
        load_weight(plan, row_ref, pieces, w_ref, sem_ref)

    @pl.when(pl.program_id(0) <= last_block(len_ref[0]))
    def work():
        hot = onehot_rows(pass_ref[0])
        entry = tok_ref[...].astype(f32) + dot_tn(hot, table_ref[...])
        unit, unused = normalized(entry)
        normed = (unit * gain_ref[...]).astype(bf16)
        for part in range(3):
            out_ref[part] = dot_nn(normed, w_ref[:, part * D : (part + 1) * D]).astype(bf16)


def project(plan, length, piece_rows, tokens, pass_rows, table, gain, pieces):
    rows = tokens.shape[0]
    at = lambda b, n, r: (jnp.minimum(b, last_block(n[0])), 0)
    return pl.pallas_call(
        functools.partial(project_kernel, plan),
        grid_spec=pltpu.PrefetchScalarGridSpec(
            num_scalar_prefetch=2,
            grid=(rows // ROWS,),
            in_specs=[
                pl.BlockSpec((ROWS, D), at),
                pl.BlockSpec((1, 1, ROWS), lambda b, n, r: at(b, n, r) + (0,)),
                pl.BlockSpec((8, D), lambda b, n, r: (0, 0)),
                pl.BlockSpec((1, D), lambda b, n, r: (0, 0)),
            ]
            + [pl.BlockSpec(memory_space=pl.ANY)] * len(pieces),
            out_specs=pl.BlockSpec((3, ROWS, D), lambda b, n, r: (0,) + at(b, n, r)),
            scratch_shapes=[pltpu.VMEM((D, 3 * D), bf16), pltpu.SemaphoreType.DMA((1,))],
        ),
        out_shape=jax.ShapeDtypeStruct((3, rows, D), bf16),
        compiler_params=params(),
        cost_estimate=pl.CostEstimate(
            flops=2 * rows * D * 3 * D, bytes_accessed=rows * D * 8 + D * D * 6, transcendentals=0
        ),
        name="project",
    )(length, piece_rows, tokens, pass_rows, table, gain, *pieces)


def attend_kernel(len_ref, p_ref, out_ref, lse_ref):
    blocks = p_ref.shape[1] // ROWS
    lane = lax.broadcasted_iota(jnp.int32, (ROWS, 128), 1)
    first_head = lane < HEAD
    here = lax.broadcasted_iota(jnp.int32, (ROWS, ROWS), 0)
    there = lax.broadcasted_iota(jnp.int32, (ROWS, ROWS), 1)
    allowed = there <= here
    for i in range(blocks):
        rows = slice(i * ROWS, (i + 1) * ROWS)

        @pl.when(i * ROWS < len_ref[0])
        def work():
            query = p_ref[0, rows, :] * jnp.asarray(1.0 / math.sqrt(HEAD), bf16)
            found = []
            for head in range(2):
                mine = first_head if head == 0 else jnp.logical_not(first_head)
                q = jnp.where(mine, query, jnp.zeros_like(query))
                diag = dot_nt(q, p_ref[1, rows, :])
                diag = jnp.where(allowed, diag, -1e30)
                largest = jnp.max(diag, axis=-1, keepdims=True)
                if i > 0:
                    before = dot_nt(q, p_ref[1, : i * ROWS, :])
                    largest = jnp.maximum(largest, jnp.max(before, axis=-1, keepdims=True))
                diag = jnp.exp(diag - largest)
                total = jnp.sum(diag, axis=-1, keepdims=True)
                out = dot_nn(diag.astype(bf16), p_ref[2, rows, :])
                if i > 0:
                    before = jnp.exp(before - largest)
                    total = total + jnp.sum(before, axis=-1, keepdims=True)
                    out = out + dot_nn(before.astype(bf16), p_ref[2, : i * ROWS, :])
                found.append(out * (1.0 / total))
                lse = jnp.broadcast_to(largest + jnp.log(total), (ROWS, 128))
                lse_ref[0, head : head + 1, rows] = lse.T[0:1]
            out_ref[rows, :] = jnp.where(first_head, found[0], found[1]).astype(bf16)


def attend(length, projected):
    rows = projected.shape[1]
    pairs = HEADS // 2
    return pl.pallas_call(
        attend_kernel,
        grid_spec=pltpu.PrefetchScalarGridSpec(
            num_scalar_prefetch=1,
            grid=(pairs,),
            in_specs=[pl.BlockSpec((3, rows, 128), lambda h, n: (0, 0, h))],
            out_specs=[
                pl.BlockSpec((rows, 128), lambda h, n: (0, h)),
                pl.BlockSpec((1, 8, rows), lambda h, n: (h, 0, 0)),
            ],
        ),
        out_shape=[
            jax.ShapeDtypeStruct((rows, D), bf16),
            jax.ShapeDtypeStruct((pairs, 8, rows), f32),
        ],
        compiler_params=params(),
        cost_estimate=pl.CostEstimate(
            flops=2 * rows * rows * D, bytes_accessed=rows * D * 8, transcendentals=HEADS * rows * rows // 2
        ),
        name="attend",
    )(length, projected)


def attend_back_kernel(len_ref, p_ref, o_ref, g_ref, lse_ref, out_ref, dk_ref, dv_ref, kz_ref, vz_ref, kt_ref):
    blocks = p_ref.shape[1] // ROWS
    scaling = 1.0 / math.sqrt(HEAD)
    lane = lax.broadcasted_iota(jnp.int32, (ROWS, 128), 1)
    first_head = lane < HEAD
    row8 = lax.broadcasted_iota(jnp.int32, (8, 128), 0)
    lane8 = lax.broadcasted_iota(jnp.int32, (8, 128), 1)
    chooser = (lax.div(lane8, HEAD) == row8).astype(f32)
    key_at = lax.broadcasted_iota(jnp.int32, (2, ROWS, ROWS), 1)
    row_at = lax.broadcasted_iota(jnp.int32, (2, ROWS, ROWS), 2)
    allowed = (key_at <= row_at).reshape(2 * ROWS, ROWS)
    for i in range(blocks):
        rows = slice(i * ROWS, (i + 1) * ROWS)
        two = slice(2 * i * ROWS, 2 * (i + 1) * ROWS)

        @pl.when(i * ROWS < len_ref[0])
        def work():
            dk_ref[two, :] = jnp.zeros((2 * ROWS, 128), f32)
            dv_ref[two, :] = jnp.zeros((2 * ROWS, 128), f32)
            key, value = p_ref[1, rows, :], p_ref[2, rows, :]
            zero = jnp.zeros_like(key)
            k2 = jnp.concatenate([jnp.where(first_head, key, zero), jnp.where(first_head, zero, key)], axis=0)
            kz_ref[two, :] = k2
            kt_ref[:, two] = k2.T
            vz_ref[two, :] = jnp.concatenate([jnp.where(first_head, value, zero), jnp.where(first_head, zero, value)], axis=0)
            query = p_ref[0, rows, :] * jnp.asarray(scaling, bf16)
            grad = g_ref[rows, :]
            product = grad.astype(f32) * o_ref[rows, :].astype(f32)
            delta = lax.dot_general(chooser, product, (((1,), (1,)), ((), ())), precision=lax.Precision.HIGHEST, preferred_element_type=f32)
            def both(a, b):
                return jnp.concatenate([jnp.broadcast_to(a, (ROWS, ROWS)), jnp.broadcast_to(b, (ROWS, ROWS))], axis=0)
            lse2 = both(lse_ref[0, 0:1, rows], lse_ref[0, 1:2, rows])
            delta2 = both(delta[0:1], delta[1:2])
            dqt = jnp.zeros((128, ROWS), f32)
            for j in range(i + 1):
                cols = slice(2 * j * ROWS, 2 * (j + 1) * ROWS)
                prob = jnp.exp(dot_nt(kz_ref[cols, :], query) - lse2)
                if i == j:
                    prob = jnp.where(allowed, prob, 0.0)
                ds = (prob * (dot_nt(vz_ref[cols, :], grad) - delta2)).astype(bf16)
                dv_ref[cols, :] += dot_nn(prob.astype(bf16), grad)
                dk_ref[cols, :] += dot_nn(ds, query)
                dqt = dqt + dot_nn(kt_ref[:, cols], ds)
            out_ref[0, rows, :] = (dqt * scaling).T.astype(bf16)
    for i in range(blocks):
        rows = slice(i * ROWS, (i + 1) * ROWS)
        a = slice(2 * i * ROWS, (2 * i + 1) * ROWS); b = slice((2 * i + 1) * ROWS, 2 * (i + 1) * ROWS)

        @pl.when(i * ROWS < len_ref[0])
        def finish():
            out_ref[1, rows, :] = jnp.where(first_head, dk_ref[a, :], dk_ref[b, :]).astype(bf16)
            out_ref[2, rows, :] = jnp.where(first_head, dv_ref[a, :], dv_ref[b, :]).astype(bf16)


def blank_kernel(ready_ref, out_ref):
    pass


def blank(ready, shape):
    return pl.pallas_call(
        blank_kernel,
        in_specs=[pl.BlockSpec(memory_space=pltpu.SMEM)],
        out_specs=pl.BlockSpec(memory_space=pl.ANY),
        out_shape=shape,
        name="blank",
    )(ready)


def attend_back(choice, share, projected, heads_out, grad_heads, lse, before):
    rows = projected.shape[1]
    cols = lambda h, n: (0, n[2] + h)
    blocks = lambda h, n: (0, 0, n[2] + h)

    def kernel(n, p, o, g, l, unused, *rest):
        attend_back_kernel(n, p, o, g, l, *rest)

    return pl.pallas_call(
        kernel,
        grid_spec=pltpu.PrefetchScalarGridSpec(
            num_scalar_prefetch=1,
            grid=(share,),
            in_specs=[
                pl.BlockSpec((3, rows, 128), blocks),
                pl.BlockSpec((rows, 128), cols),
                pl.BlockSpec((None, rows, 128), lambda h, n: (n[1], 0, n[2] + h)),
                pl.BlockSpec((1, 8, rows), lambda h, n: (n[2] + h, 0, 0)),
                pl.BlockSpec(memory_space=pl.ANY),
            ],
            out_specs=pl.BlockSpec((3, rows, 128), blocks),
            scratch_shapes=[
                pltpu.VMEM((2 * rows, 128), f32),
                pltpu.VMEM((2 * rows, 128), f32),
                pltpu.VMEM((2 * rows, 128), bf16),
                pltpu.VMEM((2 * rows, 128), bf16),
                pltpu.VMEM((128, 2 * rows), bf16),
            ],
        ),
        out_shape=jax.ShapeDtypeStruct((3, rows, D), bf16),
        input_output_aliases={5: 0},
        compiler_params=params(),
        cost_estimate=pl.CostEstimate(
            flops=8 * share * rows * rows * D, bytes_accessed=share * rows * D * 3, transcendentals=share * rows * rows
        ),
        name="attend_back",
    )(choice, projected, heads_out, grad_heads, lse, before)


def feed_kernel(plan, len_ref, row_ref, *refs):
    tok0, tok1, pass0, pass1, ho0, ho1, cot, table_ref, gain_ref = refs[:9]
    many = 2 * plan.sharers if plan.paired else 1
    grad_ref, pieces, refs = refs[9], refs[10 : 10 + many], refs[10 + many :]
    res, gh, hid, small_ref = refs[:4]
    outs, (w_ref, acc_ref, sums_ref, stage_ref, sem_ref) = refs[4:-5], refs[-5:]
    b = pl.program_id(0)
    many0 = last_block(len_ref[0]) + 1
    many1 = last_block(len_ref[1]) + 1
    early = b < many0

    @pl.when(b == 0)
    def clear():
        load_weight(plan, row_ref, pieces, w_ref, sem_ref, acc_ref, sums_ref)

    @pl.when(b < many0 + many1)
    def block():
        hot = onehot_rows(jnp.where(early, pass0[0], pass1[0]))
        entry = jnp.where(early, tok0[...], tok1[...]).astype(f32) + dot_tn(hot, table_ref[...])
        at = jnp.where(early, b, b - many0) * ROWS + lax.broadcasted_iota(jnp.int32, (ROWS, 1), 0)
        live = at < jnp.where(early, len_ref[0], len_ref[1])
        heads = jnp.where(early, ho0[...], ho1[...])
        attention = dot_nn(heads, w_ref[:, 0:D])
        hidden = entry + attention
        unit, scale = normalized(hidden)
        gain = gain_ref[...]
        normed = (unit * gain).astype(bf16)
        grad_feed = jnp.where(live, cot[...].reshape(ROWS, D).astype(f32), 0.0).astype(bf16)
        @pl.when(b == 0)
        def rest_of_weight():
            for copy in weight_copies(plan, row_ref, pieces, w_ref, sem_ref, 1):
                copy.wait()

        feed = jnp.zeros((ROWS, D), f32)
        grad_normed = jnp.zeros((ROWS, D), f32)
        for k in range(CHUNKS):
            up = slice(D + k * D, D + (k + 1) * D)
            down = slice(D + FF + k * D, D + FF + (k + 1) * D)
            x = dot_nn(normed, w_ref[:, up])
            grad_act = dot_nt(grad_feed, w_ref[:, down])
            c0 = math.sqrt(2.0 / math.pi)
            square = x * x
            bent = jnp.tanh(x * (c0 + (c0 * 0.044715) * square))
            half = 0.5 + 0.5 * bent
            slope = half + (0.5 * x) * (1.0 - bent * bent) * (c0 + (3.0 * c0 * 0.044715) * square)
            act = (x * half).astype(bf16)
            grad_x = (slope * grad_act).astype(bf16)
            feed = feed + dot_nn(act, w_ref[:, down])
            grad_normed = grad_normed + dot_nt(grad_x, w_ref[:, up])
            acc_ref[:, up] += dot_tn(normed, grad_x)
            acc_ref[:, down] += dot_tn(act, grad_feed)
        res[...] = jnp.where(live, hidden + feed, 0.0).astype(bf16).reshape(res.shape)
        sums_ref[0:8] += fold_rows(grad_normed * unit)
        sums_ref[8:16] += fold_rows(jnp.where(live, entry * entry, 0.0))
        sums_ref[16:24] += fold_rows(jnp.where(live, attention * attention, 0.0))
        sums_ref[24:32] += fold_rows(jnp.where(live, feed * feed, 0.0))
        grad_hidden = grad_feed.astype(f32) + norm_back(grad_normed * gain, unit, scale)
        hid[...] = grad_hidden
        grad_attention = grad_hidden.astype(bf16)
        acc_ref[:, 0:D] += dot_tn(heads, grad_attention)
        gh[...] = dot_nt(grad_attention, w_ref[:, 0:D]).astype(bf16)

    @pl.when(b == pl.num_programs(0) - 1)
    def finish():
        counted = (len_ref[0] + len_ref[1]).astype(f32)
        small_ref[...] = jnp.full(small_ref.shape, counted, f32)
        for n in range(4):
            small_ref[n : n + 1] = jnp.sum(sums_ref[8 * n : 8 * n + 8], axis=0, keepdims=True)
        store_grads(plan, plan.wide_orders, grad_ref, acc_ref, outs, stage_ref, sem_ref)


def feed(plan, part, lengths, piece_rows, grad_rows, tokens, pass_rows, heads_out, cotangent, table, gain, pieces, width):
    rows = tokens[0].shape[0]
    per = ROWS // part

    def at0(b, n, r):
        return jnp.minimum(b, last_block(n[0])), 0

    def at1(b, n, r):
        return jnp.clip(b - last_block(n[0]) - 1, 0, last_block(n[1])), 0

    def both(b, n, r):
        early = b <= last_block(n[0])
        return jnp.where(early, b, at1(b, n, r)[0]), jnp.where(early, 0, 1)

    row0 = pl.BlockSpec((ROWS, D), at0)
    row1 = pl.BlockSpec((ROWS, D), at1)
    pas0 = pl.BlockSpec((1, 1, ROWS), lambda *a: at0(*a) + (0,))
    pas1 = pl.BlockSpec((1, 1, ROWS), lambda *a: at1(*a) + (0,))
    dealt = pl.BlockSpec((per, 1, part, D), lambda *a: both(*a) + (0, 0))
    local = pl.BlockSpec((None, ROWS, D), lambda *a: both(*a)[::-1] + (0,))
    grads = grad_shapes(plan, width, plan.wide_orders)
    anywhere = pl.BlockSpec(memory_space=pl.ANY)
    return pl.pallas_call(
        functools.partial(feed_kernel, plan),
        grid_spec=pltpu.PrefetchScalarGridSpec(
            num_scalar_prefetch=2,
            grid=(2 * rows // ROWS,),
            in_specs=[
                row0, row1, pas0, pas1, row0, row1, dealt,
                pl.BlockSpec((8, D), lambda *a: (0, 0)),
                pl.BlockSpec((1, D), lambda *a: (0, 0)),
                pl.BlockSpec(memory_space=pltpu.SMEM),
            ]
            + [anywhere] * len(pieces),
            out_specs=[dealt, local, local, pl.BlockSpec((8, D), lambda *a: (0, 0))] + [anywhere] * len(grads),
            scratch_shapes=[
                pltpu.VMEM((D, width), bf16),
                pltpu.VMEM((D, width), f32),
                pltpu.VMEM((32, D), f32),
                pltpu.VMEM(stage_shape(plan), bf16),
                pltpu.SemaphoreType.DMA((2,)),
            ],
        ),
        out_shape=[
            jax.ShapeDtypeStruct(cotangent.shape, bf16),
            jax.ShapeDtypeStruct((2, rows, D), bf16),
            jax.ShapeDtypeStruct((2, rows, D), f32),
            jax.ShapeDtypeStruct((8, D), f32),
        ]
        + grads,
        compiler_params=params(),
        cost_estimate=pl.CostEstimate(
            flops=2 * 6 * rows * D * width, bytes_accessed=2 * rows * D * 14 + D * width * 4, transcendentals=2 * rows * FF
        ),
        name="feed",
    )(lengths, piece_rows, tokens[0], tokens[1], pass_rows[0], pass_rows[1], heads_out[0], heads_out[1],
      cotangent, table, gain, grad_rows, *pieces)


def project_back_kernel(plan, weight, rows_back, final, len_ref, row_ref, grad_ref, tok_ref, pass_ref, g_ref, *rest):
    rest = list(rest)
    hid_ref = rest.pop(0) if rows_back else None
    table_ref, gain_ref = rest.pop(0), rest.pop(0)
    before_ref = rest.pop(0) if final else None
    many = plan.sharers if plan.paired else 1
    pieces = [rest.pop(0) for n in range(many)] if rows_back else []
    if rows_back:
        out_ref, small_ref = rest.pop(0), rest.pop(0)
    if weight and not final:
        acc_ref = rest.pop(0)
    outs = [rest.pop(0) for shape in grad_shapes(plan, 3 * D, plan.head_orders)] if final else []
    if rows_back:
        w_ref, sums_ref = rest.pop(0), rest.pop(0)
    if final:
        acc_ref, stage_ref = rest.pop(0), rest.pop(0)
    sem_ref = rest.pop(0)
    b = pl.program_id(0)

    @pl.when(b == 0)
    def clear():
        if rows_back:
            load_weight(plan, row_ref, pieces, w_ref, sem_ref, sums_ref, *([acc_ref] if weight and not final else []))
        if final:
            copy = pltpu.make_async_copy(before_ref, acc_ref, sem_ref.at[0])
            copy.start()
            copy.wait()

    @pl.when(b <= last_block(len_ref[0]))
    def work():
        hot = onehot_rows(pass_ref[0])
        entry = tok_ref[...].astype(f32) + dot_tn(hot, table_ref[...])
        unit, scale = normalized(entry)
        gain = gain_ref[...]
        if weight:
            normed = (unit * gain).astype(bf16)
            for part in range(3):
                acc_ref[:, part * D : (part + 1) * D] += dot_tn(normed, g_ref[part])
        if rows_back:
            grad_normed = jnp.zeros((ROWS, D), f32)
            for part in range(3):
                grad_normed = grad_normed + dot_nt(g_ref[part], w_ref[:, part * D : (part + 1) * D])
            sums_ref[0:8] += fold_rows(grad_normed * unit)
            grad_entry = hid_ref[...] + norm_back(grad_normed * gain, unit, scale)
            high = grad_entry.astype(bf16)
            out_ref[...] = high
            rest_one = grad_entry - high.astype(f32)
            low = rest_one.astype(bf16)
            lower = (rest_one - low.astype(f32)).astype(bf16)
            sums_ref[8:16] += dot_nn(hot, high) + dot_nn(hot, low) + dot_nn(hot, lower)

    if rows_back:
        @pl.when(b == pl.num_programs(0) - 1)
        def sums():
            small_ref[...] = sums_ref[8:16]
            small_ref[PASSES : PASSES + 1] = jnp.sum(sums_ref[0:8], axis=0, keepdims=True)

    if final:
        @pl.when(b == pl.num_programs(0) - 1)
        def finish():
            store_grads(plan, plan.head_orders, grad_ref, acc_ref, outs, stage_ref, sem_ref)


def project_back(
    plan, weight, rows_back, which, length, piece_rows, grad_rows, tokens, pass_rows, grads, grad_hidden, table, gain,
    pieces, before=None,
):
    rows = tokens.shape[0]
    final = before is not None
    at = lambda b, n, r, g: (jnp.minimum(b, last_block(n[0])), 0)
    row = pl.BlockSpec((ROWS, D), at)
    anywhere = pl.BlockSpec(memory_space=pl.ANY)
    in_specs = [
        row,
        pl.BlockSpec((1, 1, ROWS), lambda *a: at(*a) + (0,)),
        pl.BlockSpec((3, ROWS, D), lambda *a: (0,) + at(*a)),
    ]
    operands = [length, piece_rows, grad_rows, tokens, pass_rows, grads]
    if rows_back:
        in_specs.append(pl.BlockSpec((None, ROWS, D), lambda *a: (which,) + at(*a)))
        operands.append(grad_hidden)
    in_specs += [pl.BlockSpec((8, D), lambda *a: (0, 0)), pl.BlockSpec((1, D), lambda *a: (0, 0))]
    operands += [table, gain]
    out_shape, out_specs, scratch = [], [], []
    if final:
        in_specs.append(anywhere)
        operands.append(before)
    if rows_back:
        in_specs += [anywhere] * len(pieces)
        operands += pieces
        out_shape += [jax.ShapeDtypeStruct((rows, D), bf16), jax.ShapeDtypeStruct((8, D), f32)]
        out_specs += [row, pl.BlockSpec((8, D), lambda *a: (0, 0))]
        scratch += [pltpu.VMEM((D, 3 * D), bf16), pltpu.VMEM((16, D), f32)]
    if weight and not final:
        out_shape.append(jax.ShapeDtypeStruct((D, 3 * D), f32))
        out_specs.append(pl.BlockSpec((D, 3 * D), lambda *a: (0, 0)))
    if final:
        shapes = grad_shapes(plan, 3 * D, plan.head_orders)
        out_shape += shapes
        out_specs += [anywhere] * len(shapes)
        scratch += [pltpu.VMEM((D, 3 * D), f32), pltpu.VMEM(stage_shape(plan), bf16)]
    return pl.pallas_call(
        functools.partial(project_back_kernel, plan, weight, rows_back, final),
        grid_spec=pltpu.PrefetchScalarGridSpec(
            num_scalar_prefetch=3,
            grid=(rows // ROWS,),
            in_specs=in_specs,
            out_specs=out_specs,
            scratch_shapes=scratch + [pltpu.SemaphoreType.DMA((2,))],
        ),
        out_shape=out_shape,
        compiler_params=params(),
        cost_estimate=pl.CostEstimate(
            flops=2 * (weight + rows_back) * rows * D * 3 * D, bytes_accessed=rows * D * 14 + D * D * 6, transcendentals=0
        ),
        name="project_back",
    )(*operands)


def pick_kernel(index_ref, in_ref, out_ref, sem_ref):
    copies = [
        pltpu.make_async_copy(in_ref.at[index_ref[n]], out_ref.at[n], sem_ref) for n in range(out_ref.shape[0])
    ]
    for copy in copies:
        copy.start()
    for copy in copies:
        copy.wait()


def pick(index, blocks):
    shape = index.shape + blocks.shape[1:]
    return pl.pallas_call(
        pick_kernel,
        grid_spec=pltpu.PrefetchScalarGridSpec(
            num_scalar_prefetch=1,
            grid=(1,),
            in_specs=[pl.BlockSpec(memory_space=pl.ANY)],
            out_specs=pl.BlockSpec(shape, lambda b, n: (0, 0, 0)),
            scratch_shapes=[pltpu.SemaphoreType.DMA],
        ),
        out_shape=jax.ShapeDtypeStruct(shape, blocks.dtype),
        compiler_params=params(),
        cost_estimate=pl.CostEstimate(flops=0, bytes_accessed=4 * math.prod(shape), transcendentals=0),
        name="pick",
    )(index, blocks)


def settle_kernel(index_ref, *refs):
    arrays, out_ref = refs[:-1], refs[-1]
    first = pl.program_id(0) * out_ref.shape[0]
    rows = out_ref.shape[1]
    at = lax.broadcasted_iota(jnp.int32, (rows, 1), 0)
    for n in range(out_ref.shape[0]):
        live = at < index_ref[2, first + n]
        source, late = index_ref[1, first + n], index_ref[0, first + n]
        if len(arrays) == 1:
            found = arrays[0][2 * source + late]
        else:
            found = jnp.where(late == 0, arrays[0][source], arrays[1][source])
        out_ref[n] = jnp.where(live, found.astype(f32), 0.0)


def settle(index, *arrays):
    many = index.shape[1]
    step = 4
    shape = arrays[0].shape
    whole = pl.BlockSpec(shape, lambda b, n: (0, 0, 0), pipeline_mode=pl.Buffered(1))
    return pl.pallas_call(
        settle_kernel,
        grid_spec=pltpu.PrefetchScalarGridSpec(
            num_scalar_prefetch=1,
            grid=(many // step,),
            in_specs=[whole] * len(arrays),
            out_specs=pl.BlockSpec((step,) + shape[1:], lambda b, n: (b, 0, 0)),
        ),
        out_shape=jax.ShapeDtypeStruct((many,) + shape[1:], f32),
        compiler_params=params(),
        cost_estimate=pl.CostEstimate(flops=0, bytes_accessed=6 * many * math.prod(shape[1:]), transcendentals=0),
        name="settle",
    )(index, *arrays)


def after(values, *others):
    return lax.optimization_barrier((values, others))[0]


def swap(blocks):
    return lax.all_to_all(blocks, "dp", split_axis=0, concat_axis=0, tiled=True)


def per_device(
    groups,
    width_all,
    tokens,
    passes,
    lengths,
    dealing,
    pass_table,
    gain_first,
    to_heads,
    from_heads,
    gain_second,
    expand,
    shrink,
    cotangent,
):
    axes = ("dp", "fsdp")
    slots, part, unused_width = tokens.shape
    seq_len = part * groups
    order = jnp.arange(slots, dtype=jnp.int32)
    here = lax.axis_index("dp")
    ordering = dealing[0, 0]
    sizes = lengths[0]

    ahead = (sizes[None, :] > sizes[:, None]) | (
        (sizes[None, :] == sizes[:, None]) & (order[None, :] < order[:, None])
    )
    rank = jnp.sum(ahead.astype(jnp.int32), axis=1)
    ranked = jnp.sum(jnp.where(rank[None, :] == order[:, None], order[None, :], 0), axis=1)
    place = jnp.sum(jnp.where(ordering[None, :] == order[:, None], order[None, :], 0), axis=1)
    early_seqs = ranked[:groups]
    late_seqs = ranked[groups:][::-1]
    from_early = jnp.sum(jnp.where(early_seqs[:, None] == order[None, :], place[None, :], 0), axis=1)
    from_late = jnp.sum(jnp.where(late_seqs[:, None] == order[None, :], place[None, :], 0), axis=1)
    slot_rank = jnp.sum(jnp.where(ordering[:, None] == order[None, :], rank[None, :], 0), axis=1)
    slot_size = jnp.sum(jnp.where(ordering[:, None] == order[None, :], sizes[None, :], 0), axis=1)
    is_late = (slot_rank >= groups).astype(jnp.int32)
    source = jnp.where(is_late == 1, slots - 1 - slot_rank, slot_rank)
    back_index = jnp.stack([is_late, source, slot_size - here * part])
    my_seqs = jnp.stack([early_seqs[here], late_seqs[here]])
    my_sizes = jnp.sum(jnp.where(my_seqs[:, None] == order[None, :], sizes[None, :], 0), axis=1)

    row_count = to_heads.shape[0]
    narrow = jnp.concatenate(
        [
            from_heads,
            expand.reshape(row_count, D, CHUNKS).transpose(0, 2, 1).reshape(row_count, FF),
            shrink.reshape(row_count, CHUNKS * D),
        ],
        axis=1,
    )
    plan = Plan(groups, width_all // groups, row_count)
    index_here = here * (width_all // groups) + lax.axis_index("fsdp")
    my_passes = [passes[my_seqs[m]].reshape(seq_len // ROWS, 1, ROWS) for m in range(2)]
    one_size = [my_sizes[m : m + 1] for m in range(2)]
    table = jnp.zeros((8, D), bf16).at[:PASSES].set(pass_table)
    gain_one = gain_first.astype(f32).reshape(1, D)
    gain_two = gain_second.astype(f32).reshape(1, D)

    pairs_index = jnp.stack([from_early, from_late], axis=1).reshape(slots)
    picked = [pick(from_early, tokens), pick(from_late, tokens), pick(pairs_index, cotangent)]
    if plan.paired:
        piece_rows = plan.piece_rows(index_here)
        wide_rows = plan.grad_rows(index_here, plan.wide_orders)
        head_rows = plan.grad_rows(index_here, plan.head_orders)
        head_far = plan.gather(to_heads[None], plan.far)
        head_near = plan.gather(head_far, [plan.near])
        wide_one = plan.gather(after(narrow, head_far)[None], plan.far[:1])
        ready = (my_passes, one_size, piece_rows, table, gain_one)
        tokens0 = swap(after(picked[0], head_near, wide_one, ready))
        head_pieces = plan.gather_core(plan.gather_x(head_near))
    else:
        piece_rows = wide_rows = head_rows = jnp.zeros((1,), jnp.int32)
        head_pieces = (lax.all_gather(to_heads, axes, axis=0, tiled=True),)
        wide_pieces = (lax.all_gather(narrow, axes, axis=0, tiled=True),)
        tokens0 = swap(picked[0])
        wide_far = wide_pieces

    def forward(m, *gate):
        return project(
            plan, after(one_size[m], gate), piece_rows, my_tokens[m], my_passes[m], table, gain_one, head_pieces
        )

    def mix(m, *gate):
        return attend(after(one_size[m], gate), projected[m])

    choices = [jnp.stack([my_sizes[m], jnp.int32(m), jnp.int32(0)]) for m in range(2)]

    def mix_back(m, *gate):
        space = jax.ShapeDtypeStruct((3, seq_len, D), bf16)
        return attend_back(
            after(choices[m], gate), HEADS // 2, projected[m], heads_out[m], grad_heads, lse[m], blank(one_size[m], space)
        )

    def back(m, weight, rows_back, *gate, before=None):
        return project_back(
            plan, weight, rows_back, m, after(one_size[m], gate), piece_rows, head_rows, my_tokens[m], my_passes[m],
            grad_parts[m], grad_hidden, table, gain_one, head_pieces, before,
        )

    def send_back(rows, *gate):
        return swap(after(rows, gate).reshape(groups, part, D))

    projected, heads_out, lse, grad_parts = [None, None], [None, None], [None, None], [None, None]
    my_tokens = [tokens0.reshape(seq_len, D)]
    projected[0] = forward(0)
    if plan.paired:
        wide_far = plan.gather(wide_one, plan.far[1:], head_pieces, projected[0])
        cut = D + FF
    tokens1 = swap(after(picked[1], tokens0, picked[2], wide_far))
    my_tokens.append(tokens1.reshape(seq_len, D))
    heads_out[0], lse[0] = mix(0, wide_far)
    if plan.paired:
        first = plan.gather_near({0: wide_far[:, :, :cut]}, (), lse[0])
        second = plan.gather_x(wide_far[:, :, cut:], ())
        ready = (first, second)
    else:
        ready = ()
    my_grads = swap(after(picked[2].reshape(groups, 2, part, D), tokens1, lse[0], ready))
    projected[1] = forward(1, lse[0])
    if plan.paired:
        first = plan.gather_x(first[0])
        second = plan.gather_near(second, lse[0], projected[1])
    heads_out[1], lse[1] = mix(1)
    if plan.paired:
        wide_pieces = plan.gather_core(first, lse[1]) + plan.gather_core(second, lse[1])

    res, grad_heads, grad_hidden, feed_small, *wide_grads = feed(
        plan, part, after(my_sizes, choices), piece_rows, wide_rows, my_tokens, my_passes, heads_out, my_grads, table, gain_two,
        wide_pieces, D + 2 * FF,
    )

    def begin(grads):
        if not plan.paired:
            return lax.psum_scatter(grads[0], axes, scatter_dimension=0, tiled=True).astype(f32)
        return [grads[n : n + 2] for n in range(0, len(grads), 2)]

    def advance(state, stage, gate, late):
        return plan.reduce_stage(state, plan.wide_orders, stage, (gate,), (late,)) if plan.paired else state

    wide0 = begin(wide_grads)
    result = swap(res)
    grad_parts[0] = mix_back(0)
    wide1 = advance(wide0, 0, (), grad_parts[0])
    entry0, small0, head_sum = back(0, True, True, wide1)
    wide2 = advance(wide1, 1, (), entry0)
    moved0 = send_back(entry0, result)
    grad_parts[1] = mix_back(1, entry0, wide2, result)
    wide3 = advance(wide2, 2, (), grad_parts[1])
    entry1, small1 = back(1, False, True, wide3)
    wide_owned = advance(wide3, 3, (), entry1)
    moved1 = send_back(entry1, moved0)
    totals = jnp.concatenate([small0 + small1, feed_small], axis=0)
    stages = plan.head_orders[0]
    head_grads = back(1, True, False, entry1, moved0, wide_owned, before=head_sum)
    head_state = begin(head_grads)
    if plan.paired:
        totals = plan.total_stage(totals, stages[0], (), head_grads[:1])
        head_state = plan.reduce_stage(head_state, plan.head_orders, 0, (wide_owned,))
        wide_owned = wide_owned[0]
    output = settle(after(back_index, head_state), result.reshape(slots, part, D))
    grad_tokens = settle(after(back_index, output), moved0, moved1)
    grad_from = wide_owned[:, :D]
    grad_expand = wide_owned[:, D : D + FF].reshape(row_count, CHUNKS, D).transpose(0, 2, 1).reshape(row_count, FF)
    grad_shrink = wide_owned[:, D + FF :].reshape(row_count * CHUNKS, D)
    if plan.paired:
        for bits in stages[1]:
            totals = near = plan.total_stage(totals, [bits])
        totals = plan.total_stage(totals, stages[2][:1], (), (output,))
        late = (output, grad_tokens, grad_from, grad_expand, grad_shrink)
        head_state = plan.reduce_stage(head_state, plan.head_orders, 1, (near,), late)
        totals = plan.total_stage(totals, stages[2][1:], (head_state,))
        head_owned = plan.reduce_stage(head_state, plan.head_orders, 2)[0]
    else:
        totals = lax.psum(totals, axes)
        head_owned = head_state
    root_squares = jnp.sqrt(jnp.sum(totals[9:12], axis=1) / (totals[12, 0] * D))

    return (
        output,
        grad_tokens,
        totals[:PASSES],
        totals[PASSES],
        head_owned,
        grad_from,
        totals[8],
        grad_expand,
        grad_shrink,
        root_squares,
    )


def solution(mesh):
    groups = mesh.shape["dp"]
    weight_spec = P(("dp", "fsdp"), None)
    block_spec = P("fsdp", "dp", None)
    in_specs = (
        block_spec,
        P("fsdp", None),
        P("fsdp", None),
        P("dp", "fsdp", None),
        P(),
        P(),
        weight_spec,
        weight_spec,
        P(),
        weight_spec,
        weight_spec,
        block_spec,
    )
    out_specs = (
        block_spec,
        block_spec,
        P(),
        P(),
        weight_spec,
        weight_spec,
        P(),
        weight_spec,
        weight_spec,
        P(),
    )
    body = functools.partial(per_device, groups, groups * mesh.shape["fsdp"])
    return jax.shard_map(body, mesh=mesh, in_specs=in_specs, out_specs=out_specs, check_vma=False)
```

```python
import math
import functools

import jax
import jax.numpy as jnp
from jax import lax
from jax.experimental import pallas as pl
from jax.experimental.pallas import tpu as pltpu
from jax.sharding import PartitionSpec as P

D = 768
HEADS = 12
HEAD = 64
FF = 3072
PASSES = 5
EPS = 1e-05
ROWS = 256
CHUNKS = FF // D
VMEM_MOST = 64000 * 1024

f32 = jnp.float32
bf16 = jnp.bfloat16


def dot_nn(a, b):
    return lax.dot_general(a, b, (((1,), (0,)), ((), ())), preferred_element_type=f32)


def dot_nt(a, b):
    return lax.dot_general(a, b, (((1,), (1,)), ((), ())), preferred_element_type=f32)


def dot_tn(a, b):
    return lax.dot_general(a, b, (((0,), (0,)), ((), ())), preferred_element_type=f32)


def params(**more):
    return pltpu.CompilerParams(vmem_limit_bytes=VMEM_MOST, **more)


def normalized(values):
    centred = values - jnp.mean(values, axis=-1, keepdims=True)
    spread = jnp.mean(centred * centred, axis=-1, keepdims=True)
    scale = lax.rsqrt(spread + EPS)
    return centred * scale, scale


def norm_back(grad_unit, unit, scale):
    first = jnp.mean(grad_unit, axis=-1, keepdims=True)
    second = jnp.mean(grad_unit * unit, axis=-1, keepdims=True)
    return scale * (grad_unit - first - unit * second)


def onehot_rows(pass_row):
    ids = lax.broadcasted_iota(jnp.int32, (8, pass_row.shape[-1]), 0)
    return (ids == pass_row).astype(f32).astype(bf16)


def fold_rows(values):
    rows, width = values.shape
    return jnp.sum(values.reshape(rows // 8, 8, width), axis=0)


def last_block(length):
    return lax.div(length + (ROWS - 1), ROWS) - 1


def bits_of(count):
    return count.bit_length() - 1


class Plan:
    def __init__(self, groups, sharers, rows):
        self.groups, self.sharers, self.rows = groups, sharers, rows
        self.count = groups * sharers
        self.paired = rows % 8 == 0 and self.count & (self.count - 1) == 0 and sharers >= 4 and groups >= 4
        core, *over_x = [1 << bit for bit in range(bits_of(sharers))]
        near, *far = [sharers << bit for bit in range(bits_of(groups))]
        self.core, self.over_x, self.near, self.far = core, over_x, near, far[::-1]
        self.wide_orders = ([[core], over_x, [near], far], [[core], [near], over_x, far])
        self.head_orders = ([[core], over_x + [near], far],)

    def exchange(self, values, bits):
        pairs = [(i, i ^ bits) for i in range(self.count)]
        return lax.ppermute(values, ("dp", "fsdp"), pairs)

    def gather(self, held, masks, gate=(), late=()):
        for bits in masks:
            held = jnp.concatenate([after(held, late), self.exchange(after(held, gate), bits)], axis=0)
        return held

    def gather_x(self, held, *gate):
        pieces = {0: held}
        for bits in self.over_x[::-1]:
            for name in list(pieces):
                pieces[name | bits] = self.exchange(after(pieces[name], gate), bits)
        return pieces

    def gather_near(self, pieces, gate=(), late=()):
        return {name: self.gather(held, [self.near], gate, late) for name, held in pieces.items()}

    def gather_core(self, pieces, *gate):
        found = dict(pieces)
        for name in pieces:
            found[name | self.core] = self.exchange(after(pieces[name], gate), self.core)
        return tuple(found[name] for name in range(self.sharers))

    def piece_rows(self, here):
        masks = self.far + [self.near]
        found = []
        for f in range(self.sharers):
            for n in range(self.groups):
                rel = f | ways_bits(masks, n)
                found.append((here ^ rel) * self.rows)
        return jnp.stack(found).astype(jnp.int32)

    def grad_rows(self, here, orders):
        found = []
        for order in orders:
            for place in range(self.count):
                rel, left = 0, self.count
                for masks in order:
                    left >>= len(masks)
                    rel |= ways_bits(masks, (place // left) % (1 << len(masks)))
                found.append((here ^ rel) * self.rows)
        return jnp.stack(found).astype(jnp.int32)

    def total_stage(self, values, masks, gate=(), late=()):
        found = [after(values, late)]
        found += [self.exchange(after(values, gate), ways_bits(masks, way)) for way in range(1, 1 << len(masks))]
        while len(found) > 1:
            found = [found[k] + found[k + 1] for k in range(0, len(found), 2)]
        return found[0]

    def reduce_stage(self, states, orders, stage, gate=(), late=()):
        sums = []
        for ways, order in zip(states, orders):
            sums.append(
                [after(ways[0], late)]
                + [
                    self.exchange(after(ways[n], gate), ways_bits(order[stage], n))
                    for n in range(1, len(ways))
                ]
            )
        if stage == len(orders[0]) - 1:
            return [sum(part.astype(f32) for part in parts)[0] for parts in sums]
        ways = 1 << len(orders[0][stage + 1])
        if stage == len(orders[0]) - 2:
            return [merge(sums, ways)]
        return [merge([parts], ways) for parts in sums]


def ways_bits(masks, way):
    return sum(bits for n, bits in enumerate(masks) if (way >> n) & 1)


def merge_kernel(widths, many, ways, *refs):
    ins, outs = refs[: len(widths) * many * ways], refs[len(widths) * many * ways :]
    for way in range(ways):
        first = 0
        for k, width in enumerate(widths):
            views = [ins[(k * many + n) * ways + way] for n in range(many)]
            total = views[0][...].astype(f32)
            for view in views[1:]:
                total = total + view[...].astype(f32)
            outs[way][:, :, first : first + width] = total.astype(bf16)
            first += width


def merge(groups, ways):
    blocks, rows, unused = groups[0][0].shape
    widths = [parts[0].shape[2] for parts in groups]
    share = blocks // ways
    steps = min(share, 4)

    def view(way, width):
        return pl.BlockSpec((share // steps, rows, width), lambda b: (b + way * steps, 0, 0))

    out = jax.ShapeDtypeStruct((share, rows, sum(widths)), bf16)
    many = len(groups[0])
    size = blocks * rows * sum(widths)
    return pl.pallas_call(
        functools.partial(merge_kernel, widths, many, ways),
        grid=(steps,),
        in_specs=[view(way, width) for width in widths for n in range(many) for way in range(ways)],
        out_specs=[view(0, sum(widths))] * ways,
        out_shape=[out] * ways,
        compiler_params=params(),
        cost_estimate=pl.CostEstimate(flops=many * size, bytes_accessed=(2 + 2 * many) * size, transcendentals=0),
        name="merge",
    )(*[part for parts in groups for part in parts for way in range(ways)])


def weight_copies(plan, rows_ref, pieces, weight_ref, sem_ref, group):
    if not plan.paired:
        return [pltpu.make_async_copy(pieces[0], weight_ref, sem_ref.at[0])] if group == 0 else []
    mine = pieces[group * plan.sharers : (group + 1) * plan.sharers]
    if len(mine) == 0:
        return []
    first = pieces[0].shape[-1] * group
    copies = []
    for f, piece in enumerate(mine):
        for n in range(plan.groups):
            at = pl.multiple_of(rows_ref[f * plan.groups + n], 8)
            target = weight_ref.at[pl.ds(at, plan.rows), first : first + piece.shape[-1]]
            copies.append(pltpu.make_async_copy(piece.at[n], target, sem_ref.at[group]))
    return copies


def load_weight(plan, rows_ref, pieces, weight_ref, sem_ref, *cleared):
    first, second = [weight_copies(plan, rows_ref, pieces, weight_ref, sem_ref, group) for group in range(2)]
    for copy in first + second:
        copy.start()
    for ref in cleared:
        ref[...] = jnp.zeros_like(ref)
    for copy in first:
        copy.wait()


def grad_shapes(plan, width, orders):
    if not plan.paired:
        return [jax.ShapeDtypeStruct((D, width), bf16)]
    half = plan.count // 2
    cut = first_part(width, orders)
    return [jax.ShapeDtypeStruct((half, plan.rows, w), bf16) for w in (cut, cut, width - cut, width - cut) if w > 0]


def first_part(width, orders):
    return width // D // 2 * D if len(orders) == 2 else width


def stage_shape(plan):
    return (2, plan.count, plan.rows, D) if plan.paired else (2, D, D)


def store_grads(plan, orders, rows_ref, acc_ref, outs, stage_ref, sem_ref):
    width, step = acc_ref.shape[1], D
    cut = first_part(width, orders)
    half = plan.count // 2
    waiting = []
    for n in range(width // step):
        slot = n % 2
        cols = slice(n * step, (n + 1) * step)
        if len(waiting) == 2:
            for copy in waiting.pop(0):
                copy.wait()
        if not plan.paired:
            stage_ref[slot] = acc_ref[:, cols].astype(bf16)
            copies = [pltpu.make_async_copy(stage_ref.at[slot], outs[0].at[:, cols], sem_ref.at[slot])]
        else:
            late = n * step >= cut
            base = plan.count if late else 0
            start = n * step - (cut if late else 0)

            def fill(place, carry):
                at = pl.multiple_of(rows_ref[base + place], 8)
                stage_ref[slot, place] = acc_ref[pl.ds(at, plan.rows), cols].astype(bf16)
                return carry

            lax.fori_loop(0, plan.count, fill, 0, unroll=8)
            keep, send = outs[2:4] if late else outs[0:2]
            there = slice(start, start + step)
            copies = [
                pltpu.make_async_copy(stage_ref.at[slot, 0:half], keep.at[:, :, there], sem_ref.at[slot]),
                pltpu.make_async_copy(stage_ref.at[slot, half:], send.at[:, :, there], sem_ref.at[slot]),
            ]
        for copy in copies:
            copy.start()
        waiting.append(copies)
    for copies in waiting:
        for copy in copies:
            copy.wait()


def project_kernel(plan, len_ref, row_ref, tok_ref, pass_ref, table_ref, gain_ref, *rest):
    pieces, (out_ref, w_ref, sem_ref) = rest[:-3], rest[-3:]

    @pl.when(pl.program_id(0) == 0)
    def load():
        load_weight(plan, row_ref, pieces, w_ref, sem_ref)

    @pl.when(pl.program_id(0) <= last_block(len_ref[0]))
    def work():
        hot = onehot_rows(pass_ref[0])
        entry = tok_ref[...].astype(f32) + dot_tn(hot, table_ref[...])
        unit, unused = normalized(entry)
        normed = (unit * gain_ref[...]).astype(bf16)
        for part in range(3):
            out_ref[part] = dot_nn(normed, w_ref[:, part * D : (part + 1) * D]).astype(bf16)


def project(plan, length, piece_rows, tokens, pass_rows, table, gain, pieces):
    rows = tokens.shape[0]
    at = lambda b, n, r: (jnp.minimum(b, last_block(n[0])), 0)
    return pl.pallas_call(
        functools.partial(project_kernel, plan),
        grid_spec=pltpu.PrefetchScalarGridSpec(
            num_scalar_prefetch=2,
            grid=(rows // ROWS,),
            in_specs=[
                pl.BlockSpec((ROWS, D), at),
                pl.BlockSpec((1, 1, ROWS), lambda b, n, r: at(b, n, r) + (0,)),
                pl.BlockSpec((8, D), lambda b, n, r: (0, 0)),
                pl.BlockSpec((1, D), lambda b, n, r: (0, 0)),
            ]
            + [pl.BlockSpec(memory_space=pl.ANY)] * len(pieces),
            out_specs=pl.BlockSpec((3, ROWS, D), lambda b, n, r: (0,) + at(b, n, r)),
            scratch_shapes=[pltpu.VMEM((D, 3 * D), bf16), pltpu.SemaphoreType.DMA((1,))],
        ),
        out_shape=jax.ShapeDtypeStruct((3, rows, D), bf16),
        compiler_params=params(),
        cost_estimate=pl.CostEstimate(
            flops=2 * rows * D * 3 * D, bytes_accessed=rows * D * 8 + D * D * 6, transcendentals=0
        ),
        name="project",
    )(length, piece_rows, tokens, pass_rows, table, gain, *pieces)


def attend_kernel(len_ref, p_ref, out_ref, lse_ref):
    blocks = p_ref.shape[1] // ROWS
    lane = lax.broadcasted_iota(jnp.int32, (ROWS, 128), 1)
    first_head = lane < HEAD
    here = lax.broadcasted_iota(jnp.int32, (ROWS, ROWS), 0)
    there = lax.broadcasted_iota(jnp.int32, (ROWS, ROWS), 1)
    allowed = there <= here
    for i in range(blocks):
        rows = slice(i * ROWS, (i + 1) * ROWS)

        @pl.when(i * ROWS < len_ref[0])
        def work():
            query = p_ref[0, rows, :] * jnp.asarray(1.0 / math.sqrt(HEAD), bf16)
            found = []
            for head in range(2):
                mine = first_head if head == 0 else jnp.logical_not(first_head)
                q = jnp.where(mine, query, jnp.zeros_like(query))
                diag = dot_nt(q, p_ref[1, rows, :])
                diag = jnp.where(allowed, diag, -1e30)
                largest = jnp.max(diag, axis=-1, keepdims=True)
                if i > 0:
                    before = dot_nt(q, p_ref[1, : i * ROWS, :])
                    largest = jnp.maximum(largest, jnp.max(before, axis=-1, keepdims=True))
                diag = jnp.exp(diag - largest)
                total = jnp.sum(diag, axis=-1, keepdims=True)
                out = dot_nn(diag.astype(bf16), p_ref[2, rows, :])
                if i > 0:
                    before = jnp.exp(before - largest)
                    total = total + jnp.sum(before, axis=-1, keepdims=True)
                    out = out + dot_nn(before.astype(bf16), p_ref[2, : i * ROWS, :])
                found.append(out * (1.0 / total))
                lse = jnp.broadcast_to(largest + jnp.log(total), (ROWS, 128))
                lse_ref[0, head : head + 1, rows] = lse.T[0:1]
            out_ref[rows, :] = jnp.where(first_head, found[0], found[1]).astype(bf16)


def attend(length, projected):
    rows = projected.shape[1]
    pairs = HEADS // 2
    return pl.pallas_call(
        attend_kernel,
        grid_spec=pltpu.PrefetchScalarGridSpec(
            num_scalar_prefetch=1,
            grid=(pairs,),
            in_specs=[pl.BlockSpec((3, rows, 128), lambda h, n: (0, 0, h))],
            out_specs=[
                pl.BlockSpec((rows, 128), lambda h, n: (0, h)),
                pl.BlockSpec((1, 8, rows), lambda h, n: (h, 0, 0)),
            ],
        ),
        out_shape=[
            jax.ShapeDtypeStruct((rows, D), bf16),
            jax.ShapeDtypeStruct((pairs, 8, rows), f32),
        ],
        compiler_params=params(),
        cost_estimate=pl.CostEstimate(
            flops=2 * rows * rows * D, bytes_accessed=rows * D * 8, transcendentals=HEADS * rows * rows // 2
        ),
        name="attend",
    )(length, projected)


def attend_back_kernel(len_ref, p_ref, o_ref, g_ref, lse_ref, out_ref, dk_ref, dv_ref, kz_ref, vz_ref, kt_ref):
    blocks = p_ref.shape[1] // ROWS
    scaling = 1.0 / math.sqrt(HEAD)
    lane = lax.broadcasted_iota(jnp.int32, (ROWS, 128), 1)
    first_head = lane < HEAD
    row8 = lax.broadcasted_iota(jnp.int32, (8, 128), 0)
    lane8 = lax.broadcasted_iota(jnp.int32, (8, 128), 1)
    chooser = (lax.div(lane8, HEAD) == row8).astype(f32)
    key_at = lax.broadcasted_iota(jnp.int32, (2, ROWS, ROWS), 1)
    row_at = lax.broadcasted_iota(jnp.int32, (2, ROWS, ROWS), 2)
    allowed = (key_at <= row_at).reshape(2 * ROWS, ROWS)
    for i in range(blocks):
        rows = slice(i * ROWS, (i + 1) * ROWS)
        two = slice(2 * i * ROWS, 2 * (i + 1) * ROWS)

        @pl.when(i * ROWS < len_ref[0])
        def work():
            dk_ref[two, :] = jnp.zeros((2 * ROWS, 128), f32)
            dv_ref[two, :] = jnp.zeros((2 * ROWS, 128), f32)
            key, value = p_ref[1, rows, :], p_ref[2, rows, :]
            zero = jnp.zeros_like(key)
            k2 = jnp.concatenate([jnp.where(first_head, key, zero), jnp.where(first_head, zero, key)], axis=0)
            kz_ref[two, :] = k2
            kt_ref[:, two] = k2.T
            vz_ref[two, :] = jnp.concatenate([jnp.where(first_head, value, zero), jnp.where(first_head, zero, value)], axis=0)
            query = p_ref[0, rows, :] * jnp.asarray(scaling, bf16)
            grad = g_ref[rows, :]
            product = grad.astype(f32) * o_ref[rows, :].astype(f32)
            delta = lax.dot_general(chooser, product, (((1,), (1,)), ((), ())), precision=lax.Precision.HIGHEST, preferred_element_type=f32)
            def both(a, b):
                return jnp.concatenate([jnp.broadcast_to(a, (ROWS, ROWS)), jnp.broadcast_to(b, (ROWS, ROWS))], axis=0)
            lse2 = both(lse_ref[0, 0:1, rows], lse_ref[0, 1:2, rows])
            delta2 = both(delta[0:1], delta[1:2])
            dqt = jnp.zeros((128, ROWS), f32)
            for j in range(i + 1):
                cols = slice(2 * j * ROWS, 2 * (j + 1) * ROWS)
                prob = jnp.exp(dot_nt(kz_ref[cols, :], query) - lse2)
                if i == j:
                    prob = jnp.where(allowed, prob, 0.0)
                ds = (prob * (dot_nt(vz_ref[cols, :], grad) - delta2)).astype(bf16)
                dv_ref[cols, :] += dot_nn(prob.astype(bf16), grad)
                dk_ref[cols, :] += dot_nn(ds, query)
                dqt = dqt + dot_nn(kt_ref[:, cols], ds)
            out_ref[0, rows, :] = (dqt * scaling).T.astype(bf16)
    for i in range(blocks):
        rows = slice(i * ROWS, (i + 1) * ROWS)
        a = slice(2 * i * ROWS, (2 * i + 1) * ROWS); b = slice((2 * i + 1) * ROWS, 2 * (i + 1) * ROWS)

        @pl.when(i * ROWS < len_ref[0])
        def finish():
            out_ref[1, rows, :] = jnp.where(first_head, dk_ref[a, :], dk_ref[b, :]).astype(bf16)
            out_ref[2, rows, :] = jnp.where(first_head, dv_ref[a, :], dv_ref[b, :]).astype(bf16)


def blank_kernel(ready_ref, out_ref):
    pass


def blank(ready, shape):
    return pl.pallas_call(
        blank_kernel,
        in_specs=[pl.BlockSpec(memory_space=pltpu.SMEM)],
        out_specs=pl.BlockSpec(memory_space=pl.ANY),
        out_shape=shape,
        name="blank",
    )(ready)


def attend_back(choice, share, projected, heads_out, grad_heads, lse, before):
    rows = projected.shape[1]
    cols = lambda h, n: (0, n[2] + h)
    blocks = lambda h, n: (0, 0, n[2] + h)

    def kernel(n, p, o, g, l, unused, *rest):
        attend_back_kernel(n, p, o, g, l, *rest)

    return pl.pallas_call(
        kernel,
        grid_spec=pltpu.PrefetchScalarGridSpec(
            num_scalar_prefetch=1,
            grid=(share,),
            in_specs=[
                pl.BlockSpec((3, rows, 128), blocks),
                pl.BlockSpec((rows, 128), cols),
                pl.BlockSpec((None, rows, 128), lambda h, n: (n[1], 0, n[2] + h)),
                pl.BlockSpec((1, 8, rows), lambda h, n: (n[2] + h, 0, 0)),
                pl.BlockSpec(memory_space=pl.ANY),
            ],
            out_specs=pl.BlockSpec((3, rows, 128), blocks),
            scratch_shapes=[
                pltpu.VMEM((2 * rows, 128), f32),
                pltpu.VMEM((2 * rows, 128), f32),
                pltpu.VMEM((2 * rows, 128), bf16),
                pltpu.VMEM((2 * rows, 128), bf16),
                pltpu.VMEM((128, 2 * rows), bf16),
            ],
        ),
        out_shape=jax.ShapeDtypeStruct((3, rows, D), bf16),
        input_output_aliases={5: 0},
        compiler_params=params(),
        cost_estimate=pl.CostEstimate(
            flops=1 * share * rows * rows * D, bytes_accessed=share * rows * D * 3, transcendentals=share * rows * rows
        ),
        name="attend_back",
    )(choice, projected, heads_out, grad_heads, lse, before)


def feed_kernel(plan, len_ref, row_ref, *refs):
    tok0, tok1, pass0, pass1, ho0, ho1, cot, table_ref, gain_ref = refs[:9]
    many = 2 * plan.sharers if plan.paired else 1
    grad_ref, pieces, refs = refs[9], refs[10 : 10 + many], refs[10 + many :]
    res, gh, hid, small_ref = refs[:4]
    outs, (w_ref, acc_ref, sums_ref, stage_ref, sem_ref) = refs[4:-5], refs[-5:]
    b = pl.program_id(0)
    many0 = last_block(len_ref[0]) + 1
    many1 = last_block(len_ref[1]) + 1
    early = b < many0

    @pl.when(b == 0)
    def clear():
        load_weight(plan, row_ref, pieces, w_ref, sem_ref, acc_ref, sums_ref)

    @pl.when(b < many0 + many1)
    def block():
        hot = onehot_rows(jnp.where(early, pass0[0], pass1[0]))
        entry = jnp.where(early, tok0[...], tok1[...]).astype(f32) + dot_tn(hot, table_ref[...])
        at = jnp.where(early, b, b - many0) * ROWS + lax.broadcasted_iota(jnp.int32, (ROWS, 1), 0)
        live = at < jnp.where(early, len_ref[0], len_ref[1])
        heads = jnp.where(early, ho0[...], ho1[...])
        attention = dot_nn(heads, w_ref[:, 0:D])
        hidden = entry + attention
        unit, scale = normalized(hidden)
        gain = gain_ref[...]
        normed = (unit * gain).astype(bf16)
        grad_feed = jnp.where(live, cot[...].reshape(ROWS, D).astype(f32), 0.0).astype(bf16)
        @pl.when(b == 0)
        def rest_of_weight():
            for copy in weight_copies(plan, row_ref, pieces, w_ref, sem_ref, 1):
                copy.wait()

        feed = jnp.zeros((ROWS, D), f32)
        grad_normed = jnp.zeros((ROWS, D), f32)
        for k in range(CHUNKS):
            up = slice(D + k * D, D + (k + 1) * D)
            down = slice(D + FF + k * D, D + FF + (k + 1) * D)
            x = dot_nn(normed, w_ref[:, up])
            grad_act = dot_nt(grad_feed, w_ref[:, down])
            c0 = math.sqrt(2.0 / math.pi)
            square = x * x
            bent = jnp.tanh(x * (c0 + (c0 * 0.044715) * square))
            half = 0.5 + 0.5 * bent
            slope = half + (0.5 * x) * (1.0 - bent * bent) * (c0 + (3.0 * c0 * 0.044715) * square)
            act = (x * half).astype(bf16)
            grad_x = (slope * grad_act).astype(bf16)
            feed = feed + dot_nn(act, w_ref[:, down])
            grad_normed = grad_normed + dot_nt(grad_x, w_ref[:, up])
            acc_ref[:, up] += dot_tn(normed, grad_x)
            acc_ref[:, down] += dot_tn(act, grad_feed)
        res[...] = jnp.where(live, hidden + feed, 0.0).astype(bf16).reshape(res.shape)
        sums_ref[0:8] += fold_rows(grad_normed * unit)
        sums_ref[8:16] += fold_rows(jnp.where(live, entry * entry, 0.0))
        sums_ref[16:24] += fold_rows(jnp.where(live, attention * attention, 0.0))
        sums_ref[24:32] += fold_rows(jnp.where(live, feed * feed, 0.0))
        grad_hidden = grad_feed.astype(f32) + norm_back(grad_normed * gain, unit, scale)
        hid[...] = grad_hidden
        grad_attention = grad_hidden.astype(bf16)
        acc_ref[:, 0:D] += dot_tn(heads, grad_attention)
        gh[...] = dot_nt(grad_attention, w_ref[:, 0:D]).astype(bf16)

    @pl.when(b == pl.num_programs(0) - 1)
    def finish():
        counted = (len_ref[0] + len_ref[1]).astype(f32)
        small_ref[...] = jnp.full(small_ref.shape, counted, f32)
        for n in range(4):
            small_ref[n : n + 1] = jnp.sum(sums_ref[8 * n : 8 * n + 8], axis=0, keepdims=True)
        store_grads(plan, plan.wide_orders, grad_ref, acc_ref, outs, stage_ref, sem_ref)


def feed(plan, part, lengths, piece_rows, grad_rows, tokens, pass_rows, heads_out, cotangent, table, gain, pieces, width):
    rows = tokens[0].shape[0]
    per = ROWS // part

    def at0(b, n, r):
        return jnp.minimum(b, last_block(n[0])), 0

    def at1(b, n, r):
        return jnp.clip(b - last_block(n[0]) - 1, 0, last_block(n[1])), 0

    def both(b, n, r):
        early = b <= last_block(n[0])
        return jnp.where(early, b, at1(b, n, r)[0]), jnp.where(early, 0, 1)

    row0 = pl.BlockSpec((ROWS, D), at0)
    row1 = pl.BlockSpec((ROWS, D), at1)
    pas0 = pl.BlockSpec((1, 1, ROWS), lambda *a: at0(*a) + (0,))
    pas1 = pl.BlockSpec((1, 1, ROWS), lambda *a: at1(*a) + (0,))
    dealt = pl.BlockSpec((per, 1, part, D), lambda *a: both(*a) + (0, 0))
    local = pl.BlockSpec((None, ROWS, D), lambda *a: both(*a)[::-1] + (0,))
    grads = grad_shapes(plan, width, plan.wide_orders)
    anywhere = pl.BlockSpec(memory_space=pl.ANY)
    return pl.pallas_call(
        functools.partial(feed_kernel, plan),
        grid_spec=pltpu.PrefetchScalarGridSpec(
            num_scalar_prefetch=2,
            grid=(2 * rows // ROWS,),
            in_specs=[
                row0, row1, pas0, pas1, row0, row1, dealt,
                pl.BlockSpec((8, D), lambda *a: (0, 0)),
                pl.BlockSpec((1, D), lambda *a: (0, 0)),
                pl.BlockSpec(memory_space=pltpu.SMEM),
            ]
            + [anywhere] * len(pieces),
            out_specs=[dealt, local, local, pl.BlockSpec((8, D), lambda *a: (0, 0))] + [anywhere] * len(grads),
            scratch_shapes=[
                pltpu.VMEM((D, width), bf16),
                pltpu.VMEM((D, width), f32),
                pltpu.VMEM((32, D), f32),
                pltpu.VMEM(stage_shape(plan), bf16),
                pltpu.SemaphoreType.DMA((2,)),
            ],
        ),
        out_shape=[
            jax.ShapeDtypeStruct(cotangent.shape, bf16),
            jax.ShapeDtypeStruct((2, rows, D), bf16),
            jax.ShapeDtypeStruct((2, rows, D), f32),
            jax.ShapeDtypeStruct((8, D), f32),
        ]
        + grads,
        compiler_params=params(),
        cost_estimate=pl.CostEstimate(
            flops=2 * 6 * rows * D * width, bytes_accessed=2 * rows * D * 14 + D * width * 4, transcendentals=2 * rows * FF
        ),
        name="feed",
    )(lengths, piece_rows, tokens[0], tokens[1], pass_rows[0], pass_rows[1], heads_out[0], heads_out[1],
      cotangent, table, gain, grad_rows, *pieces)


def project_back_kernel(plan, weight, rows_back, final, len_ref, row_ref, grad_ref, tok_ref, pass_ref, g_ref, *rest):
    rest = list(rest)
    hid_ref = rest.pop(0) if rows_back else None
    table_ref, gain_ref = rest.pop(0), rest.pop(0)
    before_ref = rest.pop(0) if final else None
    many = plan.sharers if plan.paired else 1
    pieces = [rest.pop(0) for n in range(many)] if rows_back else []
    if rows_back:
        out_ref, small_ref = rest.pop(0), rest.pop(0)
    if weight and not final:
        acc_ref = rest.pop(0)
    outs = [rest.pop(0) for shape in grad_shapes(plan, 3 * D, plan.head_orders)] if final else []
    if rows_back:
        w_ref, sums_ref = rest.pop(0), rest.pop(0)
    if final:
        acc_ref, stage_ref = rest.pop(0), rest.pop(0)
    sem_ref = rest.pop(0)
    b = pl.program_id(0)

    @pl.when(b == 0)
    def clear():
        if rows_back:
            load_weight(plan, row_ref, pieces, w_ref, sem_ref, sums_ref, *([acc_ref] if weight and not final else []))
        if final:
            copy = pltpu.make_async_copy(before_ref, acc_ref, sem_ref.at[0])
            copy.start()
            copy.wait()

    @pl.when(b <= last_block(len_ref[0]))
    def work():
        hot = onehot_rows(pass_ref[0])
        entry = tok_ref[...].astype(f32) + dot_tn(hot, table_ref[...])
        unit, scale = normalized(entry)
        gain = gain_ref[...]
        if weight:
            normed = (unit * gain).astype(bf16)
            for part in range(3):
                acc_ref[:, part * D : (part + 1) * D] += dot_tn(normed, g_ref[part])
        if rows_back:
            grad_normed = jnp.zeros((ROWS, D), f32)
            for part in range(3):
                grad_normed = grad_normed + dot_nt(g_ref[part], w_ref[:, part * D : (part + 1) * D])
            sums_ref[0:8] += fold_rows(grad_normed * unit)
            grad_entry = hid_ref[...] + norm_back(grad_normed * gain, unit, scale)
            high = grad_entry.astype(bf16)
            out_ref[...] = high
            rest_one = grad_entry - high.astype(f32)
            low = rest_one.astype(bf16)
            lower = (rest_one - low.astype(f32)).astype(bf16)
            sums_ref[8:16] += dot_nn(hot, high) + dot_nn(hot, low) + dot_nn(hot, lower)

    if rows_back:
        @pl.when(b == pl.num_programs(0) - 1)
        def sums():
            small_ref[...] = sums_ref[8:16]
            small_ref[PASSES : PASSES + 1] = jnp.sum(sums_ref[0:8], axis=0, keepdims=True)

    if final:
        @pl.when(b == pl.num_programs(0) - 1)
        def finish():
            store_grads(plan, plan.head_orders, grad_ref, acc_ref, outs, stage_ref, sem_ref)


def project_back(
    plan, weight, rows_back, which, length, piece_rows, grad_rows, tokens, pass_rows, grads, grad_hidden, table, gain,
    pieces, before=None,
):
    rows = tokens.shape[0]
    final = before is not None
    at = lambda b, n, r, g: (jnp.minimum(b, last_block(n[0])), 0)
    row = pl.BlockSpec((ROWS, D), at)
    anywhere = pl.BlockSpec(memory_space=pl.ANY)
    in_specs = [
        row,
        pl.BlockSpec((1, 1, ROWS), lambda *a: at(*a) + (0,)),
        pl.BlockSpec((3, ROWS, D), lambda *a: (0,) + at(*a)),
    ]
    operands = [length, piece_rows, grad_rows, tokens, pass_rows, grads]
    if rows_back:
        in_specs.append(pl.BlockSpec((None, ROWS, D), lambda *a: (which,) + at(*a)))
        operands.append(grad_hidden)
    in_specs += [pl.BlockSpec((8, D), lambda *a: (0, 0)), pl.BlockSpec((1, D), lambda *a: (0, 0))]
    operands += [table, gain]
    out_shape, out_specs, scratch = [], [], []
    if final:
        in_specs.append(anywhere)
        operands.append(before)
    if rows_back:
        in_specs += [anywhere] * len(pieces)
        operands += pieces
        out_shape += [jax.ShapeDtypeStruct((rows, D), bf16), jax.ShapeDtypeStruct((8, D), f32)]
        out_specs += [row, pl.BlockSpec((8, D), lambda *a: (0, 0))]
        scratch += [pltpu.VMEM((D, 3 * D), bf16), pltpu.VMEM((16, D), f32)]
    if weight and not final:
        out_shape.append(jax.ShapeDtypeStruct((D, 3 * D), f32))
        out_specs.append(pl.BlockSpec((D, 3 * D), lambda *a: (0, 0)))
    if final:
        shapes = grad_shapes(plan, 3 * D, plan.head_orders)
        out_shape += shapes
        out_specs += [anywhere] * len(shapes)
        scratch += [pltpu.VMEM((D, 3 * D), f32), pltpu.VMEM(stage_shape(plan), bf16)]
    return pl.pallas_call(
        functools.partial(project_back_kernel, plan, weight, rows_back, final),
        grid_spec=pltpu.PrefetchScalarGridSpec(
            num_scalar_prefetch=3,
            grid=(rows // ROWS,),
            in_specs=in_specs,
            out_specs=out_specs,
            scratch_shapes=scratch + [pltpu.SemaphoreType.DMA((2,))],
        ),
        out_shape=out_shape,
        compiler_params=params(),
        cost_estimate=pl.CostEstimate(
            flops=2 * (weight + rows_back) * rows * D * 3 * D, bytes_accessed=rows * D * 14 + D * D * 6, transcendentals=0
        ),
        name="project_back",
    )(*operands)


def pick_kernel(index_ref, in_ref, out_ref, sem_ref):
    copies = [
        pltpu.make_async_copy(in_ref.at[index_ref[n]], out_ref.at[n], sem_ref) for n in range(out_ref.shape[0])
    ]
    for copy in copies:
        copy.start()
    for copy in copies:
        copy.wait()


def pick(index, blocks):
    shape = index.shape + blocks.shape[1:]
    return pl.pallas_call(
        pick_kernel,
        grid_spec=pltpu.PrefetchScalarGridSpec(
            num_scalar_prefetch=1,
            grid=(1,),
            in_specs=[pl.BlockSpec(memory_space=pl.ANY)],
            out_specs=pl.BlockSpec(shape, lambda b, n: (0, 0, 0)),
            scratch_shapes=[pltpu.SemaphoreType.DMA],
        ),
        out_shape=jax.ShapeDtypeStruct(shape, blocks.dtype),
        compiler_params=params(),
        cost_estimate=pl.CostEstimate(flops=0, bytes_accessed=4 * math.prod(shape), transcendentals=0),
        name="pick",
    )(index, blocks)


def settle_kernel(index_ref, *refs):
    arrays, out_ref = refs[:-1], refs[-1]
    first = pl.program_id(0) * out_ref.shape[0]
    rows = out_ref.shape[1]
    at = lax.broadcasted_iota(jnp.int32, (rows, 1), 0)
    for n in range(out_ref.shape[0]):
        live = at < index_ref[2, first + n]
        source, late = index_ref[1, first + n], index_ref[0, first + n]
        if len(arrays) == 1:
            found = arrays[0][2 * source + late]
        else:
            found = jnp.where(late == 0, arrays[0][source], arrays[1][source])
        out_ref[n] = jnp.where(live, found.astype(f32), 0.0)


def settle(index, *arrays):
    many = index.shape[1]
    step = 4
    shape = arrays[0].shape
    whole = pl.BlockSpec(shape, lambda b, n: (0, 0, 0), pipeline_mode=pl.Buffered(1))
    return pl.pallas_call(
        settle_kernel,
        grid_spec=pltpu.PrefetchScalarGridSpec(
            num_scalar_prefetch=1,
            grid=(many // step,),
            in_specs=[whole] * len(arrays),
            out_specs=pl.BlockSpec((step,) + shape[1:], lambda b, n: (b, 0, 0)),
        ),
        out_shape=jax.ShapeDtypeStruct((many,) + shape[1:], f32),
        compiler_params=params(),
        cost_estimate=pl.CostEstimate(flops=0, bytes_accessed=6 * many * math.prod(shape[1:]), transcendentals=0),
        name="settle",
    )(index, *arrays)


def after(values, *others):
    return lax.optimization_barrier((values, others))[0]


def swap(blocks):
    return lax.all_to_all(blocks, "dp", split_axis=0, concat_axis=0, tiled=True)


def per_device(
    groups,
    width_all,
    tokens,
    passes,
    lengths,
    dealing,
    pass_table,
    gain_first,
    to_heads,
    from_heads,
    gain_second,
    expand,
    shrink,
    cotangent,
):
    axes = ("dp", "fsdp")
    slots, part, unused_width = tokens.shape
    seq_len = part * groups
    order = jnp.arange(slots, dtype=jnp.int32)
    here = lax.axis_index("dp")
    ordering = dealing[0, 0]
    sizes = lengths[0]

    ahead = (sizes[None, :] > sizes[:, None]) | (
        (sizes[None, :] == sizes[:, None]) & (order[None, :] < order[:, None])
    )
    rank = jnp.sum(ahead.astype(jnp.int32), axis=1)
    ranked = jnp.sum(jnp.where(rank[None, :] == order[:, None], order[None, :], 0), axis=1)
    place = jnp.sum(jnp.where(ordering[None, :] == order[:, None], order[None, :], 0), axis=1)
    early_seqs = ranked[:groups]
    late_seqs = ranked[groups:][::-1]
    from_early = jnp.sum(jnp.where(early_seqs[:, None] == order[None, :], place[None, :], 0), axis=1)
    from_late = jnp.sum(jnp.where(late_seqs[:, None] == order[None, :], place[None, :], 0), axis=1)
    slot_rank = jnp.sum(jnp.where(ordering[:, None] == order[None, :], rank[None, :], 0), axis=1)
    slot_size = jnp.sum(jnp.where(ordering[:, None] == order[None, :], sizes[None, :], 0), axis=1)
    is_late = (slot_rank >= groups).astype(jnp.int32)
    source = jnp.where(is_late == 1, slots - 1 - slot_rank, slot_rank)
    back_index = jnp.stack([is_late, source, slot_size - here * part])
    my_seqs = jnp.stack([early_seqs[here], late_seqs[here]])
    my_sizes = jnp.sum(jnp.where(my_seqs[:, None] == order[None, :], sizes[None, :], 0), axis=1)

    row_count = to_heads.shape[0]
    narrow = jnp.concatenate(
        [
            from_heads,
            expand.reshape(row_count, D, CHUNKS).transpose(0, 2, 1).reshape(row_count, FF),
            shrink.reshape(row_count, CHUNKS * D),
        ],
        axis=1,
    )
    plan = Plan(groups, width_all // groups, row_count)
    index_here = here * (width_all // groups) + lax.axis_index("fsdp")
    my_passes = [passes[my_seqs[m]].reshape(seq_len // ROWS, 1, ROWS) for m in range(2)]
    one_size = [my_sizes[m : m + 1] for m in range(2)]
    table = jnp.zeros((8, D), bf16).at[:PASSES].set(pass_table)
    gain_one = gain_first.astype(f32).reshape(1, D)
    gain_two = gain_second.astype(f32).reshape(1, D)

    pairs_index = jnp.stack([from_early, from_late], axis=1).reshape(slots)
    picked = [pick(from_early, tokens), pick(from_late, tokens), pick(pairs_index, cotangent)]
    if plan.paired:
        piece_rows = plan.piece_rows(index_here)
        wide_rows = plan.grad_rows(index_here, plan.wide_orders)
        head_rows = plan.grad_rows(index_here, plan.head_orders)
        head_far = plan.gather(to_heads[None], plan.far)
        head_near = plan.gather(head_far, [plan.near])
        wide_one = plan.gather(after(narrow, head_far)[None], plan.far[:1])
        ready = (my_passes, one_size, piece_rows, table, gain_one)
        tokens0 = swap(after(picked[0], head_near, wide_one, ready))
        head_pieces = plan.gather_core(plan.gather_x(head_near))
    else:
        piece_rows = wide_rows = head_rows = jnp.zeros((1,), jnp.int32)
        head_pieces = (lax.all_gather(to_heads, axes, axis=0, tiled=True),)
        wide_pieces = (lax.all_gather(narrow, axes, axis=0, tiled=True),)
        tokens0 = swap(picked[0])
        wide_far = wide_pieces

    def forward(m, *gate):
        return project(
            plan, after(one_size[m], gate), piece_rows, my_tokens[m], my_passes[m], table, gain_one, head_pieces
        )

    def mix(m, *gate):
        return attend(after(one_size[m], gate), projected[m])

    half = HEADS // 4
    choices = {
        (m, first): jnp.stack([my_sizes[m], jnp.int32(m), jnp.int32(first)]) for m, first in ((0, 0), (1, 0), (1, half))
    }

    def mix_back(m, first, share, before, *gate):
        choice = after(choices[m, first], gate)
        return attend_back(choice, share, projected[m], heads_out[m], grad_heads, lse[m], before)

    def back(m, weight, rows_back, *gate, before=None):
        return project_back(
            plan, weight, rows_back, m, after(one_size[m], gate), piece_rows, head_rows, my_tokens[m], my_passes[m],
            grad_parts[m], grad_hidden, table, gain_one, head_pieces, before,
        )

    def send_back(rows, *gate):
        return swap(after(rows, gate).reshape(groups, part, D))

    projected, heads_out, lse, grad_parts = [None, None], [None, None], [None, None], [None, None]
    my_tokens = [tokens0.reshape(seq_len, D)]
    projected[0] = forward(0)
    if plan.paired:
        wide_far = plan.gather(wide_one, plan.far[1:], head_pieces, projected[0])
        cut = D + FF
    tokens1 = swap(after(picked[1], tokens0, picked[2], wide_far))
    my_tokens.append(tokens1.reshape(seq_len, D))
    heads_out[0], lse[0] = mix(0, wide_far)
    if plan.paired:
        first = plan.gather_near({0: wide_far[:, :, :cut]}, (), lse[0])
        second = plan.gather_x(wide_far[:, :, cut:], ())
        ready = (first, second)
    else:
        ready = ()
    my_grads = swap(after(picked[2].reshape(groups, 2, part, D), tokens1, lse[0], ready))
    projected[1] = forward(1, lse[0])
    if plan.paired:
        first = plan.gather_x(first[0])
        second = plan.gather_near(second, lse[0], projected[1])
    heads_out[1], lse[1] = mix(1)
    if plan.paired:
        wide_pieces = plan.gather_core(first, lse[1]) + plan.gather_core(second, lse[1])

    space = jax.ShapeDtypeStruct((3, seq_len, D), bf16)
    blanks = [blank(one_size[m], space) for m in range(2)]
    res, grad_heads, grad_hidden, feed_small, *wide_grads = feed(
        plan, part, after(my_sizes, choices, blanks), piece_rows, wide_rows, my_tokens, my_passes, heads_out, my_grads, table, gain_two,
        wide_pieces, D + 2 * FF,
    )

    def begin(grads):
        if not plan.paired:
            return lax.psum_scatter(grads[0], axes, scatter_dimension=0, tiled=True).astype(f32)
        return [grads[n : n + 2] for n in range(0, len(grads), 2)]

    def advance(state, stage, gate, late):
        return plan.reduce_stage(state, plan.wide_orders, stage, (gate,), (late,)) if plan.paired else state

    wide0 = begin(wide_grads)
    result = swap(res)
    grad_parts[0] = mix_back(0, 0, 2 * half, blanks[0])
    wide1 = advance(wide0, 0, (), grad_parts[0])
    entry0, small0, head_sum = back(0, True, True, wide1)
    wide2 = advance(wide1, 1, (), entry0)
    moved0 = send_back(entry0, result)
    some = mix_back(1, 0, half, blanks[1], entry0, wide2, result)
    wide3 = advance(wide2, 2, (), some)
    grad_parts[1] = mix_back(1, half, half, some, wide3)
    entry1, small1 = back(1, False, True)
    wide_owned = advance(wide3, 3, some, entry1)
    moved1 = send_back(entry1, moved0, wide_owned)
    totals = jnp.concatenate([small0 + small1, feed_small], axis=0)
    stages = plan.head_orders[0]
    head_grads = back(1, True, False, entry1, moved0, before=head_sum)
    head_state = begin(head_grads)
    if plan.paired:
        totals = plan.total_stage(totals, stages[0], (), head_grads[:1])
        head_state = plan.reduce_stage(head_state, plan.head_orders, 0, (wide_owned,))
        wide_owned = wide_owned[0]
    output = settle(after(back_index, head_state), result.reshape(slots, part, D))
    grad_tokens = settle(after(back_index, output), moved0, moved1)
    grad_from = wide_owned[:, :D]
    grad_expand = wide_owned[:, D : D + FF].reshape(row_count, CHUNKS, D).transpose(0, 2, 1).reshape(row_count, FF)
    grad_shrink = wide_owned[:, D + FF :].reshape(row_count * CHUNKS, D)
    if plan.paired:
        totals = plan.total_stage(totals, stages[1])
        late = (output, grad_tokens, grad_from, grad_expand, grad_shrink)
        head_state = plan.reduce_stage(head_state, plan.head_orders, 1, (totals,), late)
        totals = plan.total_stage(totals, stages[2], (head_state,))
        head_owned = plan.reduce_stage(head_state, plan.head_orders, 2)[0]
    else:
        totals = lax.psum(totals, axes)
        head_owned = head_state
    root_squares = jnp.sqrt(jnp.sum(totals[9:12], axis=1) / (totals[12, 0] * D))

    return (
        output,
        grad_tokens,
        totals[:PASSES],
        totals[PASSES],
        head_owned,
        grad_from,
        totals[8],
        grad_expand,
        grad_shrink,
        root_squares,
    )


def solution(mesh):
    groups = mesh.shape["dp"]
    weight_spec = P(("dp", "fsdp"), None)
    block_spec = P("fsdp", "dp", None)
    in_specs = (
        block_spec,
        P("fsdp", None),
        P("fsdp", None),
        P("dp", "fsdp", None),
        P(),
        P(),
        weight_spec,
        weight_spec,
        P(),
        weight_spec,
        weight_spec,
        block_spec,
    )
    out_specs = (
        block_spec,
        block_spec,
        P(),
        P(),
        weight_spec,
        weight_spec,
        P(),
        weight_spec,
        weight_spec,
        P(),
    )
    body = functools.partial(per_device, groups, groups * mesh.shape["fsdp"])
    return jax.shard_map(body, mesh=mesh, in_specs=in_specs, out_specs=out_specs, check_vma=False)
```

```python
import math
import functools

import jax
import jax.numpy as jnp
from jax import lax
from jax.experimental import pallas as pl
from jax.experimental.pallas import tpu as pltpu
from jax.sharding import PartitionSpec as P

D = 768
HEADS = 12
HEAD = 64
FF = 3072
PASSES = 5
EPS = 1e-05
ROWS = 256
CHUNKS = FF // D
VMEM_MOST = 64000 * 1024

f32 = jnp.float32
bf16 = jnp.bfloat16


def dot_nn(a, b):
    return lax.dot_general(a, b, (((1,), (0,)), ((), ())), preferred_element_type=f32)


def dot_nt(a, b):
    return lax.dot_general(a, b, (((1,), (1,)), ((), ())), preferred_element_type=f32)


def dot_tn(a, b):
    return lax.dot_general(a, b, (((0,), (0,)), ((), ())), preferred_element_type=f32)


def params(**more):
    return pltpu.CompilerParams(vmem_limit_bytes=VMEM_MOST, **more)


def normalized(values):
    centred = values - jnp.mean(values, axis=-1, keepdims=True)
    spread = jnp.mean(centred * centred, axis=-1, keepdims=True)
    scale = lax.rsqrt(spread + EPS)
    return centred * scale, scale


def norm_back(grad_unit, unit, scale):
    first = jnp.mean(grad_unit, axis=-1, keepdims=True)
    second = jnp.mean(grad_unit * unit, axis=-1, keepdims=True)
    return scale * (grad_unit - first - unit * second)


def onehot_rows(pass_row):
    ids = lax.broadcasted_iota(jnp.int32, (8, pass_row.shape[-1]), 0)
    return (ids == pass_row).astype(f32).astype(bf16)


def fold_rows(values):
    rows, width = values.shape
    return jnp.sum(values.reshape(rows // 8, 8, width), axis=0)


def last_block(length):
    return lax.div(length + (ROWS - 1), ROWS) - 1


def bits_of(count):
    return count.bit_length() - 1


class Plan:
    def __init__(self, groups, sharers, rows):
        self.groups, self.sharers, self.rows = groups, sharers, rows
        self.count = groups * sharers
        self.paired = rows % 8 == 0 and self.count & (self.count - 1) == 0 and sharers >= 4 and groups >= 4
        core, *over_x = [1 << bit for bit in range(bits_of(sharers))]
        near, *far = [sharers << bit for bit in range(bits_of(groups))]
        self.core, self.over_x, self.near, self.far = core, over_x, near, far[::-1]
        self.wide_orders = ([[core], over_x, [near], far], [[core], [near], over_x, far])
        self.head_orders = ([[core], over_x + [near], far],)

    def exchange(self, values, bits):
        pairs = [(i, i ^ bits) for i in range(self.count)]
        return lax.ppermute(values, ("dp", "fsdp"), pairs)

    def gather(self, held, masks, gate=(), late=()):
        for bits in masks:
            held = jnp.concatenate([after(held, late), self.exchange(after(held, gate), bits)], axis=0)
        return held

    def gather_x(self, held, *gate):
        pieces = {0: held}
        for bits in self.over_x[::-1]:
            for name in list(pieces):
                pieces[name | bits] = self.exchange(after(pieces[name], gate), bits)
        return pieces

    def gather_near(self, pieces, gate=(), late=()):
        return {name: self.gather(held, [self.near], gate, late) for name, held in pieces.items()}

    def gather_core(self, pieces, *gate):
        found = dict(pieces)
        for name in pieces:
            found[name | self.core] = self.exchange(after(pieces[name], gate), self.core)
        return tuple(found[name] for name in range(self.sharers))

    def piece_rows(self, here):
        masks = self.far + [self.near]
        found = []
        for f in range(self.sharers):
            for n in range(self.groups):
                rel = f | ways_bits(masks, n)
                found.append((here ^ rel) * self.rows)
        return jnp.stack(found).astype(jnp.int32)

    def grad_rows(self, here, orders):
        found = []
        for order in orders:
            for place in range(self.count):
                rel, left = 0, self.count
                for masks in order:
                    left >>= len(masks)
                    rel |= ways_bits(masks, (place // left) % (1 << len(masks)))
                found.append((here ^ rel) * self.rows)
        return jnp.stack(found).astype(jnp.int32)

    def total_stage(self, values, masks, gate=(), late=()):
        found = [after(values, late)]
        found += [self.exchange(after(values, gate), ways_bits(masks, way)) for way in range(1, 1 << len(masks))]
        while len(found) > 1:
            found = [found[k] + found[k + 1] for k in range(0, len(found), 2)]
        return found[0]

    def reduce_stage(self, states, orders, stage, gate=(), late=()):
        sums = []
        for ways, order in zip(states, orders):
            sums.append(
                [after(ways[0], late)]
                + [
                    self.exchange(after(ways[n], gate), ways_bits(order[stage], n))
                    for n in range(1, len(ways))
                ]
            )
        if stage == len(orders[0]) - 1:
            return [sum(part.astype(f32) for part in parts)[0] for parts in sums]
        ways = 1 << len(orders[0][stage + 1])
        if stage == len(orders[0]) - 2:
            return [merge(sums, ways)]
        return [merge([parts], ways) for parts in sums]


def ways_bits(masks, way):
    return sum(bits for n, bits in enumerate(masks) if (way >> n) & 1)


def merge_kernel(widths, many, ways, *refs):
    ins, outs = refs[: len(widths) * many * ways], refs[len(widths) * many * ways :]
    for way in range(ways):
        first = 0
        for k, width in enumerate(widths):
            views = [ins[(k * many + n) * ways + way] for n in range(many)]
            total = views[0][...].astype(f32)
            for view in views[1:]:
                total = total + view[...].astype(f32)
            outs[way][:, :, first : first + width] = total.astype(bf16)
            first += width


def merge(groups, ways):
    blocks, rows, unused = groups[0][0].shape
    widths = [parts[0].shape[2] for parts in groups]
    share = blocks // ways
    steps = min(share, 4)

    def view(way, width):
        return pl.BlockSpec((share // steps, rows, width), lambda b: (b + way * steps, 0, 0))

    out = jax.ShapeDtypeStruct((share, rows, sum(widths)), bf16)
    many = len(groups[0])
    size = blocks * rows * sum(widths)
    return pl.pallas_call(
        functools.partial(merge_kernel, widths, many, ways),
        grid=(steps,),
        in_specs=[view(way, width) for width in widths for n in range(many) for way in range(ways)],
        out_specs=[view(0, sum(widths))] * ways,
        out_shape=[out] * ways,
        compiler_params=params(),
        cost_estimate=pl.CostEstimate(flops=many * size, bytes_accessed=(2 + 2 * many) * size, transcendentals=0),
        name="merge",
    )(*[part for parts in groups for part in parts for way in range(ways)])


def weight_copies(plan, rows_ref, pieces, weight_ref, sem_ref, group):
    if not plan.paired:
        return [pltpu.make_async_copy(pieces[0], weight_ref, sem_ref.at[0])] if group == 0 else []
    mine = pieces[group * plan.sharers : (group + 1) * plan.sharers]
    if len(mine) == 0:
        return []
    first = pieces[0].shape[-1] * group
    copies = []
    for f, piece in enumerate(mine):
        for n in range(plan.groups):
            at = pl.multiple_of(rows_ref[f * plan.groups + n], 8)
            target = weight_ref.at[pl.ds(at, plan.rows), first : first + piece.shape[-1]]
            copies.append(pltpu.make_async_copy(piece.at[n], target, sem_ref.at[group]))
    return copies


def load_weight(plan, rows_ref, pieces, weight_ref, sem_ref, *cleared):
    first, second = [weight_copies(plan, rows_ref, pieces, weight_ref, sem_ref, group) for group in range(2)]
    for copy in first + second:
        copy.start()
    for ref in cleared:
        ref[...] = jnp.zeros_like(ref)
    for copy in first:
        copy.wait()


def grad_shapes(plan, width, orders):
    if not plan.paired:
        return [jax.ShapeDtypeStruct((D, width), bf16)]
    half = plan.count // 2
    cut = first_part(width, orders)
    return [jax.ShapeDtypeStruct((half, plan.rows, w), bf16) for w in (cut, cut, width - cut, width - cut) if w > 0]


def first_part(width, orders):
    return width // D * 2 // 3 * D if len(orders) == 2 else width


def stage_shape(plan):
    return (2, plan.count, plan.rows, D) if plan.paired else (2, D, D)


def store_grads(plan, orders, rows_ref, acc_ref, outs, stage_ref, sem_ref):
    width, step = acc_ref.shape[1], D
    cut = first_part(width, orders)
    half = plan.count // 2
    waiting = []
    for n in range(width // step):
        slot = n % 2
        cols = slice(n * step, (n + 1) * step)
        if len(waiting) == 2:
            for copy in waiting.pop(0):
                copy.wait()
        if not plan.paired:
            stage_ref[slot] = acc_ref[:, cols].astype(bf16)
            copies = [pltpu.make_async_copy(stage_ref.at[slot], outs[0].at[:, cols], sem_ref.at[slot])]
        else:
            late = n * step >= cut
            base = plan.count if late else 0
            start = n * step - (cut if late else 0)

            def fill(place, carry):
                at = pl.multiple_of(rows_ref[base + place], 8)
                stage_ref[slot, place] = acc_ref[pl.ds(at, plan.rows), cols].astype(bf16)
                return carry

            lax.fori_loop(0, plan.count, fill, 0, unroll=8)
            keep, send = outs[2:4] if late else outs[0:2]
            there = slice(start, start + step)
            copies = [
                pltpu.make_async_copy(stage_ref.at[slot, 0:half], keep.at[:, :, there], sem_ref.at[slot]),
                pltpu.make_async_copy(stage_ref.at[slot, half:], send.at[:, :, there], sem_ref.at[slot]),
            ]
        for copy in copies:
            copy.start()
        waiting.append(copies)
    for copies in waiting:
        for copy in copies:
            copy.wait()


def project_kernel(plan, len_ref, row_ref, tok_ref, pass_ref, table_ref, gain_ref, *rest):
    pieces, (out_ref, w_ref, sem_ref) = rest[:-3], rest[-3:]

    @pl.when(pl.program_id(0) == 0)
    def load():
        load_weight(plan, row_ref, pieces, w_ref, sem_ref)

    @pl.when(pl.program_id(0) <= last_block(len_ref[0]))
    def work():
        hot = onehot_rows(pass_ref[0])
        entry = tok_ref[...].astype(f32) + dot_tn(hot, table_ref[...])
        unit, unused = normalized(entry)
        normed = (unit * gain_ref[...]).astype(bf16)
        for part in range(3):
            out_ref[part] = dot_nn(normed, w_ref[:, part * D : (part + 1) * D]).astype(bf16)


def project(plan, length, piece_rows, tokens, pass_rows, table, gain, pieces):
    rows = tokens.shape[0]
    at = lambda b, n, r: (jnp.minimum(b, last_block(n[0])), 0)
    return pl.pallas_call(
        functools.partial(project_kernel, plan),
        grid_spec=pltpu.PrefetchScalarGridSpec(
            num_scalar_prefetch=2,
            grid=(rows // ROWS,),
            in_specs=[
                pl.BlockSpec((ROWS, D), at),
                pl.BlockSpec((1, 1, ROWS), lambda b, n, r: at(b, n, r) + (0,)),
                pl.BlockSpec((8, D), lambda b, n, r: (0, 0)),
                pl.BlockSpec((1, D), lambda b, n, r: (0, 0)),
            ]
            + [pl.BlockSpec(memory_space=pl.ANY)] * len(pieces),
            out_specs=pl.BlockSpec((3, ROWS, D), lambda b, n, r: (0,) + at(b, n, r)),
            scratch_shapes=[pltpu.VMEM((D, 3 * D), bf16), pltpu.SemaphoreType.DMA((1,))],
        ),
        out_shape=jax.ShapeDtypeStruct((3, rows, D), bf16),
        compiler_params=params(),
        cost_estimate=pl.CostEstimate(
            flops=2 * rows * D * 3 * D, bytes_accessed=rows * D * 8 + D * D * 6, transcendentals=0
        ),
        name="project",
    )(length, piece_rows, tokens, pass_rows, table, gain, *pieces)


def attend_kernel(len_ref, p_ref, out_ref, lse_ref):
    blocks = p_ref.shape[1] // ROWS
    lane = lax.broadcasted_iota(jnp.int32, (ROWS, 128), 1)
    first_head = lane < HEAD
    here = lax.broadcasted_iota(jnp.int32, (ROWS, ROWS), 0)
    there = lax.broadcasted_iota(jnp.int32, (ROWS, ROWS), 1)
    allowed = there <= here
    for i in range(blocks):
        rows = slice(i * ROWS, (i + 1) * ROWS)

        @pl.when(i * ROWS < len_ref[0])
        def work():
            query = p_ref[0, rows, :] * jnp.asarray(1.0 / math.sqrt(HEAD), bf16)
            found = []
            for head in range(2):
                mine = first_head if head == 0 else jnp.logical_not(first_head)
                q = jnp.where(mine, query, jnp.zeros_like(query))
                diag = dot_nt(q, p_ref[1, rows, :])
                diag = jnp.where(allowed, diag, -1e30)
                largest = jnp.max(diag, axis=-1, keepdims=True)
                if i > 0:
                    before = dot_nt(q, p_ref[1, : i * ROWS, :])
                    largest = jnp.maximum(largest, jnp.max(before, axis=-1, keepdims=True))
                diag = jnp.exp(diag - largest)
                total = jnp.sum(diag, axis=-1, keepdims=True)
                out = dot_nn(diag.astype(bf16), p_ref[2, rows, :])
                if i > 0:
                    before = jnp.exp(before - largest)
                    total = total + jnp.sum(before, axis=-1, keepdims=True)
                    out = out + dot_nn(before.astype(bf16), p_ref[2, : i * ROWS, :])
                found.append(out * (1.0 / total))
                lse = jnp.broadcast_to(largest + jnp.log(total), (ROWS, 128))
                lse_ref[0, head : head + 1, rows] = lse.T[0:1]
            out_ref[rows, :] = jnp.where(first_head, found[0], found[1]).astype(bf16)


def attend(length, projected):
    rows = projected.shape[1]
    pairs = HEADS // 2
    return pl.pallas_call(
        attend_kernel,
        grid_spec=pltpu.PrefetchScalarGridSpec(
            num_scalar_prefetch=1,
            grid=(pairs,),
            in_specs=[pl.BlockSpec((3, rows, 128), lambda h, n: (0, 0, h))],
            out_specs=[
                pl.BlockSpec((rows, 128), lambda h, n: (0, h)),
                pl.BlockSpec((1, 8, rows), lambda h, n: (h, 0, 0)),
            ],
        ),
        out_shape=[
            jax.ShapeDtypeStruct((rows, D), bf16),
            jax.ShapeDtypeStruct((pairs, 8, rows), f32),
        ],
        compiler_params=params(),
        cost_estimate=pl.CostEstimate(
            flops=2 * rows * rows * D, bytes_accessed=rows * D * 8, transcendentals=HEADS * rows * rows // 2
        ),
        name="attend",
    )(length, projected)


def attend_back_kernel(len_ref, p_ref, o_ref, g_ref, lse_ref, out_ref, dk_ref, dv_ref, kz_ref, vz_ref, kt_ref):
    blocks = p_ref.shape[1] // ROWS
    scaling = 1.0 / math.sqrt(HEAD)
    lane = lax.broadcasted_iota(jnp.int32, (ROWS, 128), 1)
    first_head = lane < HEAD
    row8 = lax.broadcasted_iota(jnp.int32, (8, 128), 0)
    lane8 = lax.broadcasted_iota(jnp.int32, (8, 128), 1)
    chooser = (lax.div(lane8, HEAD) == row8).astype(f32)
    key_at = lax.broadcasted_iota(jnp.int32, (2, ROWS, ROWS), 1)
    row_at = lax.broadcasted_iota(jnp.int32, (2, ROWS, ROWS), 2)
    allowed = (key_at <= row_at).reshape(2 * ROWS, ROWS)
    for i in range(blocks):
        rows = slice(i * ROWS, (i + 1) * ROWS)
        two = slice(2 * i * ROWS, 2 * (i + 1) * ROWS)

        @pl.when(i * ROWS < len_ref[0])
        def work():
            dk_ref[two, :] = jnp.zeros((2 * ROWS, 128), f32)
            dv_ref[two, :] = jnp.zeros((2 * ROWS, 128), f32)
            key, value = p_ref[1, rows, :], p_ref[2, rows, :]
            zero = jnp.zeros_like(key)
            k2 = jnp.concatenate([jnp.where(first_head, key, zero), jnp.where(first_head, zero, key)], axis=0)
            kz_ref[two, :] = k2
            kt_ref[:, two] = k2.T
            vz_ref[two, :] = jnp.concatenate([jnp.where(first_head, value, zero), jnp.where(first_head, zero, value)], axis=0)
            query = p_ref[0, rows, :] * jnp.asarray(scaling, bf16)
            grad = g_ref[rows, :]
            product = grad.astype(f32) * o_ref[rows, :].astype(f32)
            delta = lax.dot_general(chooser, product, (((1,), (1,)), ((), ())), precision=lax.Precision.HIGHEST, preferred_element_type=f32)
            def both(a, b):
                return jnp.concatenate([jnp.broadcast_to(a, (ROWS, ROWS)), jnp.broadcast_to(b, (ROWS, ROWS))], axis=0)
            lse2 = both(lse_ref[0, 0:1, rows], lse_ref[0, 1:2, rows])
            delta2 = both(delta[0:1], delta[1:2])
            dqt = jnp.zeros((128, ROWS), f32)
            for j in range(i + 1):
                cols = slice(2 * j * ROWS, 2 * (j + 1) * ROWS)
                prob = jnp.exp(dot_nt(kz_ref[cols, :], query) - lse2)
                if i == j:
                    prob = jnp.where(allowed, prob, 0.0)
                ds = (prob * (dot_nt(vz_ref[cols, :], grad) - delta2)).astype(bf16)
                dv_ref[cols, :] += dot_nn(prob.astype(bf16), grad)
                dk_ref[cols, :] += dot_nn(ds, query)
                dqt = dqt + dot_nn(kt_ref[:, cols], ds)
            out_ref[0, rows, :] = (dqt * scaling).T.astype(bf16)
    for i in range(blocks):
        rows = slice(i * ROWS, (i + 1) * ROWS)
        a = slice(2 * i * ROWS, (2 * i + 1) * ROWS); b = slice((2 * i + 1) * ROWS, 2 * (i + 1) * ROWS)

        @pl.when(i * ROWS < len_ref[0])
        def finish():
            out_ref[1, rows, :] = jnp.where(first_head, dk_ref[a, :], dk_ref[b, :]).astype(bf16)
            out_ref[2, rows, :] = jnp.where(first_head, dv_ref[a, :], dv_ref[b, :]).astype(bf16)


def blank_kernel(ready_ref, out_ref):
    pass


def blank(ready, shape):
    return pl.pallas_call(
        blank_kernel,
        in_specs=[pl.BlockSpec(memory_space=pltpu.SMEM)],
        out_specs=pl.BlockSpec(memory_space=pl.ANY),
        out_shape=shape,
        name="blank",
    )(ready)


def attend_back(choice, share, projected, heads_out, grad_heads, lse, before):
    rows = projected.shape[1]
    cols = lambda h, n: (0, n[2] + h)
    blocks = lambda h, n: (0, 0, n[2] + h)

    def kernel(n, p, o, g, l, unused, *rest):
        attend_back_kernel(n, p, o, g, l, *rest)

    return pl.pallas_call(
        kernel,
        grid_spec=pltpu.PrefetchScalarGridSpec(
            num_scalar_prefetch=1,
            grid=(share,),
            in_specs=[
                pl.BlockSpec((3, rows, 128), blocks),
                pl.BlockSpec((rows, 128), cols),
                pl.BlockSpec((None, rows, 128), lambda h, n: (n[1], 0, n[2] + h)),
                pl.BlockSpec((1, 8, rows), lambda h, n: (n[2] + h, 0, 0)),
                pl.BlockSpec(memory_space=pl.ANY),
            ],
            out_specs=pl.BlockSpec((3, rows, 128), blocks),
            scratch_shapes=[
                pltpu.VMEM((2 * rows, 128), f32),
                pltpu.VMEM((2 * rows, 128), f32),
                pltpu.VMEM((2 * rows, 128), bf16),
                pltpu.VMEM((2 * rows, 128), bf16),
                pltpu.VMEM((128, 2 * rows), bf16),
            ],
        ),
        out_shape=jax.ShapeDtypeStruct((3, rows, D), bf16),
        input_output_aliases={5: 0},
        compiler_params=params(),
        cost_estimate=pl.CostEstimate(
            flops=share * rows * rows * D, bytes_accessed=share * rows * D * 3, transcendentals=share * rows * rows
        ),
        name="attend_back",
    )(choice, projected, heads_out, grad_heads, lse, before)


def feed_kernel(plan, len_ref, row_ref, *refs):
    tok0, tok1, pass0, pass1, ho0, ho1, cot, table_ref, gain_ref = refs[:9]
    many = 2 * plan.sharers if plan.paired else 1
    grad_ref, pieces, refs = refs[9], refs[10 : 10 + many], refs[10 + many :]
    res, gh, hid, small_ref = refs[:4]
    outs, (w_ref, acc_ref, sums_ref, stage_ref, sem_ref) = refs[4:-5], refs[-5:]
    b = pl.program_id(0)
    many0 = last_block(len_ref[0]) + 1
    many1 = last_block(len_ref[1]) + 1
    early = b < many0

    @pl.when(b == 0)
    def clear():
        load_weight(plan, row_ref, pieces, w_ref, sem_ref, acc_ref, sums_ref)

    @pl.when(b < many0 + many1)
    def block():
        hot = onehot_rows(jnp.where(early, pass0[0], pass1[0]))
        entry = jnp.where(early, tok0[...], tok1[...]).astype(f32) + dot_tn(hot, table_ref[...])
        at = jnp.where(early, b, b - many0) * ROWS + lax.broadcasted_iota(jnp.int32, (ROWS, 1), 0)
        live = at < jnp.where(early, len_ref[0], len_ref[1])
        heads = jnp.where(early, ho0[...], ho1[...])
        attention = dot_nn(heads, w_ref[:, 0:D])
        hidden = entry + attention
        unit, scale = normalized(hidden)
        gain = gain_ref[...]
        normed = (unit * gain).astype(bf16)
        grad_feed = jnp.where(live, cot[...].reshape(ROWS, D).astype(f32), 0.0).astype(bf16)
        @pl.when(b == 0)
        def rest_of_weight():
            for copy in weight_copies(plan, row_ref, pieces, w_ref, sem_ref, 1):
                copy.wait()

        feed = jnp.zeros((ROWS, D), f32)
        grad_normed = jnp.zeros((ROWS, D), f32)
        for k in range(CHUNKS):
            up = slice(D + k * D, D + (k + 1) * D)
            down = slice(D + FF + k * D, D + FF + (k + 1) * D)
            x = dot_nn(normed, w_ref[:, up])
            grad_act = dot_nt(grad_feed, w_ref[:, down])
            c0 = math.sqrt(2.0 / math.pi)
            square = x * x
            bent = jnp.tanh(x * (c0 + (c0 * 0.044715) * square))
            half = 0.5 + 0.5 * bent
            slope = half + (0.5 * x) * (1.0 - bent * bent) * (c0 + (3.0 * c0 * 0.044715) * square)
            act = (x * half).astype(bf16)
            grad_x = (slope * grad_act).astype(bf16)
            feed = feed + dot_nn(act, w_ref[:, down])
            grad_normed = grad_normed + dot_nt(grad_x, w_ref[:, up])
            acc_ref[:, up] += dot_tn(normed, grad_x)
            acc_ref[:, down] += dot_tn(act, grad_feed)
        res[...] = jnp.where(live, hidden + feed, 0.0).astype(bf16).reshape(res.shape)
        sums_ref[0:8] += fold_rows(grad_normed * unit)
        sums_ref[8:16] += fold_rows(jnp.where(live, entry * entry, 0.0))
        sums_ref[16:24] += fold_rows(jnp.where(live, attention * attention, 0.0))
        sums_ref[24:32] += fold_rows(jnp.where(live, feed * feed, 0.0))
        grad_hidden = grad_feed.astype(f32) + norm_back(grad_normed * gain, unit, scale)
        hid[...] = grad_hidden
        grad_attention = grad_hidden.astype(bf16)
        acc_ref[:, 0:D] += dot_tn(heads, grad_attention)
        gh[...] = dot_nt(grad_attention, w_ref[:, 0:D]).astype(bf16)

    @pl.when(b == pl.num_programs(0) - 1)
    def finish():
        counted = (len_ref[0] + len_ref[1]).astype(f32)
        small_ref[...] = jnp.full(small_ref.shape, counted, f32)
        for n in range(4):
            small_ref[n : n + 1] = jnp.sum(sums_ref[8 * n : 8 * n + 8], axis=0, keepdims=True)
        store_grads(plan, plan.wide_orders, grad_ref, acc_ref, outs, stage_ref, sem_ref)


def feed(plan, part, lengths, piece_rows, grad_rows, tokens, pass_rows, heads_out, cotangent, table, gain, pieces, width):
    rows = tokens[0].shape[0]
    per = ROWS // part

    def at0(b, n, r):
        return jnp.minimum(b, last_block(n[0])), 0

    def at1(b, n, r):
        return jnp.clip(b - last_block(n[0]) - 1, 0, last_block(n[1])), 0

    def both(b, n, r):
        early = b <= last_block(n[0])
        return jnp.where(early, b, at1(b, n, r)[0]), jnp.where(early, 0, 1)

    row0 = pl.BlockSpec((ROWS, D), at0)
    row1 = pl.BlockSpec((ROWS, D), at1)
    pas0 = pl.BlockSpec((1, 1, ROWS), lambda *a: at0(*a) + (0,))
    pas1 = pl.BlockSpec((1, 1, ROWS), lambda *a: at1(*a) + (0,))
    dealt = pl.BlockSpec((per, 1, part, D), lambda *a: both(*a) + (0, 0))
    local = pl.BlockSpec((None, ROWS, D), lambda *a: both(*a)[::-1] + (0,))
    grads = grad_shapes(plan, width, plan.wide_orders)
    anywhere = pl.BlockSpec(memory_space=pl.ANY)
    return pl.pallas_call(
        functools.partial(feed_kernel, plan),
        grid_spec=pltpu.PrefetchScalarGridSpec(
            num_scalar_prefetch=2,
            grid=(2 * rows // ROWS,),
            in_specs=[
                row0, row1, pas0, pas1, row0, row1, dealt,
                pl.BlockSpec((8, D), lambda *a: (0, 0)),
                pl.BlockSpec((1, D), lambda *a: (0, 0)),
                pl.BlockSpec(memory_space=pltpu.SMEM),
            ]
            + [anywhere] * len(pieces),
            out_specs=[dealt, local, local, pl.BlockSpec((8, D), lambda *a: (0, 0))] + [anywhere] * len(grads),
            scratch_shapes=[
                pltpu.VMEM((D, width), bf16),
                pltpu.VMEM((D, width), f32),
                pltpu.VMEM((32, D), f32),
                pltpu.VMEM(stage_shape(plan), bf16),
                pltpu.SemaphoreType.DMA((2,)),
            ],
        ),
        out_shape=[
            jax.ShapeDtypeStruct(cotangent.shape, bf16),
            jax.ShapeDtypeStruct((2, rows, D), bf16),
            jax.ShapeDtypeStruct((2, rows, D), f32),
            jax.ShapeDtypeStruct((8, D), f32),
        ]
        + grads,
        compiler_params=params(),
        cost_estimate=pl.CostEstimate(
            flops=2 * 6 * rows * D * width, bytes_accessed=2 * rows * D * 14 + D * width * 4, transcendentals=2 * rows * FF
        ),
        name="feed",
    )(lengths, piece_rows, tokens[0], tokens[1], pass_rows[0], pass_rows[1], heads_out[0], heads_out[1],
      cotangent, table, gain, grad_rows, *pieces)


def project_back_kernel(plan, weight, rows_back, final, len_ref, row_ref, grad_ref, tok_ref, pass_ref, g_ref, *rest):
    rest = list(rest)
    hid_ref = rest.pop(0) if rows_back else None
    table_ref, gain_ref = rest.pop(0), rest.pop(0)
    before_ref = rest.pop(0) if final else None
    many = plan.sharers if plan.paired else 1
    pieces = [rest.pop(0) for n in range(many)] if rows_back else []
    if rows_back:
        out_ref, small_ref = rest.pop(0), rest.pop(0)
    if weight and not final:
        acc_ref = rest.pop(0)
    outs = [rest.pop(0) for shape in grad_shapes(plan, 3 * D, plan.head_orders)] if final else []
    if rows_back:
        w_ref, sums_ref = rest.pop(0), rest.pop(0)
    if final:
        acc_ref, stage_ref = rest.pop(0), rest.pop(0)
    sem_ref = rest.pop(0)
    b = pl.program_id(0)

    @pl.when(b == 0)
    def clear():
        if rows_back:
            load_weight(plan, row_ref, pieces, w_ref, sem_ref, sums_ref, *([acc_ref] if weight and not final else []))
        if final:
            copy = pltpu.make_async_copy(before_ref, acc_ref, sem_ref.at[0])
            copy.start()
            copy.wait()

    @pl.when(b <= last_block(len_ref[0]))
    def work():
        hot = onehot_rows(pass_ref[0])
        entry = tok_ref[...].astype(f32) + dot_tn(hot, table_ref[...])
        unit, scale = normalized(entry)
        gain = gain_ref[...]
        if weight:
            normed = (unit * gain).astype(bf16)
            for part in range(3):
                acc_ref[:, part * D : (part + 1) * D] += dot_tn(normed, g_ref[part])
        if rows_back:
            grad_normed = jnp.zeros((ROWS, D), f32)
            for part in range(3):
                grad_normed = grad_normed + dot_nt(g_ref[part], w_ref[:, part * D : (part + 1) * D])
            sums_ref[0:8] += fold_rows(grad_normed * unit)
            grad_entry = hid_ref[...] + norm_back(grad_normed * gain, unit, scale)
            high = grad_entry.astype(bf16)
            out_ref[...] = high
            rest_one = grad_entry - high.astype(f32)
            low = rest_one.astype(bf16)
            lower = (rest_one - low.astype(f32)).astype(bf16)
            sums_ref[8:16] += dot_nn(hot, high) + dot_nn(hot, low) + dot_nn(hot, lower)

    if rows_back:
        @pl.when(b == pl.num_programs(0) - 1)
        def sums():
            small_ref[...] = sums_ref[8:16]
            small_ref[PASSES : PASSES + 1] = jnp.sum(sums_ref[0:8], axis=0, keepdims=True)

    if final:
        @pl.when(b == pl.num_programs(0) - 1)
        def finish():
            store_grads(plan, plan.head_orders, grad_ref, acc_ref, outs, stage_ref, sem_ref)


def project_back(
    plan, weight, rows_back, which, length, piece_rows, grad_rows, tokens, pass_rows, grads, grad_hidden, table, gain,
    pieces, before=None,
):
    rows = tokens.shape[0]
    final = before is not None
    at = lambda b, n, r, g: (jnp.minimum(b, last_block(n[0])), 0)
    row = pl.BlockSpec((ROWS, D), at)
    anywhere = pl.BlockSpec(memory_space=pl.ANY)
    in_specs = [
        row,
        pl.BlockSpec((1, 1, ROWS), lambda *a: at(*a) + (0,)),
        pl.BlockSpec((3, ROWS, D), lambda *a: (0,) + at(*a)),
    ]
    operands = [length, piece_rows, grad_rows, tokens, pass_rows, grads]
    if rows_back:
        in_specs.append(pl.BlockSpec((None, ROWS, D), lambda *a: (which,) + at(*a)))
        operands.append(grad_hidden)
    in_specs += [pl.BlockSpec((8, D), lambda *a: (0, 0)), pl.BlockSpec((1, D), lambda *a: (0, 0))]
    operands += [table, gain]
    out_shape, out_specs, scratch = [], [], []
    if final:
        in_specs.append(anywhere)
        operands.append(before)
    if rows_back:
        in_specs += [anywhere] * len(pieces)
        operands += pieces
        out_shape += [jax.ShapeDtypeStruct((rows, D), bf16), jax.ShapeDtypeStruct((8, D), f32)]
        out_specs += [row, pl.BlockSpec((8, D), lambda *a: (0, 0))]
        scratch += [pltpu.VMEM((D, 3 * D), bf16), pltpu.VMEM((16, D), f32)]
    if weight and not final:
        out_shape.append(jax.ShapeDtypeStruct((D, 3 * D), f32))
        out_specs.append(pl.BlockSpec((D, 3 * D), lambda *a: (0, 0)))
    if final:
        shapes = grad_shapes(plan, 3 * D, plan.head_orders)
        out_shape += shapes
        out_specs += [anywhere] * len(shapes)
        scratch += [pltpu.VMEM((D, 3 * D), f32), pltpu.VMEM(stage_shape(plan), bf16)]
    return pl.pallas_call(
        functools.partial(project_back_kernel, plan, weight, rows_back, final),
        grid_spec=pltpu.PrefetchScalarGridSpec(
            num_scalar_prefetch=3,
            grid=(rows // ROWS,),
            in_specs=in_specs,
            out_specs=out_specs,
            scratch_shapes=scratch + [pltpu.SemaphoreType.DMA((2,))],
        ),
        out_shape=out_shape,
        compiler_params=params(),
        cost_estimate=pl.CostEstimate(
            flops=2 * (weight + rows_back) * rows * D * 3 * D, bytes_accessed=rows * D * 14 + D * D * 6, transcendentals=0
        ),
        name="project_back",
    )(*operands)


def pick_kernel(index_ref, in_ref, out_ref, sem_ref):
    copies = [
        pltpu.make_async_copy(in_ref.at[index_ref[n]], out_ref.at[n], sem_ref) for n in range(out_ref.shape[0])
    ]
    for copy in copies:
        copy.start()
    for copy in copies:
        copy.wait()


def pick(index, blocks):
    shape = index.shape + blocks.shape[1:]
    return pl.pallas_call(
        pick_kernel,
        grid_spec=pltpu.PrefetchScalarGridSpec(
            num_scalar_prefetch=1,
            grid=(1,),
            in_specs=[pl.BlockSpec(memory_space=pl.ANY)],
            out_specs=pl.BlockSpec(shape, lambda b, n: (0, 0, 0)),
            scratch_shapes=[pltpu.SemaphoreType.DMA],
        ),
        out_shape=jax.ShapeDtypeStruct(shape, blocks.dtype),
        compiler_params=params(),
        cost_estimate=pl.CostEstimate(flops=0, bytes_accessed=4 * math.prod(shape), transcendentals=0),
        name="pick",
    )(index, blocks)


def settle_kernel(index_ref, *refs):
    arrays, out_ref = refs[:-1], refs[-1]
    first = pl.program_id(0) * out_ref.shape[0]
    rows = out_ref.shape[1]
    at = lax.broadcasted_iota(jnp.int32, (rows, 1), 0)
    for n in range(out_ref.shape[0]):
        live = at < index_ref[2, first + n]
        source, late = index_ref[1, first + n], index_ref[0, first + n]
        if len(arrays) == 1:
            found = arrays[0][2 * source + late]
        else:
            found = jnp.where(late == 0, arrays[0][source], arrays[1][source])
        out_ref[n] = jnp.where(live, found.astype(f32), 0.0)


def settle(index, *arrays):
    many = index.shape[1]
    step = 4
    shape = arrays[0].shape
    whole = pl.BlockSpec(shape, lambda b, n: (0, 0, 0), pipeline_mode=pl.Buffered(1))
    return pl.pallas_call(
        settle_kernel,
        grid_spec=pltpu.PrefetchScalarGridSpec(
            num_scalar_prefetch=1,
            grid=(many // step,),
            in_specs=[whole] * len(arrays),
            out_specs=pl.BlockSpec((step,) + shape[1:], lambda b, n: (b, 0, 0)),
        ),
        out_shape=jax.ShapeDtypeStruct((many,) + shape[1:], f32),
        compiler_params=params(),
        cost_estimate=pl.CostEstimate(flops=0, bytes_accessed=6 * many * math.prod(shape[1:]), transcendentals=0),
        name="settle",
    )(index, *arrays)


def after(values, *others):
    return lax.optimization_barrier((values, others))[0]


def swap(blocks):
    return lax.all_to_all(blocks, "dp", split_axis=0, concat_axis=0, tiled=True)


def per_device(
    groups,
    width_all,
    tokens,
    passes,
    lengths,
    dealing,
    pass_table,
    gain_first,
    to_heads,
    from_heads,
    gain_second,
    expand,
    shrink,
    cotangent,
):
    axes = ("dp", "fsdp")
    slots, part, unused_width = tokens.shape
    seq_len = part * groups
    order = jnp.arange(slots, dtype=jnp.int32)
    here = lax.axis_index("dp")
    ordering = dealing[0, 0]
    sizes = lengths[0]

    ahead = (sizes[None, :] > sizes[:, None]) | (
        (sizes[None, :] == sizes[:, None]) & (order[None, :] < order[:, None])
    )
    rank = jnp.sum(ahead.astype(jnp.int32), axis=1)
    ranked = jnp.sum(jnp.where(rank[None, :] == order[:, None], order[None, :], 0), axis=1)
    place = jnp.sum(jnp.where(ordering[None, :] == order[:, None], order[None, :], 0), axis=1)
    early_seqs = ranked[:groups]
    late_seqs = ranked[groups:][::-1]
    from_early = jnp.sum(jnp.where(early_seqs[:, None] == order[None, :], place[None, :], 0), axis=1)
    from_late = jnp.sum(jnp.where(late_seqs[:, None] == order[None, :], place[None, :], 0), axis=1)
    slot_rank = jnp.sum(jnp.where(ordering[:, None] == order[None, :], rank[None, :], 0), axis=1)
    slot_size = jnp.sum(jnp.where(ordering[:, None] == order[None, :], sizes[None, :], 0), axis=1)
    is_late = (slot_rank >= groups).astype(jnp.int32)
    source = jnp.where(is_late == 1, slots - 1 - slot_rank, slot_rank)
    back_index = jnp.stack([is_late, source, slot_size - here * part])
    my_seqs = jnp.stack([early_seqs[here], late_seqs[here]])
    my_sizes = jnp.sum(jnp.where(my_seqs[:, None] == order[None, :], sizes[None, :], 0), axis=1)

    row_count = to_heads.shape[0]
    narrow = jnp.concatenate(
        [
            from_heads,
            expand.reshape(row_count, D, CHUNKS).transpose(0, 2, 1).reshape(row_count, FF),
            shrink.reshape(row_count, CHUNKS * D),
        ],
        axis=1,
    )
    plan = Plan(groups, width_all // groups, row_count)
    index_here = here * (width_all // groups) + lax.axis_index("fsdp")
    my_passes = [passes[my_seqs[m]].reshape(seq_len // ROWS, 1, ROWS) for m in range(2)]
    one_size = [my_sizes[m : m + 1] for m in range(2)]
    table = jnp.zeros((8, D), bf16).at[:PASSES].set(pass_table)
    gain_one = gain_first.astype(f32).reshape(1, D)
    gain_two = gain_second.astype(f32).reshape(1, D)

    pairs_index = jnp.stack([from_early, from_late], axis=1).reshape(slots)
    picked = [pick(from_early, tokens), pick(from_late, tokens), pick(pairs_index, cotangent)]
    if plan.paired:
        piece_rows = plan.piece_rows(index_here)
        wide_rows = plan.grad_rows(index_here, plan.wide_orders)
        head_rows = plan.grad_rows(index_here, plan.head_orders)
        head_far = plan.gather(to_heads[None], plan.far)
        head_near = plan.gather(head_far, [plan.near])
        wide_one = plan.gather(after(narrow, head_far)[None], plan.far[:1])
        ready = (my_passes, one_size, piece_rows, table, gain_one)
        tokens0 = swap(after(picked[0], head_near, wide_one, ready))
        head_pieces = plan.gather_core(plan.gather_x(head_near))
    else:
        piece_rows = wide_rows = head_rows = jnp.zeros((1,), jnp.int32)
        head_pieces = (lax.all_gather(to_heads, axes, axis=0, tiled=True),)
        wide_pieces = (lax.all_gather(narrow, axes, axis=0, tiled=True),)
        tokens0 = swap(picked[0])
        wide_far = wide_pieces

    def forward(m, *gate):
        return project(
            plan, after(one_size[m], gate), piece_rows, my_tokens[m], my_passes[m], table, gain_one, head_pieces
        )

    def mix(m, *gate):
        return attend(after(one_size[m], gate), projected[m])

    half = HEADS // 4
    choices = {
        (m, first): jnp.stack([my_sizes[m], jnp.int32(m), jnp.int32(first)]) for m in range(2) for first in (0, half)
    }

    def mix_back(m, first, before, *gate):
        return attend_back(after(choices[m, first], gate), half, projected[m], heads_out[m], grad_heads, lse[m], before)

    def back(m, weight, rows_back, *gate, before=None):
        return project_back(
            plan, weight, rows_back, m, after(one_size[m], gate), piece_rows, head_rows, my_tokens[m], my_passes[m],
            grad_parts[m], grad_hidden, table, gain_one, head_pieces, before,
        )

    def send_back(rows, *gate):
        return swap(after(rows, gate).reshape(groups, part, D))

    projected, heads_out, lse, grad_parts = [None, None], [None, None], [None, None], [None, None]
    my_tokens = [tokens0.reshape(seq_len, D)]
    projected[0] = forward(0)
    if plan.paired:
        wide_far = plan.gather(wide_one, plan.far[1:], head_pieces, projected[0])
        cut = D + FF
    tokens1 = swap(after(picked[1], tokens0, picked[2], wide_far))
    my_tokens.append(tokens1.reshape(seq_len, D))
    heads_out[0], lse[0] = mix(0, wide_far)
    if plan.paired:
        first = plan.gather_near({0: wide_far[:, :, :cut]}, (), lse[0])
        second = plan.gather_x(wide_far[:, :, cut:], ())
        ready = (first, second)
    else:
        ready = ()
    my_grads = swap(after(picked[2].reshape(groups, 2, part, D), tokens1, lse[0], ready))
    projected[1] = forward(1, lse[0])
    if plan.paired:
        first = plan.gather_x(first[0])
        second = plan.gather_near(second, lse[0], projected[1])
    heads_out[1], lse[1] = mix(1)
    if plan.paired:
        wide_pieces = plan.gather_core(first, lse[1]) + plan.gather_core(second, lse[1])

    space = jax.ShapeDtypeStruct((3, seq_len, D), bf16)
    blanks = [blank(one_size[m], space) for m in range(2)]
    res, grad_heads, grad_hidden, feed_small, *wide_grads = feed(
        plan, part, after(my_sizes, choices, blanks), piece_rows, wide_rows, my_tokens, my_passes, heads_out, my_grads, table, gain_two,
        wide_pieces, D + 2 * FF,
    )

    def begin(grads):
        if not plan.paired:
            return lax.psum_scatter(grads[0], axes, scatter_dimension=0, tiled=True).astype(f32)
        return [grads[n : n + 2] for n in range(0, len(grads), 2)]

    def advance(state, stage, gate, late):
        return plan.reduce_stage(state, plan.wide_orders, stage, (gate,), (late,)) if plan.paired else state

    wide0 = begin(wide_grads)
    result = swap(res)
    some = mix_back(0, 0, blanks[0])
    wide1 = advance(wide0, 0, (), some)
    grad_parts[0] = mix_back(0, half, some, wide1)
    entry0, small0, head_sum = back(0, True, True)
    wide2 = advance(wide1, 1, some, entry0)
    moved0 = send_back(entry0, result)
    some = mix_back(1, 0, blanks[1], entry0, wide2, result)
    wide3 = advance(wide2, 2, entry0, some)
    grad_parts[1] = mix_back(1, half, some, wide3)
    entry1, small1 = back(1, False, True)
    wide_owned = advance(wide3, 3, some, entry1)
    moved1 = send_back(entry1, moved0, wide_owned)
    totals = jnp.concatenate([small0 + small1, feed_small], axis=0)
    stages = plan.head_orders[0]
    head_grads = back(1, True, False, entry1, moved0, before=head_sum)
    head_state = begin(head_grads)
    if plan.paired:
        totals = plan.total_stage(totals, stages[0], (), head_grads[:1])
        head_state = plan.reduce_stage(head_state, plan.head_orders, 0, (wide_owned,))
        wide_owned = wide_owned[0]
    output = settle(after(back_index, head_state), result.reshape(slots, part, D))
    grad_tokens = settle(after(back_index, output), moved0, moved1)
    grad_from = wide_owned[:, :D]
    grad_expand = wide_owned[:, D : D + FF].reshape(row_count, CHUNKS, D).transpose(0, 2, 1).reshape(row_count, FF)
    grad_shrink = wide_owned[:, D + FF :].reshape(row_count * CHUNKS, D)
    if plan.paired:
        totals = plan.total_stage(totals, stages[1])
        late = (output, grad_tokens, grad_from, grad_expand, grad_shrink)
        head_state = plan.reduce_stage(head_state, plan.head_orders, 1, (totals,), late)
        totals = plan.total_stage(totals, stages[2], (head_state,))
        head_owned = plan.reduce_stage(head_state, plan.head_orders, 2)[0]
    else:
        totals = lax.psum(totals, axes)
        head_owned = head_state
    root_squares = jnp.sqrt(jnp.sum(totals[9:12], axis=1) / (totals[12, 0] * D))

    return (
        output,
        grad_tokens,
        totals[:PASSES],
        totals[PASSES],
        head_owned,
        grad_from,
        totals[8],
        grad_expand,
        grad_shrink,
        root_squares,
    )


def solution(mesh):
    groups = mesh.shape["dp"]
    weight_spec = P(("dp", "fsdp"), None)
    block_spec = P("fsdp", "dp", None)
    in_specs = (
        block_spec,
        P("fsdp", None),
        P("fsdp", None),
        P("dp", "fsdp", None),
        P(),
        P(),
        weight_spec,
        weight_spec,
        P(),
        weight_spec,
        weight_spec,
        block_spec,
    )
    out_specs = (
        block_spec,
        block_spec,
        P(),
        P(),
        weight_spec,
        weight_spec,
        P(),
        weight_spec,
        weight_spec,
        P(),
    )
    body = functools.partial(per_device, groups, groups * mesh.shape["fsdp"])
    return jax.shard_map(body, mesh=mesh, in_specs=in_specs, out_specs=out_specs, check_vma=False)
```

```python
import math
import functools

import jax
import jax.numpy as jnp
from jax import lax
from jax.experimental import pallas as pl
from jax.experimental.pallas import tpu as pltpu
from jax.sharding import PartitionSpec as P

D = 768
HEADS = 12
HEAD = 64
FF = 3072
PASSES = 5
EPS = 1e-05
ROWS = 256
CHUNKS = FF // D
VMEM_MOST = 64000 * 1024

f32 = jnp.float32
bf16 = jnp.bfloat16


def dot_nn(a, b):
    return lax.dot_general(a, b, (((1,), (0,)), ((), ())), preferred_element_type=f32)


def dot_nt(a, b):
    return lax.dot_general(a, b, (((1,), (1,)), ((), ())), preferred_element_type=f32)


def dot_tn(a, b):
    return lax.dot_general(a, b, (((0,), (0,)), ((), ())), preferred_element_type=f32)


def params(**more):
    return pltpu.CompilerParams(vmem_limit_bytes=VMEM_MOST, **more)


def normalized(values):
    centred = values - jnp.mean(values, axis=-1, keepdims=True)
    spread = jnp.mean(centred * centred, axis=-1, keepdims=True)
    scale = lax.rsqrt(spread + EPS)
    return centred * scale, scale


def norm_back(grad_unit, unit, scale):
    first = jnp.mean(grad_unit, axis=-1, keepdims=True)
    second = jnp.mean(grad_unit * unit, axis=-1, keepdims=True)
    return scale * (grad_unit - first - unit * second)


def onehot_rows(pass_row):
    ids = lax.broadcasted_iota(jnp.int32, (8, pass_row.shape[-1]), 0)
    return (ids == pass_row).astype(f32).astype(bf16)


def fold_rows(values):
    rows, width = values.shape
    return jnp.sum(values.reshape(rows // 8, 8, width), axis=0)


def last_block(length):
    return lax.div(length + (ROWS - 1), ROWS) - 1


def bits_of(count):
    return count.bit_length() - 1


class Plan:
    def __init__(self, groups, sharers, rows):
        self.groups, self.sharers, self.rows = groups, sharers, rows
        self.count = groups * sharers
        self.paired = rows % 8 == 0 and self.count & (self.count - 1) == 0 and sharers >= 4 and groups >= 4
        core, *over_x = [1 << bit for bit in range(bits_of(sharers))]
        near, *far = [sharers << bit for bit in range(bits_of(groups))]
        self.core, self.over_x, self.near, self.far = core, over_x, near, far[::-1]
        self.wide_orders = ([[core], over_x, [near], far], [[core], [near], over_x, far])
        self.head_orders = ([[core], over_x + [near], far],)

    def exchange(self, values, bits):
        pairs = [(i, i ^ bits) for i in range(self.count)]
        return lax.ppermute(values, ("dp", "fsdp"), pairs)

    def gather(self, held, masks, gate=(), late=()):
        for bits in masks:
            held = jnp.concatenate([after(held, late), self.exchange(after(held, gate), bits)], axis=0)
        return held

    def gather_x(self, held, *gate):
        pieces = {0: held}
        for bits in self.over_x[::-1]:
            for name in list(pieces):
                pieces[name | bits] = self.exchange(after(pieces[name], gate), bits)
        return pieces

    def gather_near(self, pieces, gate=(), late=()):
        return {name: self.gather(held, [self.near], gate, late) for name, held in pieces.items()}

    def gather_core(self, pieces, *gate):
        found = dict(pieces)
        for name in pieces:
            found[name | self.core] = self.exchange(after(pieces[name], gate), self.core)
        return tuple(found[name] for name in range(self.sharers))

    def piece_rows(self, here):
        masks = self.far + [self.near]
        found = []
        for f in range(self.sharers):
            for n in range(self.groups):
                rel = f | ways_bits(masks, n)
                found.append((here ^ rel) * self.rows)
        return jnp.stack(found).astype(jnp.int32)

    def grad_rows(self, here, orders):
        found = []
        for order in orders:
            for place in range(self.count):
                rel, left = 0, self.count
                for masks in order:
                    left >>= len(masks)
                    rel |= ways_bits(masks, (place // left) % (1 << len(masks)))
                found.append((here ^ rel) * self.rows)
        return jnp.stack(found).astype(jnp.int32)

    def total_stage(self, values, masks, gate=(), late=()):
        found = [after(values, late)]
        found += [self.exchange(after(values, gate), ways_bits(masks, way)) for way in range(1, 1 << len(masks))]
        while len(found) > 1:
            found = [found[k] + found[k + 1] for k in range(0, len(found), 2)]
        return found[0]

    def reduce_stage(self, states, orders, stage, gate=(), late=()):
        sums = []
        for ways, order in zip(states, orders):
            sums.append(
                [after(ways[0], late)]
                + [
                    self.exchange(after(ways[n], gate), ways_bits(order[stage], n))
                    for n in range(1, len(ways))
                ]
            )
        if stage == len(orders[0]) - 1:
            return [sum(part.astype(f32) for part in parts)[0] for parts in sums]
        ways = 1 << len(orders[0][stage + 1])
        if stage == len(orders[0]) - 2:
            return [merge(sums, ways)]
        return [merge([parts], ways) for parts in sums]


def ways_bits(masks, way):
    return sum(bits for n, bits in enumerate(masks) if (way >> n) & 1)


def merge_kernel(widths, many, ways, *refs):
    ins, outs = refs[: len(widths) * many * ways], refs[len(widths) * many * ways :]
    for way in range(ways):
        first = 0
        for k, width in enumerate(widths):
            views = [ins[(k * many + n) * ways + way] for n in range(many)]
            total = views[0][...].astype(f32)
            for view in views[1:]:
                total = total + view[...].astype(f32)
            outs[way][:, :, first : first + width] = total.astype(bf16)
            first += width


def merge(groups, ways):
    blocks, rows, unused = groups[0][0].shape
    widths = [parts[0].shape[2] for parts in groups]
    share = blocks // ways
    steps = min(share, 4)

    def view(way, width):
        return pl.BlockSpec((share // steps, rows, width), lambda b: (b + way * steps, 0, 0))

    out = jax.ShapeDtypeStruct((share, rows, sum(widths)), bf16)
    many = len(groups[0])
    size = blocks * rows * sum(widths)
    return pl.pallas_call(
        functools.partial(merge_kernel, widths, many, ways),
        grid=(steps,),
        in_specs=[view(way, width) for width in widths for n in range(many) for way in range(ways)],
        out_specs=[view(0, sum(widths))] * ways,
        out_shape=[out] * ways,
        compiler_params=params(),
        cost_estimate=pl.CostEstimate(flops=many * size, bytes_accessed=(2 + 2 * many) * size, transcendentals=0),
        name="merge",
    )(*[part for parts in groups for part in parts for way in range(ways)])


def weight_copies(plan, rows_ref, pieces, weight_ref, sem_ref, group):
    if not plan.paired:
        return [pltpu.make_async_copy(pieces[0], weight_ref, sem_ref.at[0])] if group == 0 else []
    mine = pieces[group * plan.sharers : (group + 1) * plan.sharers]
    if len(mine) == 0:
        return []
    first = pieces[0].shape[-1] * group
    copies = []
    for f, piece in enumerate(mine):
        for n in range(plan.groups):
            at = pl.multiple_of(rows_ref[f * plan.groups + n], 8)
            target = weight_ref.at[pl.ds(at, plan.rows), first : first + piece.shape[-1]]
            copies.append(pltpu.make_async_copy(piece.at[n], target, sem_ref.at[group]))
    return copies


def load_weight(plan, rows_ref, pieces, weight_ref, sem_ref, *cleared):
    first, second = [weight_copies(plan, rows_ref, pieces, weight_ref, sem_ref, group) for group in range(2)]
    for copy in first + second:
        copy.start()
    for ref in cleared:
        ref[...] = jnp.zeros_like(ref)
    for copy in first:
        copy.wait()


def grad_shapes(plan, width, orders):
    if not plan.paired:
        return [jax.ShapeDtypeStruct((D, width), bf16)]
    half = plan.count // 2
    cut = first_part(width, orders)
    return [jax.ShapeDtypeStruct((half, plan.rows, w), bf16) for w in (cut, cut, width - cut, width - cut) if w > 0]


def first_part(width, orders):
    return (width // D + 1) // 2 * D if len(orders) == 2 else width


def stage_shape(plan):
    return (2, plan.count, plan.rows, D) if plan.paired else (2, D, D)


def store_grads(plan, orders, rows_ref, acc_ref, outs, stage_ref, sem_ref):
    width, step = acc_ref.shape[1], D
    cut = first_part(width, orders)
    half = plan.count // 2
    waiting = []
    for n in range(width // step):
        slot = n % 2
        cols = slice(n * step, (n + 1) * step)
        if len(waiting) == 2:
            for copy in waiting.pop(0):
                copy.wait()
        if not plan.paired:
            stage_ref[slot] = acc_ref[:, cols].astype(bf16)
            copies = [pltpu.make_async_copy(stage_ref.at[slot], outs[0].at[:, cols], sem_ref.at[slot])]
        else:
            late = n * step >= cut
            base = plan.count if late else 0
            start = n * step - (cut if late else 0)

            def fill(place, carry):
                at = pl.multiple_of(rows_ref[base + place], 8)
                stage_ref[slot, place] = acc_ref[pl.ds(at, plan.rows), cols].astype(bf16)
                return carry

            lax.fori_loop(0, plan.count, fill, 0, unroll=8)
            keep, send = outs[2:4] if late else outs[0:2]
            there = slice(start, start + step)
            copies = [
                pltpu.make_async_copy(stage_ref.at[slot, 0:half], keep.at[:, :, there], sem_ref.at[slot]),
                pltpu.make_async_copy(stage_ref.at[slot, half:], send.at[:, :, there], sem_ref.at[slot]),
            ]
        for copy in copies:
            copy.start()
        waiting.append(copies)
    for copies in waiting:
        for copy in copies:
            copy.wait()


def project_kernel(plan, len_ref, row_ref, tok_ref, pass_ref, table_ref, gain_ref, *rest):
    pieces, (out_ref, w_ref, sem_ref) = rest[:-3], rest[-3:]

    @pl.when(pl.program_id(0) == 0)
    def load():
        load_weight(plan, row_ref, pieces, w_ref, sem_ref)

    @pl.when(pl.program_id(0) <= last_block(len_ref[0]))
    def work():
        hot = onehot_rows(pass_ref[0])
        entry = tok_ref[...].astype(f32) + dot_tn(hot, table_ref[...])
        unit, unused = normalized(entry)
        normed = (unit * gain_ref[...]).astype(bf16)
        for part in range(3):
            out_ref[part] = dot_nn(normed, w_ref[:, part * D : (part + 1) * D]).astype(bf16)


def project(plan, length, piece_rows, tokens, pass_rows, table, gain, pieces):
    rows = tokens.shape[0]
    at = lambda b, n, r: (jnp.minimum(b, last_block(n[0])), 0)
    return pl.pallas_call(
        functools.partial(project_kernel, plan),
        grid_spec=pltpu.PrefetchScalarGridSpec(
            num_scalar_prefetch=2,
            grid=(rows // ROWS,),
            in_specs=[
                pl.BlockSpec((ROWS, D), at),
                pl.BlockSpec((1, 1, ROWS), lambda b, n, r: at(b, n, r) + (0,)),
                pl.BlockSpec((8, D), lambda b, n, r: (0, 0)),
                pl.BlockSpec((1, D), lambda b, n, r: (0, 0)),
            ]
            + [pl.BlockSpec(memory_space=pl.ANY)] * len(pieces),
            out_specs=pl.BlockSpec((3, ROWS, D), lambda b, n, r: (0,) + at(b, n, r)),
            scratch_shapes=[pltpu.VMEM((D, 3 * D), bf16), pltpu.SemaphoreType.DMA((1,))],
        ),
        out_shape=jax.ShapeDtypeStruct((3, rows, D), bf16),
        compiler_params=params(),
        cost_estimate=pl.CostEstimate(
            flops=2 * rows * D * 3 * D, bytes_accessed=rows * D * 8 + D * D * 6, transcendentals=0
        ),
        name="project",
    )(length, piece_rows, tokens, pass_rows, table, gain, *pieces)


def attend_kernel(len_ref, p_ref, out_ref, lse_ref):
    blocks = p_ref.shape[1] // ROWS
    lane = lax.broadcasted_iota(jnp.int32, (ROWS, 128), 1)
    first_head = lane < HEAD
    here = lax.broadcasted_iota(jnp.int32, (ROWS, ROWS), 0)
    there = lax.broadcasted_iota(jnp.int32, (ROWS, ROWS), 1)
    allowed = there <= here
    for i in range(blocks):
        rows = slice(i * ROWS, (i + 1) * ROWS)

        @pl.when(i * ROWS < len_ref[0])
        def work():
            query = p_ref[0, rows, :] * jnp.asarray(1.0 / math.sqrt(HEAD), bf16)
            found = []
            for head in range(2):
                mine = first_head if head == 0 else jnp.logical_not(first_head)
                q = jnp.where(mine, query, jnp.zeros_like(query))
                diag = dot_nt(q, p_ref[1, rows, :])
                diag = jnp.where(allowed, diag, -1e30)
                largest = jnp.max(diag, axis=-1, keepdims=True)
                if i > 0:
                    before = dot_nt(q, p_ref[1, : i * ROWS, :])
                    largest = jnp.maximum(largest, jnp.max(before, axis=-1, keepdims=True))
                diag = jnp.exp(diag - largest)
                total = jnp.sum(diag, axis=-1, keepdims=True)
                out = dot_nn(diag.astype(bf16), p_ref[2, rows, :])
                if i > 0:
                    before = jnp.exp(before - largest)
                    total = total + jnp.sum(before, axis=-1, keepdims=True)
                    out = out + dot_nn(before.astype(bf16), p_ref[2, : i * ROWS, :])
                found.append(out * (1.0 / total))
                lse = jnp.broadcast_to(largest + jnp.log(total), (ROWS, 128))
                lse_ref[0, head : head + 1, rows] = lse.T[0:1]
            out_ref[rows, :] = jnp.where(first_head, found[0], found[1]).astype(bf16)


def attend(length, projected):
    rows = projected.shape[1]
    pairs = HEADS // 2
    return pl.pallas_call(
        attend_kernel,
        grid_spec=pltpu.PrefetchScalarGridSpec(
            num_scalar_prefetch=1,
            grid=(pairs,),
            in_specs=[pl.BlockSpec((3, rows, 128), lambda h, n: (0, 0, h))],
            out_specs=[
                pl.BlockSpec((rows, 128), lambda h, n: (0, h)),
                pl.BlockSpec((1, 8, rows), lambda h, n: (h, 0, 0)),
            ],
        ),
        out_shape=[
            jax.ShapeDtypeStruct((rows, D), bf16),
            jax.ShapeDtypeStruct((pairs, 8, rows), f32),
        ],
        compiler_params=params(),
        cost_estimate=pl.CostEstimate(
            flops=2 * rows * rows * D, bytes_accessed=rows * D * 8, transcendentals=HEADS * rows * rows // 2
        ),
        name="attend",
    )(length, projected)


def attend_back_kernel(len_ref, p_ref, o_ref, g_ref, lse_ref, out_ref, dk_ref, dv_ref, kz_ref, vz_ref, kt_ref):
    blocks = p_ref.shape[1] // ROWS
    scaling = 1.0 / math.sqrt(HEAD)
    lane = lax.broadcasted_iota(jnp.int32, (ROWS, 128), 1)
    first_head = lane < HEAD
    row8 = lax.broadcasted_iota(jnp.int32, (8, 128), 0)
    lane8 = lax.broadcasted_iota(jnp.int32, (8, 128), 1)
    chooser = (lax.div(lane8, HEAD) == row8).astype(f32)
    key_at = lax.broadcasted_iota(jnp.int32, (2, ROWS, ROWS), 1)
    row_at = lax.broadcasted_iota(jnp.int32, (2, ROWS, ROWS), 2)
    allowed = (key_at <= row_at).reshape(2 * ROWS, ROWS)
    for i in range(blocks):
        rows = slice(i * ROWS, (i + 1) * ROWS)
        two = slice(2 * i * ROWS, 2 * (i + 1) * ROWS)

        @pl.when(i * ROWS < len_ref[0])
        def work():
            dk_ref[two, :] = jnp.zeros((2 * ROWS, 128), f32)
            dv_ref[two, :] = jnp.zeros((2 * ROWS, 128), f32)
            key, value = p_ref[1, rows, :], p_ref[2, rows, :]
            zero = jnp.zeros_like(key)
            k2 = jnp.concatenate([jnp.where(first_head, key, zero), jnp.where(first_head, zero, key)], axis=0)
            kz_ref[two, :] = k2
            kt_ref[:, two] = k2.T
            vz_ref[two, :] = jnp.concatenate([jnp.where(first_head, value, zero), jnp.where(first_head, zero, value)], axis=0)
            query = p_ref[0, rows, :] * jnp.asarray(scaling, bf16)
            grad = g_ref[rows, :]
            product = grad.astype(f32) * o_ref[rows, :].astype(f32)
            delta = lax.dot_general(chooser, product, (((1,), (1,)), ((), ())), precision=lax.Precision.HIGHEST, preferred_element_type=f32)
            def both(a, b):
                return jnp.concatenate([jnp.broadcast_to(a, (ROWS, ROWS)), jnp.broadcast_to(b, (ROWS, ROWS))], axis=0)
            lse2 = both(lse_ref[0, 0:1, rows], lse_ref[0, 1:2, rows])
            delta2 = both(delta[0:1], delta[1:2])
            dqt = jnp.zeros((128, ROWS), f32)
            for j in range(i + 1):
                cols = slice(2 * j * ROWS, 2 * (j + 1) * ROWS)
                prob = jnp.exp(dot_nt(kz_ref[cols, :], query) - lse2)
                if i == j:
                    prob = jnp.where(allowed, prob, 0.0)
                ds = (prob * (dot_nt(vz_ref[cols, :], grad) - delta2)).astype(bf16)
                dv_ref[cols, :] += dot_nn(prob.astype(bf16), grad)
                dk_ref[cols, :] += dot_nn(ds, query)
                dqt = dqt + dot_nn(kt_ref[:, cols], ds)
            out_ref[0, rows, :] = (dqt * scaling).T.astype(bf16)
    for i in range(blocks):
        rows = slice(i * ROWS, (i + 1) * ROWS)
        a = slice(2 * i * ROWS, (2 * i + 1) * ROWS); b = slice((2 * i + 1) * ROWS, 2 * (i + 1) * ROWS)

        @pl.when(i * ROWS < len_ref[0])
        def finish():
            out_ref[1, rows, :] = jnp.where(first_head, dk_ref[a, :], dk_ref[b, :]).astype(bf16)
            out_ref[2, rows, :] = jnp.where(first_head, dv_ref[a, :], dv_ref[b, :]).astype(bf16)


def blank_kernel(ready_ref, out_ref):
    pass


def blank(ready, shape):
    return pl.pallas_call(
        blank_kernel,
        in_specs=[pl.BlockSpec(memory_space=pltpu.SMEM)],
        out_specs=pl.BlockSpec(memory_space=pl.ANY),
        out_shape=shape,
        name="blank",
    )(ready)


def attend_back(choice, share, projected, heads_out, grad_heads, lse, before):
    rows = projected.shape[1]
    cols = lambda h, n: (0, n[2] + h)
    blocks = lambda h, n: (0, 0, n[2] + h)

    def kernel(n, p, o, g, l, unused, *rest):
        attend_back_kernel(n, p, o, g, l, *rest)

    return pl.pallas_call(
        kernel,
        grid_spec=pltpu.PrefetchScalarGridSpec(
            num_scalar_prefetch=1,
            grid=(share,),
            in_specs=[
                pl.BlockSpec((3, rows, 128), blocks),
                pl.BlockSpec((rows, 128), cols),
                pl.BlockSpec((None, rows, 128), lambda h, n: (n[1], 0, n[2] + h)),
                pl.BlockSpec((1, 8, rows), lambda h, n: (n[2] + h, 0, 0)),
                pl.BlockSpec(memory_space=pl.ANY),
            ],
            out_specs=pl.BlockSpec((3, rows, 128), blocks),
            scratch_shapes=[
                pltpu.VMEM((2 * rows, 128), f32),
                pltpu.VMEM((2 * rows, 128), f32),
                pltpu.VMEM((2 * rows, 128), bf16),
                pltpu.VMEM((2 * rows, 128), bf16),
                pltpu.VMEM((128, 2 * rows), bf16),
            ],
        ),
        out_shape=jax.ShapeDtypeStruct((3, rows, D), bf16),
        input_output_aliases={5: 0},
        compiler_params=params(),
        cost_estimate=pl.CostEstimate(
            flops=share * rows * rows * D, bytes_accessed=share * rows * D * 3, transcendentals=share * rows * rows
        ),
        name="attend_back",
    )(choice, projected, heads_out, grad_heads, lse, before)


def feed_kernel(plan, len_ref, row_ref, *refs):
    tok0, tok1, pass0, pass1, ho0, ho1, cot, table_ref, gain_ref = refs[:9]
    many = 2 * plan.sharers if plan.paired else 1
    grad_ref, pieces, refs = refs[9], refs[10 : 10 + many], refs[10 + many :]
    res, gh, hid, small_ref = refs[:4]
    outs, (w_ref, acc_ref, sums_ref, stage_ref, sem_ref) = refs[4:-5], refs[-5:]
    b = pl.program_id(0)
    many0 = last_block(len_ref[0]) + 1
    many1 = last_block(len_ref[1]) + 1
    early = b < many0

    @pl.when(b == 0)
    def clear():
        load_weight(plan, row_ref, pieces, w_ref, sem_ref, acc_ref, sums_ref)

    @pl.when(b < many0 + many1)
    def block():
        hot = onehot_rows(jnp.where(early, pass0[0], pass1[0]))
        entry = jnp.where(early, tok0[...], tok1[...]).astype(f32) + dot_tn(hot, table_ref[...])
        at = jnp.where(early, b, b - many0) * ROWS + lax.broadcasted_iota(jnp.int32, (ROWS, 1), 0)
        live = at < jnp.where(early, len_ref[0], len_ref[1])
        heads = jnp.where(early, ho0[...], ho1[...])
        attention = dot_nn(heads, w_ref[:, 0:D])
        hidden = entry + attention
        unit, scale = normalized(hidden)
        gain = gain_ref[...]
        normed = (unit * gain).astype(bf16)
        grad_feed = jnp.where(live, cot[...].reshape(ROWS, D).astype(f32), 0.0).astype(bf16)
        @pl.when(b == 0)
        def rest_of_weight():
            for copy in weight_copies(plan, row_ref, pieces, w_ref, sem_ref, 1):
                copy.wait()

        feed = jnp.zeros((ROWS, D), f32)
        grad_normed = jnp.zeros((ROWS, D), f32)
        for k in range(CHUNKS):
            up = slice(D + k * D, D + (k + 1) * D)
            down = slice(D + FF + k * D, D + FF + (k + 1) * D)
            x = dot_nn(normed, w_ref[:, up])
            grad_act = dot_nt(grad_feed, w_ref[:, down])
            c0 = math.sqrt(2.0 / math.pi)
            square = x * x
            bent = jnp.tanh(x * (c0 + (c0 * 0.044715) * square))
            half = 0.5 + 0.5 * bent
            slope = half + (0.5 * x) * (1.0 - bent * bent) * (c0 + (3.0 * c0 * 0.044715) * square)
            act = (x * half).astype(bf16)
            grad_x = (slope * grad_act).astype(bf16)
            feed = feed + dot_nn(act, w_ref[:, down])
            grad_normed = grad_normed + dot_nt(grad_x, w_ref[:, up])
            acc_ref[:, up] += dot_tn(normed, grad_x)
            acc_ref[:, down] += dot_tn(act, grad_feed)
        res[...] = jnp.where(live, hidden + feed, 0.0).astype(bf16).reshape(res.shape)
        sums_ref[0:8] += fold_rows(grad_normed * unit)
        sums_ref[8:16] += fold_rows(jnp.where(live, entry * entry, 0.0))
        sums_ref[16:24] += fold_rows(jnp.where(live, attention * attention, 0.0))
        sums_ref[24:32] += fold_rows(jnp.where(live, feed * feed, 0.0))
        grad_hidden = grad_feed.astype(f32) + norm_back(grad_normed * gain, unit, scale)
        hid[...] = grad_hidden
        grad_attention = grad_hidden.astype(bf16)
        acc_ref[:, 0:D] += dot_tn(heads, grad_attention)
        gh[...] = dot_nt(grad_attention, w_ref[:, 0:D]).astype(bf16)

    @pl.when(b == pl.num_programs(0) - 1)
    def finish():
        counted = (len_ref[0] + len_ref[1]).astype(f32)
        small_ref[...] = jnp.full(small_ref.shape, counted, f32)
        for n in range(4):
            small_ref[n : n + 1] = jnp.sum(sums_ref[8 * n : 8 * n + 8], axis=0, keepdims=True)
        store_grads(plan, plan.wide_orders, grad_ref, acc_ref, outs, stage_ref, sem_ref)


def feed(plan, part, lengths, piece_rows, grad_rows, tokens, pass_rows, heads_out, cotangent, table, gain, pieces, width):
    rows = tokens[0].shape[0]
    per = ROWS // part

    def at0(b, n, r):
        return jnp.minimum(b, last_block(n[0])), 0

    def at1(b, n, r):
        return jnp.clip(b - last_block(n[0]) - 1, 0, last_block(n[1])), 0

    def both(b, n, r):
        early = b <= last_block(n[0])
        return jnp.where(early, b, at1(b, n, r)[0]), jnp.where(early, 0, 1)

    row0 = pl.BlockSpec((ROWS, D), at0)
    row1 = pl.BlockSpec((ROWS, D), at1)
    pas0 = pl.BlockSpec((1, 1, ROWS), lambda *a: at0(*a) + (0,))
    pas1 = pl.BlockSpec((1, 1, ROWS), lambda *a: at1(*a) + (0,))
    dealt = pl.BlockSpec((per, 1, part, D), lambda *a: both(*a) + (0, 0))
    local = pl.BlockSpec((None, ROWS, D), lambda *a: both(*a)[::-1] + (0,))
    grads = grad_shapes(plan, width, plan.wide_orders)
    anywhere = pl.BlockSpec(memory_space=pl.ANY)
    return pl.pallas_call(
        functools.partial(feed_kernel, plan),
        grid_spec=pltpu.PrefetchScalarGridSpec(
            num_scalar_prefetch=2,
            grid=(2 * rows // ROWS,),
            in_specs=[
                row0, row1, pas0, pas1, row0, row1, dealt,
                pl.BlockSpec((8, D), lambda *a: (0, 0)),
                pl.BlockSpec((1, D), lambda *a: (0, 0)),
                pl.BlockSpec(memory_space=pltpu.SMEM),
            ]
            + [anywhere] * len(pieces),
            out_specs=[dealt, local, local, pl.BlockSpec((8, D), lambda *a: (0, 0))] + [anywhere] * len(grads),
            scratch_shapes=[
                pltpu.VMEM((D, width), bf16),
                pltpu.VMEM((D, width), f32),
                pltpu.VMEM((32, D), f32),
                pltpu.VMEM(stage_shape(plan), bf16),
                pltpu.SemaphoreType.DMA((2,)),
            ],
        ),
        out_shape=[
            jax.ShapeDtypeStruct(cotangent.shape, bf16),
            jax.ShapeDtypeStruct((2, rows, D), bf16),
            jax.ShapeDtypeStruct((2, rows, D), f32),
            jax.ShapeDtypeStruct((8, D), f32),
        ]
        + grads,
        compiler_params=params(),
        cost_estimate=pl.CostEstimate(
            flops=2 * 6 * rows * D * width, bytes_accessed=2 * rows * D * 14 + D * width * 4, transcendentals=2 * rows * FF
        ),
        name="feed",
    )(lengths, piece_rows, tokens[0], tokens[1], pass_rows[0], pass_rows[1], heads_out[0], heads_out[1],
      cotangent, table, gain, grad_rows, *pieces)


def project_back_kernel(plan, weight, rows_back, final, len_ref, row_ref, grad_ref, tok_ref, pass_ref, g_ref, *rest):
    rest = list(rest)
    hid_ref = rest.pop(0) if rows_back else None
    table_ref, gain_ref = rest.pop(0), rest.pop(0)
    before_ref = rest.pop(0) if final else None
    many = plan.sharers if plan.paired else 1
    pieces = [rest.pop(0) for n in range(many)] if rows_back else []
    if rows_back:
        out_ref, small_ref = rest.pop(0), rest.pop(0)
    if weight and not final:
        acc_ref = rest.pop(0)
    outs = [rest.pop(0) for shape in grad_shapes(plan, 3 * D, plan.head_orders)] if final else []
    if rows_back:
        w_ref, sums_ref = rest.pop(0), rest.pop(0)
    if final:
        acc_ref, stage_ref = rest.pop(0), rest.pop(0)
    sem_ref = rest.pop(0)
    b = pl.program_id(0)

    @pl.when(b == 0)
    def clear():
        if rows_back:
            load_weight(plan, row_ref, pieces, w_ref, sem_ref, sums_ref, *([acc_ref] if weight and not final else []))
        if final:
            copy = pltpu.make_async_copy(before_ref, acc_ref, sem_ref.at[0])
            copy.start()
            copy.wait()

    @pl.when(b <= last_block(len_ref[0]))
    def work():
        hot = onehot_rows(pass_ref[0])
        entry = tok_ref[...].astype(f32) + dot_tn(hot, table_ref[...])
        unit, scale = normalized(entry)
        gain = gain_ref[...]
        if weight:
            normed = (unit * gain).astype(bf16)
            for part in range(3):
                acc_ref[:, part * D : (part + 1) * D] += dot_tn(normed, g_ref[part])
        if rows_back:
            grad_normed = jnp.zeros((ROWS, D), f32)
            for part in range(3):
                grad_normed = grad_normed + dot_nt(g_ref[part], w_ref[:, part * D : (part + 1) * D])
            sums_ref[0:8] += fold_rows(grad_normed * unit)
            grad_entry = hid_ref[...] + norm_back(grad_normed * gain, unit, scale)
            high = grad_entry.astype(bf16)
            out_ref[...] = high
            rest_one = grad_entry - high.astype(f32)
            low = rest_one.astype(bf16)
            lower = (rest_one - low.astype(f32)).astype(bf16)
            sums_ref[8:16] += dot_nn(hot, high) + dot_nn(hot, low) + dot_nn(hot, lower)

    if rows_back:
        @pl.when(b == pl.num_programs(0) - 1)
        def sums():
            small_ref[...] = sums_ref[8:16]
            small_ref[PASSES : PASSES + 1] = jnp.sum(sums_ref[0:8], axis=0, keepdims=True)

    if final:
        @pl.when(b == pl.num_programs(0) - 1)
        def finish():
            store_grads(plan, plan.head_orders, grad_ref, acc_ref, outs, stage_ref, sem_ref)


def project_back(
    plan, weight, rows_back, which, length, piece_rows, grad_rows, tokens, pass_rows, grads, grad_hidden, table, gain,
    pieces, before=None,
):
    rows = tokens.shape[0]
    final = before is not None
    at = lambda b, n, r, g: (jnp.minimum(b, last_block(n[0])), 0)
    row = pl.BlockSpec((ROWS, D), at)
    anywhere = pl.BlockSpec(memory_space=pl.ANY)
    in_specs = [
        row,
        pl.BlockSpec((1, 1, ROWS), lambda *a: at(*a) + (0,)),
        pl.BlockSpec((3, ROWS, D), lambda *a: (0,) + at(*a)),
    ]
    operands = [length, piece_rows, grad_rows, tokens, pass_rows, grads]
    if rows_back:
        in_specs.append(pl.BlockSpec((None, ROWS, D), lambda *a: (which,) + at(*a)))
        operands.append(grad_hidden)
    in_specs += [pl.BlockSpec((8, D), lambda *a: (0, 0)), pl.BlockSpec((1, D), lambda *a: (0, 0))]
    operands += [table, gain]
    out_shape, out_specs, scratch = [], [], []
    if final:
        in_specs.append(anywhere)
        operands.append(before)
    if rows_back:
        in_specs += [anywhere] * len(pieces)
        operands += pieces
        out_shape += [jax.ShapeDtypeStruct((rows, D), bf16), jax.ShapeDtypeStruct((8, D), f32)]
        out_specs += [row, pl.BlockSpec((8, D), lambda *a: (0, 0))]
        scratch += [pltpu.VMEM((D, 3 * D), bf16), pltpu.VMEM((16, D), f32)]
    if weight and not final:
        out_shape.append(jax.ShapeDtypeStruct((D, 3 * D), f32))
        out_specs.append(pl.BlockSpec((D, 3 * D), lambda *a: (0, 0)))
    if final:
        shapes = grad_shapes(plan, 3 * D, plan.head_orders)
        out_shape += shapes
        out_specs += [anywhere] * len(shapes)
        scratch += [pltpu.VMEM((D, 3 * D), f32), pltpu.VMEM(stage_shape(plan), bf16)]
    return pl.pallas_call(
        functools.partial(project_back_kernel, plan, weight, rows_back, final),
        grid_spec=pltpu.PrefetchScalarGridSpec(
            num_scalar_prefetch=3,
            grid=(rows // ROWS,),
            in_specs=in_specs,
            out_specs=out_specs,
            scratch_shapes=scratch + [pltpu.SemaphoreType.DMA((2,))],
        ),
        out_shape=out_shape,
        compiler_params=params(),
        cost_estimate=pl.CostEstimate(
            flops=2 * (weight + rows_back) * rows * D * 3 * D, bytes_accessed=rows * D * 14 + D * D * 6, transcendentals=0
        ),
        name="project_back",
    )(*operands)


def pick_kernel(index_ref, in_ref, out_ref, sem_ref):
    copies = [
        pltpu.make_async_copy(in_ref.at[index_ref[n]], out_ref.at[n], sem_ref) for n in range(out_ref.shape[0])
    ]
    for copy in copies:
        copy.start()
    for copy in copies:
        copy.wait()


def pick(index, blocks):
    shape = index.shape + blocks.shape[1:]
    return pl.pallas_call(
        pick_kernel,
        grid_spec=pltpu.PrefetchScalarGridSpec(
            num_scalar_prefetch=1,
            grid=(1,),
            in_specs=[pl.BlockSpec(memory_space=pl.ANY)],
            out_specs=pl.BlockSpec(shape, lambda b, n: (0, 0, 0)),
            scratch_shapes=[pltpu.SemaphoreType.DMA],
        ),
        out_shape=jax.ShapeDtypeStruct(shape, blocks.dtype),
        compiler_params=params(),
        cost_estimate=pl.CostEstimate(flops=0, bytes_accessed=4 * math.prod(shape), transcendentals=0),
        name="pick",
    )(index, blocks)


def settle_kernel(index_ref, *refs):
    arrays, out_ref = refs[:-1], refs[-1]
    first = pl.program_id(0) * out_ref.shape[0]
    rows = out_ref.shape[1]
    at = lax.broadcasted_iota(jnp.int32, (rows, 1), 0)
    for n in range(out_ref.shape[0]):
        live = at < index_ref[2, first + n]
        source, late = index_ref[1, first + n], index_ref[0, first + n]
        if len(arrays) == 1:
            found = arrays[0][2 * source + late]
        else:
            found = jnp.where(late == 0, arrays[0][source], arrays[1][source])
        out_ref[n] = jnp.where(live, found.astype(f32), 0.0)


def settle(index, *arrays):
    many = index.shape[1]
    step = 4
    shape = arrays[0].shape
    whole = pl.BlockSpec(shape, lambda b, n: (0, 0, 0), pipeline_mode=pl.Buffered(1))
    return pl.pallas_call(
        settle_kernel,
        grid_spec=pltpu.PrefetchScalarGridSpec(
            num_scalar_prefetch=1,
            grid=(many // step,),
            in_specs=[whole] * len(arrays),
            out_specs=pl.BlockSpec((step,) + shape[1:], lambda b, n: (b, 0, 0)),
        ),
        out_shape=jax.ShapeDtypeStruct((many,) + shape[1:], f32),
        compiler_params=params(),
        cost_estimate=pl.CostEstimate(flops=0, bytes_accessed=6 * many * math.prod(shape[1:]), transcendentals=0),
        name="settle",
    )(index, *arrays)


def after(values, *others):
    return lax.optimization_barrier((values, others))[0]


def swap(blocks):
    return lax.all_to_all(blocks, "dp", split_axis=0, concat_axis=0, tiled=True)


def per_device(
    groups,
    width_all,
    tokens,
    passes,
    lengths,
    dealing,
    pass_table,
    gain_first,
    to_heads,
    from_heads,
    gain_second,
    expand,
    shrink,
    cotangent,
):
    axes = ("dp", "fsdp")
    slots, part, unused_width = tokens.shape
    seq_len = part * groups
    order = jnp.arange(slots, dtype=jnp.int32)
    here = lax.axis_index("dp")
    ordering = dealing[0, 0]
    sizes = lengths[0]

    ahead = (sizes[None, :] > sizes[:, None]) | (
        (sizes[None, :] == sizes[:, None]) & (order[None, :] < order[:, None])
    )
    rank = jnp.sum(ahead.astype(jnp.int32), axis=1)
    ranked = jnp.sum(jnp.where(rank[None, :] == order[:, None], order[None, :], 0), axis=1)
    place = jnp.sum(jnp.where(ordering[None, :] == order[:, None], order[None, :], 0), axis=1)
    early_seqs = ranked[:groups]
    late_seqs = ranked[groups:][::-1]
    from_early = jnp.sum(jnp.where(early_seqs[:, None] == order[None, :], place[None, :], 0), axis=1)
    from_late = jnp.sum(jnp.where(late_seqs[:, None] == order[None, :], place[None, :], 0), axis=1)
    slot_rank = jnp.sum(jnp.where(ordering[:, None] == order[None, :], rank[None, :], 0), axis=1)
    slot_size = jnp.sum(jnp.where(ordering[:, None] == order[None, :], sizes[None, :], 0), axis=1)
    is_late = (slot_rank >= groups).astype(jnp.int32)
    source = jnp.where(is_late == 1, slots - 1 - slot_rank, slot_rank)
    back_index = jnp.stack([is_late, source, slot_size - here * part])
    my_seqs = jnp.stack([early_seqs[here], late_seqs[here]])
    my_sizes = jnp.sum(jnp.where(my_seqs[:, None] == order[None, :], sizes[None, :], 0), axis=1)

    row_count = to_heads.shape[0]
    narrow = jnp.concatenate(
        [
            from_heads,
            expand.reshape(row_count, D, CHUNKS).transpose(0, 2, 1).reshape(row_count, FF),
            shrink.reshape(row_count, CHUNKS * D),
        ],
        axis=1,
    )
    plan = Plan(groups, width_all // groups, row_count)
    index_here = here * (width_all // groups) + lax.axis_index("fsdp")
    my_passes = [passes[my_seqs[m]].reshape(seq_len // ROWS, 1, ROWS) for m in range(2)]
    one_size = [my_sizes[m : m + 1] for m in range(2)]
    table = jnp.zeros((8, D), bf16).at[:PASSES].set(pass_table)
    gain_one = gain_first.astype(f32).reshape(1, D)
    gain_two = gain_second.astype(f32).reshape(1, D)

    pairs_index = jnp.stack([from_early, from_late], axis=1).reshape(slots)
    picked = [pick(from_early, tokens), pick(from_late, tokens), pick(pairs_index, cotangent)]
    if plan.paired:
        piece_rows = plan.piece_rows(index_here)
        wide_rows = plan.grad_rows(index_here, plan.wide_orders)
        head_rows = plan.grad_rows(index_here, plan.head_orders)
        head_far = plan.gather(to_heads[None], plan.far)
        head_near = plan.gather(head_far, [plan.near])
        wide_one = plan.gather(after(narrow, head_far)[None], plan.far[:1])
        ready = (my_passes, one_size, piece_rows, table, gain_one)
        tokens0 = swap(after(picked[0], head_near, wide_one, ready))
        head_pieces = plan.gather_core(plan.gather_x(head_near))
    else:
        piece_rows = wide_rows = head_rows = jnp.zeros((1,), jnp.int32)
        head_pieces = (lax.all_gather(to_heads, axes, axis=0, tiled=True),)
        wide_pieces = (lax.all_gather(narrow, axes, axis=0, tiled=True),)
        tokens0 = swap(picked[0])
        wide_far = wide_pieces

    def forward(m, *gate):
        return project(
            plan, after(one_size[m], gate), piece_rows, my_tokens[m], my_passes[m], table, gain_one, head_pieces
        )

    def mix(m, *gate):
        return attend(after(one_size[m], gate), projected[m])

    half = HEADS // 4
    choices = {
        (m, first): jnp.stack([my_sizes[m], jnp.int32(m), jnp.int32(first)]) for m in range(2) for first in (0, half)
    }

    def mix_back(m, first, before, *gate):
        return attend_back(after(choices[m, first], gate), half, projected[m], heads_out[m], grad_heads, lse[m], before)

    def back(m, weight, rows_back, *gate, before=None):
        return project_back(
            plan, weight, rows_back, m, after(one_size[m], gate), piece_rows, head_rows, my_tokens[m], my_passes[m],
            grad_parts[m], grad_hidden, table, gain_one, head_pieces, before,
        )

    def send_back(rows, *gate):
        return swap(after(rows, gate).reshape(groups, part, D))

    projected, heads_out, lse, grad_parts = [None, None], [None, None], [None, None], [None, None]
    my_tokens = [tokens0.reshape(seq_len, D)]
    projected[0] = forward(0)
    if plan.paired:
        wide_far = plan.gather(wide_one, plan.far[1:], head_pieces, projected[0])
        cut = D + FF
    tokens1 = swap(after(picked[1], tokens0, picked[2], wide_far))
    my_tokens.append(tokens1.reshape(seq_len, D))
    heads_out[0], lse[0] = mix(0, wide_far)
    if plan.paired:
        first = plan.gather_near({0: wide_far[:, :, :cut]}, (), lse[0])
        second = plan.gather_x(wide_far[:, :, cut:], ())
        ready = (first, second)
    else:
        ready = ()
    my_grads = swap(after(picked[2].reshape(groups, 2, part, D), tokens1, lse[0], ready))
    projected[1] = forward(1, lse[0])
    if plan.paired:
        first = plan.gather_x(first[0])
        second = plan.gather_near(second, lse[0], projected[1])
    heads_out[1], lse[1] = mix(1)
    if plan.paired:
        wide_pieces = plan.gather_core(first, lse[1]) + plan.gather_core(second, lse[1])

    space = jax.ShapeDtypeStruct((3, seq_len, D), bf16)
    blanks = [blank(one_size[m], space) for m in range(2)]
    res, grad_heads, grad_hidden, feed_small, *wide_grads = feed(
        plan, part, after(my_sizes, choices, blanks), piece_rows, wide_rows, my_tokens, my_passes, heads_out, my_grads, table, gain_two,
        wide_pieces, D + 2 * FF,
    )

    def begin(grads):
        if not plan.paired:
            return lax.psum_scatter(grads[0], axes, scatter_dimension=0, tiled=True).astype(f32)
        return [grads[n : n + 2] for n in range(0, len(grads), 2)]

    def advance(state, stage, gate, late):
        return plan.reduce_stage(state, plan.wide_orders, stage, (gate,), (late,)) if plan.paired else state

    wide0 = begin(wide_grads)
    result = swap(res)
    some = mix_back(0, 0, blanks[0])
    wide1 = advance(wide0, 0, (), some)
    grad_parts[0] = mix_back(0, half, some, wide1)
    entry0, small0, head_sum = back(0, True, True)
    wide2 = advance(wide1, 1, some, entry0)
    moved0 = send_back(entry0, result)
    some = mix_back(1, 0, blanks[1], entry0, wide2, result)
    wide3 = advance(wide2, 2, entry0, some)
    grad_parts[1] = mix_back(1, half, some, wide3)
    entry1, small1 = back(1, False, True)
    wide_owned = advance(wide3, 3, some, entry1)
    moved1 = send_back(entry1, moved0, wide_owned)
    totals = jnp.concatenate([small0 + small1, feed_small], axis=0)
    stages = plan.head_orders[0]
    head_grads = back(1, True, False, entry1, moved0, before=head_sum)
    head_state = begin(head_grads)
    if plan.paired:
        totals = plan.total_stage(totals, stages[0], (), head_grads[:1])
        head_state = plan.reduce_stage(head_state, plan.head_orders, 0, (wide_owned,))
        wide_owned = wide_owned[0]
    output = settle(after(back_index, head_state), result.reshape(slots, part, D))
    grad_tokens = settle(after(back_index, output), moved0, moved1)
    grad_from = wide_owned[:, :D]
    grad_expand = wide_owned[:, D : D + FF].reshape(row_count, CHUNKS, D).transpose(0, 2, 1).reshape(row_count, FF)
    grad_shrink = wide_owned[:, D + FF :].reshape(row_count * CHUNKS, D)
    if plan.paired:
        totals = plan.total_stage(totals, stages[1])
        late = (output, grad_tokens, grad_from, grad_expand, grad_shrink)
        head_state = plan.reduce_stage(head_state, plan.head_orders, 1, (totals,), late)
        totals = plan.total_stage(totals, stages[2], (head_state,))
        head_owned = plan.reduce_stage(head_state, plan.head_orders, 2)[0]
    else:
        totals = lax.psum(totals, axes)
        head_owned = head_state
    root_squares = jnp.sqrt(jnp.sum(totals[9:12], axis=1) / (totals[12, 0] * D))

    return (
        output,
        grad_tokens,
        totals[:PASSES],
        totals[PASSES],
        head_owned,
        grad_from,
        totals[8],
        grad_expand,
        grad_shrink,
        root_squares,
    )


def solution(mesh):
    groups = mesh.shape["dp"]
    weight_spec = P(("dp", "fsdp"), None)
    block_spec = P("fsdp", "dp", None)
    in_specs = (
        block_spec,
        P("fsdp", None),
        P("fsdp", None),
        P("dp", "fsdp", None),
        P(),
        P(),
        weight_spec,
        weight_spec,
        P(),
        weight_spec,
        weight_spec,
        block_spec,
    )
    out_specs = (
        block_spec,
        block_spec,
        P(),
        P(),
        weight_spec,
        weight_spec,
        P(),
        weight_spec,
        weight_spec,
        P(),
    )
    body = functools.partial(per_device, groups, groups * mesh.shape["fsdp"])
    return jax.shard_map(body, mesh=mesh, in_specs=in_specs, out_specs=out_specs, check_vma=False)
```
